32 devices in a mesh: fsdp: 2 (over x), context: 8 (over z, core), tensor: 2 (over y).
Axes of the slice: x: 2, y: 2, z: 4, core: 2. Of those that a mesh axis runs over, the one named last changes fastest.
Arguments:
- inputs: bfloat16 [2, 1024, 768], P('fsdp', 'context'), may hold values from -6 to 6
- memory: bfloat16 [2, 40, 768], P('fsdp', 'context'), may hold values from -6 to 6
- teacher: bfloat16 [2, 1024, 768], P('fsdp', 'context'), may hold values from -6 to 6
- segments: int32 [2, 1024], P('fsdp', 'context'), may hold values from 0 to 1, as said below
- memory_owner: int32 [2, 40], P('fsdp', 'context'), may hold values from 0 to 1, as said below
- valid_mask: int32 [2, 1024], P('fsdp', 'context'), may hold values from 0 to 1
- attention_gain: bfloat16 [768], P(('fsdp', 'context')), may hold values from 0.5 to 1.5
- query_weight: bfloat16 [768, 768], P(('fsdp', 'context'), 'tensor'), may hold values from -0.109375 to 0.109375
- key_weight: bfloat16 [768, 768], P(('fsdp', 'context'), 'tensor'), may hold values from -0.109375 to 0.109375
- value_weight: bfloat16 [768, 768], P(('fsdp', 'context'), 'tensor'), may hold values from -0.21875 to 0.21875
- attention_out_weight: bfloat16 [768, 768], P(('fsdp', 'context'), 'tensor'), may hold values from -0.875 to 0.875
- position_bias: bfloat16 [12, 32], P('tensor'), may hold values from -4 to 4
- feedforward_gain: bfloat16 [768], P(('fsdp', 'context')), may hold values from 0.5 to 1.5
- inner_weight: bfloat16 [768, 3072], P(('fsdp', 'context'), 'tensor'), may hold values from -0.21875 to 0.21875
- feedforward_out_weight: bfloat16 [768, 3072], P(('fsdp', 'context'), 'tensor'), may hold values from -0.15625 to 0.15625
Outputs:
- loss: float32 [], replicated
- output: bfloat16 [2, 1024, 768], P('fsdp', 'context')
- grad_inputs: float32 [2, 1024, 768], P('fsdp', 'context')
- grad_memory: float32 [2, 40, 768], P('fsdp', 'context')
- grad_attention_gain: float32 [768], P(('fsdp', 'context'))
- grad_query_weight: float32 [768, 768], P(('fsdp', 'context'), 'tensor')
- grad_key_weight: float32 [768, 768], P(('fsdp', 'context'), 'tensor')
- grad_value_weight: float32 [768, 768], P(('fsdp', 'context'), 'tensor')
- grad_output_weight: float32 [768, 768], P(('fsdp', 'context'), 'tensor')
- grad_position_bias: float32 [12, 32], P('tensor')
- grad_feedforward_gain: float32 [768], P(('fsdp', 'context'))
- grad_inner_weight: float32 [768, 3072], P(('fsdp', 'context'), 'tensor')
- grad_outer_weight: float32 [768, 3072], P(('fsdp', 'context'), 'tensor')
The draws below stay inside these ranges and needn't reach their ends.
Inputs may be any that keep to these rules, and one draw needn't show every extreme that they name: `segments`: within a sequence the ids never fall; each of the 2 documents is one run of 200 or more tokens. `memory_owner`: each document of a sequence is named by exactly 20 memory slots of that sequence.
All inputs are finite; a program needn't handle non-finite values.
Results may differ from the reference program's by a relative error of at most 0.017.
Values may be sent and summed in bfloat16 or wider, within the bound.
No kernel may reach another device: no remote copies, remote signals or barrier semaphores. Data moves between devices by JAX's collectives and lax.ppermute only.
A program may use at most 192 MiB of HBM per device.

```python
import jax
import jax.numpy as jnp
from jax import lax

D = 768
H = 12
DH = 64
FF = 3072
BUCKETS = 32
MEM = 20
DOC_MIN = 200
INNER = 768
LEN = 1024
SEQS = 2
DOCS = 2
MSLOTS = 40


def draw_segments(key, part):
    weights = jax.random.randint(key, (SEQS, DOCS), 1, 1000, dtype=jnp.int32)
    spare = LEN - DOCS * DOC_MIN
    shares = spare * weights // jnp.sum(weights, axis=1, keepdims=True)
    leftover = spare - jnp.sum(shares, axis=1, keepdims=True)
    shares = jnp.concatenate([shares[:, :1] + leftover, shares[:, 1:]], axis=1)
    ends = jnp.cumsum(shares + DOC_MIN, axis=1).astype(jnp.int32)
    places = jnp.arange(LEN, dtype=jnp.int32)
    return jnp.sum((places[None, :, None] >= ends[:, None, :]).astype(jnp.int32), axis=2).astype(jnp.int32)


def draw_memory_owner(key, part):
    sub_keys = jax.random.split(key, SEQS)
    orders = jax.vmap(lambda sub_key: jax.random.permutation(sub_key, MSLOTS))(sub_keys)
    return (orders // MEM).astype(jnp.int32)


def draw_valid_mask(key, part):
    rolls = jax.random.randint(key, (SEQS, LEN), 0, 100, dtype=jnp.int32)
    flat_places = jnp.arange(SEQS * LEN, dtype=jnp.int32).reshape(SEQS, LEN)
    limits = 15 + 75 * flat_places // (SEQS * LEN)
    return (rolls < limits).astype(jnp.int32)


def levels(stream_key, dims, pieces, smallest, high):
    def one(axis_at, shards_of):
        heights = jax.random.uniform(jax.random.fold_in(jax.random.fold_in(stream_key, 6), axis_at), (shards_of,), jnp.float32, smallest / len(pieces), high / len(pieces))
        return jnp.repeat(jnp.exp(heights), dims[axis_at] // shards_of).reshape((-1,) + (1,) * (len(dims) - axis_at - 1))

    factor_of = one(*pieces[0])
    for cut in pieces[1:]:
        factor_of = factor_of * one(*cut)
    return factor_of


def scatter_about(stream_key, dims, spread, reach, pieces=(), kind=jnp.bfloat16):
    values = jax.random.normal(stream_key, dims, jnp.float32) * spread
    if len(pieces) > 0:
        values = levels(stream_key, dims, pieces, -0.22, 0.18) * values
    return jnp.clip(values, min=-reach, max=reach).astype(kind)


def setup_inputs(seed: int = 0) -> dict:
    seeds = jax.random.split(jax.random.key(seed), 16)
    return {
        "inputs": scatter_about(seeds[0], (SEQS, LEN, D), 1.0, 6.0, ((0, 2), (1, 8))),
        "memory": scatter_about(seeds[1], (SEQS, MSLOTS, D), 1.0, 6.0, ((0, 2), (1, 8))),
        "teacher": scatter_about(seeds[2], (SEQS, LEN, D), 1.0, 6.0, ((0, 2), (1, 8))),
        "segments": draw_segments(jax.random.fold_in(seeds[15], 71), 0),
        "memory_owner": draw_memory_owner(jax.random.fold_in(seeds[15], 71), 0),
        "valid_mask": draw_valid_mask(jax.random.fold_in(seeds[15], 71), 0),
        "attention_gain": jnp.clip(1.0 + 0.1 * jax.random.normal(seeds[6], (D,), jnp.float32), 0.5, 1.5).astype(jnp.bfloat16),
        "query_weight": scatter_about(seeds[7], (D, INNER), (4 * D) ** -0.5, 0.109375, ((0, 16), (1, 2))),
        "key_weight": scatter_about(seeds[8], (D, INNER), (4 * D) ** -0.5, 0.109375, ((0, 16), (1, 2))),
        "value_weight": scatter_about(seeds[9], (D, INNER), D ** -0.5, 0.21875, ((0, 16), (1, 2))),
        "attention_out_weight": scatter_about(seeds[10], (D, INNER), (INNER // 16) ** -0.5, 0.875, ((0, 16), (1, 2))),
        "position_bias": scatter_about(seeds[11], (H, BUCKETS), 1.0, 4.0, ((0, 2),)),
        "feedforward_gain": jnp.clip(1.0 + 0.1 * jax.random.normal(seeds[12], (D,), jnp.float32), 0.5, 1.5).astype(jnp.bfloat16),
        "inner_weight": scatter_about(seeds[13], (D, FF), D ** -0.5, 0.21875, ((0, 16), (1, 2))),
        "feedforward_out_weight": scatter_about(seeds[14], (D, FF), (FF // 2) ** -0.5, 0.15625, ((0, 16), (1, 2))),
    }


norm_eps = 1e-06
score_floor = -1e+30
highest_precision = lax.Precision.HIGHEST

@jax.custom_vjp
def low(v):
    return lax.optimization_barrier(v.astype(jnp.bfloat16)).astype(jnp.float32)

@jax.custom_vjp
def low_back(v):
    return v

def low_keep(v):
    return (low(v), None)

def low_pass(kept, grad):
    return (grad,)

def back_keep(v):
    return (v, None)

def back_low(kept, grad):
    return (low(grad),)
low.defvjp(low_keep, low_pass)
low_back.defvjp(back_keep, back_low)

def relative_bucket(distance):
    half_count = BUCKETS // 2
    exact_count = half_count // 2
    magnitude = jnp.minimum(jnp.abs(distance), 1024).astype(jnp.int32)
    far_bucket = jnp.full(distance.shape, exact_count, jnp.int32)
    for level_index in range(1, half_count - exact_count):
        far_bucket = far_bucket + (magnitude * magnitude >= exact_count * exact_count * 2 ** level_index).astype(jnp.int32)
    bucket_ids = jnp.where(magnitude < exact_count, magnitude, far_bucket)
    return (bucket_ids + (distance > 0).astype(jnp.int32) * half_count).astype(jnp.int32)

def rms_norm(values, gain_in):
    return values * lax.rsqrt(lax.optimization_barrier(jnp.mean(values * values, axis=-1, keepdims=True)) + norm_eps) * gain_in

def attend_sequence(packed, bias_table):
    queries, key_rows, value_rows, query_docs, key_docs = packed
    key_count = key_rows.shape[0]
    key_place = jnp.concatenate([jnp.arange(LEN, dtype=jnp.int32), jnp.zeros((MSLOTS,), jnp.int32)])
    key_token = jnp.arange(key_count, dtype=jnp.int32) < LEN
    tile_rows = min(256, LEN)
    tiles = LEN // tile_rows
    query_tiles = queries.reshape(tiles, tile_rows, H, DH)
    place_tiles = jnp.arange(LEN, dtype=jnp.int32).reshape(tiles, tile_rows)
    doc_tiles = query_docs.reshape(tiles, tile_rows)

    def one_block(block_parts):
        query_blk, query_place, doc_blk = block_parts
        scores = jnp.einsum('qhd,khd->hqk', query_blk, key_rows, precision=highest_precision)
        bucket = relative_bucket(key_place[None, :] - query_place[:, None])
        rel_terms = jnp.where(key_token[None, None, :], jnp.take(bias_table, bucket, axis=1), 0.0)
        scores = low_back(scores + rel_terms)
        same_doc = (doc_blk[:, None] == key_docs[None, :])[None]
        scores = jnp.where(same_doc, scores, score_floor)
        probabilities = jax.nn.softmax(scores, axis=-1)
        return jnp.einsum('hqk,khd->qhd', low(probabilities), value_rows, precision=highest_precision)
    result = lax.map(jax.checkpoint(one_block), (query_tiles, place_tiles, doc_tiles))
    return result.reshape(LEN, H * DH)

def forward(inputs, memory, teacher, attention_gain, query_weight, key_weight, value_weight, attention_out_weight, position_bias, feedforward_gain, inner_weight, feedforward_out_weight, segments, memory_owner, valid_mask):
    normed = low(rms_norm(inputs, attention_gain))
    memory_normed = low(rms_norm(memory, attention_gain))
    both_rows = jnp.concatenate([normed, memory_normed], axis=1)
    queries = low(low_back(jnp.dot(normed, query_weight, precision=highest_precision)))
    key_rows = low(low_back(jnp.dot(both_rows, key_weight, precision=highest_precision)))
    value_rows = low(low_back(jnp.dot(both_rows, value_weight, precision=highest_precision)))
    key_docs = jnp.concatenate([segments, memory_owner], axis=1)
    key_count = LEN + MSLOTS
    attended_values = lax.map(lambda packed: attend_sequence(packed, position_bias), (queries.reshape(SEQS, LEN, H, DH), key_rows.reshape(SEQS, key_count, H, DH), value_rows.reshape(SEQS, key_count, H, DH), segments, key_docs))
    attended_values = low(low_back(attended_values))
    attention_output = low_back(jnp.einsum('ypw,kw->ypk', attended_values, attention_out_weight, precision=highest_precision))
    residual = inputs + attention_output
    dense_normed = low(rms_norm(residual, feedforward_gain))
    inner_pre = low_back(jnp.dot(dense_normed, inner_weight, precision=highest_precision))
    hidden_units = low(jax.nn.gelu(inner_pre, approximate=True))
    dense_output = low_back(jnp.einsum('zta,ba->ztb', hidden_units, feedforward_out_weight, precision=highest_precision))
    result = residual + dense_output
    weights_mask = valid_mask.astype(jnp.float32)
    token_count = jnp.sum(weights_mask)
    misfit = result - teacher
    loss_value = 0.5 * jnp.sum(weights_mask[..., None] * misfit * misfit) / (token_count * D)
    return (loss_value, result)

def reference(inputs, memory, teacher, segments, memory_owner, valid_mask, attention_gain, query_weight, key_weight, value_weight, attention_out_weight, position_bias, feedforward_gain, inner_weight, feedforward_out_weight):
    floats = tuple((item.astype(jnp.float32) for item in (inputs, memory, teacher, attention_gain, query_weight, key_weight, value_weight, attention_out_weight, position_bias, feedforward_gain, inner_weight, feedforward_out_weight)))

    def wrapped(*float_args):
        loss_value, result = forward(*float_args, segments, memory_owner, valid_mask)
        return (loss_value, result)
    loss_value, pullback, result = jax.vjp(wrapped, *floats, has_aux=True)
    scale_factor = jnp.asarray(float(SEQS * LEN * D), dtype=loss_value.dtype)
    gradients = pullback(scale_factor)
    grad_inputs, grad_memory, grad_teacher, grad_attention_gain, grad_query, grad_key, grad_value, grad_output, grad_bias, grad_feedforward_gain, grad_inner, grad_outer = gradients
    return (loss_value.astype(jnp.float32), result.astype(jnp.bfloat16), grad_inputs.astype(jnp.float32), grad_memory.astype(jnp.float32), grad_attention_gain.astype(jnp.float32), grad_query.astype(jnp.float32), grad_key.astype(jnp.float32), grad_value.astype(jnp.float32), grad_output.astype(jnp.float32), grad_bias.astype(jnp.float32), grad_feedforward_gain.astype(jnp.float32), grad_inner.astype(jnp.float32), grad_outer.astype(jnp.float32))
```

```python
import jax
import jax.numpy as jnp
from jax import lax
from jax.experimental import pallas as pl
from jax.experimental.pallas import tpu as pltpu
from jax.sharding import PartitionSpec as P

BUCKETS = 32


norm_eps = 1e-06
score_floor = -1e30


def relative_bucket(distance):
    half_count = BUCKETS // 2
    exact_count = half_count // 2
    magnitude = jnp.minimum(jnp.abs(distance), 1024)
    far_bucket = jnp.full(distance.shape, exact_count, jnp.int32)
    for level_index in range(1, half_count - exact_count):
        far_bucket = far_bucket + (
            magnitude * magnitude >= exact_count * exact_count * 2**level_index
        ).astype(jnp.int32)
    bucket_ids = jnp.where(magnitude < exact_count, magnitude, far_bucket)
    return bucket_ids + (distance > 0).astype(jnp.int32) * half_count


def rms_norm(values, gain_in):
    inv_rms = lax.rsqrt(jnp.mean(values * values, axis=-1, keepdims=True) + norm_eps)
    return (values * inv_rms * gain_in, inv_rms)


def norm_back(values, inv_rms, gain_in, grad_in):
    scaled = grad_in * gain_in
    inner_mean = jnp.mean(scaled * values, axis=-1, keepdims=True)
    grad_values = inv_rms * scaled - values * inv_rms * inv_rms * inv_rms * inner_mean
    grad_gain = jnp.sum(grad_in * values * inv_rms, axis=tuple(range(values.ndim - 1)))
    return (grad_values, grad_gain)


def smooth_gate(values):
    return jax.nn.gelu(values, approximate=True)


def block_size():
    return 512


def pad_rows(values_in, block_rows, fill_value):
    blocks = -(-values_in.shape[1] // block_rows)
    missing = blocks * block_rows - values_in.shape[1]
    padding = [(0, 0)] * values_in.ndim
    padding[1] = (0, missing)
    return (jnp.pad(values_in, padding, constant_values=fill_value), blocks)


def key_places(row_ids, shard_rows, key_span):
    within = row_ids % key_span
    return (row_ids // key_span * shard_rows + within, within < shard_rows)


def scores_with_bias(
    query_blk, key_blk, query_place, query_doc, key_place, key_doc, key_token, bias_table
):
    scores = jnp.einsum("sqhd,skhd->sqhk", query_blk, key_blk, preferred_element_type=jnp.float32)
    bucket = relative_bucket(key_place[None, :] - query_place[:, None])
    rel_terms = jnp.where(key_token[None, None, :], jnp.take(bias_table, bucket, axis=1), 0.0)
    scores = scores + jnp.moveaxis(rel_terms, 0, 1)[None]
    same_doc = (query_doc[:, :, None] == key_doc[:, None, :])[:, :, None, :]
    return (scores, same_doc, bucket)


def sum_grads(grad_items):
    return (
        lax.psum_scatter(grad_items[0], ("fsdp", "context"), scatter_dimension=0, tiled=True),
        lax.psum_scatter(grad_items[1], ("fsdp", "context"), scatter_dimension=0, tiled=True),
        lax.psum_scatter(grad_items[2], ("fsdp", "context"), scatter_dimension=0, tiled=True),
        lax.psum_scatter(grad_items[3], ("fsdp", "context"), scatter_dimension=0, tiled=True),
        lax.psum_scatter(grad_items[4], ("fsdp", "context"), scatter_dimension=0, tiled=True),
        lax.psum_scatter(grad_items[5], ("fsdp", "context"), scatter_dimension=0, tiled=True),
        lax.psum_scatter(grad_items[6], ("fsdp", "context"), scatter_dimension=0, tiled=True),
        lax.psum_scatter(grad_items[7], ("fsdp", "context"), scatter_dimension=0, tiled=True),
    )


def general_local(
    inputs,
    memory,
    teacher,
    segments,
    memory_owner,
    valid_mask,
    attention_gain,
    query_weight,
    key_weight,
    value_weight,
    attention_out_weight,
    position_bias,
    feedforward_gain,
    inner_weight,
    feedforward_out_weight,
):
    sequences, shard_rows, model_width = inputs.shape
    key_span = shard_rows + memory.shape[1]
    context_size = lax.axis_size("context")
    length = shard_rows * context_size
    context_place = lax.axis_index("context")
    local_heads = position_bias.shape[0]
    bucket_count = position_bias.shape[1]
    head_size = query_weight.shape[1] // local_heads
    local_inner = local_heads * head_size
    total_rows = sequences * length * lax.axis_size("fsdp")
    bias_table = position_bias.astype(jnp.float32)
    (
        full_query,
        full_key,
        full_value,
        full_output,
        full_inner,
        full_outer,
        full_attn_gain,
        full_dense_gain,
    ) = (
        lax.all_gather(query_weight, ("fsdp", "context"), axis=0, tiled=True),
        lax.all_gather(key_weight, ("fsdp", "context"), axis=0, tiled=True),
        lax.all_gather(value_weight, ("fsdp", "context"), axis=0, tiled=True),
        lax.all_gather(attention_out_weight, ("fsdp", "context"), axis=0, tiled=True),
        lax.all_gather(inner_weight, ("fsdp", "context"), axis=0, tiled=True),
        lax.all_gather(feedforward_out_weight, ("fsdp", "context"), axis=0, tiled=True),
        lax.all_gather(attention_gain, ("fsdp", "context"), axis=0, tiled=True),
        lax.all_gather(feedforward_gain, ("fsdp", "context"), axis=0, tiled=True),
    )
    attn_gain = full_attn_gain.astype(jnp.float32)
    dense_gain = full_dense_gain.astype(jnp.float32)
    local_docs = jnp.concatenate([segments, memory_owner], axis=1)
    key_docs = lax.all_gather(local_docs, "context", axis=1, tiled=True)
    query_docs_all = key_docs.reshape(sequences, context_size, key_span)[:, :, :shard_rows].reshape(
        sequences, length
    )
    token_count = lax.psum(jnp.sum(valid_mask.astype(jnp.float32)), ("fsdp", "context"))
    inputs_float = inputs.astype(jnp.float32)
    memory_float = memory.astype(jnp.float32)
    normed, input_scale = rms_norm(inputs_float, attn_gain)
    memory_normed, memory_scale = rms_norm(memory_float, attn_gain)
    normed_low = normed.astype(jnp.bfloat16)
    both_rows = jnp.concatenate([normed_low, memory_normed.astype(jnp.bfloat16)], axis=1)
    queries = jnp.dot(normed_low, full_query, preferred_element_type=jnp.float32).astype(
        jnp.bfloat16
    )
    key_local = jnp.dot(both_rows, full_key, preferred_element_type=jnp.float32).astype(
        jnp.bfloat16
    )
    value_local = jnp.dot(both_rows, full_value, preferred_element_type=jnp.float32).astype(
        jnp.bfloat16
    )
    query_heads = queries.reshape(sequences, shard_rows, local_heads, head_size)
    query_place = context_place * shard_rows + jnp.arange(shard_rows, dtype=jnp.int32)
    fold_init = (
        jnp.full((sequences, shard_rows, local_heads), score_floor, jnp.float32),
        jnp.zeros((sequences, shard_rows, local_heads), jnp.float32),
        jnp.zeros((sequences, shard_rows, local_heads, head_size), jnp.float32),
    )
    fold_state = fold_init
    key_piece = lax.all_gather(key_local, "context", axis=1, tiled=True)
    value_piece = lax.all_gather(value_local, "context", axis=1, tiled=True)
    block_rows = block_size()
    key_pad, blocks = pad_rows(key_piece, block_rows, 0)
    value_pad, blocks = pad_rows(value_piece, block_rows, 0)
    doc_pad, blocks = pad_rows(key_docs, block_rows, -1)

    def attend_advance(running, block_index):
        running_best, running_sum, summed = running
        offset = block_index * block_rows
        key_blk = lax.dynamic_slice_in_dim(key_pad, offset, block_rows, 1).reshape(
            sequences, block_rows, local_heads, head_size
        )
        value_blk = lax.dynamic_slice_in_dim(value_pad, offset, block_rows, 1).reshape(
            sequences, block_rows, local_heads, head_size
        )
        doc_blk = lax.dynamic_slice_in_dim(doc_pad, offset, block_rows, 1)
        key_place, key_token = key_places(
            offset + jnp.arange(block_rows, dtype=jnp.int32), shard_rows, key_span
        )
        scores, same_doc, bucket = scores_with_bias(
            query_heads, key_blk, query_place, segments, key_place, doc_blk, key_token, bias_table
        )
        masked = jnp.where(same_doc, scores, score_floor)
        new_best = jnp.maximum(running_best, jnp.max(masked, axis=-1))
        weights = jnp.where(same_doc, jnp.exp(scores - new_best[..., None]), 0.0)
        factor = jnp.exp(running_best - new_best)
        running_sum = running_sum * factor + jnp.sum(weights, axis=-1)
        summed = summed * factor[..., None] + jnp.einsum(
            "sqhk,skhd->sqhd",
            weights.astype(jnp.bfloat16),
            value_blk,
            preferred_element_type=jnp.float32,
        )
        return ((new_best, running_sum, summed), None)

    fold_state, unused = lax.scan(attend_advance, fold_state, jnp.arange(blocks, dtype=jnp.int32))
    running_best, running_sum, summed = fold_state
    attended_values = summed / running_sum[..., None]
    attended_low = attended_values.reshape(sequences, shard_rows, local_inner).astype(jnp.bfloat16)
    attention_part = jnp.einsum(
        "sci,di->scd", attended_low, full_output, preferred_element_type=jnp.float32
    )
    residual = inputs_float + lax.psum(attention_part.astype(jnp.bfloat16), "tensor").astype(
        jnp.float32
    )
    dense_normed, dense_scale = rms_norm(residual, dense_gain)
    dense_low = dense_normed.astype(jnp.bfloat16)
    inner_pre = jnp.dot(dense_low, full_inner, preferred_element_type=jnp.float32)
    hidden_float, gate_pullback = jax.vjp(smooth_gate, inner_pre)
    hidden_low = hidden_float.astype(jnp.bfloat16)
    dense_part = jnp.einsum(
        "scf,df->scd", hidden_low, full_outer, preferred_element_type=jnp.float32
    )
    result = residual + lax.psum(dense_part.astype(jnp.bfloat16), "tensor").astype(jnp.float32)
    target_mask = valid_mask.astype(jnp.float32)[..., None]
    misfit = result - teacher.astype(jnp.float32)
    loss_local = 0.5 * jnp.sum(target_mask * misfit * misfit)
    grad_result = total_rows / token_count * target_mask * misfit
    dense_back = grad_result.astype(jnp.bfloat16)
    grad_outer = jnp.einsum(
        "scd,scf->df", dense_back, hidden_low, preferred_element_type=jnp.float32
    )
    grad_hidden = jnp.einsum(
        "scd,df->scf", dense_back, full_outer, preferred_element_type=jnp.float32
    )
    grad_pre = gate_pullback(grad_hidden)[0].astype(jnp.bfloat16)
    grad_inner = jnp.einsum("scd,scf->df", dense_low, grad_pre, preferred_element_type=jnp.float32)
    grad_dense_part = jnp.einsum(
        "scf,df->scd", grad_pre, full_inner, preferred_element_type=jnp.float32
    )
    grad_dense_normed = lax.psum(grad_dense_part.astype(jnp.bfloat16), "tensor").astype(jnp.float32)
    back_residual, grad_dense_gain = norm_back(residual, dense_scale, dense_gain, grad_dense_normed)
    grad_residual = grad_result + back_residual
    attention_back = grad_residual.astype(jnp.bfloat16)
    grad_output = jnp.einsum(
        "scd,sci->di", attention_back, attended_low, preferred_element_type=jnp.float32
    )
    grad_attended = jnp.einsum(
        "scd,di->sci", attention_back, full_output, preferred_element_type=jnp.float32
    ).astype(jnp.bfloat16)
    grad_heads = grad_attended.reshape(sequences, shard_rows, local_heads, head_size)
    log_total = running_best + jnp.log(running_sum)
    delta_rows = jnp.sum(grad_heads.astype(jnp.float32) * attended_values, axis=-1)
    all_log_total, all_delta = (
        lax.all_gather(log_total, "context", axis=1, tiled=True),
        lax.all_gather(delta_rows, "context", axis=1, tiled=True),
    )
    query_init = (
        jnp.zeros((sequences, shard_rows, local_heads, head_size), jnp.float32),
        jnp.zeros((local_heads, bucket_count), jnp.float32),
    )
    fold_state = query_init
    key_piece = lax.all_gather(key_local, "context", axis=1, tiled=True)
    value_piece = lax.all_gather(value_local, "context", axis=1, tiled=True)
    query_block_rows = block_size()
    query_key_pad, blocks = pad_rows(key_piece, query_block_rows, 0)
    query_value_pad, blocks = pad_rows(value_piece, query_block_rows, 0)
    query_doc_pad, blocks = pad_rows(key_docs, query_block_rows, -1)

    def query_advance(running, block_index):
        grad_query, grad_bias = running
        offset = block_index * query_block_rows
        key_blk = lax.dynamic_slice_in_dim(query_key_pad, offset, query_block_rows, 1).reshape(
            sequences, query_block_rows, local_heads, head_size
        )
        value_blk = lax.dynamic_slice_in_dim(query_value_pad, offset, query_block_rows, 1).reshape(
            sequences, query_block_rows, local_heads, head_size
        )
        doc_blk = lax.dynamic_slice_in_dim(query_doc_pad, offset, query_block_rows, 1)
        key_place, key_token = key_places(
            offset + jnp.arange(query_block_rows, dtype=jnp.int32), shard_rows, key_span
        )
        scores, same_doc, bucket = scores_with_bias(
            query_heads, key_blk, query_place, segments, key_place, doc_blk, key_token, bias_table
        )
        probabilities = jnp.where(same_doc, jnp.exp(scores - log_total[..., None]), 0.0)
        value_dots = jnp.einsum(
            "sqhd,skhd->sqhk", grad_heads, value_blk, preferred_element_type=jnp.float32
        )
        grad_scores = (probabilities * (value_dots - delta_rows[..., None])).astype(jnp.bfloat16)
        grad_query = grad_query + jnp.einsum(
            "sqhk,skhd->sqhd", grad_scores, key_blk, preferred_element_type=jnp.float32
        )
        bucket_hits = (
            (bucket[:, :, None] == jnp.arange(bucket_count, dtype=jnp.int32)[None, None, :])
            & key_token[None, :, None]
        ).astype(jnp.bfloat16)
        grad_bias = grad_bias + jnp.einsum(
            "sqhk,qkb->hb", grad_scores, bucket_hits, preferred_element_type=jnp.float32
        )
        return ((grad_query, grad_bias), None)

    fold_state, unused = lax.scan(query_advance, fold_state, jnp.arange(blocks, dtype=jnp.int32))
    grad_query, grad_bias = fold_state
    key_heads = key_local.reshape(sequences, key_span, local_heads, head_size)
    value_heads = value_local.reshape(sequences, key_span, local_heads, head_size)
    local_place, local_token = key_places(
        context_place * key_span + jnp.arange(key_span, dtype=jnp.int32), shard_rows, key_span
    )
    key_init = (
        jnp.zeros((sequences, key_span, local_heads, head_size), jnp.float32),
        jnp.zeros((sequences, key_span, local_heads, head_size), jnp.float32),
    )
    fold_state = key_init
    query_piece = lax.all_gather(queries, "context", axis=1, tiled=True)
    grad_piece = lax.all_gather(grad_attended, "context", axis=1, tiled=True)
    key_block_rows = block_size()
    query_pad, blocks = pad_rows(query_piece, key_block_rows, 0)
    grad_pad, blocks = pad_rows(grad_piece, key_block_rows, 0)
    key_doc_pad, blocks = pad_rows(query_docs_all, key_block_rows, -1)
    total_pad, blocks = pad_rows(all_log_total, key_block_rows, 0.0)
    delta_pad, blocks = pad_rows(all_delta, key_block_rows, 0.0)

    def key_advance(running, block_index):
        grad_key, grad_value = running
        offset = block_index * key_block_rows
        query_blk = lax.dynamic_slice_in_dim(query_pad, offset, key_block_rows, 1).reshape(
            sequences, key_block_rows, local_heads, head_size
        )
        grad_blk = lax.dynamic_slice_in_dim(grad_pad, offset, key_block_rows, 1).reshape(
            sequences, key_block_rows, local_heads, head_size
        )
        doc_blk = lax.dynamic_slice_in_dim(key_doc_pad, offset, key_block_rows, 1)
        total_blk = lax.dynamic_slice_in_dim(total_pad, offset, key_block_rows, 1)
        delta_blk = lax.dynamic_slice_in_dim(delta_pad, offset, key_block_rows, 1)
        row_place = offset + jnp.arange(key_block_rows, dtype=jnp.int32)
        scores, same_doc, bucket = scores_with_bias(
            query_blk,
            key_heads,
            row_place,
            doc_blk,
            local_place,
            local_docs,
            local_token,
            bias_table,
        )
        probabilities = jnp.where(same_doc, jnp.exp(scores - total_blk[..., None]), 0.0)
        grad_value = grad_value + jnp.einsum(
            "sqhk,sqhd->skhd",
            probabilities.astype(jnp.bfloat16),
            grad_blk,
            preferred_element_type=jnp.float32,
        )
        value_dots = jnp.einsum(
            "sqhd,skhd->sqhk", grad_blk, value_heads, preferred_element_type=jnp.float32
        )
        grad_scores = (probabilities * (value_dots - delta_blk[..., None])).astype(jnp.bfloat16)
        grad_key = grad_key + jnp.einsum(
            "sqhk,sqhd->skhd", grad_scores, query_blk, preferred_element_type=jnp.float32
        )
        return ((grad_key, grad_value), None)

    fold_state, unused = lax.scan(key_advance, fold_state, jnp.arange(blocks, dtype=jnp.int32))
    grad_key, grad_value = fold_state
    grad_query_low = grad_query.reshape(sequences, shard_rows, local_inner).astype(jnp.bfloat16)
    grad_key_low = grad_key.reshape(sequences, key_span, local_inner).astype(jnp.bfloat16)
    grad_value_low = grad_value.reshape(sequences, key_span, local_inner).astype(jnp.bfloat16)
    grad_query_weight = jnp.einsum(
        "scd,sci->di", normed_low, grad_query_low, preferred_element_type=jnp.float32
    )
    grad_key_weight = jnp.einsum(
        "sjd,sji->di", both_rows, grad_key_low, preferred_element_type=jnp.float32
    )
    grad_value_weight = jnp.einsum(
        "sjd,sji->di", both_rows, grad_value_low, preferred_element_type=jnp.float32
    )
    row_part = jnp.einsum(
        "sji,di->sjd", grad_key_low, full_key, preferred_element_type=jnp.float32
    ) + jnp.einsum("sji,di->sjd", grad_value_low, full_value, preferred_element_type=jnp.float32)
    token_part = row_part[:, :shard_rows] + jnp.einsum(
        "sci,di->scd", grad_query_low, full_query, preferred_element_type=jnp.float32
    )
    grad_normed, grad_memory_normed = (
        lax.psum(token_part.astype(jnp.bfloat16), "tensor").astype(jnp.float32),
        lax.psum(row_part[:, shard_rows:].astype(jnp.bfloat16), "tensor").astype(jnp.float32),
    )
    back_inputs, gain_tokens = norm_back(inputs_float, input_scale, attn_gain, grad_normed)
    back_memory, gain_memory = norm_back(memory_float, memory_scale, attn_gain, grad_memory_normed)
    grad_inputs = grad_residual + back_inputs
    grad_attn_gain = gain_tokens + gain_memory
    (
        shard_query,
        shard_key,
        shard_value,
        shard_output,
        shard_inner,
        shard_outer,
        shard_attn_gain,
        shard_dense_gain,
    ) = sum_grads(
        (
            grad_query_weight,
            grad_key_weight,
            grad_value_weight,
            grad_output,
            grad_inner,
            grad_outer,
            grad_attn_gain,
            grad_dense_gain,
        )
    )
    loss_sum, grad_bias_sum = lax.psum((loss_local, grad_bias), ("fsdp", "context"))
    return (
        loss_sum / (token_count * model_width),
        result.astype(jnp.bfloat16),
        grad_inputs,
        back_memory,
        shard_attn_gain,
        shard_query,
        shard_key,
        shard_value,
        shard_output,
        grad_bias_sum,
        shard_dense_gain,
        shard_inner,
        shard_outer,
    )


PAD = 16
BF = jnp.bfloat16
F32 = jnp.float32
VMEM_LIMIT = 60 * 1024 * 1024


def fits(mesh):
    sizes = dict(mesh.shape)
    return sizes["fsdp"] == 2 and sizes["context"] == 8 and sizes["tensor"] == 2


def swap_context(value, mask):
    return lax.ppermute(value, "context", [(i, i ^ mask) for i in range(8)])


def swap_fsdp(value):
    return lax.ppermute(value, "fsdp", [(0, 1), (1, 0)])


def swap_tensor(value):
    return lax.ppermute(value, "tensor", [(0, 1), (1, 0)])


def dot_nn(left, right):
    return lax.dot_general(left, right, (((1,), (0,)), ((), ())), preferred_element_type=F32)


def dot_nt(left, right):
    return lax.dot_general(left, right, (((1,), (1,)), ((), ())), preferred_element_type=F32)


def dot_tn(left, right):
    return lax.dot_general(left, right, (((0,), (0,)), ((), ())), preferred_element_type=F32)


def call(kernel, outs, ins_any=0, scratch=(), flops=0, bytes_moved=0):
    def run(*operands):
        count = len(operands)
        specs = [pl.BlockSpec(memory_space=pltpu.VMEM)] * (count - ins_any)
        specs += [pl.BlockSpec(memory_space=pl.ANY)] * ins_any
        return pl.pallas_call(
            kernel,
            out_shape=[jax.ShapeDtypeStruct(shape, dtype) for shape, dtype in outs],
            in_specs=specs,
            out_specs=[pl.BlockSpec(memory_space=pltpu.VMEM)] * len(outs),
            scratch_shapes=list(scratch),
            compiler_params=pltpu.CompilerParams(vmem_limit_bytes=VMEM_LIMIT),
            cost_estimate=pl.CostEstimate(
                flops=flops, bytes_accessed=bytes_moved, transcendentals=0
            ),
        )(*operands)

    return run


def diagonal(rows):
    return lax.broadcasted_iota(jnp.int32, (rows, 128), 0) == lax.broadcasted_iota(
        jnp.int32, (rows, 128), 1
    )


def row_to_column(row, rows):
    return jnp.sum(
        jnp.where(diagonal(rows), jnp.broadcast_to(row, (rows, 128)), 0.0), axis=1, keepdims=True
    )


def bucket_onehot(block_distance, span):
    lane = lax.broadcasted_iota(jnp.int32, (BUCKETS, 2 * span), 1)
    offset = jnp.where(lane < span, lane, lane - 2 * span)
    bucket = relative_bucket(block_distance * span - offset)
    return bucket == lax.broadcasted_iota(jnp.int32, (BUCKETS, 2 * span), 0)


def attend_kernel(
    *refs, span, slots, tokens, inner, rows_each
):
    blocks = refs[:8]
    weight_refs = refs[8:24]
    bias_ref = refs[24]
    (normed_ref, kv_ref, q_ref, w_ref, p_ref, low_ref, wide_ref, gains_ref) = refs[25:33]
    (mask_ref, toep_ref, score_ref, extra_ref) = refs[33:]
    place = lax.axis_index("context")
    group = lax.axis_index("fsdp") * 8 + place
    for p in range(16):
        start = pl.multiple_of((group ^ p) * rows_each, 16)
        w_ref[pl.ds(start, rows_each), :] = weight_refs[p][:, : 3 * inner]
        extra_ref[pl.ds(start, rows_each), :] = weight_refs[p][:, 3 * inner :].astype(F32)
    extra_rows = jnp.transpose(extra_ref[...])[0:8, :]
    row_ids = lax.broadcasted_iota(jnp.int32, extra_rows.shape, 0)
    count = jnp.sum(extra_rows[2:3, :]) / rows_each
    gains_ref[...] = jnp.where(row_ids == 2, count, extra_rows)
    gain = extra_rows[0:1, :]
    own_docs = None
    for p in range(8):
        block = place ^ p
        token_at = pl.multiple_of(block * span, span)
        slot_at = pl.multiple_of(tokens + block * PAD, PAD)
        values = blocks[p][0:span, :].astype(F32)
        scale = lax.rsqrt(jnp.mean(values * values, axis=-1, keepdims=True) + norm_eps)
        normed_ref[pl.ds(token_at, span), :] = (values * scale * gain).astype(BF)
        tail = blocks[p][span : span + PAD, :].astype(F32)
        docs = tail[slots : slots + 1, 0:256]
        tail_rows = lax.broadcasted_iota(jnp.int32, tail.shape, 0)
        tail = jnp.where(tail_rows < slots, tail, 0.0)
        scale = lax.rsqrt(jnp.mean(tail * tail, axis=-1, keepdims=True) + norm_eps)
        normed_ref[pl.ds(slot_at, PAD), :] = (tail * scale * gain).astype(BF)
        if p == 0:
            own_docs = docs[:, 0:span]
        token_docs = row_to_column(docs[:, 0:span], span)
        mask_ref[pl.ds(token_at, span), :] = jnp.where(token_docs == own_docs, 0.0, score_floor)
        slot_docs = row_to_column(docs[:, span : 2 * span], PAD)
        slot_rows = lax.broadcasted_iota(jnp.int32, (PAD, 1), 0)
        slot_docs = jnp.where(slot_rows < slots, slot_docs, -1.0)
        mask_ref[pl.ds(slot_at, PAD), :] = jnp.where(slot_docs == own_docs, 0.0, score_floor)
    kv_ref[...] = dot_nn(normed_ref[...], w_ref[:, inner:]).astype(BF)
    own_at = pl.multiple_of(place * span, span)
    q_ref[...] = dot_nn(normed_ref[pl.ds(own_at, span), :], w_ref[:, :inner]).astype(BF)
    heads = bias_ref.shape[0]
    for e in range(5):
        table = dot_nn(bias_ref[...], jnp.where(bucket_onehot(e - 2, span), 1.0, 0.0).astype(BF))
        for h in range(heads):
            line = jnp.broadcast_to(table[h : h + 1, :], (span, 2 * span))
            if abs(e - 2) < 2:
                line = pltpu.roll(line, 0, 1, stride=1, stride_axis=0)
            toep_ref[h, e] = line[:, :span]
    lane = lax.broadcasted_iota(jnp.int32, (span, span), 1)
    sub = lax.broadcasted_iota(jnp.int32, (span, span), 0)
    count_blocks = tokens // span
    slot_rows_all = score_ref.shape[0] - tokens
    for t in range(inner // span):
        keys = kv_ref[:, t * span : (t + 1) * span]
        values = kv_ref[:, inner + t * span : inner + (t + 1) * span]
        pair = q_ref[:, t * span : (t + 1) * span]
        zero = jnp.zeros_like(pair)
        both = jnp.concatenate(
            [jnp.where(lane < span // 2, pair, zero), jnp.where(lane < span // 2, zero, pair)], axis=0
        )
        score_ref[...] = dot_nt(keys, both)
        best = jnp.full((1, 2 * span), score_floor, F32)
        for s in range(count_blocks):
            e = jnp.clip(s - place, -2, 2) + 2
            at = slice(s * span, (s + 1) * span)
            terms = jnp.concatenate([toep_ref[2 * t, e], toep_ref[2 * t + 1, e]], axis=1)
            mask = mask_ref[at, :]
            block = score_ref[at, :] + terms + jnp.concatenate([mask, mask], axis=1)
            score_ref[at, :] = block
            best = jnp.maximum(best, jnp.max(block, axis=0, keepdims=True))
        at = slice(tokens, tokens + slot_rows_all)
        mask = mask_ref[at, :]
        block = score_ref[at, :] + jnp.concatenate([mask, mask], axis=1)
        score_ref[at, :] = block
        best = jnp.maximum(best, jnp.max(block, axis=0, keepdims=True))
        total = jnp.zeros((1, 2 * span), F32)
        for s in range(score_ref.shape[0] // span):
            at = slice(s * span, (s + 1) * span)
            weights = jnp.exp(score_ref[at, :] - best)
            score_ref[at, :] = weights
            total = total + jnp.sum(weights, axis=0, keepdims=True)
        inverse = 1.0 / total
        for s in range(score_ref.shape[0] // span):
            at = slice(s * span, (s + 1) * span)
            p_ref[t, at, :] = (score_ref[at, :] * inverse).astype(BF)
        out = dot_tn(values, p_ref[t])
        out = jnp.where(sub < span // 2, out[:, :span], out[:, span:])
        wide_ref[t * span : (t + 1) * span, :] = out
        low_ref[:, t * span : (t + 1) * span] = jnp.transpose(out).astype(BF)


def fetch_rows(pieces, columns, target, sems, group, rows_each):
    copies = []
    for p in range(16):
        start = pl.multiple_of((group ^ p) * rows_each, 16)
        copies.append(
            pltpu.make_async_copy(
                pieces[p].at[:, columns], target.at[pl.ds(start, rows_each), :], sems.at[p]
            )
        )
    return copies


def out_kernel(low_ref, *refs, inner, rows_each):
    pieces, part_ref, wo_ref, sems = refs[:16], refs[16], refs[17], refs[18]
    group = lax.axis_index("fsdp") * 8 + lax.axis_index("context")
    copies = fetch_rows(pieces, slice(0, inner), wo_ref, sems, group, rows_each)
    for copy in copies:
        copy.start()
    for copy in copies:
        copy.wait()
    part_ref[...] = dot_nt(low_ref[...], wo_ref[...]).astype(BF)


def forward_kernel(x_ref, own_ref, far_ref, gains_ref, *refs, inner, hidden, rows_each):
    pieces = refs[:16]
    residual_ref, dense_ref, hidden_ref, slope_ref, part_ref = refs[16:21]
    wi_ref, wf_ref, sems_in, sems_out = refs[21:]
    group = lax.axis_index("fsdp") * 8 + lax.axis_index("context")
    first = fetch_rows(pieces, slice(inner, inner + hidden), wi_ref, sems_in, group, rows_each)
    second = fetch_rows(
        pieces, slice(inner + hidden, inner + 2 * hidden), wf_ref, sems_out, group, rows_each
    )
    for copy in first + second:
        copy.start()
    residual = x_ref[...].astype(F32) + (own_ref[...].astype(F32) + far_ref[...].astype(F32))
    residual_ref[...] = residual
    scale = lax.rsqrt(jnp.mean(residual * residual, axis=-1, keepdims=True) + norm_eps)
    dense_ref[...] = (residual * scale * gains_ref[1:2, :]).astype(BF)
    for copy in first:
        copy.wait()
    step = 256
    for at in range(0, hidden, step):
        pre = dot_nn(dense_ref[...], wi_ref[:, at : at + step])
        square = pre * pre
        root = 0.7978845608028654
        tanh = jnp.tanh(root * (pre + 0.044715 * pre * square))
        hidden_ref[:, at : at + step] = (0.5 * pre * (1.0 + tanh)).astype(BF)
        slope_ref[:, at : at + step] = 0.5 * (1.0 + tanh) + 0.5 * pre * (1.0 - tanh * tanh) * (
            root * (1.0 + 3.0 * 0.044715 * square)
        )
    for copy in second:
        copy.wait()
    part_ref[...] = dot_nt(hidden_ref[...], wf_ref[...]).astype(BF)


def backward_kernel(
    residual_ref,
    own_ref,
    far_ref,
    teacher_ref,
    valid_ref,
    gains_ref,
    slope_ref,
    *refs,
    inner,
    hidden,
    rows_each,
    total_rows,
):
    pieces = refs[:16]
    out_ref, grad_ref, back_ref, pre_ref, part_ref, loss_ref = refs[16:22]
    wi_ref, wf_ref, sems_in, sems_out = refs[22:]
    group = lax.axis_index("fsdp") * 8 + lax.axis_index("context")
    first = fetch_rows(
        pieces, slice(inner + hidden, inner + 2 * hidden), wf_ref, sems_out, group, rows_each
    )
    second = fetch_rows(pieces, slice(inner, inner + hidden), wi_ref, sems_in, group, rows_each)
    for copy in first + second:
        copy.start()
    result = residual_ref[...] + (own_ref[...].astype(F32) + far_ref[...].astype(F32))
    out_ref[...] = result.astype(BF)
    rows = result.shape[0]
    valid = row_to_column(valid_ref[...].astype(F32), rows)
    misfit = result - teacher_ref[...].astype(F32)
    loss = 0.5 * jnp.sum(valid * misfit * misfit)
    loss_ref[...] = jnp.full(loss_ref.shape, loss, F32)
    factor = total_rows / gains_ref[2:3, 0:1]
    grad = factor * valid * misfit
    grad_ref[...] = grad
    back_ref[...] = grad.astype(BF)
    for copy in first:
        copy.wait()
    step = 256
    for at in range(0, hidden, step):
        grad_hidden = dot_nn(back_ref[...], wf_ref[:, at : at + step])
        pre_ref[:, at : at + step] = (grad_hidden * slope_ref[:, at : at + step]).astype(BF)
    for copy in second:
        copy.wait()
    part_ref[...] = dot_nt(pre_ref[...], wi_ref[...]).astype(BF)


def split_rows(value, target_ref, rows_each):
    place = lax.axis_index("context")
    mine = lax.rem(place, 2)
    half = value.shape[0] // 2
    source = target_ref.at[0]
    source[...] = value
    ordered = target_ref.at[1]
    for g in range(8):
        keep = pl.multiple_of((2 * g + mine) * rows_each, 16)
        send = pl.multiple_of((2 * g + 1 - mine) * rows_each, 16)
        ordered[g * rows_each : (g + 1) * rows_each, :] = source[pl.ds(keep, rows_each), :]
        ordered[half + g * rows_each : half + (g + 1) * rows_each, :] = source[
            pl.ds(send, rows_each), :
        ]


def dense_grad_kernel(
    back_ref, hidden_ref, dense_ref, pre_ref, keep_ref, send_ref, lines_ref, *, rows_each
):
    hidden = hidden_ref.shape[1]
    for which, (left, right) in enumerate(((dense_ref, pre_ref), (back_ref, hidden_ref))):
        split_rows(jnp.transpose(left[...].astype(F32)).astype(BF), lines_ref, rows_each)
        for at in range(0, hidden, 512):
            product = dot_nn(lines_ref[1], right[:, at : at + 512]).astype(BF)
            cols = slice(which * hidden + at, which * hidden + at + 512)
            for g in range(8):
                keep_ref[g, :, cols] = product[g * rows_each : (g + 1) * rows_each, :]
                send_ref[g, :, cols] = product[(8 + g) * rows_each : (9 + g) * rows_each, :]


def attention_back_kernel(
    own_ref,
    far_ref,
    grad_ref,
    residual_ref,
    gains_ref,
    wide_ref,
    p_ref,
    kv_ref,
    q_ref,
    loss_ref,
    *refs,
    inner,
    span,
    tokens,
    rows_each,
):
    pieces = refs[:16]
    residual_grad_ref, back_ref, dq_ref, dkv_ref, gain_ref, small_ref = refs[16:22]
    wo_ref, ds_ref, diag_ref, sems = refs[22:]
    place = lax.axis_index("context")
    group = lax.axis_index("fsdp") * 8 + place
    copies = fetch_rows(pieces, slice(0, inner), wo_ref, sems, group, rows_each)
    for copy in copies:
        copy.start()
    incoming = own_ref[...].astype(F32) + far_ref[...].astype(F32)
    residual = residual_ref[...]
    scale = lax.rsqrt(jnp.mean(residual * residual, axis=-1, keepdims=True) + norm_eps)
    scaled = incoming * gains_ref[1:2, :]
    mean = jnp.mean(scaled * residual, axis=-1, keepdims=True)
    residual_grad = grad_ref[...] + (scale * scaled - residual * (scale * scale * scale * mean))
    residual_grad_ref[...] = residual_grad
    gain_ref[...] = jnp.broadcast_to(
        jnp.sum(incoming * residual * scale, axis=0, keepdims=True), gain_ref.shape
    )
    back_ref[...] = residual_grad.astype(BF)
    for copy in copies:
        copy.wait()
    grads = dot_nn(back_ref[...], wo_ref[...])
    lane = lax.broadcasted_iota(jnp.int32, (span, span), 1)
    sub = lax.broadcasted_iota(jnp.int32, (span, span), 0)
    keys_all = p_ref.shape[1]
    blocks = tokens // span
    small_ref[...] = jnp.zeros_like(small_ref)
    tables = [bucket_onehot(d, span).astype(F32) for d in (-1, 0, 1)]
    zero = jnp.zeros((span, span), BF)
    for t in range(inner // span):
        cols = slice(t * span, (t + 1) * span)
        keys = kv_ref[:, cols]
        values = kv_ref[:, inner + t * span : inner + (t + 1) * span]
        pair = grads[:, cols].astype(BF)
        pair_back = jnp.transpose(pair.astype(F32)) * wide_ref[cols, :]
        delta = jnp.concatenate(
            [
                jnp.sum(pair_back[: span // 2], axis=0, keepdims=True),
                jnp.sum(pair_back[span // 2 :], axis=0, keepdims=True),
            ],
            axis=1,
        )
        grad_both = jnp.concatenate(
            [jnp.where(lane < span // 2, pair, zero), jnp.where(lane < span // 2, zero, pair)], axis=0
        )
        query = q_ref[:, cols]
        query_both = jnp.concatenate(
            [jnp.where(lane < span // 2, query, zero), jnp.where(lane < span // 2, zero, query)],
            axis=0,
        )
        low_sum = jnp.zeros((1, 2 * span), F32)
        high_sum = jnp.zeros((1, 2 * span), F32)
        for s in range(keys_all // span):
            at = slice(s * span, (s + 1) * span)
            dots = dot_nt(values[at, :], grad_both)
            ds = (p_ref[t, at, :].astype(F32) * (dots - delta)).astype(BF)
            ds_ref[at, :] = ds
            if s < blocks:
                line = jnp.sum(ds.astype(F32), axis=0, keepdims=True)
                low_sum = low_sum + jnp.where(s < place - 1, line, 0.0)
                high_sum = high_sum + jnp.where(s > place + 1, line, 0.0)
        dkv_ref[:, cols] = dot_nn(ds_ref[...], query_both).astype(BF)
        dkv_ref[:, inner + t * span : inner + (t + 1) * span] = dot_nn(p_ref[t], grad_both).astype(
            BF
        )
        dq = dot_tn(keys, ds_ref[...])
        dq = jnp.where(sub < span // 2, dq[:, :span], dq[:, span:])
        dq_ref[:, cols] = jnp.transpose(dq).astype(BF)
        for head in range(2):
            for which in range(3):
                s = place + which - 1
                inside = (s >= 0) & (s < blocks)
                start = pl.multiple_of(jnp.clip(s, 0, blocks - 1) * span, span)
                block = ds_ref[pl.ds(start, span), head * span : (head + 1) * span].astype(F32)
                block = jnp.where(inside, block, 0.0)
                block = jnp.concatenate([block, jnp.zeros((span, span), F32)], axis=1)
                size = span
                while size > 8:
                    size = size // 2
                    block = block[:size] + pltpu.roll(block[size:], 2 * span - size, 1)
                line = block[0:1]
                for j in range(1, 8):
                    line = line + pltpu.roll(block, 2 * span - j, 1)[j : j + 1]
                diag_ref[which, 2 * t + head : 2 * t + head + 1, :] = line
            bucket = lax.broadcasted_iota(jnp.int32, (1, 128), 1)
            part = slice(head * span, (head + 1) * span)
            low_total = jnp.sum(low_sum[:, part], axis=1, keepdims=True)
            high_total = jnp.sum(high_sum[:, part], axis=1, keepdims=True)
            small_ref[2 * t + head : 2 * t + head + 1, :] = jnp.where(
                bucket == BUCKETS // 2 - 1, low_total, 0.0
            ) + jnp.where(bucket == BUCKETS - 1, high_total, 0.0)
    heads = inner * 2 // span
    for which in range(3):
        line = lax.dot_general(
            diag_ref[which],
            tables[which],
            (((1,), (1,)), ((), ())),
            preferred_element_type=F32,
            precision=lax.Precision.HIGHEST,
        )
        small_ref[0:heads, 0:BUCKETS] += line[0:heads, :]
    small_ref[heads : heads + 1, :] = loss_ref[0:1, :]


def rows_grad_kernel(
    dq_ref,
    dkv_ref,
    w_ref,
    normed_ref,
    gains_ref,
    keep_ref,
    send_ref,
    gain_ref,
    part_ref,
    *,
    inner,
    span,
    tokens,
):
    place = lax.axis_index("context")
    mine = lax.rem(place, 2)
    part_ref[...] = dot_nt(dkv_ref[...], w_ref[:, inner:])
    own_at = pl.multiple_of(place * span, span)
    part_ref[pl.ds(own_at, span), :] += dot_nt(dq_ref[...], w_ref[:, :inner])
    total = jnp.zeros((1, part_ref.shape[1]), F32)
    for s in range(part_ref.shape[0] // span):
        at = slice(s * span, (s + 1) * span)
        total = total + jnp.sum(
            part_ref[at, :] * normed_ref[at, :].astype(F32), axis=0, keepdims=True
        )
    gain_ref[...] = jnp.broadcast_to(total / gains_ref[0:1, :], gain_ref.shape)
    for g in range(4):
        for target, block in ((keep_ref, 2 * g + mine), (send_ref, 2 * g + 1 - mine)):
            token_at = pl.multiple_of(block * span, span)
            slot_at = pl.multiple_of(tokens + block * PAD, PAD)
            target[g, 0:span, :] = part_ref[pl.ds(token_at, span), :].astype(BF)
            target[g, span : span + PAD, :] = part_ref[pl.ds(slot_at, PAD), :].astype(BF)


def weight_grad_kernel(
    dq_ref,
    dkv_ref,
    normed_ref,
    back_ref,
    low_ref,
    gain_ref,
    dense_gain_ref,
    keep_ref,
    send_ref,
    wide_ref,
    line_ref,
    extra_ref,
    *,
    inner,
    span,
    rows_each,
):
    place = lax.axis_index("context")

    def put(product, start):
        cols = slice(start, start + product.shape[1])
        low = product.astype(BF)
        for g in range(8):
            keep_ref[g, :, cols] = low[g * rows_each : (g + 1) * rows_each, :]
            send_ref[g, :, cols] = low[(8 + g) * rows_each : (9 + g) * rows_each, :]

    split_rows(jnp.transpose(back_ref[...].astype(F32)).astype(BF), line_ref, rows_each)
    put(dot_nn(line_ref[1], low_ref[...]), 3 * inner)
    own_at = pl.multiple_of(place * span, span)
    own = normed_ref[pl.ds(own_at, span), :].astype(F32)
    split_rows(jnp.transpose(own).astype(BF), line_ref, rows_each)
    put(dot_nn(line_ref[1], dq_ref[...]), 0)
    split_rows(jnp.transpose(normed_ref[...].astype(F32)).astype(BF), wide_ref, rows_each)
    for at in range(0, 2 * inner, 256):
        put(dot_nn(wide_ref[1], dkv_ref[:, at : at + 256]), inner + at)
    row_ids = lax.broadcasted_iota(jnp.int32, (128, gain_ref.shape[1]), 0)
    rows = jnp.where(row_ids == 0, gain_ref[0:1, :], 0.0) + jnp.where(
        row_ids == 1, dense_gain_ref[0:1, :], 0.0
    )
    split_rows(jnp.transpose(rows), extra_ref, rows_each)
    put(extra_ref[1], 4 * inner)


def halve_kernel(keep_ref, far_ref, next_ref, send_ref):
    mine = lax.axis_index("fsdp")
    for g in range(4):
        for target, start in ((next_ref, 4 * mine), (send_ref, 4 - 4 * mine)):
            target[g] = (keep_ref[start + g].astype(F32) + far_ref[start + g].astype(F32)).astype(BF)


def spread_kernel(keep_ref, far_ref, own_ref, *send_refs):
    place = lax.axis_index("context") // 2
    for p in range(4):
        block = place ^ p
        total = keep_ref[block].astype(F32) + far_ref[block].astype(F32)
        if p == 0:
            own_ref[...] = total
        else:
            send_refs[p - 1][...] = total.astype(BF)


def gather_kernel(own_ref, one_ref, two_ref, three_ref, *out_refs):
    at = 0
    for out in out_refs:
        cols = slice(at, at + out.shape[1])
        out[...] = (own_ref[:, cols] + one_ref[:, cols].astype(F32)) + (
            two_ref[:, cols].astype(F32) + three_ref[:, cols].astype(F32)
        ).astype(out.dtype)
        at += out.shape[1]


def columns_kernel(keep_ref, far_ref, next_ref, send_ref):
    mine = lax.axis_index("tensor")
    width = next_ref.shape[2]
    for target, start in ((next_ref, mine * width), (send_ref, (1 - mine) * width)):
        cols = pl.ds(pl.multiple_of(start, 128), width)
        target[...] = (keep_ref[:, :, cols].astype(F32) + far_ref[:, :, cols].astype(F32)).astype(BF)


def half_sum_kernel(own_ref, one_ref, two_ref, three_ref, out_ref):
    out_ref[...] = (
        (own_ref[...] + one_ref[...].astype(F32))
        + (two_ref[...].astype(F32) + three_ref[...].astype(F32))
    ).astype(BF)


def finish_kernel(
    own_ref,
    far_ref,
    block_ref,
    gains_ref,
    residual_grad_ref,
    extra_ref,
    extra_far_ref,
    small_ref,
    inputs_ref,
    memory_ref,
    gain_ref,
    dense_gain_ref,
    bias_ref,
    loss_ref,
    full_ref,
    *,
    span,
    slots,
):
    mine = lax.axis_index("tensor")
    width = own_ref.shape[1]
    full_ref[:, pl.ds(pl.multiple_of(mine * width, 128), width)] = own_ref[...].astype(F32)
    full_ref[:, pl.ds(pl.multiple_of((1 - mine) * width, 128), width)] = far_ref[...].astype(F32)
    values = block_ref[...].astype(F32)
    scale = lax.rsqrt(jnp.mean(values * values, axis=-1, keepdims=True) + norm_eps)
    scaled = full_ref[...] * gains_ref[0:1, :]
    mean = jnp.mean(scaled * values, axis=-1, keepdims=True)
    back = scale * scaled - values * (scale * scale * scale * mean)
    inputs_ref[...] = residual_grad_ref[...] + back[0:span]
    memory_ref[...] = back[span : span + slots]
    rows = extra_ref.shape[0]
    both = extra_ref[...] + extra_far_ref[...]
    eye = diagonal(rows)
    gain_ref[...] = jnp.sum(jnp.where(eye, both[:, 0:1], 0.0), axis=0, keepdims=True)[:, :rows]
    dense_gain_ref[...] = jnp.sum(jnp.where(eye, extra_ref[:, 1:2], 0.0), axis=0, keepdims=True)[
        :, :rows
    ]
    heads = bias_ref.shape[0]
    bias_ref[...] = small_ref[0:heads, 0:BUCKETS]
    loss = small_ref[heads : heads + 1, 0:128] / (gains_ref[2:3, 0:128] * full_ref.shape[1])
    loss_ref[...] = loss


def fast_local(
    inputs,
    memory,
    teacher,
    segments,
    memory_owner,
    valid_mask,
    attention_gain,
    query_weight,
    key_weight,
    value_weight,
    attention_out_weight,
    position_bias,
    feedforward_gain,
    inner_weight,
    feedforward_out_weight,
):
    span, width = inputs.shape[1:]
    slots = memory.shape[1]
    rows_each, inner = query_weight.shape
    hidden = inner_weight.shape[1]
    heads = position_bias.shape[0]
    tokens = 8 * span
    keys_all = 8 * (span + PAD)
    total_rows = 2 * tokens
    x = inputs[0]
    docs = jnp.concatenate([segments, memory_owner], axis=1).astype(BF)
    docs = jnp.pad(docs, ((0, 0), (0, width - span - slots)))
    block = jnp.concatenate(
        [x, memory[0], docs, jnp.zeros((PAD - slots - 1, width), BF)], axis=0
    )
    valid_total = jnp.sum(valid_mask).astype(BF)
    extras = jnp.concatenate(
        [
            attention_gain[:, None],
            feedforward_gain[:, None],
            jnp.broadcast_to(valid_total, (rows_each, 1)),
            jnp.zeros((rows_each, 125), BF),
        ],
        axis=1,
    )
    first = jnp.concatenate([query_weight, key_weight, value_weight, extras], axis=1)
    later = jnp.concatenate([attention_out_weight, inner_weight, feedforward_out_weight], axis=1)

    def gather_sixteen(shard):
        near = [shard] + [swap_context(shard, m) for m in (2, 4, 6)]
        near = near + [swap_fsdp(piece) for piece in near]
        other = [swap_context(piece, 1) for piece in near]
        order = [None] * 16
        for at, piece in enumerate(near):
            order[8 * (at // 4) + 2 * (at % 4)] = piece
        for at, piece in enumerate(other):
            order[8 * (at // 4) + 2 * (at % 4) + 1] = piece
        return order

    first_all = gather_sixteen(first)
    block_near = [block] + [swap_context(block, m) for m in (2, 4, 6)]
    block_other = [swap_context(piece, 1) for piece in block_near]
    blocks = [piece for pair in zip(block_near, block_other) for piece in pair]
    later_all = gather_sixteen(later)

    attend_flops = 2 * keys_all * width * 2 * inner + 4 * keys_all * 2 * span * inner
    (normed, kv, queries, w_all, probs, low, wide, gains) = call(
        lambda *refs: attend_kernel(
            *refs, span=span, slots=slots, tokens=tokens, inner=inner, rows_each=rows_each
        ),
        [
            ((keys_all, width), BF),
            ((keys_all, 2 * inner), BF),
            ((span, inner), BF),
            ((width, 3 * inner), BF),
            ((inner // span, keys_all, 2 * span), BF),
            ((span, inner), BF),
            ((inner, span), F32),
            ((8, width), F32),
        ],
        scratch=(
            pltpu.VMEM((keys_all, span), F32),
            pltpu.VMEM((heads, 5, span, span), F32),
            pltpu.VMEM((keys_all, 2 * span), F32),
            pltpu.VMEM((width, 128), F32),
        ),
        flops=attend_flops,
        bytes_moved=10_000_000,
    )(*blocks, *first_all, position_bias)

    sems = pltpu.SemaphoreType.DMA((16,))
    (part,) = call(
        lambda *refs: out_kernel(*refs, inner=inner, rows_each=rows_each),
        [((span, width), BF)],
        ins_any=16,
        scratch=(pltpu.VMEM((width, inner), BF), sems),
        flops=2 * span * width * inner,
        bytes_moved=900_000,
    )(low, *later_all)
    far = swap_tensor(part)
    (residual, dense_low, hidden_low, slope, dense_part) = call(
        lambda *refs: forward_kernel(*refs, inner=inner, hidden=hidden, rows_each=rows_each),
        [
            ((span, width), F32),
            ((span, width), BF),
            ((span, hidden), BF),
            ((span, hidden), F32),
            ((span, width), BF),
        ],
        ins_any=16,
        scratch=(pltpu.VMEM((width, hidden), BF), pltpu.VMEM((width, hidden), BF), sems, sems),
        flops=4 * span * width * hidden,
        bytes_moved=7_000_000,
    )(x, part, far, gains, *later_all)
    dense_far = swap_tensor(dense_part)
    (output, grad_result, dense_back, grad_pre, grad_part, loss_part) = call(
        lambda *refs: backward_kernel(
            *refs, inner=inner, hidden=hidden, rows_each=rows_each, total_rows=total_rows
        ),
        [
            ((span, width), BF),
            ((span, width), F32),
            ((span, width), BF),
            ((span, hidden), BF),
            ((span, width), BF),
            ((8, 128), F32),
        ],
        ins_any=16,
        scratch=(pltpu.VMEM((width, hidden), BF), pltpu.VMEM((width, hidden), BF), sems, sems),
        flops=4 * span * width * hidden,
        bytes_moved=7_000_000,
    )(residual, dense_part, dense_far, teacher[0], valid_mask, gains, slope, *later_all)
    grad_far = swap_tensor(grad_part)
    dense_keep, dense_send = call(
        lambda *refs: dense_grad_kernel(*refs, rows_each=rows_each),
        [((8, rows_each, 2 * hidden), BF)] * 2,
        scratch=(pltpu.VMEM((2, width, span), BF),),
        flops=4 * span * width * hidden,
        bytes_moved=6_000_000,
    )(dense_back, hidden_low, dense_low, grad_pre)

    (grad_residual, attention_back, dq, dkv, dense_gain_rows, small) = call(
        lambda *refs: attention_back_kernel(
            *refs, inner=inner, span=span, tokens=tokens, rows_each=rows_each
        ),
        [
            ((span, width), F32),
            ((span, width), BF),
            ((span, inner), BF),
            ((keys_all, 2 * inner), BF),
            ((8, width), F32),
            ((8, 128), F32),
        ],
        ins_any=16,
        scratch=(
            pltpu.VMEM((width, inner), BF),
            pltpu.VMEM((keys_all, 2 * span), BF),
            pltpu.VMEM((3, 8, 2 * span), F32),
            sems,
        ),
        flops=8 * keys_all * 2 * span * inner,
        bytes_moved=7_000_000,
    )(
        grad_part,
        grad_far,
        grad_result,
        residual,
        gains,
        wide,
        probs,
        kv,
        queries,
        loss_part,
        *later_all,
    )
    rows_keep, rows_send, gain_rows = call(
        lambda *refs: rows_grad_kernel(*refs, inner=inner, span=span, tokens=tokens),
        [((4, span + PAD, width), BF)] * 2 + [((8, width), F32)],
        scratch=(pltpu.VMEM((keys_all, width), F32),),
        flops=4 * keys_all * width * inner,
        bytes_moved=7_000_000,
    )(dq, dkv, w_all, normed, gains)
    weight_keep, weight_send = call(
        lambda *refs: weight_grad_kernel(*refs, inner=inner, span=span, rows_each=rows_each),
        [((8, rows_each, 4 * inner + 128), BF)] * 2,
        scratch=(
            pltpu.VMEM((2, width, keys_all), BF),
            pltpu.VMEM((2, width, span), BF),
            pltpu.VMEM((2, width, 128), F32),
        ),
        flops=4 * keys_all * width * inner,
        bytes_moved=7_000_000,
    )(dq, dkv, normed, attention_back, low, gain_rows, dense_gain_rows)

    def scatter_sixteen(keep, send):
        columns = keep.shape[2]
        far_core = swap_context(send, 1)
        keep_next, send_next = call(
            halve_kernel, [((4, rows_each, columns), BF)] * 2, bytes_moved=keep.size * 6
        )(keep, far_core)
        far_fsdp = swap_fsdp(send_next)
        own, *sends = call(
            spread_kernel,
            [((rows_each, columns), F32)] + [((rows_each, columns), BF)] * 3,
            bytes_moved=keep.size * 3,
        )(keep_next, far_fsdp)
        return own, [swap_context(piece, m) for piece, m in zip(sends, (2, 4, 6))]

    own, pieces = scatter_sixteen(dense_keep, dense_send)
    grad_inner, grad_outer = call(
        gather_kernel, [((rows_each, hidden), F32)] * 2, bytes_moved=own.size * 14
    )(own, *pieces)

    rows_far = swap_context(rows_send, 1)
    rows_next, rows_over = call(
        columns_kernel, [((4, span + PAD, width // 2), BF)] * 2, bytes_moved=rows_keep.size * 6
    )(rows_keep, rows_far)
    rows_far = swap_tensor(rows_over)
    own, *sends = call(
        spread_kernel,
        [((span + PAD, width // 2), F32)] + [((span + PAD, width // 2), BF)] * 3,
        bytes_moved=rows_next.size * 6,
    )(rows_next, rows_far)
    pieces = [swap_context(piece, m) for piece, m in zip(sends, (2, 4, 6))]
    (rows_half,) = call(
        half_sum_kernel, [((span + PAD, width // 2), BF)], bytes_moved=own.size * 12
    )(own, *pieces)
    rows_other = swap_tensor(rows_half)

    own, pieces = scatter_sixteen(weight_keep, weight_send)
    *weight_grads, extra = call(
        gather_kernel,
        [((rows_each, inner), F32)] * 4 + [((rows_each, 128), F32)],
        bytes_moved=own.size * 14,
    )(own, *pieces)
    extra_far = swap_tensor(extra)

    small = small + swap_context(small, 1)
    small = small + swap_fsdp(small)
    small = (small + swap_context(small, 2)) + (swap_context(small, 4) + swap_context(small, 6))

    (grad_inputs, grad_memory, grad_gain, grad_dense_gain, grad_bias, loss) = call(
        lambda *refs: finish_kernel(*refs, span=span, slots=slots),
        [
            ((span, width), F32),
            ((slots, width), F32),
            ((1, rows_each), F32),
            ((1, rows_each), F32),
            ((heads, BUCKETS), F32),
            ((1, 128), F32),
        ],
        scratch=(pltpu.VMEM((span + PAD, width), F32),),
        bytes_moved=2_000_000,
    )(rows_half, rows_other, block, gains, grad_residual, extra, extra_far, small)
    return (
        loss[0, 0],
        output[None],
        grad_inputs[None],
        grad_memory[None],
        grad_gain[0],
        weight_grads[0],
        weight_grads[1],
        weight_grads[2],
        weight_grads[3],
        grad_bias,
        grad_dense_gain[0],
        grad_inner,
        grad_outer,
    )


def solution(mesh):
    return jax.shard_map(
        fast_local if fits(mesh) else general_local,
        mesh=mesh,
        in_specs=(
            P("fsdp", "context", None),
            P("fsdp", "context", None),
            P("fsdp", "context", None),
            P("fsdp", "context"),
            P("fsdp", "context"),
            P("fsdp", "context"),
            P(("fsdp", "context")),
            P(("fsdp", "context"), "tensor"),
            P(("fsdp", "context"), "tensor"),
            P(("fsdp", "context"), "tensor"),
            P(("fsdp", "context"), "tensor"),
            P("tensor", None),
            P(("fsdp", "context")),
            P(("fsdp", "context"), "tensor"),
            P(("fsdp", "context"), "tensor"),
        ),
        out_specs=(
            P(),
            P("fsdp", "context", None),
            P("fsdp", "context", None),
            P("fsdp", "context", None),
            P(("fsdp", "context")),
            P(("fsdp", "context"), "tensor"),
            P(("fsdp", "context"), "tensor"),
            P(("fsdp", "context"), "tensor"),
            P(("fsdp", "context"), "tensor"),
            P("tensor", None),
            P(("fsdp", "context")),
            P(("fsdp", "context"), "tensor"),
            P(("fsdp", "context"), "tensor"),
        ),
        check_vma=False,
    )
```

```python
import jax
import jax.numpy as jnp
from jax import lax
from jax.experimental import pallas as pl
from jax.experimental.pallas import tpu as pltpu
from jax.sharding import PartitionSpec as P

BUCKETS = 32
FSDP = "fsdp"
CONTEXT = "context"
TENSOR = "tensor"
ROWS = (FSDP, CONTEXT)
PRODUCT_0 = "scd,df->scf"
PRODUCT_1 = "scd,di->sci"
PRODUCT_2 = "scd,scf->df"
PRODUCT_3 = "scd,sci->di"
PRODUCT_4 = "scf,df->scd"
PRODUCT_5 = "sci,di->scd"
PRODUCT_6 = "sjd,sji->di"
PRODUCT_7 = "sji,di->sjd"
PRODUCT_8 = "sqhd,skhd->sqhk"
PRODUCT_9 = "sqhk,qkb->hb"
PRODUCT_10 = "sqhk,skhd->sqhd"
PRODUCT_11 = "sqhk,sqhd->skhd"


norm_eps = 1e-06
score_floor = -1e30


def relative_bucket(distance):
    half_count = BUCKETS // 2
    exact_count = half_count // 2
    magnitude = jnp.minimum(jnp.abs(distance), 1024)
    far_bucket = jnp.full(distance.shape, exact_count, jnp.int32)
    for level_index in range(1, half_count - exact_count):
        far_bucket = far_bucket + (
            magnitude * magnitude >= exact_count * exact_count * 2**level_index
        ).astype(jnp.int32)
    bucket_ids = jnp.where(magnitude < exact_count, magnitude, far_bucket)
    return bucket_ids + (distance > 0).astype(jnp.int32) * half_count


def rms_norm(values, gain_in):
    inv_rms = lax.rsqrt(jnp.mean(values * values, axis=-1, keepdims=True) + norm_eps)
    return (values * inv_rms * gain_in, inv_rms)


def norm_back(values, inv_rms, gain_in, grad_in):
    scaled = grad_in * gain_in
    inner_mean = jnp.mean(scaled * values, axis=-1, keepdims=True)
    grad_values = inv_rms * scaled - values * inv_rms * inv_rms * inv_rms * inner_mean
    grad_gain = jnp.sum(grad_in * values * inv_rms, axis=tuple(range(values.ndim - 1)))
    return (grad_values, grad_gain)


def smooth_gate(values):
    return jax.nn.gelu(values, approximate=True)


def block_size():
    return 512


def pad_rows(values_in, block_rows, fill_value):
    blocks = -(-values_in.shape[1] // block_rows)
    missing = blocks * block_rows - values_in.shape[1]
    padding = [(0, 0)] * values_in.ndim
    padding[1] = (0, missing)
    return (jnp.pad(values_in, padding, constant_values=fill_value), blocks)


def key_places(row_ids, shard_rows, key_span):
    within = row_ids % key_span
    return (row_ids // key_span * shard_rows + within, within < shard_rows)


def scores_with_bias(
    query_blk, key_blk, query_place, query_doc, key_place, key_doc, key_token, bias_table
):
    scores = jnp.einsum(PRODUCT_8, query_blk, key_blk, preferred_element_type=jnp.float32)
    bucket = relative_bucket(key_place[None, :] - query_place[:, None])
    rel_terms = jnp.where(key_token[None, None, :], jnp.take(bias_table, bucket, axis=1), 0.0)
    scores = scores + jnp.moveaxis(rel_terms, 0, 1)[None]
    same_doc = (query_doc[:, :, None] == key_doc[:, None, :])[:, :, None, :]
    return (scores, same_doc, bucket)


def sum_grads(grad_items):
    return (
        lax.psum_scatter(grad_items[0], ROWS, scatter_dimension=0, tiled=True),
        lax.psum_scatter(grad_items[1], ROWS, scatter_dimension=0, tiled=True),
        lax.psum_scatter(grad_items[2], ROWS, scatter_dimension=0, tiled=True),
        lax.psum_scatter(grad_items[3], ROWS, scatter_dimension=0, tiled=True),
        lax.psum_scatter(grad_items[4], ROWS, scatter_dimension=0, tiled=True),
        lax.psum_scatter(grad_items[5], ROWS, scatter_dimension=0, tiled=True),
        lax.psum_scatter(grad_items[6], ROWS, scatter_dimension=0, tiled=True),
        lax.psum_scatter(grad_items[7], ROWS, scatter_dimension=0, tiled=True),
    )


def general_local(
    inputs,
    memory,
    teacher,
    segments,
    memory_owner,
    valid_mask,
    attention_gain,
    query_weight,
    key_weight,
    value_weight,
    attention_out_weight,
    position_bias,
    feedforward_gain,
    inner_weight,
    feedforward_out_weight,
):
    sequences, shard_rows, model_width = inputs.shape
    key_span = shard_rows + memory.shape[1]
    context_size = lax.axis_size(CONTEXT)
    length = shard_rows * context_size
    context_place = lax.axis_index(CONTEXT)
    local_heads = position_bias.shape[0]
    bucket_count = position_bias.shape[1]
    head_size = query_weight.shape[1] // local_heads
    local_inner = local_heads * head_size
    total_rows = sequences * length * lax.axis_size(FSDP)
    bias_table = position_bias.astype(jnp.float32)
    (
        full_query,
        full_key,
        full_value,
        full_output,
        full_inner,
        full_outer,
        full_attn_gain,
        full_dense_gain,
    ) = (
        lax.all_gather(query_weight, ROWS, axis=0, tiled=True),
        lax.all_gather(key_weight, ROWS, axis=0, tiled=True),
        lax.all_gather(value_weight, ROWS, axis=0, tiled=True),
        lax.all_gather(attention_out_weight, ROWS, axis=0, tiled=True),
        lax.all_gather(inner_weight, ROWS, axis=0, tiled=True),
        lax.all_gather(feedforward_out_weight, ROWS, axis=0, tiled=True),
        lax.all_gather(attention_gain, ROWS, axis=0, tiled=True),
        lax.all_gather(feedforward_gain, ROWS, axis=0, tiled=True),
    )
    attn_gain = full_attn_gain.astype(jnp.float32)
    dense_gain = full_dense_gain.astype(jnp.float32)
    local_docs = jnp.concatenate([segments, memory_owner], axis=1)
    key_docs = lax.all_gather(local_docs, CONTEXT, axis=1, tiled=True)
    query_docs_all = key_docs.reshape(sequences, context_size, key_span)[:, :, :shard_rows].reshape(
        sequences, length
    )
    token_count = lax.psum(jnp.sum(valid_mask.astype(jnp.float32)), ROWS)
    inputs_float = inputs.astype(jnp.float32)
    memory_float = memory.astype(jnp.float32)
    normed, input_scale = rms_norm(inputs_float, attn_gain)
    memory_normed, memory_scale = rms_norm(memory_float, attn_gain)
    normed_low = normed.astype(jnp.bfloat16)
    both_rows = jnp.concatenate([normed_low, memory_normed.astype(jnp.bfloat16)], axis=1)
    queries = jnp.dot(normed_low, full_query, preferred_element_type=jnp.float32).astype(
        jnp.bfloat16
    )
    key_local = jnp.dot(both_rows, full_key, preferred_element_type=jnp.float32).astype(
        jnp.bfloat16
    )
    value_local = jnp.dot(both_rows, full_value, preferred_element_type=jnp.float32).astype(
        jnp.bfloat16
    )
    query_heads = queries.reshape(sequences, shard_rows, local_heads, head_size)
    query_place = context_place * shard_rows + jnp.arange(shard_rows, dtype=jnp.int32)
    fold_init = (
        jnp.full((sequences, shard_rows, local_heads), score_floor, jnp.float32),
        jnp.zeros((sequences, shard_rows, local_heads), jnp.float32),
        jnp.zeros((sequences, shard_rows, local_heads, head_size), jnp.float32),
    )
    fold_state = fold_init
    key_piece = lax.all_gather(key_local, CONTEXT, axis=1, tiled=True)
    value_piece = lax.all_gather(value_local, CONTEXT, axis=1, tiled=True)
    block_rows = block_size()
    key_pad, blocks = pad_rows(key_piece, block_rows, 0)
    value_pad, blocks = pad_rows(value_piece, block_rows, 0)
    doc_pad, blocks = pad_rows(key_docs, block_rows, -1)

    def attend_advance(running, block_index):
        running_best, running_sum, summed = running
        offset = block_index * block_rows
        key_blk = lax.dynamic_slice_in_dim(key_pad, offset, block_rows, 1).reshape(
            sequences, block_rows, local_heads, head_size
        )
        value_blk = lax.dynamic_slice_in_dim(value_pad, offset, block_rows, 1).reshape(
            sequences, block_rows, local_heads, head_size
        )
        doc_blk = lax.dynamic_slice_in_dim(doc_pad, offset, block_rows, 1)
        key_place, key_token = key_places(
            offset + jnp.arange(block_rows, dtype=jnp.int32), shard_rows, key_span
        )
        scores, same_doc, bucket = scores_with_bias(
            query_heads, key_blk, query_place, segments, key_place, doc_blk, key_token, bias_table
        )
        masked = jnp.where(same_doc, scores, score_floor)
        new_best = jnp.maximum(running_best, jnp.max(masked, axis=-1))
        weights = jnp.where(same_doc, jnp.exp(scores - new_best[..., None]), 0.0)
        factor = jnp.exp(running_best - new_best)
        running_sum = running_sum * factor + jnp.sum(weights, axis=-1)
        summed = summed * factor[..., None] + jnp.einsum(
            PRODUCT_10,
            weights.astype(jnp.bfloat16),
            value_blk,
            preferred_element_type=jnp.float32,
        )
        return ((new_best, running_sum, summed), None)

    fold_state, unused = lax.scan(attend_advance, fold_state, jnp.arange(blocks, dtype=jnp.int32))
    running_best, running_sum, summed = fold_state
    attended_values = summed / running_sum[..., None]
    attended_low = attended_values.reshape(sequences, shard_rows, local_inner).astype(jnp.bfloat16)
    attention_part = jnp.einsum(
        PRODUCT_5, attended_low, full_output, preferred_element_type=jnp.float32
    )
    residual = inputs_float + lax.psum(attention_part.astype(jnp.bfloat16), TENSOR).astype(
        jnp.float32
    )
    dense_normed, dense_scale = rms_norm(residual, dense_gain)
    dense_low = dense_normed.astype(jnp.bfloat16)
    inner_pre = jnp.dot(dense_low, full_inner, preferred_element_type=jnp.float32)
    hidden_float, gate_pullback = jax.vjp(smooth_gate, inner_pre)
    hidden_low = hidden_float.astype(jnp.bfloat16)
    dense_part = jnp.einsum(
        PRODUCT_4, hidden_low, full_outer, preferred_element_type=jnp.float32
    )
    result = residual + lax.psum(dense_part.astype(jnp.bfloat16), TENSOR).astype(jnp.float32)
    target_mask = valid_mask.astype(jnp.float32)[..., None]
    misfit = result - teacher.astype(jnp.float32)
    loss_local = 0.5 * jnp.sum(target_mask * misfit * misfit)
    grad_result = total_rows / token_count * target_mask * misfit
    dense_back = grad_result.astype(jnp.bfloat16)
    grad_outer = jnp.einsum(
        PRODUCT_2, dense_back, hidden_low, preferred_element_type=jnp.float32
    )
    grad_hidden = jnp.einsum(
        PRODUCT_0, dense_back, full_outer, preferred_element_type=jnp.float32
    )
    grad_pre = gate_pullback(grad_hidden)[0].astype(jnp.bfloat16)
    grad_inner = jnp.einsum(PRODUCT_2, dense_low, grad_pre, preferred_element_type=jnp.float32)
    grad_dense_part = jnp.einsum(
        PRODUCT_4, grad_pre, full_inner, preferred_element_type=jnp.float32
    )
    grad_dense_normed = lax.psum(grad_dense_part.astype(jnp.bfloat16), TENSOR).astype(jnp.float32)
    back_residual, grad_dense_gain = norm_back(residual, dense_scale, dense_gain, grad_dense_normed)
    grad_residual = grad_result + back_residual
    attention_back = grad_residual.astype(jnp.bfloat16)
    grad_output = jnp.einsum(
        PRODUCT_3, attention_back, attended_low, preferred_element_type=jnp.float32
    )
    grad_attended = jnp.einsum(
        PRODUCT_1, attention_back, full_output, preferred_element_type=jnp.float32
    ).astype(jnp.bfloat16)
    grad_heads = grad_attended.reshape(sequences, shard_rows, local_heads, head_size)
    log_total = running_best + jnp.log(running_sum)
    delta_rows = jnp.sum(grad_heads.astype(jnp.float32) * attended_values, axis=-1)
    all_log_total, all_delta = (
        lax.all_gather(log_total, CONTEXT, axis=1, tiled=True),
        lax.all_gather(delta_rows, CONTEXT, axis=1, tiled=True),
    )
    query_init = (
        jnp.zeros((sequences, shard_rows, local_heads, head_size), jnp.float32),
        jnp.zeros((local_heads, bucket_count), jnp.float32),
    )
    fold_state = query_init
    key_piece = lax.all_gather(key_local, CONTEXT, axis=1, tiled=True)
    value_piece = lax.all_gather(value_local, CONTEXT, axis=1, tiled=True)
    query_block_rows = block_size()
    query_key_pad, blocks = pad_rows(key_piece, query_block_rows, 0)
    query_value_pad, blocks = pad_rows(value_piece, query_block_rows, 0)
    query_doc_pad, blocks = pad_rows(key_docs, query_block_rows, -1)

    def query_advance(running, block_index):
        grad_query, grad_bias = running
        offset = block_index * query_block_rows
        key_blk = lax.dynamic_slice_in_dim(query_key_pad, offset, query_block_rows, 1).reshape(
            sequences, query_block_rows, local_heads, head_size
        )
        value_blk = lax.dynamic_slice_in_dim(query_value_pad, offset, query_block_rows, 1).reshape(
            sequences, query_block_rows, local_heads, head_size
        )
        doc_blk = lax.dynamic_slice_in_dim(query_doc_pad, offset, query_block_rows, 1)
        key_place, key_token = key_places(
            offset + jnp.arange(query_block_rows, dtype=jnp.int32), shard_rows, key_span
        )
        scores, same_doc, bucket = scores_with_bias(
            query_heads, key_blk, query_place, segments, key_place, doc_blk, key_token, bias_table
        )
        probabilities = jnp.where(same_doc, jnp.exp(scores - log_total[..., None]), 0.0)
        value_dots = jnp.einsum(
            PRODUCT_8, grad_heads, value_blk, preferred_element_type=jnp.float32
        )
        grad_scores = (probabilities * (value_dots - delta_rows[..., None])).astype(jnp.bfloat16)
        grad_query = grad_query + jnp.einsum(
            PRODUCT_10, grad_scores, key_blk, preferred_element_type=jnp.float32
        )
        bucket_hits = (
            (bucket[:, :, None] == jnp.arange(bucket_count, dtype=jnp.int32)[None, None, :])
            & key_token[None, :, None]
        ).astype(jnp.bfloat16)
        grad_bias = grad_bias + jnp.einsum(
            PRODUCT_9, grad_scores, bucket_hits, preferred_element_type=jnp.float32
        )
        return ((grad_query, grad_bias), None)

    fold_state, unused = lax.scan(query_advance, fold_state, jnp.arange(blocks, dtype=jnp.int32))
    grad_query, grad_bias = fold_state
    key_heads = key_local.reshape(sequences, key_span, local_heads, head_size)
    value_heads = value_local.reshape(sequences, key_span, local_heads, head_size)
    local_place, local_token = key_places(
        context_place * key_span + jnp.arange(key_span, dtype=jnp.int32), shard_rows, key_span
    )
    key_init = (
        jnp.zeros((sequences, key_span, local_heads, head_size), jnp.float32),
        jnp.zeros((sequences, key_span, local_heads, head_size), jnp.float32),
    )
    fold_state = key_init
    query_piece = lax.all_gather(queries, CONTEXT, axis=1, tiled=True)
    grad_piece = lax.all_gather(grad_attended, CONTEXT, axis=1, tiled=True)
    key_block_rows = block_size()
    query_pad, blocks = pad_rows(query_piece, key_block_rows, 0)
    grad_pad, blocks = pad_rows(grad_piece, key_block_rows, 0)
    key_doc_pad, blocks = pad_rows(query_docs_all, key_block_rows, -1)
    total_pad, blocks = pad_rows(all_log_total, key_block_rows, 0.0)
    delta_pad, blocks = pad_rows(all_delta, key_block_rows, 0.0)

    def key_advance(running, block_index):
        grad_key, grad_value = running
        offset = block_index * key_block_rows
        query_blk = lax.dynamic_slice_in_dim(query_pad, offset, key_block_rows, 1).reshape(
            sequences, key_block_rows, local_heads, head_size
        )
        grad_blk = lax.dynamic_slice_in_dim(grad_pad, offset, key_block_rows, 1).reshape(
            sequences, key_block_rows, local_heads, head_size
        )
        doc_blk = lax.dynamic_slice_in_dim(key_doc_pad, offset, key_block_rows, 1)
        total_blk = lax.dynamic_slice_in_dim(total_pad, offset, key_block_rows, 1)
        delta_blk = lax.dynamic_slice_in_dim(delta_pad, offset, key_block_rows, 1)
        row_place = offset + jnp.arange(key_block_rows, dtype=jnp.int32)
        scores, same_doc, bucket = scores_with_bias(
            query_blk,
            key_heads,
            row_place,
            doc_blk,
            local_place,
            local_docs,
            local_token,
            bias_table,
        )
        probabilities = jnp.where(same_doc, jnp.exp(scores - total_blk[..., None]), 0.0)
        grad_value = grad_value + jnp.einsum(
            PRODUCT_11,
            probabilities.astype(jnp.bfloat16),
            grad_blk,
            preferred_element_type=jnp.float32,
        )
        value_dots = jnp.einsum(
            PRODUCT_8, grad_blk, value_heads, preferred_element_type=jnp.float32
        )
        grad_scores = (probabilities * (value_dots - delta_blk[..., None])).astype(jnp.bfloat16)
        grad_key = grad_key + jnp.einsum(
            PRODUCT_11, grad_scores, query_blk, preferred_element_type=jnp.float32
        )
        return ((grad_key, grad_value), None)

    fold_state, unused = lax.scan(key_advance, fold_state, jnp.arange(blocks, dtype=jnp.int32))
    grad_key, grad_value = fold_state
    grad_query_low = grad_query.reshape(sequences, shard_rows, local_inner).astype(jnp.bfloat16)
    grad_key_low = grad_key.reshape(sequences, key_span, local_inner).astype(jnp.bfloat16)
    grad_value_low = grad_value.reshape(sequences, key_span, local_inner).astype(jnp.bfloat16)
    grad_query_weight = jnp.einsum(
        PRODUCT_3, normed_low, grad_query_low, preferred_element_type=jnp.float32
    )
    grad_key_weight = jnp.einsum(
        PRODUCT_6, both_rows, grad_key_low, preferred_element_type=jnp.float32
    )
    grad_value_weight = jnp.einsum(
        PRODUCT_6, both_rows, grad_value_low, preferred_element_type=jnp.float32
    )
    row_part = jnp.einsum(
        PRODUCT_7, grad_key_low, full_key, preferred_element_type=jnp.float32
    ) + jnp.einsum(PRODUCT_7, grad_value_low, full_value, preferred_element_type=jnp.float32)
    token_part = row_part[:, :shard_rows] + jnp.einsum(
        PRODUCT_5, grad_query_low, full_query, preferred_element_type=jnp.float32
    )
    grad_normed, grad_memory_normed = (
        lax.psum(token_part.astype(jnp.bfloat16), TENSOR).astype(jnp.float32),
        lax.psum(row_part[:, shard_rows:].astype(jnp.bfloat16), TENSOR).astype(jnp.float32),
    )
    back_inputs, gain_tokens = norm_back(inputs_float, input_scale, attn_gain, grad_normed)
    back_memory, gain_memory = norm_back(memory_float, memory_scale, attn_gain, grad_memory_normed)
    grad_inputs = grad_residual + back_inputs
    grad_attn_gain = gain_tokens + gain_memory
    (
        shard_query,
        shard_key,
        shard_value,
        shard_output,
        shard_inner,
        shard_outer,
        shard_attn_gain,
        shard_dense_gain,
    ) = sum_grads(
        (
            grad_query_weight,
            grad_key_weight,
            grad_value_weight,
            grad_output,
            grad_inner,
            grad_outer,
            grad_attn_gain,
            grad_dense_gain,
        )
    )
    loss_sum, grad_bias_sum = lax.psum((loss_local, grad_bias), ROWS)
    return (
        loss_sum / (token_count * model_width),
        result.astype(jnp.bfloat16),
        grad_inputs,
        back_memory,
        shard_attn_gain,
        shard_query,
        shard_key,
        shard_value,
        shard_output,
        grad_bias_sum,
        shard_dense_gain,
        shard_inner,
        shard_outer,
    )


PAD = 16
BF = jnp.bfloat16
F32 = jnp.float32


def fits(mesh):
    sizes = dict(mesh.shape)
    return sizes[FSDP] == 2 and sizes[CONTEXT] == 8 and sizes[TENSOR] == 2


def swap_context(value, mask):
    return lax.ppermute(value, CONTEXT, [(i, i ^ mask) for i in range(8)])


def swap_core(pieces):
    return [swap_context(piece, 1) for piece in pieces]


def swap_fsdp(value):
    return lax.ppermute(value, FSDP, [(0, 1), (1, 0)])


def swap_tensor(value):
    return lax.ppermute(value, TENSOR, [(0, 1), (1, 0)])


def dot_nn(left, right):
    return lax.dot_general(left, right, (((1,), (0,)), ((), ())), preferred_element_type=F32)


def dot_nt(left, right):
    return lax.dot_general(left, right, (((1,), (1,)), ((), ())), preferred_element_type=F32)


def dot_tn(left, right):
    return lax.dot_general(left, right, (((0,), (0,)), ((), ())), preferred_element_type=F32)


def padded_bytes(shape, dtype):
    size = jnp.dtype(dtype).itemsize
    rows = 8 * (4 // size)
    lead = 1
    for count in shape[:-2]:
        lead *= count
    second = shape[-2] if len(shape) > 1 else 1
    return lead * -(-second // rows) * rows * -(-shape[-1] // 128) * 128 * size


def call(kernel, outs, name, ins_hbm=0, scratch=(), waits=()):
    def run(*operands):
        count = len(operands)
        specs = [pl.BlockSpec(memory_space=pltpu.VMEM)] * (count - ins_hbm)
        specs += [pl.BlockSpec(memory_space=pltpu.HBM)] * ins_hbm
        specs += [pl.BlockSpec(memory_space=pl.ANY)] * len(waits)
        held = [(item.shape, item.dtype) for item in operands[: count - ins_hbm]] + list(outs)
        held += [(item.shape, item.dtype) for item in scratch if item.memory_space == pltpu.VMEM]
        limit = 6 * 1024 * 1024 + sum(padded_bytes(shape, dtype) for shape, dtype in held)

        placed = list(operands)
        for at in range(count - ins_hbm, count):
            placed[at] = pltpu.with_memory_space_constraint(placed[at], pltpu.HBM)

        def body(*refs):
            kernel(*refs[:count], *refs[count + len(waits) :])

        return pl.pallas_call(
            body,
            out_shape=[jax.ShapeDtypeStruct(shape, dtype) for shape, dtype in outs],
            in_specs=specs,
            out_specs=[pl.BlockSpec(memory_space=pltpu.VMEM)] * len(outs),
            scratch_shapes=list(scratch),
            compiler_params=pltpu.CompilerParams(vmem_limit_bytes=limit),
            name=name,
        )(*placed, *waits)

    return run


def gate(value, *waits):
    def body(*refs):
        del refs

    return pl.pallas_call(
        body,
        out_shape=jax.ShapeDtypeStruct(value.shape, value.dtype),
        in_specs=[pl.BlockSpec(memory_space=pl.ANY)] * (1 + len(waits)),
        out_specs=pl.BlockSpec(memory_space=pl.ANY),
        input_output_aliases={0: 0},
        compiler_params=pltpu.CompilerParams(vmem_limit_bytes=1024 * 1024),
    )(value, *waits)


def diagonal(rows):
    return lax.broadcasted_iota(jnp.int32, (rows, 128), 0) == lax.broadcasted_iota(
        jnp.int32, (rows, 128), 1
    )


def row_to_column(row, rows):
    return jnp.sum(
        jnp.where(diagonal(rows), jnp.broadcast_to(row, (rows, 128)), 0.0), axis=1, keepdims=True
    )


def bucket_onehot(block_distance, span):
    lane = lax.broadcasted_iota(jnp.int32, (BUCKETS, 2 * span), 1)
    offset = jnp.where(lane < span, lane, lane - 2 * span)
    bucket = relative_bucket(block_distance * span - offset)
    return bucket == lax.broadcasted_iota(jnp.int32, (BUCKETS, 2 * span), 0)


def pack_kernel(*refs):
    sources, (early_ref, later_ref) = refs[:13], refs[13:15]
    small, tail_ref, sems = refs[15:21], refs[21], refs[22]
    x, memory, segments, owner, valid, wq, wk, wv, wo, wi, wf, gain, dense_gain = sources
    span, slots = x.shape[0], memory.shape[0]
    rows_each, inner = wq.shape
    hidden = wi.shape[1]
    base = span + PAD
    lower = slice(base, base + rows_each)
    upper = slice(base + rows_each, base + 2 * rows_each)
    left, right = slice(0, inner), slice(inner, 2 * inner)
    targets = [
        (memory, small[0]),
        (segments, small[1]),
        (owner, small[2]),
        (valid, small[3]),
        (gain, small[4]),
        (dense_gain, small[5]),
        (wq, early_ref.at[lower, left]),
        (wk, early_ref.at[lower, right]),
        (wv, early_ref.at[upper, left]),
        (wo, early_ref.at[upper, right]),
        (x, early_ref.at[slice(0, span), :]),
        (wi, later_ref.at[:, slice(0, hidden)]),
        (wf, later_ref.at[:, slice(hidden, 2 * hidden)]),
    ]
    copies = [
        pltpu.make_async_copy(source, target, sems.at[i])
        for i, (source, target) in enumerate(targets)
    ]
    for copy in copies:
        copy.start()
    for copy in copies[:6]:
        copy.wait()
    memory, segments, owner, valid, gain, dense_gain = small
    tail_ref[...] = jnp.zeros_like(tail_ref)
    tail_ref[0:slots, :] = memory[...].astype(F32)
    tail_ref[slots : slots + 1, 0:span] = segments[...].astype(F32)
    tail_ref[slots : slots + 1, span : span + slots] = owner[...].astype(F32)
    early_ref[span:base, :] = tail_ref[...].astype(BF)
    tail_ref[...] = jnp.zeros_like(tail_ref)
    tail_ref[0:1, 0:rows_each] = gain[...].astype(F32)
    tail_ref[1:2, 0:rows_each] = dense_gain[...].astype(F32)
    tail_ref[2:3, 0:1] = jnp.sum(valid[...].astype(F32), axis=1, keepdims=True)
    early_ref[base + 2 * rows_each : base + 2 * rows_each + PAD, :] = tail_ref[...].astype(BF)
    for copy in copies[6:]:
        copy.wait()


def stack_kernel(one_ref, two_ref, out_ref):
    rows = one_ref.shape[0]
    out_ref[0:rows, :] = one_ref[...]
    out_ref[rows : 2 * rows, :] = two_ref[...]


def order_kernel(*refs, rows_each):
    group = lax.axis_index(FSDP) * 8 + lax.axis_index(CONTEXT)
    for p in range(16):
        source = refs[(p >> 1 & 1) + 2 * (p >> 3) + 4 * (p & 1)]
        at = (p >> 2 & 1) * rows_each
        start = pl.multiple_of((group ^ p) * rows_each, 16)
        refs[8][pl.ds(start, rows_each), :] = source[at : at + rows_each, :]


def split_kernel(own_ref, far_ref, block_ref, first_ref):
    rows, first_rows = block_ref.shape[0] // 2, first_ref.shape[0] // 2
    for at, source in enumerate((own_ref, far_ref)):
        block_ref[at * rows : (at + 1) * rows, :] = source[0:rows, :]
        first_ref[at * first_rows : (at + 1) * first_rows, :] = source[rows:, :]


def attend_kernel(*refs, span, slots, tokens, inner, rows_each):
    weight_refs = refs[0:8]
    block_refs = refs[8:12]
    bias_ref = refs[12]
    (normed_ref, kv_ref, q_ref, w_ref, p_ref, low_ref, wide_ref, gains_ref, part_ref) = refs[13:22]
    (mask_ref, toep_ref, score_ref) = refs[22:]
    place = lax.axis_index(CONTEXT)
    group = lax.axis_index(FSDP) * 8 + place
    piece = 2 * rows_each + PAD
    gathered = jnp.zeros((8, gains_ref.shape[1]), F32)
    for p in range(16):
        source = weight_refs[(p >> 1 & 1) + 2 * (p >> 3) + 4 * (p & 1)]
        at = (p >> 2 & 1) * piece
        start = pl.multiple_of((group ^ p) * rows_each, 16)
        w_ref[pl.ds(start, rows_each), 0 : 2 * inner] = source[at : at + rows_each, :]
        w_ref[pl.ds(start, rows_each), 2 * inner :] = source[at + rows_each : at + 2 * rows_each, :]
        lines = source[at + 2 * rows_each : at + piece, :].astype(F32)[0:8, :]
        gathered = gathered + pltpu.roll(lines, (group ^ p) * rows_each, 1)
    row_ids = lax.broadcasted_iota(jnp.int32, gathered.shape, 0)
    count = jnp.sum(gathered[2:3, :])
    gains_ref[...] = jnp.where(row_ids == 2, count, gathered)
    gain = gathered[0:1, :]
    own_docs = None
    for p in range(8):
        block = place ^ p
        source = block_refs[(p >> 1 & 1) + 2 * (p & 1)]
        at = (p >> 2) * (span + PAD)
        token_at = pl.multiple_of(block * span, span)
        slot_at = pl.multiple_of(tokens + block * PAD, PAD)
        values = source[at : at + span, :].astype(F32)
        scale = lax.rsqrt(jnp.mean(values * values, axis=-1, keepdims=True) + norm_eps)
        normed_ref[pl.ds(token_at, span), :] = (values * scale * gain).astype(BF)
        tail = source[at + span : at + span + PAD, :].astype(F32)
        docs = tail[slots : slots + 1, 0 : 2 * span]
        tail_rows = lax.broadcasted_iota(jnp.int32, tail.shape, 0)
        tail = jnp.where(tail_rows < slots, tail, 0.0)
        scale = lax.rsqrt(jnp.mean(tail * tail, axis=-1, keepdims=True) + norm_eps)
        normed_ref[pl.ds(slot_at, PAD), :] = (tail * scale * gain).astype(BF)
        if p == 0:
            own_docs = docs[:, 0:span]
        token_docs = row_to_column(docs[:, 0:span], span)
        mask_ref[pl.ds(token_at, span), :] = jnp.where(token_docs == own_docs, 0.0, score_floor)
        slot_docs = row_to_column(docs[:, span : 2 * span], PAD)
        slot_rows = lax.broadcasted_iota(jnp.int32, (PAD, 1), 0)
        slot_docs = jnp.where(slot_rows < slots, slot_docs, -1.0)
        mask_ref[pl.ds(slot_at, PAD), :] = jnp.where(slot_docs == own_docs, 0.0, score_floor)
    kv_ref[...] = dot_nn(normed_ref[...], w_ref[:, inner : 3 * inner]).astype(BF)
    own_at = pl.multiple_of(place * span, span)
    q_ref[...] = dot_nn(normed_ref[pl.ds(own_at, span), :], w_ref[:, :inner]).astype(BF)
    heads = bias_ref.shape[0]
    for e in range(5):
        table = dot_nn(bias_ref[...], jnp.where(bucket_onehot(e - 2, span), 1.0, 0.0).astype(BF))
        for h in range(heads):
            line = jnp.broadcast_to(table[h : h + 1, :], (span, 2 * span))
            if abs(e - 2) < 2:
                line = pltpu.roll(line, 0, 1, stride=1, stride_axis=0)
            toep_ref[h, e] = line[:, :span]
    lane = lax.broadcasted_iota(jnp.int32, (span, span), 1)
    sub = lax.broadcasted_iota(jnp.int32, (span, span), 0)
    count_blocks = tokens // span
    slot_rows_all = score_ref.shape[0] - tokens
    for t in range(inner // span):
        keys = kv_ref[:, t * span : (t + 1) * span]
        values = kv_ref[:, inner + t * span : inner + (t + 1) * span]
        pair = q_ref[:, t * span : (t + 1) * span]
        zero = jnp.zeros_like(pair)
        both = jnp.concatenate(
            [jnp.where(lane < span // 2, pair, zero), jnp.where(lane < span // 2, zero, pair)], axis=0
        )
        score_ref[...] = dot_nt(keys, both)
        best = jnp.full((1, 2 * span), score_floor, F32)
        for s in range(count_blocks):
            e = jnp.clip(s - place, -2, 2) + 2
            at = slice(s * span, (s + 1) * span)
            terms = jnp.concatenate([toep_ref[2 * t, e], toep_ref[2 * t + 1, e]], axis=1)
            mask = mask_ref[at, :]
            block = score_ref[at, :] + terms + jnp.concatenate([mask, mask], axis=1)
            score_ref[at, :] = block
            best = jnp.maximum(best, jnp.max(block, axis=0, keepdims=True))
        at = slice(tokens, tokens + slot_rows_all)
        mask = mask_ref[at, :]
        block = score_ref[at, :] + jnp.concatenate([mask, mask], axis=1)
        score_ref[at, :] = block
        best = jnp.maximum(best, jnp.max(block, axis=0, keepdims=True))
        total = jnp.zeros((1, 2 * span), F32)
        for s in range(score_ref.shape[0] // span):
            at = slice(s * span, (s + 1) * span)
            weights = jnp.exp(score_ref[at, :] - best)
            score_ref[at, :] = weights
            total = total + jnp.sum(weights, axis=0, keepdims=True)
        inverse = 1.0 / total
        for s in range(score_ref.shape[0] // span):
            at = slice(s * span, (s + 1) * span)
            p_ref[t, at, :] = (score_ref[at, :] * inverse).astype(BF)
        out = dot_tn(values, p_ref[t])
        out = jnp.where(sub < span // 2, out[:, :span], out[:, span:])
        wide_ref[t * span : (t + 1) * span, :] = out
        low_ref[:, t * span : (t + 1) * span] = jnp.transpose(out).astype(BF)
    part_ref[...] = dot_nt(low_ref[...], w_ref[:, 3 * inner :]).astype(BF)


def forward_kernel(
    x_ref,
    own_ref,
    far_ref,
    gains_ref,
    weights_ref,
    residual_ref,
    dense_ref,
    hidden_ref,
    slope_ref,
    part_ref,
):
    hidden = hidden_ref.shape[1]
    residual = x_ref[...].astype(F32) + (own_ref[...].astype(F32) + far_ref[...].astype(F32))
    residual_ref[...] = residual
    scale = lax.rsqrt(jnp.mean(residual * residual, axis=-1, keepdims=True) + norm_eps)
    dense_ref[...] = (residual * scale * gains_ref[1:2, :]).astype(BF)
    step = 256
    for at in range(0, hidden, step):
        pre = dot_nn(dense_ref[...], weights_ref[:, at : at + step])
        square = pre * pre
        root = 0.7978845608028654
        tanh = jnp.tanh(root * (pre + 0.044715 * pre * square))
        hidden_ref[:, at : at + step] = (0.5 * pre * (1.0 + tanh)).astype(BF)
        slope_ref[:, at : at + step] = 0.5 * (1.0 + tanh) + 0.5 * pre * (1.0 - tanh * tanh) * (
            root * (1.0 + 3.0 * 0.044715 * square)
        )
    part_ref[...] = dot_nt(hidden_ref[...], weights_ref[:, hidden:]).astype(BF)


def backward_kernel(
    residual_ref,
    own_ref,
    far_ref,
    teacher_ref,
    valid_ref,
    gains_ref,
    slope_ref,
    weights_ref,
    hidden_ref,
    dense_ref,
    out_ref,
    grad_ref,
    part_ref,
    loss_ref,
    outer_keep_ref,
    outer_send_ref,
    inner_keep_ref,
    inner_send_ref,
    back_ref,
    pre_ref,
    lines_ref,
    *,
    total_rows,
    rows_each,
):
    hidden = pre_ref.shape[1]
    result = residual_ref[...] + (own_ref[...].astype(F32) + far_ref[...].astype(F32))
    out_ref[...] = result.astype(BF)
    rows = result.shape[0]
    valid = row_to_column(valid_ref[...].astype(F32), rows)
    misfit = result - teacher_ref[...].astype(F32)
    loss = 0.5 * jnp.sum(valid * misfit * misfit)
    loss_ref[...] = jnp.full(loss_ref.shape, loss, F32)
    factor = total_rows / gains_ref[2:3, 0:1]
    grad = factor * valid * misfit
    grad_ref[...] = grad
    back_ref[...] = grad.astype(BF)
    step = 256
    for at in range(0, hidden, step):
        grad_hidden = dot_nn(back_ref[...], weights_ref[:, hidden + at : hidden + at + step])
        pre_ref[:, at : at + step] = (grad_hidden * slope_ref[:, at : at + step]).astype(BF)
    part_ref[...] = dot_nt(pre_ref[...], weights_ref[:, :hidden]).astype(BF)
    dense_grad(back_ref[...], hidden_ref, outer_keep_ref, outer_send_ref, lines_ref, rows_each)
    dense_grad(dense_ref[...], pre_ref, inner_keep_ref, inner_send_ref, lines_ref, rows_each)


def split_rows(value, target_ref, rows_each):
    place = lax.axis_index(CONTEXT)
    mine = lax.rem(place, 2)
    half = value.shape[0] // 2
    source = target_ref.at[0]
    source[...] = value
    ordered = target_ref.at[1]
    for g in range(8):
        keep = pl.multiple_of((2 * g + mine) * rows_each, 16)
        send = pl.multiple_of((2 * g + 1 - mine) * rows_each, 16)
        ordered[g * rows_each : (g + 1) * rows_each, :] = source[pl.ds(keep, rows_each), :]
        ordered[half + g * rows_each : half + (g + 1) * rows_each, :] = source[
            pl.ds(send, rows_each), :
        ]


def put_rows(product, start, keep_ref, send_refs):
    rows_each = keep_ref.shape[1]
    cols = slice(start, start + product.shape[1])
    low = product.astype(BF)
    for g in range(8):
        keep_ref[g, :, cols] = low[g * rows_each : (g + 1) * rows_each, :]
        send_ref = send_refs[g * len(send_refs) // 8]
        send_ref[g % send_ref.shape[0], :, cols] = low[(8 + g) * rows_each : (9 + g) * rows_each, :]


def dense_grad(left, right_ref, keep_ref, send_ref, lines_ref, rows_each):
    split_rows(jnp.transpose(left.astype(F32)).astype(BF), lines_ref, rows_each)
    for at in range(0, right_ref.shape[1], 512):
        put_rows(dot_nn(lines_ref[1], right_ref[:, at : at + 512]), at, keep_ref, [send_ref])


def attention_back_kernel(
    own_ref,
    far_ref,
    grad_ref,
    residual_ref,
    gains_ref,
    wide_ref,
    p_ref,
    kv_ref,
    q_ref,
    w_ref,
    residual_grad_ref,
    back_ref,
    dq_ref,
    dkv_ref,
    gain_ref,
    small_ref,
    ds_ref,
    diag_ref,
    *,
    inner,
    span,
    tokens,
):
    place = lax.axis_index(CONTEXT)
    incoming = own_ref[...].astype(F32) + far_ref[...].astype(F32)
    residual = residual_ref[...]
    scale = lax.rsqrt(jnp.mean(residual * residual, axis=-1, keepdims=True) + norm_eps)
    scaled = incoming * gains_ref[1:2, :]
    mean = jnp.mean(scaled * residual, axis=-1, keepdims=True)
    residual_grad = grad_ref[...] + (scale * scaled - residual * (scale * scale * scale * mean))
    residual_grad_ref[...] = residual_grad
    gain_ref[...] = jnp.broadcast_to(
        jnp.sum(incoming * residual * scale, axis=0, keepdims=True), gain_ref.shape
    )
    back_ref[...] = residual_grad.astype(BF)
    grads = dot_nn(back_ref[...], w_ref[:, 3 * inner :])
    lane = lax.broadcasted_iota(jnp.int32, (span, span), 1)
    sub = lax.broadcasted_iota(jnp.int32, (span, span), 0)
    keys_all = p_ref.shape[1]
    blocks = tokens // span
    small_ref[...] = jnp.zeros_like(small_ref)
    tables = [bucket_onehot(d, span).astype(F32) for d in (-1, 0, 1)]
    zero = jnp.zeros((span, span), BF)
    for t in range(inner // span):
        cols = slice(t * span, (t + 1) * span)
        keys = kv_ref[:, cols]
        values = kv_ref[:, inner + t * span : inner + (t + 1) * span]
        pair = grads[:, cols].astype(BF)
        pair_back = jnp.transpose(pair.astype(F32)) * wide_ref[cols, :]
        delta = jnp.concatenate(
            [
                jnp.sum(pair_back[: span // 2], axis=0, keepdims=True),
                jnp.sum(pair_back[span // 2 :], axis=0, keepdims=True),
            ],
            axis=1,
        )
        grad_both = jnp.concatenate(
            [jnp.where(lane < span // 2, pair, zero), jnp.where(lane < span // 2, zero, pair)], axis=0
        )
        query = q_ref[:, cols]
        query_both = jnp.concatenate(
            [jnp.where(lane < span // 2, query, zero), jnp.where(lane < span // 2, zero, query)],
            axis=0,
        )
        low_sum = jnp.zeros((1, 2 * span), F32)
        high_sum = jnp.zeros((1, 2 * span), F32)
        for s in range(keys_all // span):
            at = slice(s * span, (s + 1) * span)
            dots = dot_nt(values[at, :], grad_both)
            ds = (p_ref[t, at, :].astype(F32) * (dots - delta)).astype(BF)
            ds_ref[at, :] = ds
            if s < blocks:
                line = jnp.sum(ds.astype(F32), axis=0, keepdims=True)
                low_sum = low_sum + jnp.where(s < place - 1, line, 0.0)
                high_sum = high_sum + jnp.where(s > place + 1, line, 0.0)
        dkv_ref[:, cols] = dot_nn(ds_ref[...], query_both).astype(BF)
        dkv_ref[:, inner + t * span : inner + (t + 1) * span] = dot_nn(p_ref[t], grad_both).astype(
            BF
        )
        dq = dot_tn(keys, ds_ref[...])
        dq = jnp.where(sub < span // 2, dq[:, :span], dq[:, span:])
        dq_ref[:, cols] = jnp.transpose(dq).astype(BF)
        for head in range(2):
            for which in range(3):
                s = place + which - 1
                inside = (s >= 0) & (s < blocks)
                start = pl.multiple_of(jnp.clip(s, 0, blocks - 1) * span, span)
                block = ds_ref[pl.ds(start, span), head * span : (head + 1) * span].astype(F32)
                block = jnp.where(inside, block, 0.0)
                block = jnp.concatenate([block, jnp.zeros((span, span), F32)], axis=1)
                size = span
                while size > 8:
                    size = size // 2
                    block = block[:size] + pltpu.roll(block[size:], 2 * span - size, 1)
                line = block[0:1]
                for j in range(1, 8):
                    line = line + pltpu.roll(block, 2 * span - j, 1)[j : j + 1]
                diag_ref[which, 2 * t + head : 2 * t + head + 1, :] = line
            bucket = lax.broadcasted_iota(jnp.int32, (1, 128), 1)
            part = slice(head * span, (head + 1) * span)
            low_total = jnp.sum(low_sum[:, part], axis=1, keepdims=True)
            high_total = jnp.sum(high_sum[:, part], axis=1, keepdims=True)
            small_ref[2 * t + head : 2 * t + head + 1, :] = jnp.where(
                bucket == BUCKETS // 2 - 1, low_total, 0.0
            ) + jnp.where(bucket == BUCKETS - 1, high_total, 0.0)
    heads = inner * 2 // span
    for which in range(3):
        line = lax.dot_general(
            diag_ref[which],
            tables[which],
            (((1,), (1,)), ((), ())),
            preferred_element_type=F32,
            precision=lax.Precision.HIGHEST,
        )
        small_ref[0:heads, 0:BUCKETS] += line[0:heads, :]


def rows_grad_kernel(
    dq_ref,
    dkv_ref,
    w_ref,
    normed_ref,
    gains_ref,
    dense_gain_ref,
    small_ref,
    loss_ref,
    keep_ref,
    *refs,
    inner,
    span,
    tokens,
    slots,
    heads,
):
    send_refs, (part_ref, line_ref) = refs[:-2], refs[-2:]
    place = lax.axis_index(CONTEXT)
    mine = lax.rem(place, 2)
    side = lax.axis_index(TENSOR)
    part_ref[...] = dot_nt(dkv_ref[...], w_ref[:, inner : 3 * inner])
    own_at = pl.multiple_of(place * span, span)
    part_ref[pl.ds(own_at, span), :] += dot_nt(dq_ref[...], w_ref[:, :inner])
    total = jnp.zeros((1, part_ref.shape[1]), F32)
    for s in range(part_ref.shape[0] // span):
        at = slice(s * span, (s + 1) * span)
        total = total + jnp.sum(
            part_ref[at, :] * normed_ref[at, :].astype(F32), axis=0, keepdims=True
        )
    line_ref[...] = jnp.zeros_like(line_ref)
    line_ref[slots : slots + 1, :] = total / gains_ref[0:1, :]
    line_ref[slots + 1 : slots + 2, :] = 0.5 * dense_gain_ref[0:1, :]
    for h in range(heads):
        start = pl.multiple_of(side * 128, 128)
        line_ref[slots + 2 + h : slots + 3 + h, pl.ds(start, 128)] = small_ref[h : h + 1, :]
    line_ref[slots + 2 : slots + 3, 256:384] = 0.5 * loss_ref[0:1, :]
    keep_rows = lax.broadcasted_iota(jnp.int32, line_ref.shape, 0) < slots
    for g in range(4):
        for target, block in (
            (keep_ref.at[g], 2 * g + mine),
            (send_refs[g // 2].at[g % 2], 2 * g + 1 - mine),
        ):
            token_at = pl.multiple_of(block * span, span)
            slot_at = pl.multiple_of(tokens + block * PAD, PAD)
            target[0:span, :] = part_ref[pl.ds(token_at, span), :].astype(BF)
            tail = jnp.where(keep_rows, part_ref[pl.ds(slot_at, PAD), :], line_ref[...])
            target[span : span + PAD, :] = tail.astype(BF)


def weight_grad_kernel(
    dq_ref,
    dkv_ref,
    normed_ref,
    back_ref,
    low_ref,
    keep_ref,
    *refs,
    inner,
    span,
    rows_each,
):
    send_refs, (wide_ref, line_ref) = refs[:-2], refs[-2:]
    place = lax.axis_index(CONTEXT)

    def put(product, start):
        put_rows(product, start, keep_ref, send_refs)

    split_rows(jnp.transpose(back_ref[...].astype(F32)).astype(BF), line_ref, rows_each)
    put(dot_nn(line_ref[1], low_ref[...]), 3 * inner)
    own_at = pl.multiple_of(place * span, span)
    own = normed_ref[pl.ds(own_at, span), :].astype(F32)
    split_rows(jnp.transpose(own).astype(BF), line_ref, rows_each)
    put(dot_nn(line_ref[1], dq_ref[...]), 0)
    split_rows(jnp.transpose(normed_ref[...].astype(F32)).astype(BF), wide_ref, rows_each)
    for at in range(0, 2 * inner, 256):
        put(dot_nn(wide_ref[1], dkv_ref[:, at : at + 256]), inner + at)


def halve_kernel(keep_ref, *refs):
    far_refs, targets = refs[:-2], refs[-2:]
    mine = lax.axis_index(FSDP)
    for flip in range(2):

        @pl.when(mine == flip)
        def _():
            for half in range(2):
                target = targets[half ^ flip]
                for g in range(4):
                    at = 4 * half + g
                    total = keep_ref[at].astype(F32) + far_refs[at * len(far_refs) // 8][at % far_refs[0].shape[0]].astype(F32)
                    target[g] = total.astype(BF)


def quarter_kernel(keep_ref, far_ref, next_ref, send_ref):
    place = lax.axis_index(CONTEXT) // 2
    for target, flip in ((next_ref, 0), (send_ref, 1)):
        for g in range(2):
            block = place ^ (flip + 2 * g)
            total = keep_ref[block].astype(F32) + far_ref[block].astype(F32)
            target[g] = total.astype(BF)


def eighth_kernel(keep_ref, far_ref, own_ref, send_ref):
    own_ref[...] = (keep_ref[0].astype(F32) + far_ref[0].astype(F32)).astype(own_ref.dtype)
    send_ref[...] = (keep_ref[1].astype(F32) + far_ref[1].astype(F32)).astype(BF)


def total_kernel(own_ref, far_ref, *out_refs):
    at = 0
    for out in out_refs:
        cols = slice(at, at + out.shape[1])
        out[...] = (own_ref[:, cols].astype(F32) + far_ref[:, cols].astype(F32)).astype(out.dtype)
        at += out.shape[1]


def columns_kernel(keep_ref, one_ref, two_ref, next_ref, send_ref):
    mine = lax.axis_index(TENSOR)
    width = next_ref.shape[2]
    for target, start in ((next_ref, mine * width), (send_ref, (1 - mine) * width)):
        cols = pl.ds(pl.multiple_of(start, 128), width)
        for half, far_ref in ((slice(0, 2), one_ref), (slice(2, 4), two_ref)):
            total = keep_ref[half, :, cols].astype(F32) + far_ref[:, :, cols].astype(F32)
            target[half] = total.astype(BF)


def tail_kernel(own_ref, far_ref, out_ref, *, span):
    mine = lax.axis_index(TENSOR)
    width = own_ref.shape[1]
    rows = slice(span, span + PAD)
    out_ref[:, pl.ds(pl.multiple_of(mine * width, 128), width)] = own_ref[rows, :].astype(F32)
    out_ref[:, pl.ds(pl.multiple_of((1 - mine) * width, 128), width)] = far_ref[rows, :].astype(F32)


def finish_kernel(
    own_ref,
    far_ref,
    block_ref,
    gains_ref,
    residual_grad_ref,
    tail_own_ref,
    tail_far_ref,
    inputs_ref,
    memory_ref,
    gain_ref,
    dense_gain_ref,
    bias_ref,
    loss_ref,
    full_ref,
    line_ref,
    *,
    span,
    slots,
):
    mine = lax.axis_index(TENSOR)
    group = lax.axis_index(FSDP) * 8 + lax.axis_index(CONTEXT)
    width = own_ref.shape[1]
    full_ref[:, pl.ds(pl.multiple_of(mine * width, 128), width)] = own_ref[...].astype(F32)
    full_ref[:, pl.ds(pl.multiple_of((1 - mine) * width, 128), width)] = far_ref[...].astype(F32)
    values = block_ref[0 : span + PAD, :].astype(F32)
    row_ids = lax.broadcasted_iota(jnp.int32, values.shape, 0)
    values = jnp.where(row_ids < span + slots, values, 0.0)
    scale = lax.rsqrt(jnp.mean(values * values, axis=-1, keepdims=True) + norm_eps)
    scaled = full_ref[...] * gains_ref[0:1, :]
    mean = jnp.mean(scaled * values, axis=-1, keepdims=True)
    back = scale * scaled - values * (scale * scale * scale * mean)
    inputs_ref[...] = residual_grad_ref[...] + back[0:span]
    memory_ref[...] = back[span : span + slots]
    line_ref[...] = tail_own_ref[...] + tail_far_ref[...]
    lines = pltpu.roll(line_ref[...], full_ref.shape[1] - group * gain_ref.shape[1], 1)
    rows_each = gain_ref.shape[1]
    gain_ref[...] = lines[slots : slots + 1, 0:rows_each]
    dense_gain_ref[...] = lines[slots + 1 : slots + 2, 0:rows_each]
    heads = bias_ref.shape[0]
    start = pl.multiple_of(mine * 128, 128)
    bias_ref[...] = line_ref[slots + 2 : slots + 2 + heads, pl.ds(start, 128)][:, 0:BUCKETS]
    loss_ref[...] = line_ref[slots + 2 : slots + 3, 256:384] / (
        gains_ref[2:3, 0:128] * full_ref.shape[1]
    )


def fast_local(
    inputs,
    memory,
    teacher,
    segments,
    memory_owner,
    valid_mask,
    attention_gain,
    query_weight,
    key_weight,
    value_weight,
    attention_out_weight,
    position_bias,
    feedforward_gain,
    inner_weight,
    feedforward_out_weight,
):
    span, width = inputs.shape[1:]
    slots = memory.shape[1]
    rows_each, inner = query_weight.shape
    hidden = inner_weight.shape[1]
    heads = position_bias.shape[0]
    tokens = 8 * span
    keys_all = 8 * (span + PAD)
    total_rows = 2 * tokens
    x = inputs[0]
    early, later = call(
        pack_kernel,
        [
            ((span + 2 * PAD + 2 * rows_each, width), BF),
            ((rows_each, 2 * hidden), BF),
        ],
        ins_hbm=13,
        name="pack",
        scratch=(
            pltpu.VMEM((slots, width), BF),
            pltpu.VMEM((1, span), jnp.int32),
            pltpu.VMEM((1, slots), jnp.int32),
            pltpu.VMEM((1, span), jnp.int32),
            pltpu.VMEM((1, rows_each), BF),
            pltpu.VMEM((1, rows_each), BF),
            pltpu.VMEM((PAD, width), F32),
            pltpu.SemaphoreType.DMA((13,)),
        ),
    )(
        x,
        memory[0],
        segments,
        memory_owner,
        valid_mask,
        query_weight,
        key_weight,
        value_weight,
        attention_out_weight,
        inner_weight,
        feedforward_out_weight,
        attention_gain[None],
        feedforward_gain[None],
    )

    def stack(one, two, *waits):
        rows, columns = one.shape
        return call(stack_kernel, [((2 * rows, columns), BF)], name="stack", waits=waits)(one, two)[0]

    block_two, first_two = call(
        split_kernel,
        [((2 * (span + PAD), width), BF), ((2 * (2 * rows_each + PAD), width), BF)],
        name="split",
    )(early, swap_context(early, 4))
    first_all = [first_two, swap_context(first_two, 2)]
    first_all += [swap_fsdp(piece) for piece in first_all]
    first_all += [swap_context(piece, 1) for piece in first_all]
    block_all = [block_two, swap_context(block_two, 2)]
    block_all += [swap_context(piece, 1) for piece in block_all]
    later = gate(later, first_two)
    later_two = stack(later, swap_context(later, 4), *first_all[2:4], block_all[1])
    later_all = [later_two, swap_context(later_two, 2)]
    later_far = swap_fsdp(later_two)

    (normed, kv, queries, w_all, probs, low, wide, gains, part) = call(
        lambda *refs: attend_kernel(
            *refs, span=span, slots=slots, tokens=tokens, inner=inner, rows_each=rows_each
        ),
        [
            ((keys_all, width), BF),
            ((keys_all, 2 * inner), BF),
            ((span, inner), BF),
            ((width, 4 * inner), BF),
            ((inner // span, keys_all, 2 * span), BF),
            ((span, inner), BF),
            ((inner, span), F32),
            ((8, width), F32),
            ((span, width), BF),
        ],
        name="attend",
        scratch=(
            pltpu.VMEM((keys_all, span), F32),
            pltpu.VMEM((heads, 5, span, span), F32),
            pltpu.VMEM((keys_all, 2 * span), F32),
        ),
    )(*first_all, *block_all, position_bias)
    far = swap_tensor(part)
    later_all[1] = gate(later_all[1], part)
    later_all += [gate(later_far, part), gate(swap_fsdp(later_all[1]), far)]
    later_all += [swap_context(piece, 1) for piece in later_all]
    (dense_weights,) = call(
        lambda *refs: order_kernel(*refs, rows_each=rows_each),
        [((width, 2 * hidden), BF)],
        name="order",
        waits=(part,),
    )(*later_all)
    (residual, dense_low, hidden_low, slope, dense_part) = call(
        forward_kernel,
        [
            ((span, width), F32),
            ((span, width), BF),
            ((span, hidden), BF),
            ((span, hidden), F32),
            ((span, width), BF),
        ],
        name="forward",
    )(x, part, far, gains, dense_weights)
    dense_far = swap_tensor(dense_part)
    (output, grad_result, grad_part, loss_part, *dense_grads) = call(
        lambda *refs: backward_kernel(*refs, total_rows=total_rows, rows_each=rows_each),
        [
            ((span, width), BF),
            ((span, width), F32),
            ((span, width), BF),
            ((8, 128), F32),
        ]
        + [((8, rows_each, hidden), BF)] * 4,
        name="backward",
        scratch=(
            pltpu.VMEM((span, width), BF),
            pltpu.VMEM((span, hidden), BF),
            pltpu.VMEM((2, width, span), BF),
        ),
    )(
        residual,
        dense_part,
        dense_far,
        teacher[0],
        valid_mask,
        gains,
        slope,
        dense_weights,
        hidden_low,
        dense_low,
    )
    outer_keep, outer_send, inner_keep, inner_send = dense_grads
    grad_far = swap_tensor(grad_part)

    def halve(keep, far_core, *waits):
        return call(
            halve_kernel,
            [((4, rows_each, keep.shape[2]), BF)] * 2,
            name="halve",
            waits=waits,
        )(keep, *far_core)

    def quarter(keep, far_half, *waits):
        rows, columns = keep.shape[1:]
        return call(
            quarter_kernel,
            [((2, rows, columns), BF)] * 2,
            name="quarter",
            waits=waits,
        )(keep, far_half)

    def eighth(keep, far_quarter, own_type, *waits):
        rows, columns = keep.shape[1:]
        return call(
            eighth_kernel,
            [((rows, columns), own_type), ((rows, columns), BF)],
            name="eighth",
            waits=waits,
        )(keep, far_quarter)

    def total(own, far_eighth, outs, *waits):
        return call(total_kernel, outs, name="total", waits=waits)(own, far_eighth)

    outer_far = swap_core([outer_send])
    inner_far = swap_core([inner_send])
    outer_next, outer_over = halve(outer_keep, outer_far)
    outer_far = swap_fsdp(outer_over)

    (grad_residual, attention_back, dq, dkv, dense_gain_rows, small) = call(
        lambda *refs: attention_back_kernel(*refs, inner=inner, span=span, tokens=tokens),
        [
            ((span, width), F32),
            ((span, width), BF),
            ((span, inner), BF),
            ((keys_all, 2 * inner), BF),
            ((8, width), F32),
            ((8, 128), F32),
        ],
        name="attend_back",
        scratch=(
            pltpu.VMEM((keys_all, 2 * span), BF),
            pltpu.VMEM((3, 8, 2 * span), F32),
        ),
        waits=(outer_over,),
    )(grad_part, grad_far, grad_result, residual, gains, wide, probs, kv, queries, w_all)

    rows_keep, *rows_send = call(
        lambda *refs: rows_grad_kernel(
            *refs, inner=inner, span=span, tokens=tokens, slots=slots, heads=heads
        ),
        [((4, span + PAD, width), BF)] + [((2, span + PAD, width), BF)] * 2,
        name="rows_grad",
        scratch=(pltpu.VMEM((keys_all, width), F32), pltpu.VMEM((PAD, width), F32)),
    )(dq, dkv, w_all, normed, gains, dense_gain_rows, small, loss_part)
    rows_far = swap_core(rows_send)

    weight_keep, *weight_send = call(
        lambda *refs: weight_grad_kernel(*refs, inner=inner, span=span, rows_each=rows_each),
        [((8, rows_each, 4 * inner), BF)] + [((4, rows_each, 4 * inner), BF)] * 2,
        name="weight_grad",
        scratch=(
            pltpu.VMEM((2, width, keys_all), BF),
            pltpu.VMEM((2, width, span), BF),
        ),
        waits=(rows_send[0],),
    )(dq, dkv, normed, attention_back, low)
    weight_far = swap_core(weight_send)
    inner_next, inner_over = halve(inner_keep, inner_far, weight_send[0], outer_far)
    inner_far = swap_fsdp(inner_over)
    outer_next, outer_over = quarter(outer_next, outer_far, inner_over)
    outer_far = swap_context(outer_over, 2)

    rows_next, rows_over = call(
        columns_kernel,
        [((4, span + PAD, width // 2), BF)] * 2,
        name="columns",
        waits=(outer_over,),
    )(rows_keep, *rows_far)
    rows_far = swap_tensor(rows_over)
    outer_own, outer_over = eighth(outer_next, outer_far, F32, rows_over)
    outer_far = swap_context(outer_over, 4)
    weight_next, weight_over = halve(weight_keep, weight_far, outer_over)
    weight_far = swap_fsdp(weight_over)
    inner_next, inner_over = quarter(inner_next, inner_far, weight_over)
    inner_far = swap_context(inner_over, 2)
    rows_next, rows_over = quarter(rows_next, rows_far, inner_over)
    rows_far = swap_context(rows_over, 2)
    (grad_outer,) = total(outer_own, outer_far, [((rows_each, hidden), F32)], rows_over)
    rows_own, rows_over = eighth(rows_next, rows_far, BF, grad_outer)
    rows_far = swap_context(rows_over, 4)
    inner_own, inner_over = eighth(inner_next, inner_far, F32, rows_over)
    inner_far = swap_context(inner_over, 4)
    weight_next, weight_over = quarter(weight_next, weight_far, inner_over)
    weight_far = swap_context(weight_over, 2)
    (rows_half,) = total(rows_own, rows_far, [((span + PAD, width // 2), BF)], weight_over)
    rows_other = swap_tensor(rows_half)
    (grad_inner,) = total(inner_own, inner_far, [((rows_each, hidden), F32)], rows_half)
    weight_own, weight_over = eighth(weight_next, weight_far, F32, grad_inner)
    weight_far = swap_context(weight_over, 4)
    (tail,) = call(
        lambda *refs: tail_kernel(*refs, span=span),
        [((PAD, width), F32)],
        name="tail",
        waits=(weight_over,),
    )(rows_half, rows_other)
    tail_far = swap_fsdp(tail)
    weight_grads = total(weight_own, weight_far, [((rows_each, inner), F32)] * 4)

    (grad_inputs, grad_memory, grad_gain, grad_dense_gain, grad_bias, loss) = call(
        lambda *refs: finish_kernel(*refs, span=span, slots=slots),
        [
            ((span, width), F32),
            ((slots, width), F32),
            ((1, rows_each), F32),
            ((1, rows_each), F32),
            ((heads, BUCKETS), F32),
            ((1, 128), F32),
        ],
        name="finish",
        scratch=(pltpu.VMEM((span + PAD, width), F32), pltpu.VMEM((PAD, width), F32)),
    )(rows_half, rows_other, block_two, gains, grad_residual, tail, tail_far)
    return (
        loss[0, 0],
        output[None],
        grad_inputs[None],
        grad_memory[None],
        grad_gain[0],
        weight_grads[0],
        weight_grads[1],
        weight_grads[2],
        weight_grads[3],
        grad_bias,
        grad_dense_gain[0],
        grad_inner,
        grad_outer,
    )


def solution(mesh):
    return jax.shard_map(
        fast_local if fits(mesh) else general_local,
        mesh=mesh,
        in_specs=(
            P(FSDP, CONTEXT, None),
            P(FSDP, CONTEXT, None),
            P(FSDP, CONTEXT, None),
            P(FSDP, CONTEXT),
            P(FSDP, CONTEXT),
            P(FSDP, CONTEXT),
            P(ROWS),
            P(ROWS, TENSOR),
            P(ROWS, TENSOR),
            P(ROWS, TENSOR),
            P(ROWS, TENSOR),
            P(TENSOR, None),
            P(ROWS),
            P(ROWS, TENSOR),
            P(ROWS, TENSOR),
        ),
        out_specs=(
            P(),
            P(FSDP, CONTEXT, None),
            P(FSDP, CONTEXT, None),
            P(FSDP, CONTEXT, None),
            P(ROWS),
            P(ROWS, TENSOR),
            P(ROWS, TENSOR),
            P(ROWS, TENSOR),
            P(ROWS, TENSOR),
            P(TENSOR, None),
            P(ROWS),
            P(ROWS, TENSOR),
            P(ROWS, TENSOR),
        ),
        check_vma=False,
    )
```

```python
import jax
import jax.numpy as jnp
from jax import lax
from jax.experimental import pallas as pl
from jax.experimental.pallas import tpu as pltpu
from jax.sharding import PartitionSpec as P

BUCKETS = 32
FSDP = "fsdp"
CONTEXT = "context"
TENSOR = "tensor"
ROWS = (FSDP, CONTEXT)
PRODUCT_0 = "scd,df->scf"
PRODUCT_1 = "scd,di->sci"
PRODUCT_2 = "scd,scf->df"
PRODUCT_3 = "scd,sci->di"
PRODUCT_4 = "scf,df->scd"
PRODUCT_5 = "sci,di->scd"
PRODUCT_6 = "sjd,sji->di"
PRODUCT_7 = "sji,di->sjd"
PRODUCT_8 = "sqhd,skhd->sqhk"
PRODUCT_9 = "sqhk,qkb->hb"
PRODUCT_10 = "sqhk,skhd->sqhd"
PRODUCT_11 = "sqhk,sqhd->skhd"


norm_eps = 1e-06
score_floor = -1e30


def relative_bucket(distance):
    half_count = BUCKETS // 2
    exact_count = half_count // 2
    magnitude = jnp.minimum(jnp.abs(distance), 1024)
    far_bucket = jnp.full(distance.shape, exact_count, jnp.int32)
    for level_index in range(1, half_count - exact_count):
        far_bucket = far_bucket + (
            magnitude * magnitude >= exact_count * exact_count * 2**level_index
        ).astype(jnp.int32)
    bucket_ids = jnp.where(magnitude < exact_count, magnitude, far_bucket)
    return bucket_ids + (distance > 0).astype(jnp.int32) * half_count


def rms_norm(values, gain_in):
    inv_rms = lax.rsqrt(jnp.mean(values * values, axis=-1, keepdims=True) + norm_eps)
    return (values * inv_rms * gain_in, inv_rms)


def norm_back(values, inv_rms, gain_in, grad_in):
    scaled = grad_in * gain_in
    inner_mean = jnp.mean(scaled * values, axis=-1, keepdims=True)
    grad_values = inv_rms * scaled - values * inv_rms * inv_rms * inv_rms * inner_mean
    grad_gain = jnp.sum(grad_in * values * inv_rms, axis=tuple(range(values.ndim - 1)))
    return (grad_values, grad_gain)


def smooth_gate(values):
    return jax.nn.gelu(values, approximate=True)


def block_size():
    return 512


def pad_rows(values_in, block_rows, fill_value):
    blocks = -(-values_in.shape[1] // block_rows)
    missing = blocks * block_rows - values_in.shape[1]
    padding = [(0, 0)] * values_in.ndim
    padding[1] = (0, missing)
    return (jnp.pad(values_in, padding, constant_values=fill_value), blocks)


def key_places(row_ids, shard_rows, key_span):
    within = row_ids % key_span
    return (row_ids // key_span * shard_rows + within, within < shard_rows)


def scores_with_bias(
    query_blk, key_blk, query_place, query_doc, key_place, key_doc, key_token, bias_table
):
    scores = jnp.einsum(PRODUCT_8, query_blk, key_blk, preferred_element_type=jnp.float32)
    bucket = relative_bucket(key_place[None, :] - query_place[:, None])
    rel_terms = jnp.where(key_token[None, None, :], jnp.take(bias_table, bucket, axis=1), 0.0)
    scores = scores + jnp.moveaxis(rel_terms, 0, 1)[None]
    same_doc = (query_doc[:, :, None] == key_doc[:, None, :])[:, :, None, :]
    return (scores, same_doc, bucket)


def sum_grads(grad_items):
    return (
        lax.psum_scatter(grad_items[0], ROWS, scatter_dimension=0, tiled=True),
        lax.psum_scatter(grad_items[1], ROWS, scatter_dimension=0, tiled=True),
        lax.psum_scatter(grad_items[2], ROWS, scatter_dimension=0, tiled=True),
        lax.psum_scatter(grad_items[3], ROWS, scatter_dimension=0, tiled=True),
        lax.psum_scatter(grad_items[4], ROWS, scatter_dimension=0, tiled=True),
        lax.psum_scatter(grad_items[5], ROWS, scatter_dimension=0, tiled=True),
        lax.psum_scatter(grad_items[6], ROWS, scatter_dimension=0, tiled=True),
        lax.psum_scatter(grad_items[7], ROWS, scatter_dimension=0, tiled=True),
    )


def general_local(
    inputs,
    memory,
    teacher,
    segments,
    memory_owner,
    valid_mask,
    attention_gain,
    query_weight,
    key_weight,
    value_weight,
    attention_out_weight,
    position_bias,
    feedforward_gain,
    inner_weight,
    feedforward_out_weight,
):
    sequences, shard_rows, model_width = inputs.shape
    key_span = shard_rows + memory.shape[1]
    context_size = lax.axis_size(CONTEXT)
    length = shard_rows * context_size
    context_place = lax.axis_index(CONTEXT)
    local_heads = position_bias.shape[0]
    bucket_count = position_bias.shape[1]
    head_size = query_weight.shape[1] // local_heads
    local_inner = local_heads * head_size
    total_rows = sequences * length * lax.axis_size(FSDP)
    bias_table = position_bias.astype(jnp.float32)
    (
        full_query,
        full_key,
        full_value,
        full_output,
        full_inner,
        full_outer,
        full_attn_gain,
        full_dense_gain,
    ) = (
        lax.all_gather(query_weight, ROWS, axis=0, tiled=True),
        lax.all_gather(key_weight, ROWS, axis=0, tiled=True),
        lax.all_gather(value_weight, ROWS, axis=0, tiled=True),
        lax.all_gather(attention_out_weight, ROWS, axis=0, tiled=True),
        lax.all_gather(inner_weight, ROWS, axis=0, tiled=True),
        lax.all_gather(feedforward_out_weight, ROWS, axis=0, tiled=True),
        lax.all_gather(attention_gain, ROWS, axis=0, tiled=True),
        lax.all_gather(feedforward_gain, ROWS, axis=0, tiled=True),
    )
    attn_gain = full_attn_gain.astype(jnp.float32)
    dense_gain = full_dense_gain.astype(jnp.float32)
    local_docs = jnp.concatenate([segments, memory_owner], axis=1)
    key_docs = lax.all_gather(local_docs, CONTEXT, axis=1, tiled=True)
    query_docs_all = key_docs.reshape(sequences, context_size, key_span)[:, :, :shard_rows].reshape(
        sequences, length
    )
    token_count = lax.psum(jnp.sum(valid_mask.astype(jnp.float32)), ROWS)
    inputs_float = inputs.astype(jnp.float32)
    memory_float = memory.astype(jnp.float32)
    normed, input_scale = rms_norm(inputs_float, attn_gain)
    memory_normed, memory_scale = rms_norm(memory_float, attn_gain)
    normed_low = normed.astype(jnp.bfloat16)
    both_rows = jnp.concatenate([normed_low, memory_normed.astype(jnp.bfloat16)], axis=1)
    queries = jnp.dot(normed_low, full_query, preferred_element_type=jnp.float32).astype(
        jnp.bfloat16
    )
    key_local = jnp.dot(both_rows, full_key, preferred_element_type=jnp.float32).astype(
        jnp.bfloat16
    )
    value_local = jnp.dot(both_rows, full_value, preferred_element_type=jnp.float32).astype(
        jnp.bfloat16
    )
    query_heads = queries.reshape(sequences, shard_rows, local_heads, head_size)
    query_place = context_place * shard_rows + jnp.arange(shard_rows, dtype=jnp.int32)
    fold_init = (
        jnp.full((sequences, shard_rows, local_heads), score_floor, jnp.float32),
        jnp.zeros((sequences, shard_rows, local_heads), jnp.float32),
        jnp.zeros((sequences, shard_rows, local_heads, head_size), jnp.float32),
    )
    fold_state = fold_init
    key_piece = lax.all_gather(key_local, CONTEXT, axis=1, tiled=True)
    value_piece = lax.all_gather(value_local, CONTEXT, axis=1, tiled=True)
    block_rows = block_size()
    key_pad, blocks = pad_rows(key_piece, block_rows, 0)
    value_pad, blocks = pad_rows(value_piece, block_rows, 0)
    doc_pad, blocks = pad_rows(key_docs, block_rows, -1)

    def attend_advance(running, block_index):
        running_best, running_sum, summed = running
        offset = block_index * block_rows
        key_blk = lax.dynamic_slice_in_dim(key_pad, offset, block_rows, 1).reshape(
            sequences, block_rows, local_heads, head_size
        )
        value_blk = lax.dynamic_slice_in_dim(value_pad, offset, block_rows, 1).reshape(
            sequences, block_rows, local_heads, head_size
        )
        doc_blk = lax.dynamic_slice_in_dim(doc_pad, offset, block_rows, 1)
        key_place, key_token = key_places(
            offset + jnp.arange(block_rows, dtype=jnp.int32), shard_rows, key_span
        )
        scores, same_doc, bucket = scores_with_bias(
            query_heads, key_blk, query_place, segments, key_place, doc_blk, key_token, bias_table
        )
        masked = jnp.where(same_doc, scores, score_floor)
        new_best = jnp.maximum(running_best, jnp.max(masked, axis=-1))
        weights = jnp.where(same_doc, jnp.exp(scores - new_best[..., None]), 0.0)
        factor = jnp.exp(running_best - new_best)
        running_sum = running_sum * factor + jnp.sum(weights, axis=-1)
        summed = summed * factor[..., None] + jnp.einsum(
            PRODUCT_10,
            weights.astype(jnp.bfloat16),
            value_blk,
            preferred_element_type=jnp.float32,
        )
        return ((new_best, running_sum, summed), None)

    fold_state, unused = lax.scan(attend_advance, fold_state, jnp.arange(blocks, dtype=jnp.int32))
    running_best, running_sum, summed = fold_state
    attended_values = summed / running_sum[..., None]
    attended_low = attended_values.reshape(sequences, shard_rows, local_inner).astype(jnp.bfloat16)
    attention_part = jnp.einsum(
        PRODUCT_5, attended_low, full_output, preferred_element_type=jnp.float32
    )
    residual = inputs_float + lax.psum(attention_part.astype(jnp.bfloat16), TENSOR).astype(
        jnp.float32
    )
    dense_normed, dense_scale = rms_norm(residual, dense_gain)
    dense_low = dense_normed.astype(jnp.bfloat16)
    inner_pre = jnp.dot(dense_low, full_inner, preferred_element_type=jnp.float32)
    hidden_float, gate_pullback = jax.vjp(smooth_gate, inner_pre)
    hidden_low = hidden_float.astype(jnp.bfloat16)
    dense_part = jnp.einsum(
        PRODUCT_4, hidden_low, full_outer, preferred_element_type=jnp.float32
    )
    result = residual + lax.psum(dense_part.astype(jnp.bfloat16), TENSOR).astype(jnp.float32)
    target_mask = valid_mask.astype(jnp.float32)[..., None]
    misfit = result - teacher.astype(jnp.float32)
    loss_local = 0.5 * jnp.sum(target_mask * misfit * misfit)
    grad_result = total_rows / token_count * target_mask * misfit
    dense_back = grad_result.astype(jnp.bfloat16)
    grad_outer = jnp.einsum(
        PRODUCT_2, dense_back, hidden_low, preferred_element_type=jnp.float32
    )
    grad_hidden = jnp.einsum(
        PRODUCT_0, dense_back, full_outer, preferred_element_type=jnp.float32
    )
    grad_pre = gate_pullback(grad_hidden)[0].astype(jnp.bfloat16)
    grad_inner = jnp.einsum(PRODUCT_2, dense_low, grad_pre, preferred_element_type=jnp.float32)
    grad_dense_part = jnp.einsum(
        PRODUCT_4, grad_pre, full_inner, preferred_element_type=jnp.float32
    )
    grad_dense_normed = lax.psum(grad_dense_part.astype(jnp.bfloat16), TENSOR).astype(jnp.float32)
    back_residual, grad_dense_gain = norm_back(residual, dense_scale, dense_gain, grad_dense_normed)
    grad_residual = grad_result + back_residual
    attention_back = grad_residual.astype(jnp.bfloat16)
    grad_output = jnp.einsum(
        PRODUCT_3, attention_back, attended_low, preferred_element_type=jnp.float32
    )
    grad_attended = jnp.einsum(
        PRODUCT_1, attention_back, full_output, preferred_element_type=jnp.float32
    ).astype(jnp.bfloat16)
    grad_heads = grad_attended.reshape(sequences, shard_rows, local_heads, head_size)
    log_total = running_best + jnp.log(running_sum)
    delta_rows = jnp.sum(grad_heads.astype(jnp.float32) * attended_values, axis=-1)
    all_log_total, all_delta = (
        lax.all_gather(log_total, CONTEXT, axis=1, tiled=True),
        lax.all_gather(delta_rows, CONTEXT, axis=1, tiled=True),
    )
    query_init = (
        jnp.zeros((sequences, shard_rows, local_heads, head_size), jnp.float32),
        jnp.zeros((local_heads, bucket_count), jnp.float32),
    )
    fold_state = query_init
    key_piece = lax.all_gather(key_local, CONTEXT, axis=1, tiled=True)
    value_piece = lax.all_gather(value_local, CONTEXT, axis=1, tiled=True)
    query_block_rows = block_size()
    query_key_pad, blocks = pad_rows(key_piece, query_block_rows, 0)
    query_value_pad, blocks = pad_rows(value_piece, query_block_rows, 0)
    query_doc_pad, blocks = pad_rows(key_docs, query_block_rows, -1)

    def query_advance(running, block_index):
        grad_query, grad_bias = running
        offset = block_index * query_block_rows
        key_blk = lax.dynamic_slice_in_dim(query_key_pad, offset, query_block_rows, 1).reshape(
            sequences, query_block_rows, local_heads, head_size
        )
        value_blk = lax.dynamic_slice_in_dim(query_value_pad, offset, query_block_rows, 1).reshape(
            sequences, query_block_rows, local_heads, head_size
        )
        doc_blk = lax.dynamic_slice_in_dim(query_doc_pad, offset, query_block_rows, 1)
        key_place, key_token = key_places(
            offset + jnp.arange(query_block_rows, dtype=jnp.int32), shard_rows, key_span
        )
        scores, same_doc, bucket = scores_with_bias(
            query_heads, key_blk, query_place, segments, key_place, doc_blk, key_token, bias_table
        )
        probabilities = jnp.where(same_doc, jnp.exp(scores - log_total[..., None]), 0.0)
        value_dots = jnp.einsum(
            PRODUCT_8, grad_heads, value_blk, preferred_element_type=jnp.float32
        )
        grad_scores = (probabilities * (value_dots - delta_rows[..., None])).astype(jnp.bfloat16)
        grad_query = grad_query + jnp.einsum(
            PRODUCT_10, grad_scores, key_blk, preferred_element_type=jnp.float32
        )
        bucket_hits = (
            (bucket[:, :, None] == jnp.arange(bucket_count, dtype=jnp.int32)[None, None, :])
            & key_token[None, :, None]
        ).astype(jnp.bfloat16)
        grad_bias = grad_bias + jnp.einsum(
            PRODUCT_9, grad_scores, bucket_hits, preferred_element_type=jnp.float32
        )
        return ((grad_query, grad_bias), None)

    fold_state, unused = lax.scan(query_advance, fold_state, jnp.arange(blocks, dtype=jnp.int32))
    grad_query, grad_bias = fold_state
    key_heads = key_local.reshape(sequences, key_span, local_heads, head_size)
    value_heads = value_local.reshape(sequences, key_span, local_heads, head_size)
    local_place, local_token = key_places(
        context_place * key_span + jnp.arange(key_span, dtype=jnp.int32), shard_rows, key_span
    )
    key_init = (
        jnp.zeros((sequences, key_span, local_heads, head_size), jnp.float32),
        jnp.zeros((sequences, key_span, local_heads, head_size), jnp.float32),
    )
    fold_state = key_init
    query_piece = lax.all_gather(queries, CONTEXT, axis=1, tiled=True)
    grad_piece = lax.all_gather(grad_attended, CONTEXT, axis=1, tiled=True)
    key_block_rows = block_size()
    query_pad, blocks = pad_rows(query_piece, key_block_rows, 0)
    grad_pad, blocks = pad_rows(grad_piece, key_block_rows, 0)
    key_doc_pad, blocks = pad_rows(query_docs_all, key_block_rows, -1)
    total_pad, blocks = pad_rows(all_log_total, key_block_rows, 0.0)
    delta_pad, blocks = pad_rows(all_delta, key_block_rows, 0.0)

    def key_advance(running, block_index):
        grad_key, grad_value = running
        offset = block_index * key_block_rows
        query_blk = lax.dynamic_slice_in_dim(query_pad, offset, key_block_rows, 1).reshape(
            sequences, key_block_rows, local_heads, head_size
        )
        grad_blk = lax.dynamic_slice_in_dim(grad_pad, offset, key_block_rows, 1).reshape(
            sequences, key_block_rows, local_heads, head_size
        )
        doc_blk = lax.dynamic_slice_in_dim(key_doc_pad, offset, key_block_rows, 1)
        total_blk = lax.dynamic_slice_in_dim(total_pad, offset, key_block_rows, 1)
        delta_blk = lax.dynamic_slice_in_dim(delta_pad, offset, key_block_rows, 1)
        row_place = offset + jnp.arange(key_block_rows, dtype=jnp.int32)
        scores, same_doc, bucket = scores_with_bias(
            query_blk,
            key_heads,
            row_place,
            doc_blk,
            local_place,
            local_docs,
            local_token,
            bias_table,
        )
        probabilities = jnp.where(same_doc, jnp.exp(scores - total_blk[..., None]), 0.0)
        grad_value = grad_value + jnp.einsum(
            PRODUCT_11,
            probabilities.astype(jnp.bfloat16),
            grad_blk,
            preferred_element_type=jnp.float32,
        )
        value_dots = jnp.einsum(
            PRODUCT_8, grad_blk, value_heads, preferred_element_type=jnp.float32
        )
        grad_scores = (probabilities * (value_dots - delta_blk[..., None])).astype(jnp.bfloat16)
        grad_key = grad_key + jnp.einsum(
            PRODUCT_11, grad_scores, query_blk, preferred_element_type=jnp.float32
        )
        return ((grad_key, grad_value), None)

    fold_state, unused = lax.scan(key_advance, fold_state, jnp.arange(blocks, dtype=jnp.int32))
    grad_key, grad_value = fold_state
    grad_query_low = grad_query.reshape(sequences, shard_rows, local_inner).astype(jnp.bfloat16)
    grad_key_low = grad_key.reshape(sequences, key_span, local_inner).astype(jnp.bfloat16)
    grad_value_low = grad_value.reshape(sequences, key_span, local_inner).astype(jnp.bfloat16)
    grad_query_weight = jnp.einsum(
        PRODUCT_3, normed_low, grad_query_low, preferred_element_type=jnp.float32
    )
    grad_key_weight = jnp.einsum(
        PRODUCT_6, both_rows, grad_key_low, preferred_element_type=jnp.float32
    )
    grad_value_weight = jnp.einsum(
        PRODUCT_6, both_rows, grad_value_low, preferred_element_type=jnp.float32
    )
    row_part = jnp.einsum(
        PRODUCT_7, grad_key_low, full_key, preferred_element_type=jnp.float32
    ) + jnp.einsum(PRODUCT_7, grad_value_low, full_value, preferred_element_type=jnp.float32)
    token_part = row_part[:, :shard_rows] + jnp.einsum(
        PRODUCT_5, grad_query_low, full_query, preferred_element_type=jnp.float32
    )
    grad_normed, grad_memory_normed = (
        lax.psum(token_part.astype(jnp.bfloat16), TENSOR).astype(jnp.float32),
        lax.psum(row_part[:, shard_rows:].astype(jnp.bfloat16), TENSOR).astype(jnp.float32),
    )
    back_inputs, gain_tokens = norm_back(inputs_float, input_scale, attn_gain, grad_normed)
    back_memory, gain_memory = norm_back(memory_float, memory_scale, attn_gain, grad_memory_normed)
    grad_inputs = grad_residual + back_inputs
    grad_attn_gain = gain_tokens + gain_memory
    (
        shard_query,
        shard_key,
        shard_value,
        shard_output,
        shard_inner,
        shard_outer,
        shard_attn_gain,
        shard_dense_gain,
    ) = sum_grads(
        (
            grad_query_weight,
            grad_key_weight,
            grad_value_weight,
            grad_output,
            grad_inner,
            grad_outer,
            grad_attn_gain,
            grad_dense_gain,
        )
    )
    loss_sum, grad_bias_sum = lax.psum((loss_local, grad_bias), ROWS)
    return (
        loss_sum / (token_count * model_width),
        result.astype(jnp.bfloat16),
        grad_inputs,
        back_memory,
        shard_attn_gain,
        shard_query,
        shard_key,
        shard_value,
        shard_output,
        grad_bias_sum,
        shard_dense_gain,
        shard_inner,
        shard_outer,
    )


PAD = 16
BF = jnp.bfloat16
F32 = jnp.float32


def fits(mesh):
    sizes = dict(mesh.shape)
    return sizes[FSDP] == 2 and sizes[CONTEXT] == 8 and sizes[TENSOR] == 2


def swap_context(value, mask):
    return lax.ppermute(value, CONTEXT, [(i, i ^ mask) for i in range(8)])


def swap_core(pieces):
    return [swap_context(piece, 1) for piece in pieces]


def swap_fsdp(value):
    return lax.ppermute(value, FSDP, [(0, 1), (1, 0)])


def swap_tensor(value):
    return lax.ppermute(value, TENSOR, [(0, 1), (1, 0)])


def dot_nn(left, right):
    return lax.dot_general(left, right, (((1,), (0,)), ((), ())), preferred_element_type=F32)


def dot_nt(left, right):
    return lax.dot_general(left, right, (((1,), (1,)), ((), ())), preferred_element_type=F32)


def dot_tn(left, right):
    return lax.dot_general(left, right, (((0,), (0,)), ((), ())), preferred_element_type=F32)


def padded_bytes(shape, dtype):
    size = jnp.dtype(dtype).itemsize
    rows = 8 * (4 // size)
    lead = 1
    for count in shape[:-2]:
        lead *= count
    second = shape[-2] if len(shape) > 1 else 1
    return lead * -(-second // rows) * rows * -(-shape[-1] // 128) * 128 * size


def call(kernel, outs, name, ins_hbm=0, scratch=(), waits=()):
    def run(*operands):
        count = len(operands)
        specs = [pl.BlockSpec(memory_space=pltpu.VMEM)] * (count - ins_hbm)
        specs += [pl.BlockSpec(memory_space=pltpu.HBM)] * ins_hbm
        specs += [pl.BlockSpec(memory_space=pl.ANY)] * len(waits)
        held = [(item.shape, item.dtype) for item in operands[: count - ins_hbm]] + list(outs)
        held += [(item.shape, item.dtype) for item in scratch if item.memory_space == pltpu.VMEM]
        limit = 6 * 1024 * 1024 + sum(padded_bytes(shape, dtype) for shape, dtype in held)

        placed = list(operands)
        for at in range(count - ins_hbm, count):
            placed[at] = pltpu.with_memory_space_constraint(placed[at], pltpu.HBM)

        def body(*refs):
            kernel(*refs[:count], *refs[count + len(waits) :])

        return pl.pallas_call(
            body,
            out_shape=[jax.ShapeDtypeStruct(shape, dtype) for shape, dtype in outs],
            in_specs=specs,
            out_specs=[pl.BlockSpec(memory_space=pltpu.VMEM)] * len(outs),
            scratch_shapes=list(scratch),
            compiler_params=pltpu.CompilerParams(vmem_limit_bytes=limit),
            name=name,
        )(*placed, *waits)

    return run


def gate(value, *waits):
    def body(*refs):
        del refs

    return pl.pallas_call(
        body,
        out_shape=jax.ShapeDtypeStruct(value.shape, value.dtype),
        in_specs=[pl.BlockSpec(memory_space=pl.ANY)] * (1 + len(waits)),
        out_specs=pl.BlockSpec(memory_space=pl.ANY),
        input_output_aliases={0: 0},
        compiler_params=pltpu.CompilerParams(vmem_limit_bytes=1024 * 1024),
    )(value, *waits)


def diagonal(rows):
    return lax.broadcasted_iota(jnp.int32, (rows, 128), 0) == lax.broadcasted_iota(
        jnp.int32, (rows, 128), 1
    )


def row_to_column(row, rows):
    return jnp.sum(
        jnp.where(diagonal(rows), jnp.broadcast_to(row, (rows, 128)), 0.0), axis=1, keepdims=True
    )


def bucket_onehot(block_distance, span):
    lane = lax.broadcasted_iota(jnp.int32, (BUCKETS, 2 * span), 1)
    offset = jnp.where(lane < span, lane, lane - 2 * span)
    bucket = relative_bucket(block_distance * span - offset)
    return bucket == lax.broadcasted_iota(jnp.int32, (BUCKETS, 2 * span), 0)


def pack_kernel(*refs):
    sources, (early_ref, later_ref) = refs[:13], refs[13:15]
    small, tail_ref, sems = refs[15:21], refs[21], refs[22]
    x, memory, segments, owner, valid, wq, wk, wv, wo, wi, wf, gain, dense_gain = sources
    span, slots = x.shape[0], memory.shape[0]
    rows_each, inner = wq.shape
    hidden = wi.shape[1]
    base = span + PAD
    half = pl.ds(pl.multiple_of(lax.axis_index(TENSOR) * inner, 128), inner)
    targets = [
        (memory, small[0]),
        (segments, small[1]),
        (owner, small[2]),
        (valid, small[3]),
        (gain, small[4]),
        (dense_gain, small[5]),
        (x.at[:, half], early_ref.at[slice(0, span), :]),
        (wi, later_ref.at[:, slice(0, hidden)]),
        (wf, later_ref.at[:, slice(hidden, 2 * hidden)]),
    ]
    for at, weight in enumerate((wq, wk, wv, wo)):
        start = base + at * rows_each
        targets.append((weight, early_ref.at[slice(start, start + rows_each), :]))
    copies = [
        pltpu.make_async_copy(source, target, sems.at[i])
        for i, (source, target) in enumerate(targets)
    ]
    for copy in copies:
        copy.start()
    for copy in copies[:6]:
        copy.wait()
    memory, segments, owner, valid, gain, dense_gain = small
    tail_ref[...] = jnp.zeros_like(tail_ref)
    tail_ref[0:slots, :] = memory[...].astype(F32)
    tail_ref[slots : slots + 1, 0:span] = segments[...].astype(F32)
    tail_ref[slots : slots + 1, span : span + slots] = owner[...].astype(F32)
    early_ref[span:base, :] = tail_ref[:, half].astype(BF)
    tail_ref[...] = jnp.zeros_like(tail_ref)
    tail_ref[0:1, 0:rows_each] = gain[...].astype(F32)
    tail_ref[1:2, 0:rows_each] = dense_gain[...].astype(F32)
    tail_ref[2:3, 0:1] = jnp.sum(valid[...].astype(F32), axis=1, keepdims=True)
    start = base + 4 * rows_each
    early_ref[start : start + PAD, :] = tail_ref[:, 0:inner].astype(BF)
    for copy in copies[6:]:
        copy.wait()


def stack_kernel(own_ref, far_ref, both_ref, left_ref, right_ref):
    rows, width = own_ref.shape[0], left_ref.shape[1]
    for at, source in enumerate((own_ref, far_ref)):
        lines = slice(at * rows, (at + 1) * rows)
        both_ref[lines, :] = source[...]
        left_ref[lines, :] = source[:, 0:width]
        right_ref[lines, :] = source[:, width:]


def order_kernel(*refs, rows_each):
    group = lax.axis_index(FSDP) * 8 + lax.axis_index(CONTEXT)
    target = refs[12]
    for p in range(16):
        start = pl.ds(pl.multiple_of((group ^ p) * rows_each, 16), rows_each)
        at = (p >> 2 & 1) * rows_each
        lines = slice(at, at + rows_each)
        x, z1, other = p >> 3, p >> 1 & 1, 6 * (p & 1)
        if z1:
            left, right = refs[other + 2 + 2 * x], refs[other + 3 + 2 * x]
            width = left.shape[1]
            target[start, 0:width] = left[lines, :]
            target[start, width:] = right[lines, :]
        else:
            target[start, :] = refs[other + x][lines, :]


def split_kernel(own_ref, far_ref, block_ref, first_ref):
    rows, first_rows = block_ref.shape[0] // 2, first_ref.shape[0] // 2
    for at, source in enumerate((own_ref, far_ref)):
        block_ref[at * rows : (at + 1) * rows, :] = source[0:rows, :]
        first_ref[at * first_rows : (at + 1) * first_rows, :] = source[rows:, :]


def attend_kernel(*refs, span, slots, tokens, inner, rows_each):
    weight_refs = refs[0:8]
    block_refs = refs[8:16]
    bias_ref = refs[16]
    (normed_ref, kv_ref, q_ref, w_ref, p_ref, low_ref, wide_ref, gains_ref, part_ref) = refs[17:26]
    (mask_ref, toep_ref, score_ref, whole_ref) = refs[26:]
    side = lax.axis_index(TENSOR)
    place = lax.axis_index(CONTEXT)
    group = lax.axis_index(FSDP) * 8 + place
    piece = 4 * rows_each + PAD
    gathered = jnp.zeros((8, gains_ref.shape[1]), F32)
    for p in range(16):
        source = weight_refs[(p >> 1 & 1) + 2 * (p >> 3) + 4 * (p & 1)]
        at = (p >> 2 & 1) * piece
        start = pl.multiple_of((group ^ p) * rows_each, 16)
        for which in range(4):
            w_ref[pl.ds(start, rows_each), which * inner : (which + 1) * inner] = source[
                at + which * rows_each : at + (which + 1) * rows_each, :
            ]
        lines = source[at + 4 * rows_each : at + piece, :].astype(F32)[0:8, :]
        lines = jnp.concatenate([lines, jnp.zeros_like(lines)], axis=1)
        gathered = gathered + pltpu.roll(lines, (group ^ p) * rows_each, 1)
    row_ids = lax.broadcasted_iota(jnp.int32, gathered.shape, 0)
    count = jnp.sum(gathered[2:3, :])
    gains_ref[...] = jnp.where(row_ids == 2, count, gathered)
    gain = gathered[0:1, :]
    own_docs = None
    for p in range(8):
        block = place ^ p
        at = (p >> 2) * (span + PAD)
        for far in range(2):
            source = block_refs[(p >> 1 & 1) + 2 * far + 4 * (p & 1)]
            cols = pl.ds(pl.multiple_of((side ^ far) * inner, 128), inner)
            whole_ref[:, cols] = source[at : at + span + PAD, :].astype(F32)
        token_at = pl.multiple_of(block * span, span)
        slot_at = pl.multiple_of(tokens + block * PAD, PAD)
        values = whole_ref[0:span, :]
        scale = lax.rsqrt(jnp.mean(values * values, axis=-1, keepdims=True) + norm_eps)
        normed_ref[pl.ds(token_at, span), :] = (values * scale * gain).astype(BF)
        tail = whole_ref[span : span + PAD, :]
        docs = tail[slots : slots + 1, 0 : 2 * span]
        tail_rows = lax.broadcasted_iota(jnp.int32, tail.shape, 0)
        tail = jnp.where(tail_rows < slots, tail, 0.0)
        scale = lax.rsqrt(jnp.mean(tail * tail, axis=-1, keepdims=True) + norm_eps)
        normed_ref[pl.ds(slot_at, PAD), :] = (tail * scale * gain).astype(BF)
        if p == 0:
            own_docs = docs[:, 0:span]
        token_docs = row_to_column(docs[:, 0:span], span)
        mask_ref[pl.ds(token_at, span), :] = jnp.where(token_docs == own_docs, 0.0, score_floor)
        slot_docs = row_to_column(docs[:, span : 2 * span], PAD)
        slot_rows = lax.broadcasted_iota(jnp.int32, (PAD, 1), 0)
        slot_docs = jnp.where(slot_rows < slots, slot_docs, -1.0)
        mask_ref[pl.ds(slot_at, PAD), :] = jnp.where(slot_docs == own_docs, 0.0, score_floor)
    kv_ref[...] = dot_nn(normed_ref[...], w_ref[:, inner : 3 * inner]).astype(BF)
    own_at = pl.multiple_of(place * span, span)
    q_ref[...] = dot_nn(normed_ref[pl.ds(own_at, span), :], w_ref[:, :inner]).astype(BF)
    heads = bias_ref.shape[0]
    for e in range(5):
        table = dot_nn(bias_ref[...], jnp.where(bucket_onehot(e - 2, span), 1.0, 0.0).astype(BF))
        for h in range(heads):
            line = jnp.broadcast_to(table[h : h + 1, :], (span, 2 * span))
            if abs(e - 2) < 2:
                line = pltpu.roll(line, 0, 1, stride=1, stride_axis=0)
            toep_ref[h, e] = line[:, :span]
    lane = lax.broadcasted_iota(jnp.int32, (span, span), 1)
    sub = lax.broadcasted_iota(jnp.int32, (span, span), 0)
    count_blocks = tokens // span
    slot_rows_all = score_ref.shape[0] - tokens
    for t in range(inner // span):
        keys = kv_ref[:, t * span : (t + 1) * span]
        values = kv_ref[:, inner + t * span : inner + (t + 1) * span]
        pair = q_ref[:, t * span : (t + 1) * span]
        zero = jnp.zeros_like(pair)
        both = jnp.concatenate(
            [jnp.where(lane < span // 2, pair, zero), jnp.where(lane < span // 2, zero, pair)], axis=0
        )
        score_ref[...] = dot_nt(keys, both)
        best = jnp.full((1, 2 * span), score_floor, F32)
        for s in range(count_blocks):
            e = jnp.clip(s - place, -2, 2) + 2
            at = slice(s * span, (s + 1) * span)
            terms = jnp.concatenate([toep_ref[2 * t, e], toep_ref[2 * t + 1, e]], axis=1)
            mask = mask_ref[at, :]
            block = score_ref[at, :] + terms + jnp.concatenate([mask, mask], axis=1)
            score_ref[at, :] = block
            best = jnp.maximum(best, jnp.max(block, axis=0, keepdims=True))
        at = slice(tokens, tokens + slot_rows_all)
        mask = mask_ref[at, :]
        block = score_ref[at, :] + jnp.concatenate([mask, mask], axis=1)
        score_ref[at, :] = block
        best = jnp.maximum(best, jnp.max(block, axis=0, keepdims=True))
        total = jnp.zeros((1, 2 * span), F32)
        for s in range(score_ref.shape[0] // span):
            at = slice(s * span, (s + 1) * span)
            weights = jnp.exp(score_ref[at, :] - best)
            score_ref[at, :] = weights
            total = total + jnp.sum(weights, axis=0, keepdims=True)
        inverse = 1.0 / total
        for s in range(score_ref.shape[0] // span):
            at = slice(s * span, (s + 1) * span)
            p_ref[t, at, :] = (score_ref[at, :] * inverse).astype(BF)
        out = dot_tn(values, p_ref[t])
        out = jnp.where(sub < span // 2, out[:, :span], out[:, span:])
        wide_ref[t * span : (t + 1) * span, :] = out
        low_ref[:, t * span : (t + 1) * span] = jnp.transpose(out).astype(BF)
    part_ref[...] = dot_nt(low_ref[...], w_ref[:, 3 * inner :]).astype(BF)


def forward_kernel(
    x_ref,
    own_ref,
    far_ref,
    gains_ref,
    weights_ref,
    residual_ref,
    dense_ref,
    hidden_ref,
    slope_ref,
    part_ref,
):
    hidden = hidden_ref.shape[1]
    residual = x_ref[...].astype(F32) + (own_ref[...].astype(F32) + far_ref[...].astype(F32))
    residual_ref[...] = residual
    scale = lax.rsqrt(jnp.mean(residual * residual, axis=-1, keepdims=True) + norm_eps)
    dense_ref[...] = (residual * scale * gains_ref[1:2, :]).astype(BF)
    step = 256
    for at in range(0, hidden, step):
        pre = dot_nn(dense_ref[...], weights_ref[:, at : at + step])
        square = pre * pre
        root = 0.7978845608028654
        tanh = jnp.tanh(root * (pre + 0.044715 * pre * square))
        hidden_ref[:, at : at + step] = (0.5 * pre * (1.0 + tanh)).astype(BF)
        slope_ref[:, at : at + step] = 0.5 * (1.0 + tanh) + 0.5 * pre * (1.0 - tanh * tanh) * (
            root * (1.0 + 3.0 * 0.044715 * square)
        )
    part_ref[...] = dot_nt(hidden_ref[...], weights_ref[:, hidden:]).astype(BF)


def backward_kernel(
    residual_ref,
    own_ref,
    far_ref,
    teacher_ref,
    valid_ref,
    gains_ref,
    slope_ref,
    weights_ref,
    hidden_ref,
    dense_ref,
    out_ref,
    grad_ref,
    part_ref,
    loss_ref,
    outer_keep_ref,
    outer_send_ref,
    inner_keep_ref,
    inner_send_ref,
    back_ref,
    pre_ref,
    lines_ref,
    *,
    total_rows,
    rows_each,
):
    hidden = pre_ref.shape[1]
    result = residual_ref[...] + (own_ref[...].astype(F32) + far_ref[...].astype(F32))
    out_ref[...] = result.astype(BF)
    rows = result.shape[0]
    valid = row_to_column(valid_ref[...].astype(F32), rows)
    misfit = result - teacher_ref[...].astype(F32)
    loss = 0.5 * jnp.sum(valid * misfit * misfit)
    loss_ref[...] = jnp.full(loss_ref.shape, loss, F32)
    factor = total_rows / gains_ref[2:3, 0:1]
    grad = factor * valid * misfit
    grad_ref[...] = grad
    back_ref[...] = grad.astype(BF)
    step = 256
    for at in range(0, hidden, step):
        grad_hidden = dot_nn(back_ref[...], weights_ref[:, hidden + at : hidden + at + step])
        pre_ref[:, at : at + step] = (grad_hidden * slope_ref[:, at : at + step]).astype(BF)
    part_ref[...] = dot_nt(pre_ref[...], weights_ref[:, :hidden]).astype(BF)
    dense_grad(back_ref[...], hidden_ref, outer_keep_ref, outer_send_ref, lines_ref, rows_each)
    dense_grad(dense_ref[...], pre_ref, inner_keep_ref, inner_send_ref, lines_ref, rows_each)


def split_rows(value, target_ref, rows_each):
    place = lax.axis_index(CONTEXT)
    mine = lax.rem(place, 2)
    half = value.shape[0] // 2
    source = target_ref.at[0]
    source[...] = value
    ordered = target_ref.at[1]
    for g in range(8):
        keep = pl.multiple_of((2 * g + mine) * rows_each, 16)
        send = pl.multiple_of((2 * g + 1 - mine) * rows_each, 16)
        ordered[g * rows_each : (g + 1) * rows_each, :] = source[pl.ds(keep, rows_each), :]
        ordered[half + g * rows_each : half + (g + 1) * rows_each, :] = source[
            pl.ds(send, rows_each), :
        ]


def put_rows(product, start, keep_ref, send_refs):
    rows_each = keep_ref.shape[1]
    cols = slice(start, start + product.shape[1])
    low = product.astype(BF)
    for g in range(8):
        keep_ref[g, :, cols] = low[g * rows_each : (g + 1) * rows_each, :]
        send_ref = send_refs[g * len(send_refs) // 8]
        send_ref[g % send_ref.shape[0], :, cols] = low[(8 + g) * rows_each : (9 + g) * rows_each, :]


def dense_grad(left, right_ref, keep_ref, send_ref, lines_ref, rows_each):
    split_rows(jnp.transpose(left.astype(F32)).astype(BF), lines_ref, rows_each)
    for at in range(0, right_ref.shape[1], 512):
        put_rows(dot_nn(lines_ref[1], right_ref[:, at : at + 512]), at, keep_ref, [send_ref])


def attention_back_kernel(
    own_ref,
    far_ref,
    grad_ref,
    residual_ref,
    gains_ref,
    wide_ref,
    p_ref,
    kv_ref,
    q_ref,
    w_ref,
    low_ref,
    residual_grad_ref,
    keep_ref,
    send_ref,
    dq_ref,
    dkv_ref,
    gain_ref,
    small_ref,
    ds_ref,
    diag_ref,
    line_ref,
    *,
    inner,
    span,
    tokens,
    rows_each,
):
    place = lax.axis_index(CONTEXT)
    incoming = own_ref[...].astype(F32) + far_ref[...].astype(F32)
    residual = residual_ref[...]
    scale = lax.rsqrt(jnp.mean(residual * residual, axis=-1, keepdims=True) + norm_eps)
    scaled = incoming * gains_ref[1:2, :]
    mean = jnp.mean(scaled * residual, axis=-1, keepdims=True)
    residual_grad = grad_ref[...] + (scale * scaled - residual * (scale * scale * scale * mean))
    residual_grad_ref[...] = residual_grad
    gain_ref[...] = jnp.broadcast_to(
        jnp.sum(incoming * residual * scale, axis=0, keepdims=True), gain_ref.shape
    )
    grads = dot_nn(residual_grad.astype(BF), w_ref[:, 3 * inner :])
    split_rows(jnp.transpose(residual_grad).astype(BF), line_ref, rows_each)
    put_rows(dot_nn(line_ref[1], low_ref[...]), 0, keep_ref, [send_ref])
    lane = lax.broadcasted_iota(jnp.int32, (span, span), 1)
    sub = lax.broadcasted_iota(jnp.int32, (span, span), 0)
    keys_all = p_ref.shape[1]
    blocks = tokens // span
    small_ref[...] = jnp.zeros_like(small_ref)
    tables = [bucket_onehot(d, span).astype(F32) for d in (-1, 0, 1)]
    zero = jnp.zeros((span, span), BF)
    for t in range(inner // span):
        cols = slice(t * span, (t + 1) * span)
        keys = kv_ref[:, cols]
        values = kv_ref[:, inner + t * span : inner + (t + 1) * span]
        pair = grads[:, cols].astype(BF)
        pair_back = jnp.transpose(pair.astype(F32)) * wide_ref[cols, :]
        delta = jnp.concatenate(
            [
                jnp.sum(pair_back[: span // 2], axis=0, keepdims=True),
                jnp.sum(pair_back[span // 2 :], axis=0, keepdims=True),
            ],
            axis=1,
        )
        grad_both = jnp.concatenate(
            [jnp.where(lane < span // 2, pair, zero), jnp.where(lane < span // 2, zero, pair)], axis=0
        )
        query = q_ref[:, cols]
        query_both = jnp.concatenate(
            [jnp.where(lane < span // 2, query, zero), jnp.where(lane < span // 2, zero, query)],
            axis=0,
        )
        low_sum = jnp.zeros((1, 2 * span), F32)
        high_sum = jnp.zeros((1, 2 * span), F32)
        for s in range(keys_all // span):
            at = slice(s * span, (s + 1) * span)
            dots = dot_nt(values[at, :], grad_both)
            ds = (p_ref[t, at, :].astype(F32) * (dots - delta)).astype(BF)
            ds_ref[at, :] = ds
            if s < blocks:
                line = jnp.sum(ds.astype(F32), axis=0, keepdims=True)
                low_sum = low_sum + jnp.where(s < place - 1, line, 0.0)
                high_sum = high_sum + jnp.where(s > place + 1, line, 0.0)
        dkv_ref[:, cols] = dot_nn(ds_ref[...], query_both).astype(BF)
        dkv_ref[:, inner + t * span : inner + (t + 1) * span] = dot_nn(p_ref[t], grad_both).astype(
            BF
        )
        dq = dot_tn(keys, ds_ref[...])
        dq = jnp.where(sub < span // 2, dq[:, :span], dq[:, span:])
        dq_ref[:, cols] = jnp.transpose(dq).astype(BF)
        for head in range(2):
            for which in range(3):
                s = place + which - 1
                inside = (s >= 0) & (s < blocks)
                start = pl.multiple_of(jnp.clip(s, 0, blocks - 1) * span, span)
                block = ds_ref[pl.ds(start, span), head * span : (head + 1) * span].astype(F32)
                block = jnp.where(inside, block, 0.0)
                block = jnp.concatenate([block, jnp.zeros((span, span), F32)], axis=1)
                size = span
                while size > 8:
                    size = size // 2
                    block = block[:size] + pltpu.roll(block[size:], 2 * span - size, 1)
                line = block[0:1]
                for j in range(1, 8):
                    line = line + pltpu.roll(block, 2 * span - j, 1)[j : j + 1]
                diag_ref[which, 2 * t + head : 2 * t + head + 1, :] = line
            bucket = lax.broadcasted_iota(jnp.int32, (1, 128), 1)
            part = slice(head * span, (head + 1) * span)
            low_total = jnp.sum(low_sum[:, part], axis=1, keepdims=True)
            high_total = jnp.sum(high_sum[:, part], axis=1, keepdims=True)
            small_ref[2 * t + head : 2 * t + head + 1, :] = jnp.where(
                bucket == BUCKETS // 2 - 1, low_total, 0.0
            ) + jnp.where(bucket == BUCKETS - 1, high_total, 0.0)
    heads = inner * 2 // span
    for which in range(3):
        line = lax.dot_general(
            diag_ref[which],
            tables[which],
            (((1,), (1,)), ((), ())),
            preferred_element_type=F32,
            precision=lax.Precision.HIGHEST,
        )
        small_ref[0:heads, 0:BUCKETS] += line[0:heads, :]


def rows_grad_kernel(
    dq_ref,
    dkv_ref,
    w_ref,
    normed_ref,
    gains_ref,
    dense_gain_ref,
    small_ref,
    loss_ref,
    keep_ref,
    *refs,
    inner,
    span,
    tokens,
    slots,
    heads,
):
    send_refs, (part_ref, line_ref) = refs[:-2], refs[-2:]
    place = lax.axis_index(CONTEXT)
    mine = lax.rem(place, 2)
    side = lax.axis_index(TENSOR)
    part_ref[...] = dot_nt(dkv_ref[...], w_ref[:, inner : 3 * inner])
    own_at = pl.multiple_of(place * span, span)
    part_ref[pl.ds(own_at, span), :] += dot_nt(dq_ref[...], w_ref[:, :inner])
    total = jnp.zeros((1, part_ref.shape[1]), F32)
    for s in range(part_ref.shape[0] // span):
        at = slice(s * span, (s + 1) * span)
        total = total + jnp.sum(
            part_ref[at, :] * normed_ref[at, :].astype(F32), axis=0, keepdims=True
        )
    line_ref[...] = jnp.zeros_like(line_ref)
    line_ref[slots : slots + 1, :] = total / gains_ref[0:1, :]
    line_ref[slots + 1 : slots + 2, :] = 0.5 * dense_gain_ref[0:1, :]
    for h in range(heads):
        start = pl.multiple_of(side * 128, 128)
        line_ref[slots + 2 + h : slots + 3 + h, pl.ds(start, 128)] = small_ref[h : h + 1, :]
    line_ref[slots + 2 : slots + 3, 256:384] = 0.5 * loss_ref[0:1, :]
    keep_rows = lax.broadcasted_iota(jnp.int32, line_ref.shape, 0) < slots
    for g in range(4):
        for target, block in (
            (keep_ref.at[g], 2 * g + mine),
            (send_refs[g // 2].at[g % 2], 2 * g + 1 - mine),
        ):
            token_at = pl.multiple_of(block * span, span)
            slot_at = pl.multiple_of(tokens + block * PAD, PAD)
            target[0:span, :] = part_ref[pl.ds(token_at, span), :].astype(BF)
            tail = jnp.where(keep_rows, part_ref[pl.ds(slot_at, PAD), :], line_ref[...])
            target[span : span + PAD, :] = tail.astype(BF)


def weight_grad_kernel(
    dq_ref,
    dkv_ref,
    normed_ref,
    keep_ref,
    *refs,
    inner,
    span,
    rows_each,
):
    send_refs, (wide_ref, line_ref) = refs[:-2], refs[-2:]
    place = lax.axis_index(CONTEXT)

    def put(product, start):
        put_rows(product, start, keep_ref, send_refs)

    own_at = pl.multiple_of(place * span, span)
    own = normed_ref[pl.ds(own_at, span), :].astype(F32)
    split_rows(jnp.transpose(own).astype(BF), line_ref, rows_each)
    put(dot_nn(line_ref[1], dq_ref[...]), 0)
    split_rows(jnp.transpose(normed_ref[...].astype(F32)).astype(BF), wide_ref, rows_each)
    for at in range(0, 2 * inner, 256):
        put(dot_nn(wide_ref[1], dkv_ref[:, at : at + 256]), inner + at)


def halve_kernel(*refs, counts):
    targets = refs[-2:]
    mine = lax.axis_index(FSDP)
    sources, at = [], 0
    for count in counts:
        sources.append((refs[at], refs[at + 1 : at + 1 + count]))
        at += 1 + count
    for flip in range(2):

        @pl.when(mine == flip)
        def _():
            start = 0
            for keep_ref, far_refs in sources:
                width = keep_ref.shape[2]
                for g in range(8):
                    far = far_refs[g * len(far_refs) // 8][g % far_refs[0].shape[0]]
                    sums = keep_ref[g].astype(F32) + far.astype(F32)
                    targets[(g // 4) ^ flip][g % 4, :, start : start + width] = sums.astype(BF)
                start += width


def turn_kernel(keep_ref, far_ref, next_ref, send_ref, *, pick):
    for which, target in enumerate((next_ref, send_ref)):
        for g in range(max(1, keep_ref.shape[0] // 2)):
            block = pick(which, g)
            sums = keep_ref[block].astype(F32) + far_ref[block].astype(F32)
            if len(target.shape) == 2:
                target[...] = sums.astype(target.dtype)
            else:
                target[g] = sums.astype(target.dtype)


def pick_z1(which, g):
    return (g // 2) * 4 + (lax.axis_index(CONTEXT) // 2 ^ (which + 2 * (g % 2)))


def pick_z2(which, g):
    return 2 * g + which


def pick_x(which, g):
    return lax.axis_index(FSDP) ^ which


def quarter_kernel(keep_ref, far_ref, next_ref, send_ref):
    place = lax.axis_index(CONTEXT) // 2
    for target, flip in ((next_ref, 0), (send_ref, 1)):
        for g in range(2):
            block = place ^ (flip + 2 * g)
            total = keep_ref[block].astype(F32) + far_ref[block].astype(F32)
            target[g] = total.astype(BF)


def eighth_kernel(keep_ref, far_ref, own_ref, send_ref):
    own_ref[...] = (keep_ref[0].astype(F32) + far_ref[0].astype(F32)).astype(own_ref.dtype)
    send_ref[...] = (keep_ref[1].astype(F32) + far_ref[1].astype(F32)).astype(BF)


def total_kernel(own_ref, far_ref, *out_refs):
    at = 0
    for out in out_refs:
        cols = slice(at, at + out.shape[1])
        out[...] = (own_ref[:, cols].astype(F32) + far_ref[:, cols].astype(F32)).astype(out.dtype)
        at += out.shape[1]


def columns_kernel(keep_ref, one_ref, two_ref, next_ref, send_ref):
    mine = lax.axis_index(TENSOR)
    width = next_ref.shape[2]
    for target, start in ((next_ref, mine * width), (send_ref, (1 - mine) * width)):
        cols = pl.ds(pl.multiple_of(start, 128), width)
        for half, far_ref in ((slice(0, 2), one_ref), (slice(2, 4), two_ref)):
            total = keep_ref[half, :, cols].astype(F32) + far_ref[:, :, cols].astype(F32)
            target[half] = total.astype(BF)


def tail_kernel(own_ref, far_ref, out_ref, *, span):
    mine = lax.axis_index(TENSOR)
    width = own_ref.shape[1]
    rows = slice(span, span + PAD)
    out_ref[:, pl.ds(pl.multiple_of(mine * width, 128), width)] = own_ref[rows, :].astype(F32)
    out_ref[:, pl.ds(pl.multiple_of((1 - mine) * width, 128), width)] = far_ref[rows, :].astype(F32)


def finish_kernel(
    own_ref,
    far_ref,
    x_ref,
    slots_ref,
    gains_ref,
    residual_grad_ref,
    tail_own_ref,
    tail_far_ref,
    inputs_ref,
    memory_ref,
    gain_ref,
    dense_gain_ref,
    bias_ref,
    loss_ref,
    full_ref,
    line_ref,
    *,
    span,
    slots,
):
    mine = lax.axis_index(TENSOR)
    group = lax.axis_index(FSDP) * 8 + lax.axis_index(CONTEXT)
    width = own_ref.shape[1]
    full_ref[:, pl.ds(pl.multiple_of(mine * width, 128), width)] = own_ref[...].astype(F32)
    full_ref[:, pl.ds(pl.multiple_of((1 - mine) * width, 128), width)] = far_ref[...].astype(F32)
    for source, target, start, extra in (
        (x_ref, inputs_ref, 0, residual_grad_ref),
        (slots_ref, memory_ref, span, None),
    ):
        values = source[...].astype(F32)
        scale = lax.rsqrt(jnp.mean(values * values, axis=-1, keepdims=True) + norm_eps)
        scaled = full_ref[start : start + values.shape[0], :] * gains_ref[0:1, :]
        mean = jnp.mean(scaled * values, axis=-1, keepdims=True)
        back = scale * scaled - values * (scale * scale * scale * mean)
        target[...] = back if extra is None else extra[...] + back
    line_ref[...] = tail_own_ref[...] + tail_far_ref[...]
    lines = pltpu.roll(line_ref[...], full_ref.shape[1] - group * gain_ref.shape[1], 1)
    rows_each = gain_ref.shape[1]
    gain_ref[...] = lines[slots : slots + 1, 0:rows_each]
    dense_gain_ref[...] = lines[slots + 1 : slots + 2, 0:rows_each]
    heads = bias_ref.shape[0]
    start = pl.multiple_of(mine * 128, 128)
    bias_ref[...] = line_ref[slots + 2 : slots + 2 + heads, pl.ds(start, 128)][:, 0:BUCKETS]
    loss_ref[...] = line_ref[slots + 2 : slots + 3, 256:384] / (
        gains_ref[2:3, 0:128] * full_ref.shape[1]
    )


def fast_local(
    inputs,
    memory,
    teacher,
    segments,
    memory_owner,
    valid_mask,
    attention_gain,
    query_weight,
    key_weight,
    value_weight,
    attention_out_weight,
    position_bias,
    feedforward_gain,
    inner_weight,
    feedforward_out_weight,
):
    span, width = inputs.shape[1:]
    slots = memory.shape[1]
    rows_each, inner = query_weight.shape
    hidden = inner_weight.shape[1]
    heads = position_bias.shape[0]
    tokens = 8 * span
    keys_all = 8 * (span + PAD)
    total_rows = 2 * tokens
    x = inputs[0]
    early, later = call(
        pack_kernel,
        [
            ((span + 2 * PAD + 4 * rows_each, inner), BF),
            ((rows_each, 2 * hidden), BF),
        ],
        ins_hbm=13,
        name="pack",
        scratch=(
            pltpu.VMEM((slots, width), BF),
            pltpu.VMEM((1, span), jnp.int32),
            pltpu.VMEM((1, slots), jnp.int32),
            pltpu.VMEM((1, span), jnp.int32),
            pltpu.VMEM((1, rows_each), BF),
            pltpu.VMEM((1, rows_each), BF),
            pltpu.VMEM((PAD, width), F32),
            pltpu.SemaphoreType.DMA((13,)),
        ),
    )(
        x,
        memory[0],
        segments,
        memory_owner,
        valid_mask,
        query_weight,
        key_weight,
        value_weight,
        attention_out_weight,
        inner_weight,
        feedforward_out_weight,
        attention_gain[None],
        feedforward_gain[None],
    )

    block_two, first_two = call(
        split_kernel,
        [((2 * (span + PAD), inner), BF), ((2 * (4 * rows_each + PAD), inner), BF)],
        name="split",
    )(early, swap_context(early, 4))
    first_all = [first_two, swap_context(first_two, 2)]
    first_all += [swap_fsdp(piece) for piece in first_all]
    block_all = [block_two, swap_context(block_two, 2)]
    block_all += [swap_tensor(piece) for piece in block_all]
    later = gate(later, first_two)
    later_two, *later_halves = call(
        stack_kernel,
        [((2 * rows_each, 2 * hidden), BF)] + [((2 * rows_each, hidden), BF)] * 2,
        name="stack",
        waits=(*first_all[2:4], block_all[1]),
    )(later, swap_context(later, 4))
    later_halves = [swap_context(piece, 2) for piece in later_halves]
    later_far = swap_fsdp(later_two)
    first_all += swap_core(first_all)
    block_all += swap_core(block_all)

    (normed, kv, queries, w_all, probs, low, wide, gains, part) = call(
        lambda *refs: attend_kernel(
            *refs, span=span, slots=slots, tokens=tokens, inner=inner, rows_each=rows_each
        ),
        [
            ((keys_all, width), BF),
            ((keys_all, 2 * inner), BF),
            ((span, inner), BF),
            ((width, 4 * inner), BF),
            ((inner // span, keys_all, 2 * span), BF),
            ((span, inner), BF),
            ((inner, span), F32),
            ((8, width), F32),
            ((span, width), BF),
        ],
        name="attend",
        scratch=(
            pltpu.VMEM((keys_all, span), F32),
            pltpu.VMEM((heads, 5, span, span), F32),
            pltpu.VMEM((keys_all, 2 * span), F32),
            pltpu.VMEM((span + PAD, width), F32),
        ),
    )(*first_all, *block_all, position_bias)
    far = swap_tensor(part)
    later_halves = [gate(piece, part) for piece in later_halves]
    later_all = [later_two, gate(later_far, part), *later_halves]
    later_all += [gate(swap_fsdp(piece), far) for piece in later_halves]
    later_all += swap_core(later_all)
    (dense_weights,) = call(
        lambda *refs: order_kernel(*refs, rows_each=rows_each),
        [((width, 2 * hidden), BF)],
        name="order",
        waits=(part,),
    )(*later_all)
    (residual, dense_low, hidden_low, slope, dense_part) = call(
        forward_kernel,
        [
            ((span, width), F32),
            ((span, width), BF),
            ((span, hidden), BF),
            ((span, hidden), F32),
            ((span, width), BF),
        ],
        name="forward",
    )(x, part, far, gains, dense_weights)
    dense_far = swap_tensor(dense_part)
    (output, grad_result, grad_part, loss_part, *dense_grads) = call(
        lambda *refs: backward_kernel(*refs, total_rows=total_rows, rows_each=rows_each),
        [
            ((span, width), BF),
            ((span, width), F32),
            ((span, width), BF),
            ((8, 128), F32),
        ]
        + [((8, rows_each, hidden), BF)] * 4,
        name="backward",
        scratch=(
            pltpu.VMEM((span, width), BF),
            pltpu.VMEM((span, hidden), BF),
            pltpu.VMEM((2, width, span), BF),
        ),
    )(
        residual,
        dense_part,
        dense_far,
        teacher[0],
        valid_mask,
        gains,
        slope,
        dense_weights,
        hidden_low,
        dense_low,
    )
    outer_keep, outer_send, inner_keep, inner_send = dense_grads
    grad_far = swap_tensor(grad_part)

    def halve(sources, *waits):
        columns = sum(keep.shape[2] for keep, _ in sources)
        return call(
            lambda *refs: halve_kernel(*refs, counts=[len(far) for _, far in sources]),
            [((4, rows_each, columns), BF)] * 2,
            name="halve",
            waits=waits,
        )(*[item for keep, far in sources for item in (keep, *far)])

    def quarter(keep, far_half, *waits):
        rows, columns = keep.shape[1:]
        return call(
            quarter_kernel,
            [((2, rows, columns), BF)] * 2,
            name="quarter",
            waits=waits,
        )(keep, far_half)

    def eighth(keep, far_quarter, own_type, *waits):
        rows, columns = keep.shape[1:]
        return call(
            eighth_kernel,
            [((rows, columns), own_type), ((rows, columns), BF)],
            name="eighth",
            waits=waits,
        )(keep, far_quarter)

    def total(own, far_eighth, outs, *waits):
        return call(total_kernel, outs, name="total", waits=waits)(own, far_eighth)

    def turn(keep, far_blocks, pick, outs, *waits):
        return call(
            lambda *refs: turn_kernel(*refs, pick=pick), outs, name="turn", waits=waits
        )(keep, far_blocks)

    def outer_blocks(count):
        return ((count, rows_each, hidden), BF)

    outer_far = swap_context(outer_send, 1)
    inner_far = swap_core([inner_send])
    outer_next, outer_over = turn(outer_keep, outer_far, pick_z1, [outer_blocks(4)] * 2, grad_far)
    outer_far = swap_context(outer_over, 2)
    inner_next, inner_over = halve([(inner_keep, inner_far)], outer_over)
    inner_far = swap_fsdp(inner_over)

    (grad_residual, out_keep, out_send, dq, dkv, dense_gain_rows, small) = call(
        lambda *refs: attention_back_kernel(
            *refs, inner=inner, span=span, tokens=tokens, rows_each=rows_each
        ),
        [
            ((span, width), F32),
            ((8, rows_each, inner), BF),
            ((8, rows_each, inner), BF),
            ((span, inner), BF),
            ((keys_all, 2 * inner), BF),
            ((8, width), F32),
            ((8, 128), F32),
        ],
        name="attend_back",
        scratch=(
            pltpu.VMEM((keys_all, 2 * span), BF),
            pltpu.VMEM((3, 8, 2 * span), F32),
            pltpu.VMEM((2, width, span), BF),
        ),
        waits=(inner_over,),
    )(grad_part, grad_far, grad_result, residual, gains, wide, probs, kv, queries, w_all, low)

    rows_keep, *rows_send = call(
        lambda *refs: rows_grad_kernel(
            *refs, inner=inner, span=span, tokens=tokens, slots=slots, heads=heads
        ),
        [((4, span + PAD, width), BF)] + [((2, span + PAD, width), BF)] * 2,
        name="rows_grad",
        scratch=(pltpu.VMEM((keys_all, width), F32), pltpu.VMEM((PAD, width), F32)),
    )(dq, dkv, w_all, normed, gains, dense_gain_rows, small, loss_part)
    rows_far = swap_core(rows_send)

    weight_keep, *weight_send = call(
        lambda *refs: weight_grad_kernel(*refs, inner=inner, span=span, rows_each=rows_each),
        [((8, rows_each, 3 * inner), BF)] + [((4, rows_each, 3 * inner), BF)] * 2,
        name="weight_grad",
        scratch=(
            pltpu.VMEM((2, width, keys_all), BF),
            pltpu.VMEM((2, width, span), BF),
        ),
        waits=(rows_send[0],),
    )(dq, dkv, normed)
    weight_far = swap_core(weight_send)
    out_far = swap_core([out_send])
    outer_next, outer_over = turn(
        outer_next, outer_far, pick_z2, [outer_blocks(2)] * 2, weight_send[0]
    )
    outer_far = swap_context(outer_over, 4)
    inner_next, inner_over = quarter(inner_next, inner_far, outer_over)
    inner_far = swap_context(inner_over, 2)
    weight_next, weight_over = halve(
        [(weight_keep, weight_far), (out_keep, out_far)], inner_over
    )
    weight_far = swap_fsdp(weight_over)
    rows_next, rows_over = call(
        columns_kernel,
        [((4, span + PAD, width // 2), BF)] * 2,
        name="columns",
        waits=(weight_over,),
    )(rows_keep, *rows_far)
    rows_far = swap_tensor(rows_over)

    rows_next, rows_over = quarter(rows_next, rows_far)
    rows_far = swap_context(rows_over, 2)
    inner_own, inner_over = eighth(inner_next, inner_far, F32, rows_over)
    inner_far = swap_context(inner_over, 4)
    outer_own, outer_over = turn(
        outer_next,
        outer_far,
        pick_x,
        [((rows_each, hidden), F32), ((rows_each, hidden), BF)],
        inner_over,
    )
    outer_far = swap_fsdp(outer_over)
    weight_next, weight_over = quarter(weight_next, weight_far, outer_over)
    weight_far = swap_context(weight_over, 2)

    rows_own, rows_over = eighth(rows_next, rows_far, BF, weight_over)
    rows_far = swap_context(rows_over, 4)
    (grad_outer,) = total(outer_own, outer_far, [((rows_each, hidden), F32)], rows_over)
    (grad_inner,) = total(inner_own, inner_far, [((rows_each, hidden), F32)], grad_outer)
    weight_own, weight_over = eighth(weight_next, weight_far, F32, grad_inner)
    weight_far = swap_context(weight_over, 4)

    (rows_half,) = total(rows_own, rows_far, [((span + PAD, width // 2), BF)], weight_over)
    rows_other = swap_tensor(rows_half)
    *weight_grads, grad_output = total(
        weight_own, weight_far, [((rows_each, inner), F32)] * 4, rows_half
    )
    (tail,) = call(
        lambda *refs: tail_kernel(*refs, span=span), [((PAD, width), F32)], name="tail"
    )(rows_half, rows_other)
    tail_far = swap_fsdp(tail)
    (grad_inputs, grad_memory, grad_gain, grad_dense_gain, grad_bias, loss) = call(
        lambda *refs: finish_kernel(*refs, span=span, slots=slots),
        [
            ((span, width), F32),
            ((slots, width), F32),
            ((1, rows_each), F32),
            ((1, rows_each), F32),
            ((heads, BUCKETS), F32),
            ((1, 128), F32),
        ],
        name="finish",
        scratch=(pltpu.VMEM((span + PAD, width), F32), pltpu.VMEM((PAD, width), F32)),
    )(rows_half, rows_other, x, memory[0], gains, grad_residual, tail, tail_far)
    return (
        loss[0, 0],
        output[None],
        grad_inputs[None],
        grad_memory[None],
        grad_gain[0],
        weight_grads[0],
        weight_grads[1],
        weight_grads[2],
        grad_output,
        grad_bias,
        grad_dense_gain[0],
        grad_inner,
        grad_outer,
    )


def solution(mesh):
    return jax.shard_map(
        fast_local if fits(mesh) else general_local,
        mesh=mesh,
        in_specs=(
            P(FSDP, CONTEXT, None),
            P(FSDP, CONTEXT, None),
            P(FSDP, CONTEXT, None),
            P(FSDP, CONTEXT),
            P(FSDP, CONTEXT),
            P(FSDP, CONTEXT),
            P(ROWS),
            P(ROWS, TENSOR),
            P(ROWS, TENSOR),
            P(ROWS, TENSOR),
            P(ROWS, TENSOR),
            P(TENSOR, None),
            P(ROWS),
            P(ROWS, TENSOR),
            P(ROWS, TENSOR),
        ),
        out_specs=(
            P(),
            P(FSDP, CONTEXT, None),
            P(FSDP, CONTEXT, None),
            P(FSDP, CONTEXT, None),
            P(ROWS),
            P(ROWS, TENSOR),
            P(ROWS, TENSOR),
            P(ROWS, TENSOR),
            P(ROWS, TENSOR),
            P(TENSOR, None),
            P(ROWS),
            P(ROWS, TENSOR),
            P(ROWS, TENSOR),
        ),
        check_vma=False,
    )
```

```python
import jax
import jax.numpy as jnp
from jax import lax
from jax.experimental import pallas as pl
from jax.experimental.pallas import tpu as pltpu
from jax.sharding import PartitionSpec as P

BUCKETS = 32
FSDP = "fsdp"
CONTEXT = "context"
TENSOR = "tensor"
ROWS = (FSDP, CONTEXT)
PRODUCT_0 = "scd,df->scf"
PRODUCT_1 = "scd,di->sci"
PRODUCT_2 = "scd,scf->df"
PRODUCT_3 = "scd,sci->di"
PRODUCT_4 = "scf,df->scd"
PRODUCT_5 = "sci,di->scd"
PRODUCT_6 = "sjd,sji->di"
PRODUCT_7 = "sji,di->sjd"
PRODUCT_8 = "sqhd,skhd->sqhk"
PRODUCT_9 = "sqhk,qkb->hb"
PRODUCT_10 = "sqhk,skhd->sqhd"
PRODUCT_11 = "sqhk,sqhd->skhd"


norm_eps = 1e-06
score_floor = -1e30


def relative_bucket(distance):
    half_count = BUCKETS // 2
    exact_count = half_count // 2
    magnitude = jnp.minimum(jnp.abs(distance), 1024)
    far_bucket = jnp.full(distance.shape, exact_count, jnp.int32)
    for level_index in range(1, half_count - exact_count):
        far_bucket = far_bucket + (
            magnitude * magnitude >= exact_count * exact_count * 2**level_index
        ).astype(jnp.int32)
    bucket_ids = jnp.where(magnitude < exact_count, magnitude, far_bucket)
    return bucket_ids + (distance > 0).astype(jnp.int32) * half_count


def rms_norm(values, gain_in):
    inv_rms = lax.rsqrt(jnp.mean(values * values, axis=-1, keepdims=True) + norm_eps)
    return (values * inv_rms * gain_in, inv_rms)


def norm_back(values, inv_rms, gain_in, grad_in):
    scaled = grad_in * gain_in
    inner_mean = jnp.mean(scaled * values, axis=-1, keepdims=True)
    grad_values = inv_rms * scaled - values * inv_rms * inv_rms * inv_rms * inner_mean
    grad_gain = jnp.sum(grad_in * values * inv_rms, axis=tuple(range(values.ndim - 1)))
    return (grad_values, grad_gain)


def smooth_gate(values):
    return jax.nn.gelu(values, approximate=True)


def block_size():
    return 512


def pad_rows(values_in, block_rows, fill_value):
    blocks = -(-values_in.shape[1] // block_rows)
    missing = blocks * block_rows - values_in.shape[1]
    padding = [(0, 0)] * values_in.ndim
    padding[1] = (0, missing)
    return (jnp.pad(values_in, padding, constant_values=fill_value), blocks)


def key_places(row_ids, shard_rows, key_span):
    within = row_ids % key_span
    return (row_ids // key_span * shard_rows + within, within < shard_rows)


def scores_with_bias(
    query_blk, key_blk, query_place, query_doc, key_place, key_doc, key_token, bias_table
):
    scores = jnp.einsum(PRODUCT_8, query_blk, key_blk, preferred_element_type=jnp.float32)
    bucket = relative_bucket(key_place[None, :] - query_place[:, None])
    rel_terms = jnp.where(key_token[None, None, :], jnp.take(bias_table, bucket, axis=1), 0.0)
    scores = scores + jnp.moveaxis(rel_terms, 0, 1)[None]
    same_doc = (query_doc[:, :, None] == key_doc[:, None, :])[:, :, None, :]
    return (scores, same_doc, bucket)


def sum_grads(grad_items):
    return (
        lax.psum_scatter(grad_items[0], ROWS, scatter_dimension=0, tiled=True),
        lax.psum_scatter(grad_items[1], ROWS, scatter_dimension=0, tiled=True),
        lax.psum_scatter(grad_items[2], ROWS, scatter_dimension=0, tiled=True),
        lax.psum_scatter(grad_items[3], ROWS, scatter_dimension=0, tiled=True),
        lax.psum_scatter(grad_items[4], ROWS, scatter_dimension=0, tiled=True),
        lax.psum_scatter(grad_items[5], ROWS, scatter_dimension=0, tiled=True),
        lax.psum_scatter(grad_items[6], ROWS, scatter_dimension=0, tiled=True),
        lax.psum_scatter(grad_items[7], ROWS, scatter_dimension=0, tiled=True),
    )


def general_local(
    inputs,
    memory,
    teacher,
    segments,
    memory_owner,
    valid_mask,
    attention_gain,
    query_weight,
    key_weight,
    value_weight,
    attention_out_weight,
    position_bias,
    feedforward_gain,
    inner_weight,
    feedforward_out_weight,
):
    sequences, shard_rows, model_width = inputs.shape
    key_span = shard_rows + memory.shape[1]
    context_size = lax.axis_size(CONTEXT)
    length = shard_rows * context_size
    context_place = lax.axis_index(CONTEXT)
    local_heads = position_bias.shape[0]
    bucket_count = position_bias.shape[1]
    head_size = query_weight.shape[1] // local_heads
    local_inner = local_heads * head_size
    total_rows = sequences * length * lax.axis_size(FSDP)
    bias_table = position_bias.astype(jnp.float32)
    (
        full_query,
        full_key,
        full_value,
        full_output,
        full_inner,
        full_outer,
        full_attn_gain,
        full_dense_gain,
    ) = (
        lax.all_gather(query_weight, ROWS, axis=0, tiled=True),
        lax.all_gather(key_weight, ROWS, axis=0, tiled=True),
        lax.all_gather(value_weight, ROWS, axis=0, tiled=True),
        lax.all_gather(attention_out_weight, ROWS, axis=0, tiled=True),
        lax.all_gather(inner_weight, ROWS, axis=0, tiled=True),
        lax.all_gather(feedforward_out_weight, ROWS, axis=0, tiled=True),
        lax.all_gather(attention_gain, ROWS, axis=0, tiled=True),
        lax.all_gather(feedforward_gain, ROWS, axis=0, tiled=True),
    )
    attn_gain = full_attn_gain.astype(jnp.float32)
    dense_gain = full_dense_gain.astype(jnp.float32)
    local_docs = jnp.concatenate([segments, memory_owner], axis=1)
    key_docs = lax.all_gather(local_docs, CONTEXT, axis=1, tiled=True)
    query_docs_all = key_docs.reshape(sequences, context_size, key_span)[:, :, :shard_rows].reshape(
        sequences, length
    )
    token_count = lax.psum(jnp.sum(valid_mask.astype(jnp.float32)), ROWS)
    inputs_float = inputs.astype(jnp.float32)
    memory_float = memory.astype(jnp.float32)
    normed, input_scale = rms_norm(inputs_float, attn_gain)
    memory_normed, memory_scale = rms_norm(memory_float, attn_gain)
    normed_low = normed.astype(jnp.bfloat16)
    both_rows = jnp.concatenate([normed_low, memory_normed.astype(jnp.bfloat16)], axis=1)
    queries = jnp.dot(normed_low, full_query, preferred_element_type=jnp.float32).astype(
        jnp.bfloat16
    )
    key_local = jnp.dot(both_rows, full_key, preferred_element_type=jnp.float32).astype(
        jnp.bfloat16
    )
    value_local = jnp.dot(both_rows, full_value, preferred_element_type=jnp.float32).astype(
        jnp.bfloat16
    )
    query_heads = queries.reshape(sequences, shard_rows, local_heads, head_size)
    query_place = context_place * shard_rows + jnp.arange(shard_rows, dtype=jnp.int32)
    fold_init = (
        jnp.full((sequences, shard_rows, local_heads), score_floor, jnp.float32),
        jnp.zeros((sequences, shard_rows, local_heads), jnp.float32),
        jnp.zeros((sequences, shard_rows, local_heads, head_size), jnp.float32),
    )
    fold_state = fold_init
    key_piece = lax.all_gather(key_local, CONTEXT, axis=1, tiled=True)
    value_piece = lax.all_gather(value_local, CONTEXT, axis=1, tiled=True)
    block_rows = block_size()
    key_pad, blocks = pad_rows(key_piece, block_rows, 0)
    value_pad, blocks = pad_rows(value_piece, block_rows, 0)
    doc_pad, blocks = pad_rows(key_docs, block_rows, -1)

    def attend_advance(running, block_index):
        running_best, running_sum, summed = running
        offset = block_index * block_rows
        key_blk = lax.dynamic_slice_in_dim(key_pad, offset, block_rows, 1).reshape(
            sequences, block_rows, local_heads, head_size
        )
        value_blk = lax.dynamic_slice_in_dim(value_pad, offset, block_rows, 1).reshape(
            sequences, block_rows, local_heads, head_size
        )
        doc_blk = lax.dynamic_slice_in_dim(doc_pad, offset, block_rows, 1)
        key_place, key_token = key_places(
            offset + jnp.arange(block_rows, dtype=jnp.int32), shard_rows, key_span
        )
        scores, same_doc, bucket = scores_with_bias(
            query_heads, key_blk, query_place, segments, key_place, doc_blk, key_token, bias_table
        )
        masked = jnp.where(same_doc, scores, score_floor)
        new_best = jnp.maximum(running_best, jnp.max(masked, axis=-1))
        weights = jnp.where(same_doc, jnp.exp(scores - new_best[..., None]), 0.0)
        factor = jnp.exp(running_best - new_best)
        running_sum = running_sum * factor + jnp.sum(weights, axis=-1)
        summed = summed * factor[..., None] + jnp.einsum(
            PRODUCT_10,
            weights.astype(jnp.bfloat16),
            value_blk,
            preferred_element_type=jnp.float32,
        )
        return ((new_best, running_sum, summed), None)

    fold_state, unused = lax.scan(attend_advance, fold_state, jnp.arange(blocks, dtype=jnp.int32))
    running_best, running_sum, summed = fold_state
    attended_values = summed / running_sum[..., None]
    attended_low = attended_values.reshape(sequences, shard_rows, local_inner).astype(jnp.bfloat16)
    attention_part = jnp.einsum(
        PRODUCT_5, attended_low, full_output, preferred_element_type=jnp.float32
    )
    residual = inputs_float + lax.psum(attention_part.astype(jnp.bfloat16), TENSOR).astype(
        jnp.float32
    )
    dense_normed, dense_scale = rms_norm(residual, dense_gain)
    dense_low = dense_normed.astype(jnp.bfloat16)
    inner_pre = jnp.dot(dense_low, full_inner, preferred_element_type=jnp.float32)
    hidden_float, gate_pullback = jax.vjp(smooth_gate, inner_pre)
    hidden_low = hidden_float.astype(jnp.bfloat16)
    dense_part = jnp.einsum(
        PRODUCT_4, hidden_low, full_outer, preferred_element_type=jnp.float32
    )
    result = residual + lax.psum(dense_part.astype(jnp.bfloat16), TENSOR).astype(jnp.float32)
    target_mask = valid_mask.astype(jnp.float32)[..., None]
    misfit = result - teacher.astype(jnp.float32)
    loss_local = 0.5 * jnp.sum(target_mask * misfit * misfit)
    grad_result = total_rows / token_count * target_mask * misfit
    dense_back = grad_result.astype(jnp.bfloat16)
    grad_outer = jnp.einsum(
        PRODUCT_2, dense_back, hidden_low, preferred_element_type=jnp.float32
    )
    grad_hidden = jnp.einsum(
        PRODUCT_0, dense_back, full_outer, preferred_element_type=jnp.float32
    )
    grad_pre = gate_pullback(grad_hidden)[0].astype(jnp.bfloat16)
    grad_inner = jnp.einsum(PRODUCT_2, dense_low, grad_pre, preferred_element_type=jnp.float32)
    grad_dense_part = jnp.einsum(
        PRODUCT_4, grad_pre, full_inner, preferred_element_type=jnp.float32
    )
    grad_dense_normed = lax.psum(grad_dense_part.astype(jnp.bfloat16), TENSOR).astype(jnp.float32)
    back_residual, grad_dense_gain = norm_back(residual, dense_scale, dense_gain, grad_dense_normed)
    grad_residual = grad_result + back_residual
    attention_back = grad_residual.astype(jnp.bfloat16)
    grad_output = jnp.einsum(
        PRODUCT_3, attention_back, attended_low, preferred_element_type=jnp.float32
    )
    grad_attended = jnp.einsum(
        PRODUCT_1, attention_back, full_output, preferred_element_type=jnp.float32
    ).astype(jnp.bfloat16)
    grad_heads = grad_attended.reshape(sequences, shard_rows, local_heads, head_size)
    log_total = running_best + jnp.log(running_sum)
    delta_rows = jnp.sum(grad_heads.astype(jnp.float32) * attended_values, axis=-1)
    all_log_total, all_delta = (
        lax.all_gather(log_total, CONTEXT, axis=1, tiled=True),
        lax.all_gather(delta_rows, CONTEXT, axis=1, tiled=True),
    )
    query_init = (
        jnp.zeros((sequences, shard_rows, local_heads, head_size), jnp.float32),
        jnp.zeros((local_heads, bucket_count), jnp.float32),
    )
    fold_state = query_init
    key_piece = lax.all_gather(key_local, CONTEXT, axis=1, tiled=True)
    value_piece = lax.all_gather(value_local, CONTEXT, axis=1, tiled=True)
    query_block_rows = block_size()
    query_key_pad, blocks = pad_rows(key_piece, query_block_rows, 0)
    query_value_pad, blocks = pad_rows(value_piece, query_block_rows, 0)
    query_doc_pad, blocks = pad_rows(key_docs, query_block_rows, -1)

    def query_advance(running, block_index):
        grad_query, grad_bias = running
        offset = block_index * query_block_rows
        key_blk = lax.dynamic_slice_in_dim(query_key_pad, offset, query_block_rows, 1).reshape(
            sequences, query_block_rows, local_heads, head_size
        )
        value_blk = lax.dynamic_slice_in_dim(query_value_pad, offset, query_block_rows, 1).reshape(
            sequences, query_block_rows, local_heads, head_size
        )
        doc_blk = lax.dynamic_slice_in_dim(query_doc_pad, offset, query_block_rows, 1)
        key_place, key_token = key_places(
            offset + jnp.arange(query_block_rows, dtype=jnp.int32), shard_rows, key_span
        )
        scores, same_doc, bucket = scores_with_bias(
            query_heads, key_blk, query_place, segments, key_place, doc_blk, key_token, bias_table
        )
        probabilities = jnp.where(same_doc, jnp.exp(scores - log_total[..., None]), 0.0)
        value_dots = jnp.einsum(
            PRODUCT_8, grad_heads, value_blk, preferred_element_type=jnp.float32
        )
        grad_scores = (probabilities * (value_dots - delta_rows[..., None])).astype(jnp.bfloat16)
        grad_query = grad_query + jnp.einsum(
            PRODUCT_10, grad_scores, key_blk, preferred_element_type=jnp.float32
        )
        bucket_hits = (
            (bucket[:, :, None] == jnp.arange(bucket_count, dtype=jnp.int32)[None, None, :])
            & key_token[None, :, None]
        ).astype(jnp.bfloat16)
        grad_bias = grad_bias + jnp.einsum(
            PRODUCT_9, grad_scores, bucket_hits, preferred_element_type=jnp.float32
        )
        return ((grad_query, grad_bias), None)

    fold_state, unused = lax.scan(query_advance, fold_state, jnp.arange(blocks, dtype=jnp.int32))
    grad_query, grad_bias = fold_state
    key_heads = key_local.reshape(sequences, key_span, local_heads, head_size)
    value_heads = value_local.reshape(sequences, key_span, local_heads, head_size)
    local_place, local_token = key_places(
        context_place * key_span + jnp.arange(key_span, dtype=jnp.int32), shard_rows, key_span
    )
    key_init = (
        jnp.zeros((sequences, key_span, local_heads, head_size), jnp.float32),
        jnp.zeros((sequences, key_span, local_heads, head_size), jnp.float32),
    )
    fold_state = key_init
    query_piece = lax.all_gather(queries, CONTEXT, axis=1, tiled=True)
    grad_piece = lax.all_gather(grad_attended, CONTEXT, axis=1, tiled=True)
    key_block_rows = block_size()
    query_pad, blocks = pad_rows(query_piece, key_block_rows, 0)
    grad_pad, blocks = pad_rows(grad_piece, key_block_rows, 0)
    key_doc_pad, blocks = pad_rows(query_docs_all, key_block_rows, -1)
    total_pad, blocks = pad_rows(all_log_total, key_block_rows, 0.0)
    delta_pad, blocks = pad_rows(all_delta, key_block_rows, 0.0)

    def key_advance(running, block_index):
        grad_key, grad_value = running
        offset = block_index * key_block_rows
        query_blk = lax.dynamic_slice_in_dim(query_pad, offset, key_block_rows, 1).reshape(
            sequences, key_block_rows, local_heads, head_size
        )
        grad_blk = lax.dynamic_slice_in_dim(grad_pad, offset, key_block_rows, 1).reshape(
            sequences, key_block_rows, local_heads, head_size
        )
        doc_blk = lax.dynamic_slice_in_dim(key_doc_pad, offset, key_block_rows, 1)
        total_blk = lax.dynamic_slice_in_dim(total_pad, offset, key_block_rows, 1)
        delta_blk = lax.dynamic_slice_in_dim(delta_pad, offset, key_block_rows, 1)
        row_place = offset + jnp.arange(key_block_rows, dtype=jnp.int32)
        scores, same_doc, bucket = scores_with_bias(
            query_blk,
            key_heads,
            row_place,
            doc_blk,
            local_place,
            local_docs,
            local_token,
            bias_table,
        )
        probabilities = jnp.where(same_doc, jnp.exp(scores - total_blk[..., None]), 0.0)
        grad_value = grad_value + jnp.einsum(
            PRODUCT_11,
            probabilities.astype(jnp.bfloat16),
            grad_blk,
            preferred_element_type=jnp.float32,
        )
        value_dots = jnp.einsum(
            PRODUCT_8, grad_blk, value_heads, preferred_element_type=jnp.float32
        )
        grad_scores = (probabilities * (value_dots - delta_blk[..., None])).astype(jnp.bfloat16)
        grad_key = grad_key + jnp.einsum(
            PRODUCT_11, grad_scores, query_blk, preferred_element_type=jnp.float32
        )
        return ((grad_key, grad_value), None)

    fold_state, unused = lax.scan(key_advance, fold_state, jnp.arange(blocks, dtype=jnp.int32))
    grad_key, grad_value = fold_state
    grad_query_low = grad_query.reshape(sequences, shard_rows, local_inner).astype(jnp.bfloat16)
    grad_key_low = grad_key.reshape(sequences, key_span, local_inner).astype(jnp.bfloat16)
    grad_value_low = grad_value.reshape(sequences, key_span, local_inner).astype(jnp.bfloat16)
    grad_query_weight = jnp.einsum(
        PRODUCT_3, normed_low, grad_query_low, preferred_element_type=jnp.float32
    )
    grad_key_weight = jnp.einsum(
        PRODUCT_6, both_rows, grad_key_low, preferred_element_type=jnp.float32
    )
    grad_value_weight = jnp.einsum(
        PRODUCT_6, both_rows, grad_value_low, preferred_element_type=jnp.float32
    )
    row_part = jnp.einsum(
        PRODUCT_7, grad_key_low, full_key, preferred_element_type=jnp.float32
    ) + jnp.einsum(PRODUCT_7, grad_value_low, full_value, preferred_element_type=jnp.float32)
    token_part = row_part[:, :shard_rows] + jnp.einsum(
        PRODUCT_5, grad_query_low, full_query, preferred_element_type=jnp.float32
    )
    grad_normed, grad_memory_normed = (
        lax.psum(token_part.astype(jnp.bfloat16), TENSOR).astype(jnp.float32),
        lax.psum(row_part[:, shard_rows:].astype(jnp.bfloat16), TENSOR).astype(jnp.float32),
    )
    back_inputs, gain_tokens = norm_back(inputs_float, input_scale, attn_gain, grad_normed)
    back_memory, gain_memory = norm_back(memory_float, memory_scale, attn_gain, grad_memory_normed)
    grad_inputs = grad_residual + back_inputs
    grad_attn_gain = gain_tokens + gain_memory
    (
        shard_query,
        shard_key,
        shard_value,
        shard_output,
        shard_inner,
        shard_outer,
        shard_attn_gain,
        shard_dense_gain,
    ) = sum_grads(
        (
            grad_query_weight,
            grad_key_weight,
            grad_value_weight,
            grad_output,
            grad_inner,
            grad_outer,
            grad_attn_gain,
            grad_dense_gain,
        )
    )
    loss_sum, grad_bias_sum = lax.psum((loss_local, grad_bias), ROWS)
    return (
        loss_sum / (token_count * model_width),
        result.astype(jnp.bfloat16),
        grad_inputs,
        back_memory,
        shard_attn_gain,
        shard_query,
        shard_key,
        shard_value,
        shard_output,
        grad_bias_sum,
        shard_dense_gain,
        shard_inner,
        shard_outer,
    )


PAD = 16
BF = jnp.bfloat16
F32 = jnp.float32


def fits(mesh):
    sizes = dict(mesh.shape)
    return sizes[FSDP] == 2 and sizes[CONTEXT] == 8 and sizes[TENSOR] == 2


def swap_context(value, mask):
    return lax.ppermute(value, CONTEXT, [(i, i ^ mask) for i in range(8)])


def swap_core(pieces):
    return [swap_context(piece, 1) for piece in pieces]


def swap_fsdp(value):
    return lax.ppermute(value, FSDP, [(0, 1), (1, 0)])


def swap_tensor(value):
    return lax.ppermute(value, TENSOR, [(0, 1), (1, 0)])


def dot_nn(left, right):
    return lax.dot_general(left, right, (((1,), (0,)), ((), ())), preferred_element_type=F32)


def dot_nt(left, right):
    return lax.dot_general(left, right, (((1,), (1,)), ((), ())), preferred_element_type=F32)


def dot_tn(left, right):
    return lax.dot_general(left, right, (((0,), (0,)), ((), ())), preferred_element_type=F32)


def padded_bytes(shape, dtype):
    size = jnp.dtype(dtype).itemsize
    rows = 8 * (4 // size)
    lead = 1
    for count in shape[:-2]:
        lead *= count
    second = shape[-2] if len(shape) > 1 else 1
    return lead * -(-second // rows) * rows * -(-shape[-1] // 128) * 128 * size


def call(kernel, outs, name, ins_hbm=0, scratch=(), waits=()):
    def run(*operands):
        count = len(operands)
        specs = [pl.BlockSpec(memory_space=pltpu.VMEM)] * (count - ins_hbm)
        specs += [pl.BlockSpec(memory_space=pltpu.HBM)] * ins_hbm
        specs += [pl.BlockSpec(memory_space=pl.ANY)] * len(waits)
        held = [(item.shape, item.dtype) for item in operands[: count - ins_hbm]] + list(outs)
        held += [(item.shape, item.dtype) for item in scratch if item.memory_space == pltpu.VMEM]
        limit = 6 * 1024 * 1024 + sum(padded_bytes(shape, dtype) for shape, dtype in held)

        placed = list(operands)
        for at in range(count - ins_hbm, count):
            placed[at] = pltpu.with_memory_space_constraint(placed[at], pltpu.HBM)

        def body(*refs):
            kernel(*refs[:count], *refs[count + len(waits) :])

        return pl.pallas_call(
            body,
            out_shape=[jax.ShapeDtypeStruct(shape, dtype) for shape, dtype in outs],
            in_specs=specs,
            out_specs=[pl.BlockSpec(memory_space=pltpu.VMEM)] * len(outs),
            scratch_shapes=list(scratch),
            compiler_params=pltpu.CompilerParams(vmem_limit_bytes=limit),
            name=name,
        )(*placed, *waits)

    return run


def gate(value, *waits):
    def body(*refs):
        del refs

    return pl.pallas_call(
        body,
        out_shape=jax.ShapeDtypeStruct(value.shape, value.dtype),
        in_specs=[pl.BlockSpec(memory_space=pl.ANY)] * (1 + len(waits)),
        out_specs=pl.BlockSpec(memory_space=pl.ANY),
        input_output_aliases={0: 0},
        compiler_params=pltpu.CompilerParams(vmem_limit_bytes=1024 * 1024),
    )(value, *waits)


def diagonal(rows):
    return lax.broadcasted_iota(jnp.int32, (rows, 128), 0) == lax.broadcasted_iota(
        jnp.int32, (rows, 128), 1
    )


def row_to_column(row, rows):
    return jnp.sum(
        jnp.where(diagonal(rows), jnp.broadcast_to(row, (rows, 128)), 0.0), axis=1, keepdims=True
    )


def bucket_onehot(block_distance, span):
    lane = lax.broadcasted_iota(jnp.int32, (BUCKETS, 2 * span), 1)
    offset = jnp.where(lane < span, lane, lane - 2 * span)
    bucket = relative_bucket(block_distance * span - offset)
    return bucket == lax.broadcasted_iota(jnp.int32, (BUCKETS, 2 * span), 0)


def pack_kernel(*refs):
    sources, (own_ref, early_ref, later_ref, over_ref, block_ref) = refs[:13], refs[13:18]
    small, tail_ref, sems = refs[18:24], refs[24], refs[25]
    x, memory, segments, owner, valid, wq, wk, wv, wo, wi, wf, gain, dense_gain = sources
    span, slots = x.shape[0], memory.shape[0]
    rows_each, inner = wq.shape
    hidden = wi.shape[1]
    base = span + PAD
    half = pl.ds(pl.multiple_of(lax.axis_index(TENSOR) * inner, 128), inner)
    targets = [
        (memory, small[0]),
        (segments, small[1]),
        (owner, small[2]),
        (valid, small[3]),
        (gain, small[4]),
        (dense_gain, small[5]),
        (x.at[:, half], own_ref.at[slice(0, span), :]),
    ]
    parts = [wq, wk, wv, wo]
    parts += [w.at[:, slice(at, at + inner)] for w in (wi, wf) for at in range(0, hidden, inner)]
    starts = [base + at * rows_each for at in range(4)]
    late = base + 4 * rows_each + PAD
    starts += [late + at * rows_each for at in range(len(parts) - 4)]
    for part, start in zip(parts, starts):
        targets.append((part, own_ref.at[slice(start, start + rows_each), :]))
    copies = [
        pltpu.make_async_copy(source, target, sems.at[i])
        for i, (source, target) in enumerate(targets)
    ]
    for copy in copies:
        copy.start()
    for copy in copies[:6]:
        copy.wait()
    memory, segments, owner, valid, gain, dense_gain = small
    tail_ref[...] = jnp.zeros_like(tail_ref)
    tail_ref[0:slots, :] = memory[...].astype(F32)
    tail_ref[slots : slots + 1, 0:span] = segments[...].astype(F32)
    tail_ref[slots : slots + 1, span : span + slots] = owner[...].astype(F32)
    own_ref[span:base, :] = tail_ref[:, half].astype(BF)
    tail_ref[...] = jnp.zeros_like(tail_ref)
    tail_ref[0:1, 0:rows_each] = gain[...].astype(F32)
    tail_ref[1:2, 0:rows_each] = dense_gain[...].astype(F32)
    tail_ref[2:3, 0:1] = jnp.sum(valid[...].astype(F32), axis=1, keepdims=True)
    own_ref[late - PAD : late, :] = tail_ref[:, 0:inner].astype(BF)
    for copy in copies[6:]:
        copy.wait()
    early_ref[...] = own_ref[0:late, :]
    later_ref[...] = own_ref[late:, :]
    over_ref[...] = own_ref[base:, :]
    block_ref[...] = own_ref[0:base, :]


def split_kernel(two_ref, one_ref, first_ref, block_ref, later_ref):
    rows, first_rows = block_ref.shape[0] // 2, first_ref.shape[0] // 2
    for at, source in enumerate((two_ref, one_ref)):
        block_ref[at * rows : (at + 1) * rows, :] = source[0:rows, :]
        first_ref[at * first_rows : (at + 1) * first_rows, :] = source[rows : rows + first_rows, :]
    later_ref[...] = one_ref[rows + first_rows :, :]


def join_kernel(*refs, block_rows, first_rows):
    near, overs, blocks = refs[0:4], refs[4:6], refs[6:8]
    first_ref, block_ref, joined_ref = refs[8:]
    early_rows = block_rows + first_rows
    block_ref[...] = near[3][0:block_rows, :]
    first_ref[...] = near[3][block_rows:early_rows, :]
    at = 0
    for source, rows in [(piece, early_rows) for piece in near] + [
        (overs[0], first_rows),
        (overs[1], 2 * first_rows),
        (blocks[0], block_rows),
        (blocks[1], 2 * block_rows),
    ]:
        joined_ref[at : at + rows, :] = source[0:rows, :]
        at += rows
    rows = near[0].shape[0] - early_rows
    for source, start in ((near[0], early_rows), (near[1], early_rows), (overs[0], first_rows)):
        joined_ref[at : at + rows, :] = source[start : start + rows, :]
        at += rows


def order_kernel(*refs, rows_each):
    group = lax.axis_index(FSDP) * 8 + lax.axis_index(CONTEXT)
    target = refs[12]
    width = refs[0].shape[1]
    rows = target.shape[1] // width * rows_each
    for p in range(16):
        start = pl.ds(pl.multiple_of((group ^ p) * rows_each, 16), rows_each)
        at = (p >> 1 & 1) + 2 * (p >> 2 & 1) + 4 * (p >> 3)
        source = refs[(0, 0, 1, 2, 0, 3, 4, 5)[at] + 6 * (p & 1)]
        base = source.shape[0] - 3 * rows
        row = (base, base + rows, 0, 0, base + 2 * rows, 0, 0, 0)[at]
        for col in range(target.shape[1] // width):
            lines = slice(row + col * rows_each, row + (col + 1) * rows_each)
            target[start, col * width : (col + 1) * width] = source[lines, :]


def weights_kernel(*refs, rows_each, inner, block_rows):
    w_ref, gains_ref = refs[4:]
    group = lax.axis_index(FSDP) * 8 + lax.axis_index(CONTEXT)
    rows = 4 * rows_each + PAD
    gathered = jnp.zeros((8, gains_ref.shape[1]), F32)
    for p in range(16):
        piece = (p >> 1 & 1) + 2 * (p >> 2 & 1) + 4 * (p >> 3)
        source = refs[2 * (p & 1) + (piece == 7)]
        early = block_rows + rows
        at = piece * early + block_rows
        if piece >= 4:
            at = (4 * early, 4 * early + 2 * rows, 4 * early + rows, 0)[piece - 4]
        start = pl.multiple_of((group ^ p) * rows_each, 16)
        for which in range(4):
            w_ref[pl.ds(start, rows_each), which * inner : (which + 1) * inner] = source[
                at + which * rows_each : at + (which + 1) * rows_each, :
            ]
        lines = source[at + 4 * rows_each : at + rows, :].astype(F32)[0:8, :]
        lines = jnp.concatenate([lines, jnp.zeros_like(lines)], axis=1)
        gathered = gathered + pltpu.roll(lines, (group ^ p) * rows_each, 1)
    row_ids = lax.broadcasted_iota(jnp.int32, gathered.shape, 0)
    count = jnp.sum(gathered[2:3, :])
    gains_ref[...] = jnp.where(row_ids == 2, count, gathered)


def bias_kernel(bias_ref, toep_ref, *, span):
    for e in range(5):
        table = dot_nn(bias_ref[...], jnp.where(bucket_onehot(e - 2, span), 1.0, 0.0).astype(BF))
        for h in range(bias_ref.shape[0]):
            line = jnp.broadcast_to(table[h : h + 1, :], (span, 2 * span))
            if abs(e - 2) < 2:
                line = pltpu.roll(line, 0, 1, stride=1, stride_axis=0)
            toep_ref[h, e] = line[:, :span]


def attend_kernel(*refs, span, slots, tokens, inner, first_rows):
    w_ref, gains_ref, toep_ref = refs[0:3]
    block_refs = refs[3:7]
    (normed_ref, kv_ref, q_ref, p_ref, low_ref, wide_ref, part_ref) = refs[7:14]
    (mask_ref, score_ref, whole_ref) = refs[14:]
    block_rows = span + PAD
    early_rows = block_rows + first_rows
    side = lax.axis_index(TENSOR)
    place = lax.axis_index(CONTEXT)
    gain = gains_ref[0:1, :]
    own_docs = None
    for p in range(8):
        block = place ^ p
        piece = (p >> 1 & 1) + 2 * (p >> 2 & 1)
        for far in range(2):
            source = block_refs[2 * (p & 1) + (far and piece == 3)]
            at = piece * early_rows
            if far:
                base = 4 * early_rows + 3 * first_rows
                at = (base, base + 2 * block_rows, base + block_rows, 0)[piece]
            cols = pl.ds(pl.multiple_of((side ^ far) * inner, 128), inner)
            whole_ref[:, cols] = source[at : at + span + PAD, :].astype(F32)
        token_at = pl.multiple_of(block * span, span)
        slot_at = pl.multiple_of(tokens + block * PAD, PAD)
        values = whole_ref[0:span, :]
        scale = lax.rsqrt(jnp.mean(values * values, axis=-1, keepdims=True) + norm_eps)
        normed_ref[pl.ds(token_at, span), :] = (values * scale * gain).astype(BF)
        tail = whole_ref[span : span + PAD, :]
        docs = tail[slots : slots + 1, 0 : 2 * span]
        tail_rows = lax.broadcasted_iota(jnp.int32, tail.shape, 0)
        tail = jnp.where(tail_rows < slots, tail, 0.0)
        scale = lax.rsqrt(jnp.mean(tail * tail, axis=-1, keepdims=True) + norm_eps)
        normed_ref[pl.ds(slot_at, PAD), :] = (tail * scale * gain).astype(BF)
        if p == 0:
            own_docs = docs[:, 0:span]
        token_docs = row_to_column(docs[:, 0:span], span)
        mask_ref[pl.ds(token_at, span), :] = jnp.where(token_docs == own_docs, 0.0, score_floor)
        slot_docs = row_to_column(docs[:, span : 2 * span], PAD)
        slot_rows = lax.broadcasted_iota(jnp.int32, (PAD, 1), 0)
        slot_docs = jnp.where(slot_rows < slots, slot_docs, -1.0)
        mask_ref[pl.ds(slot_at, PAD), :] = jnp.where(slot_docs == own_docs, 0.0, score_floor)
    kv_ref[...] = dot_nn(normed_ref[...], w_ref[:, inner : 3 * inner]).astype(BF)
    own_at = pl.multiple_of(place * span, span)
    q_ref[...] = dot_nn(normed_ref[pl.ds(own_at, span), :], w_ref[:, :inner]).astype(BF)
    lane = lax.broadcasted_iota(jnp.int32, (span, span), 1)
    sub = lax.broadcasted_iota(jnp.int32, (span, span), 0)
    count_blocks = tokens // span
    slot_rows_all = score_ref.shape[0] - tokens
    for t in range(inner // span):
        keys = kv_ref[:, t * span : (t + 1) * span]
        values = kv_ref[:, inner + t * span : inner + (t + 1) * span]
        pair = q_ref[:, t * span : (t + 1) * span]
        zero = jnp.zeros_like(pair)
        both = jnp.concatenate(
            [jnp.where(lane < span // 2, pair, zero), jnp.where(lane < span // 2, zero, pair)], axis=0
        )
        score_ref[...] = dot_nt(keys, both)
        best = jnp.full((1, 2 * span), score_floor, F32)
        for s in range(count_blocks):
            e = jnp.clip(s - place, -2, 2) + 2
            at = slice(s * span, (s + 1) * span)
            terms = jnp.concatenate([toep_ref[2 * t, e], toep_ref[2 * t + 1, e]], axis=1)
            mask = mask_ref[at, :]
            block = score_ref[at, :] + terms + jnp.concatenate([mask, mask], axis=1)
            score_ref[at, :] = block
            best = jnp.maximum(best, jnp.max(block, axis=0, keepdims=True))
        at = slice(tokens, tokens + slot_rows_all)
        mask = mask_ref[at, :]
        block = score_ref[at, :] + jnp.concatenate([mask, mask], axis=1)
        score_ref[at, :] = block
        best = jnp.maximum(best, jnp.max(block, axis=0, keepdims=True))
        total = jnp.zeros((1, 2 * span), F32)
        for s in range(score_ref.shape[0] // span):
            at = slice(s * span, (s + 1) * span)
            weights = jnp.exp(score_ref[at, :] - best)
            score_ref[at, :] = weights
            total = total + jnp.sum(weights, axis=0, keepdims=True)
        inverse = 1.0 / total
        for s in range(score_ref.shape[0] // span):
            at = slice(s * span, (s + 1) * span)
            p_ref[t, at, :] = (score_ref[at, :] * inverse).astype(BF)
        out = dot_tn(values, p_ref[t])
        out = jnp.where(sub < span // 2, out[:, :span], out[:, span:])
        wide_ref[t * span : (t + 1) * span, :] = out
        low_ref[:, t * span : (t + 1) * span] = jnp.transpose(out).astype(BF)
    part_ref[...] = dot_nt(low_ref[...], w_ref[:, 3 * inner :]).astype(BF)


def forward_kernel(
    x_ref,
    own_ref,
    far_ref,
    gains_ref,
    weights_ref,
    residual_ref,
    dense_ref,
    hidden_ref,
    slope_ref,
    part_ref,
):
    hidden = hidden_ref.shape[1]
    residual = x_ref[...].astype(F32) + (own_ref[...].astype(F32) + far_ref[...].astype(F32))
    residual_ref[...] = residual
    scale = lax.rsqrt(jnp.mean(residual * residual, axis=-1, keepdims=True) + norm_eps)
    dense_ref[...] = (residual * scale * gains_ref[1:2, :]).astype(BF)
    step = 256
    for at in range(0, hidden, step):
        pre = dot_nn(dense_ref[...], weights_ref[:, at : at + step])
        square = pre * pre
        root = 0.7978845608028654
        tanh = jnp.tanh(root * (pre + 0.044715 * pre * square))
        hidden_ref[:, at : at + step] = (0.5 * pre * (1.0 + tanh)).astype(BF)
        slope_ref[:, at : at + step] = 0.5 * (1.0 + tanh) + 0.5 * pre * (1.0 - tanh * tanh) * (
            root * (1.0 + 3.0 * 0.044715 * square)
        )
    part_ref[...] = dot_nt(hidden_ref[...], weights_ref[:, hidden:]).astype(BF)


def backward_kernel(
    residual_ref,
    own_ref,
    far_ref,
    teacher_ref,
    valid_ref,
    gains_ref,
    slope_ref,
    weights_ref,
    hidden_ref,
    dense_ref,
    out_ref,
    grad_ref,
    part_ref,
    loss_ref,
    outer_keep_ref,
    outer_send_ref,
    inner_keep_ref,
    inner_send_ref,
    back_ref,
    pre_ref,
    lines_ref,
    *,
    total_rows,
    rows_each,
):
    hidden = pre_ref.shape[1]
    result = residual_ref[...] + (own_ref[...].astype(F32) + far_ref[...].astype(F32))
    out_ref[...] = result.astype(BF)
    rows = result.shape[0]
    valid = row_to_column(valid_ref[...].astype(F32), rows)
    misfit = result - teacher_ref[...].astype(F32)
    loss = 0.5 * jnp.sum(valid * misfit * misfit)
    loss_ref[...] = jnp.full(loss_ref.shape, loss, F32)
    factor = total_rows / gains_ref[2:3, 0:1]
    grad = factor * valid * misfit
    grad_ref[...] = grad
    back_ref[...] = grad.astype(BF)
    step = 256
    for at in range(0, hidden, step):
        grad_hidden = dot_nn(back_ref[...], weights_ref[:, hidden + at : hidden + at + step])
        pre_ref[:, at : at + step] = (grad_hidden * slope_ref[:, at : at + step]).astype(BF)
    part_ref[...] = dot_nt(pre_ref[...], weights_ref[:, :hidden]).astype(BF)
    dense_grad(back_ref[...], hidden_ref, outer_keep_ref, outer_send_ref, lines_ref, rows_each)
    dense_grad(dense_ref[...], pre_ref, inner_keep_ref, inner_send_ref, lines_ref, rows_each)


def split_rows(value, target_ref, rows_each):
    place = lax.axis_index(CONTEXT)
    mine = lax.rem(place, 2)
    half = value.shape[0] // 2
    source = target_ref.at[0]
    source[...] = value
    ordered = target_ref.at[1]
    for g in range(8):
        keep = pl.multiple_of((2 * g + mine) * rows_each, 16)
        send = pl.multiple_of((2 * g + 1 - mine) * rows_each, 16)
        ordered[g * rows_each : (g + 1) * rows_each, :] = source[pl.ds(keep, rows_each), :]
        ordered[half + g * rows_each : half + (g + 1) * rows_each, :] = source[
            pl.ds(send, rows_each), :
        ]


def put_rows(product, start, keep_ref, send_refs):
    rows_each = keep_ref.shape[1]
    cols = slice(start, start + product.shape[1])
    low = product.astype(BF)
    for g in range(8):
        keep_ref[g, :, cols] = low[g * rows_each : (g + 1) * rows_each, :]
        send_ref = send_refs[g * len(send_refs) // 8]
        send_ref[g % send_ref.shape[0], :, cols] = low[(8 + g) * rows_each : (9 + g) * rows_each, :]


def dense_grad(left, right_ref, keep_ref, send_ref, lines_ref, rows_each):
    split_rows(jnp.transpose(left.astype(F32)).astype(BF), lines_ref, rows_each)
    for at in range(0, right_ref.shape[1], 512):
        put_rows(dot_nn(lines_ref[1], right_ref[:, at : at + 512]), at, keep_ref, [send_ref])


def attention_back_kernel(
    own_ref,
    far_ref,
    grad_ref,
    residual_ref,
    gains_ref,
    wide_ref,
    p_ref,
    kv_ref,
    q_ref,
    w_ref,
    low_ref,
    residual_grad_ref,
    keep_ref,
    send_ref,
    dq_ref,
    dkv_ref,
    gain_ref,
    small_ref,
    ds_ref,
    diag_ref,
    line_ref,
    *,
    inner,
    span,
    tokens,
    rows_each,
):
    place = lax.axis_index(CONTEXT)
    incoming = own_ref[...].astype(F32) + far_ref[...].astype(F32)
    residual = residual_ref[...]
    scale = lax.rsqrt(jnp.mean(residual * residual, axis=-1, keepdims=True) + norm_eps)
    scaled = incoming * gains_ref[1:2, :]
    mean = jnp.mean(scaled * residual, axis=-1, keepdims=True)
    residual_grad = grad_ref[...] + (scale * scaled - residual * (scale * scale * scale * mean))
    residual_grad_ref[...] = residual_grad
    gain_ref[...] = jnp.broadcast_to(
        jnp.sum(incoming * residual * scale, axis=0, keepdims=True), gain_ref.shape
    )
    grads = dot_nn(residual_grad.astype(BF), w_ref[:, 3 * inner :])
    split_rows(jnp.transpose(residual_grad).astype(BF), line_ref, rows_each)
    put_rows(dot_nn(line_ref[1], low_ref[...]), 0, keep_ref, [send_ref])
    lane = lax.broadcasted_iota(jnp.int32, (span, span), 1)
    sub = lax.broadcasted_iota(jnp.int32, (span, span), 0)
    keys_all = p_ref.shape[1]
    blocks = tokens // span
    small_ref[...] = jnp.zeros_like(small_ref)
    tables = [bucket_onehot(d, span).astype(F32) for d in (-1, 0, 1)]
    zero = jnp.zeros((span, span), BF)
    for t in range(inner // span):
        cols = slice(t * span, (t + 1) * span)
        keys = kv_ref[:, cols]
        values = kv_ref[:, inner + t * span : inner + (t + 1) * span]
        pair = grads[:, cols].astype(BF)
        pair_back = jnp.transpose(pair.astype(F32)) * wide_ref[cols, :]
        delta = jnp.concatenate(
            [
                jnp.sum(pair_back[: span // 2], axis=0, keepdims=True),
                jnp.sum(pair_back[span // 2 :], axis=0, keepdims=True),
            ],
            axis=1,
        )
        grad_both = jnp.concatenate(
            [jnp.where(lane < span // 2, pair, zero), jnp.where(lane < span // 2, zero, pair)], axis=0
        )
        query = q_ref[:, cols]
        query_both = jnp.concatenate(
            [jnp.where(lane < span // 2, query, zero), jnp.where(lane < span // 2, zero, query)],
            axis=0,
        )
        low_sum = jnp.zeros((1, 2 * span), F32)
        high_sum = jnp.zeros((1, 2 * span), F32)
        for s in range(keys_all // span):
            at = slice(s * span, (s + 1) * span)
            dots = dot_nt(values[at, :], grad_both)
            ds = (p_ref[t, at, :].astype(F32) * (dots - delta)).astype(BF)
            ds_ref[at, :] = ds
            if s < blocks:
                line = jnp.sum(ds.astype(F32), axis=0, keepdims=True)
                low_sum = low_sum + jnp.where(s < place - 1, line, 0.0)
                high_sum = high_sum + jnp.where(s > place + 1, line, 0.0)
        dkv_ref[:, cols] = dot_nn(ds_ref[...], query_both).astype(BF)
        dkv_ref[:, inner + t * span : inner + (t + 1) * span] = dot_nn(p_ref[t], grad_both).astype(
            BF
        )
        dq = dot_tn(keys, ds_ref[...])
        dq = jnp.where(sub < span // 2, dq[:, :span], dq[:, span:])
        dq_ref[:, cols] = jnp.transpose(dq).astype(BF)
        for head in range(2):
            for which in range(3):
                s = place + which - 1
                inside = (s >= 0) & (s < blocks)
                start = pl.multiple_of(jnp.clip(s, 0, blocks - 1) * span, span)
                block = ds_ref[pl.ds(start, span), head * span : (head + 1) * span].astype(F32)
                block = jnp.where(inside, block, 0.0)
                block = jnp.concatenate([block, jnp.zeros((span, span), F32)], axis=1)
                size = span
                while size > 8:
                    size = size // 2
                    block = block[:size] + pltpu.roll(block[size:], 2 * span - size, 1)
                line = block[0:1]
                for j in range(1, 8):
                    line = line + pltpu.roll(block, 2 * span - j, 1)[j : j + 1]
                diag_ref[which, 2 * t + head : 2 * t + head + 1, :] = line
            bucket = lax.broadcasted_iota(jnp.int32, (1, 128), 1)
            part = slice(head * span, (head + 1) * span)
            low_total = jnp.sum(low_sum[:, part], axis=1, keepdims=True)
            high_total = jnp.sum(high_sum[:, part], axis=1, keepdims=True)
            small_ref[2 * t + head : 2 * t + head + 1, :] = jnp.where(
                bucket == BUCKETS // 2 - 1, low_total, 0.0
            ) + jnp.where(bucket == BUCKETS - 1, high_total, 0.0)
    heads = inner * 2 // span
    for which in range(3):
        line = lax.dot_general(
            diag_ref[which],
            tables[which],
            (((1,), (1,)), ((), ())),
            preferred_element_type=F32,
            precision=lax.Precision.HIGHEST,
        )
        small_ref[0:heads, 0:BUCKETS] += line[0:heads, :]


def rows_grad_kernel(
    dq_ref,
    dkv_ref,
    w_ref,
    normed_ref,
    gains_ref,
    dense_gain_ref,
    small_ref,
    loss_ref,
    keep_ref,
    *refs,
    inner,
    span,
    tokens,
    slots,
    heads,
):
    send_refs, (part_ref, line_ref) = refs[:-2], refs[-2:]
    place = lax.axis_index(CONTEXT)
    mine = lax.rem(place, 2)
    side = lax.axis_index(TENSOR)
    part_ref[...] = dot_nt(dkv_ref[...], w_ref[:, inner : 3 * inner])
    own_at = pl.multiple_of(place * span, span)
    part_ref[pl.ds(own_at, span), :] += dot_nt(dq_ref[...], w_ref[:, :inner])
    total = jnp.zeros((1, part_ref.shape[1]), F32)
    for s in range(part_ref.shape[0] // span):
        at = slice(s * span, (s + 1) * span)
        total = total + jnp.sum(
            part_ref[at, :] * normed_ref[at, :].astype(F32), axis=0, keepdims=True
        )
    line_ref[...] = jnp.zeros_like(line_ref)
    line_ref[slots : slots + 1, :] = total / gains_ref[0:1, :]
    line_ref[slots + 1 : slots + 2, :] = 0.5 * dense_gain_ref[0:1, :]
    for h in range(heads):
        start = pl.multiple_of(side * 128, 128)
        line_ref[slots + 2 + h : slots + 3 + h, pl.ds(start, 128)] = small_ref[h : h + 1, :]
    line_ref[slots + 2 : slots + 3, 256:384] = 0.5 * loss_ref[0:1, :]
    keep_rows = lax.broadcasted_iota(jnp.int32, line_ref.shape, 0) < slots
    for g in range(4):
        for target, block in (
            (keep_ref.at[g], 2 * g + mine),
            (send_refs[g // 2].at[g % 2], 2 * g + 1 - mine),
        ):
            token_at = pl.multiple_of(block * span, span)
            slot_at = pl.multiple_of(tokens + block * PAD, PAD)
            target[0:span, :] = part_ref[pl.ds(token_at, span), :].astype(BF)
            tail = jnp.where(keep_rows, part_ref[pl.ds(slot_at, PAD), :], line_ref[...])
            target[span : span + PAD, :] = tail.astype(BF)


def weight_grad_kernel(
    dq_ref,
    dkv_ref,
    normed_ref,
    keep_ref,
    *refs,
    inner,
    span,
    rows_each,
):
    send_refs, (wide_ref, line_ref) = refs[:-2], refs[-2:]
    place = lax.axis_index(CONTEXT)

    def put(product, start):
        put_rows(product, start, keep_ref, send_refs)

    own_at = pl.multiple_of(place * span, span)
    own = normed_ref[pl.ds(own_at, span), :].astype(F32)
    split_rows(jnp.transpose(own).astype(BF), line_ref, rows_each)
    put(dot_nn(line_ref[1], dq_ref[...]), 0)
    split_rows(jnp.transpose(normed_ref[...].astype(F32)).astype(BF), wide_ref, rows_each)
    for at in range(0, 2 * inner, 256):
        put(dot_nn(wide_ref[1], dkv_ref[:, at : at + 256]), inner + at)


def halve_kernel(*refs, counts):
    targets = refs[-2:]
    mine = lax.axis_index(FSDP)
    sources, at = [], 0
    for count in counts:
        sources.append((refs[at], refs[at + 1 : at + 1 + count]))
        at += 1 + count
    for flip in range(2):

        @pl.when(mine == flip)
        def _():
            start = 0
            for keep_ref, far_refs in sources:
                width = keep_ref.shape[2]
                for g in range(8):
                    far = far_refs[g * len(far_refs) // 8][g % far_refs[0].shape[0]]
                    sums = keep_ref[g].astype(F32) + far.astype(F32)
                    targets[(g // 4) ^ flip][g % 4, :, start : start + width] = sums.astype(BF)
                start += width


def turn_kernel(keep_ref, far_ref, next_ref, send_ref, *, pick):
    for which, target in enumerate((next_ref, send_ref)):
        for g in range(max(1, keep_ref.shape[0] // 2)):
            block = pick(which, g)
            sums = keep_ref[block].astype(F32) + far_ref[block].astype(F32)
            if len(target.shape) == 2:
                target[...] = sums.astype(target.dtype)
            else:
                target[g] = sums.astype(target.dtype)


def pick_z1(which, g):
    return (g // 2) * 4 + (lax.axis_index(CONTEXT) // 2 ^ (which + 2 * (g % 2)))


def pick_z2(which, g):
    return 2 * g + which


def pick_x(which, g):
    return lax.axis_index(FSDP) ^ which


def quarter_kernel(keep_ref, far_ref, next_ref, send_ref):
    place = lax.axis_index(CONTEXT) // 2
    for target, flip in ((next_ref, 0), (send_ref, 1)):
        for g in range(2):
            block = place ^ (flip + 2 * g)
            total = keep_ref[block].astype(F32) + far_ref[block].astype(F32)
            target[g] = total.astype(BF)


def eighth_kernel(keep_ref, far_ref, own_ref, send_ref):
    own_ref[...] = (keep_ref[0].astype(F32) + far_ref[0].astype(F32)).astype(own_ref.dtype)
    send_ref[...] = (keep_ref[1].astype(F32) + far_ref[1].astype(F32)).astype(BF)


def total_kernel(own_ref, far_ref, token_ref, *out_refs):
    token_ref[...] = jnp.zeros_like(token_ref)
    at = 0
    for out in out_refs:
        cols = slice(at, at + out.shape[1])
        out[...] = (own_ref[:, cols].astype(F32) + far_ref[:, cols].astype(F32)).astype(out.dtype)
        at += out.shape[1]


def columns_kernel(keep_ref, one_ref, two_ref, next_ref, send_ref):
    mine = lax.axis_index(TENSOR)
    width = next_ref.shape[2]
    for target, start in ((next_ref, mine * width), (send_ref, (1 - mine) * width)):
        cols = pl.ds(pl.multiple_of(start, 128), width)
        for half, far_ref in ((slice(0, 2), one_ref), (slice(2, 4), two_ref)):
            total = keep_ref[half, :, cols].astype(F32) + far_ref[:, :, cols].astype(F32)
            target[half] = total.astype(BF)


def tail_kernel(own_ref, far_ref, out_ref, *, span):
    mine = lax.axis_index(TENSOR)
    width = own_ref.shape[1]
    rows = slice(span, span + PAD)
    out_ref[:, pl.ds(pl.multiple_of(mine * width, 128), width)] = own_ref[rows, :].astype(F32)
    out_ref[:, pl.ds(pl.multiple_of((1 - mine) * width, 128), width)] = far_ref[rows, :].astype(F32)


def finish_kernel(
    own_ref,
    far_ref,
    x_ref,
    slots_ref,
    gains_ref,
    residual_grad_ref,
    tail_far_ref,
    inputs_ref,
    memory_ref,
    gain_ref,
    dense_gain_ref,
    bias_ref,
    loss_ref,
    full_ref,
    line_ref,
    *,
    span,
    slots,
):
    mine = lax.axis_index(TENSOR)
    group = lax.axis_index(FSDP) * 8 + lax.axis_index(CONTEXT)
    width = own_ref.shape[1]
    full_ref[:, pl.ds(pl.multiple_of(mine * width, 128), width)] = own_ref[...].astype(F32)
    full_ref[:, pl.ds(pl.multiple_of((1 - mine) * width, 128), width)] = far_ref[...].astype(F32)
    for source, target, start, extra in (
        (x_ref, inputs_ref, 0, residual_grad_ref),
        (slots_ref, memory_ref, span, None),
    ):
        values = source[...].astype(F32)
        scale = lax.rsqrt(jnp.mean(values * values, axis=-1, keepdims=True) + norm_eps)
        scaled = full_ref[start : start + values.shape[0], :] * gains_ref[0:1, :]
        mean = jnp.mean(scaled * values, axis=-1, keepdims=True)
        back = scale * scaled - values * (scale * scale * scale * mean)
        if extra is None:
            target[:, 0, :] = back
        else:
            target[...] = extra[...] + back
    line_ref[...] = full_ref[span : span + PAD, :] + tail_far_ref[...]
    lines = pltpu.roll(line_ref[...], full_ref.shape[1] - group * gain_ref.shape[1], 1)
    rows_each = gain_ref.shape[1]
    gain_ref[...] = lines[slots : slots + 1, 0:rows_each]
    dense_gain_ref[...] = lines[slots + 1 : slots + 2, 0:rows_each]
    heads = bias_ref.shape[0]
    start = pl.multiple_of(mine * 128, 128)
    bias_ref[...] = line_ref[slots + 2 : slots + 2 + heads, pl.ds(start, 128)][:, 0:BUCKETS]
    loss_ref[...] = line_ref[slots + 2 : slots + 3, 256:384] / (
        gains_ref[2:3, 0:128] * full_ref.shape[1]
    )


def fast_local(
    inputs,
    memory,
    teacher,
    segments,
    memory_owner,
    valid_mask,
    attention_gain,
    query_weight,
    key_weight,
    value_weight,
    attention_out_weight,
    position_bias,
    feedforward_gain,
    inner_weight,
    feedforward_out_weight,
):
    span, width = inputs.shape[1:]
    slots = memory.shape[1]
    rows_each, inner = query_weight.shape
    hidden = inner_weight.shape[1]
    heads = position_bias.shape[0]
    tokens = 8 * span
    keys_all = 8 * (span + PAD)
    total_rows = 2 * tokens
    x = inputs[0]
    block_rows = span + PAD
    first_rows = 4 * rows_each + PAD
    early_rows = block_rows + first_rows
    later_rows = 2 * hidden // inner * rows_each
    own, early, later, over, block = call(
        pack_kernel,
        [
            ((early_rows + later_rows, inner), BF),
            ((early_rows, inner), BF),
            ((later_rows, inner), BF),
            ((first_rows + later_rows, inner), BF),
            ((block_rows, inner), BF),
        ],
        name="pack",
        ins_hbm=13,
        scratch=(
            pltpu.VMEM((slots, width), BF),
            pltpu.VMEM((1, span), jnp.int32),
            pltpu.VMEM((1, slots), jnp.int32),
            pltpu.VMEM((1, span), jnp.int32),
            pltpu.VMEM((1, rows_each), BF),
            pltpu.VMEM((1, rows_each), BF),
            pltpu.VMEM((PAD, width), F32),
            pltpu.SemaphoreType.DMA((7 + 4 + 2 * hidden // inner,)),
        ),
    )(
        x,
        memory[0],
        segments,
        memory_owner,
        valid_mask,
        query_weight,
        key_weight,
        value_weight,
        attention_out_weight,
        inner_weight,
        feedforward_out_weight,
        attention_gain[None],
        feedforward_gain[None],
    )

    (toeplitz,) = call(
        lambda *refs: bias_kernel(*refs, span=span),
        [((heads, 5, span, span), F32)],
        name="bias",
        waits=(early,),
    )(position_bias)
    two = swap_context(early, 4)
    one = swap_context(own, 2)
    over_own = swap_fsdp(over)
    block_own = swap_tensor(block)
    first_pair, block_pair, later_one = call(
        split_kernel,
        [
            ((2 * first_rows, inner), BF),
            ((2 * block_rows, inner), BF),
            ((later_rows, inner), BF),
        ],
        name="split",
        waits=(over_own, block_own, toeplitz),
    )(two, one)
    three = swap_context(two, 2)
    over_pair = swap_fsdp(first_pair)
    block_pair = swap_tensor(block_pair)
    later_two = swap_context(gate(later, first_pair), 4)
    over_one = swap_fsdp(later_one)
    first_last, block_last, joined = call(
        lambda *refs: join_kernel(*refs, block_rows=block_rows, first_rows=first_rows),
        [
            ((first_rows, inner), BF),
            ((block_rows, inner), BF),
            ((4 * early_rows + 3 * (first_rows + block_rows + later_rows), inner), BF),
        ],
        name="join",
        waits=(later_two, over_one),
    )(own, one, two, three, over_own, over_pair, block_own, block_pair)
    over_last = swap_fsdp(first_last)
    block_last = swap_tensor(block_last)
    later_three = swap_context(later_two, 2)
    over_two = swap_fsdp(later_two)
    joined_core, over_core, block_core = swap_core([joined, over_last, block_last])
    w_all, gains = call(
        lambda *refs: weights_kernel(
            *refs, rows_each=rows_each, inner=inner, block_rows=block_rows
        ),
        [((width, 4 * inner), BF), ((8, width), F32)],
        name="weights",
    )(joined, over_last, joined_core, over_core)
    (normed, kv, queries, probs, low, wide, part) = call(
        lambda *refs: attend_kernel(
            *refs, span=span, slots=slots, tokens=tokens, inner=inner, first_rows=first_rows
        ),
        [
            ((keys_all, width), BF),
            ((keys_all, 2 * inner), BF),
            ((span, inner), BF),
            ((inner // span, keys_all, 2 * span), BF),
            ((span, inner), BF),
            ((inner, span), F32),
            ((span, width), BF),
        ],
        name="attend",
        scratch=(
            pltpu.VMEM((keys_all, span), F32),
            pltpu.VMEM((keys_all, 2 * span), F32),
            pltpu.VMEM((span + PAD, width), F32),
        ),
        waits=(later_three,),
    )(w_all, gains, toeplitz, joined, block_last, joined_core, block_core)
    far = swap_tensor(part)
    over_three = gate(swap_fsdp(later_three), far)
    later_all = [later_two, later_three, over_one, over_two]
    later_all = [gate(piece, part) for piece in later_all] + [over_three]
    (dense_weights,) = call(
        lambda *refs: order_kernel(*refs, rows_each=rows_each),
        [((width, 2 * hidden), BF)],
        name="order",
        waits=(part,),
    )(joined, *later_all, joined_core, *swap_core(later_all))
    (residual, dense_low, hidden_low, slope, dense_part) = call(
        forward_kernel,
        [
            ((span, width), F32),
            ((span, width), BF),
            ((span, hidden), BF),
            ((span, hidden), F32),
            ((span, width), BF),
        ],
        name="forward",
    )(x, part, far, gains, dense_weights)
    dense_far = swap_tensor(dense_part)
    (output, grad_result, grad_part, loss_part, *dense_grads) = call(
        lambda *refs: backward_kernel(*refs, total_rows=total_rows, rows_each=rows_each),
        [
            ((span, width), BF),
            ((span, width), F32),
            ((span, width), BF),
            ((8, 128), F32),
        ]
        + [((8, rows_each, hidden), BF)] * 4,
        name="backward",
        scratch=(
            pltpu.VMEM((span, width), BF),
            pltpu.VMEM((span, hidden), BF),
            pltpu.VMEM((2, width, span), BF),
        ),
    )(
        residual,
        dense_part,
        dense_far,
        teacher[0],
        valid_mask,
        gains,
        slope,
        dense_weights,
        hidden_low,
        dense_low,
    )
    outer_keep, outer_send, inner_keep, inner_send = dense_grads
    grad_far = swap_tensor(grad_part)

    def halve(sources, *waits):
        columns = sum(keep.shape[2] for keep, _ in sources)
        return call(
            lambda *refs: halve_kernel(*refs, counts=[len(far) for _, far in sources]),
            [((4, rows_each, columns), BF)] * 2,
            name="halve",
            waits=waits,
        )(*[item for keep, far in sources for item in (keep, *far)])

    def quarter(keep, far_half, *waits):
        rows, columns = keep.shape[1:]
        return call(
            quarter_kernel,
            [((2, rows, columns), BF)] * 2,
            name="quarter",
            waits=waits,
        )(keep, far_half)

    def eighth(keep, far_quarter, own_type, *waits):
        rows, columns = keep.shape[1:]
        return call(
            eighth_kernel,
            [((rows, columns), own_type), ((rows, columns), BF)],
            name="eighth",
            waits=waits,
        )(keep, far_quarter)

    def total(own, far_eighth, outs, *waits):
        outs = [((8, 128), F32), *outs]
        return call(total_kernel, outs, name="total", waits=waits)(own, far_eighth)

    def turn(keep, far_blocks, pick, outs, *waits):
        return call(
            lambda *refs: turn_kernel(*refs, pick=pick), outs, name="turn", waits=waits
        )(keep, far_blocks)

    def outer_blocks(count):
        return ((count, rows_each, hidden), BF)

    outer_far = swap_context(outer_send, 1)
    inner_far = swap_core([inner_send])
    inner_next, inner_over = halve([(inner_keep, inner_far)])
    inner_far = swap_fsdp(inner_over)
    outer_next, outer_over = turn(
        outer_keep, outer_far, pick_z1, [outer_blocks(4)] * 2, inner_over, grad_far
    )
    outer_far = swap_context(outer_over, 2)

    (grad_residual, out_keep, out_send, dq, dkv, dense_gain_rows, small) = call(
        lambda *refs: attention_back_kernel(
            *refs, inner=inner, span=span, tokens=tokens, rows_each=rows_each
        ),
        [
            ((span, width), F32),
            ((8, rows_each, inner), BF),
            ((8, rows_each, inner), BF),
            ((span, inner), BF),
            ((keys_all, 2 * inner), BF),
            ((8, width), F32),
            ((8, 128), F32),
        ],
        name="attend_back",
        scratch=(
            pltpu.VMEM((keys_all, 2 * span), BF),
            pltpu.VMEM((3, 8, 2 * span), F32),
            pltpu.VMEM((2, width, span), BF),
        ),
        waits=(outer_over,),
    )(grad_part, grad_far, grad_result, residual, gains, wide, probs, kv, queries, w_all, low)

    rows_keep, *rows_send = call(
        lambda *refs: rows_grad_kernel(
            *refs, inner=inner, span=span, tokens=tokens, slots=slots, heads=heads
        ),
        [((4, span + PAD, width), BF)] + [((2, span + PAD, width), BF)] * 2,
        name="rows_grad",
        scratch=(pltpu.VMEM((keys_all, width), F32), pltpu.VMEM((PAD, width), F32)),
    )(dq, dkv, w_all, normed, gains, dense_gain_rows, small, loss_part)
    rows_far = swap_core(rows_send)

    weight_keep, *weight_send = call(
        lambda *refs: weight_grad_kernel(*refs, inner=inner, span=span, rows_each=rows_each),
        [((8, rows_each, 3 * inner), BF)] + [((4, rows_each, 3 * inner), BF)] * 2,
        name="weight_grad",
        scratch=(
            pltpu.VMEM((2, width, keys_all), BF),
            pltpu.VMEM((2, width, span), BF),
        ),
        waits=(rows_send[0],),
    )(dq, dkv, normed)
    weight_far = swap_core(weight_send)
    out_far = swap_core([out_send])
    outer_next, outer_over = turn(
        outer_next, outer_far, pick_z2, [outer_blocks(2)] * 2, weight_send[0]
    )
    outer_far = swap_context(outer_over, 4)
    inner_next, inner_over = quarter(inner_next, inner_far, outer_over)
    inner_far = swap_context(inner_over, 2)
    weight_next, weight_over = halve(
        [(weight_keep, weight_far), (out_keep, out_far)], inner_over
    )
    weight_far = swap_fsdp(weight_over)
    rows_next, rows_over = call(
        columns_kernel,
        [((4, span + PAD, width // 2), BF)] * 2,
        name="columns",
        waits=(weight_over,),
    )(rows_keep, *rows_far)
    rows_far = swap_tensor(rows_over)

    rows_next, rows_over = quarter(rows_next, rows_far)
    rows_far = swap_context(rows_over, 2)
    inner_own, inner_over = eighth(inner_next, inner_far, F32, rows_over)
    inner_far = swap_context(inner_over, 4)
    outer_own, outer_over = turn(
        outer_next,
        outer_far,
        pick_x,
        [((rows_each, hidden), F32), ((rows_each, hidden), BF)],
        inner_over,
    )
    outer_far = swap_fsdp(outer_over)
    weight_next, weight_over = quarter(weight_next, weight_far, outer_over)
    weight_far = swap_context(weight_over, 2)

    rows_own, rows_over = eighth(rows_next, rows_far, BF, weight_over)
    rows_far = swap_context(rows_over, 4)
    token, grad_outer = total(outer_own, outer_far, [((rows_each, hidden), F32)], rows_over)
    token, grad_inner = total(inner_own, inner_far, [((rows_each, hidden), F32)], token)
    weight_own, weight_over = eighth(weight_next, weight_far, F32, token)
    weight_far = swap_context(weight_over, 4)

    token, rows_half = total(
        rows_own, rows_far, [((span + PAD, width // 2), BF)], weight_over
    )
    rows_other = swap_tensor(rows_half)
    (tail,) = call(
        lambda *refs: tail_kernel(*refs, span=span), [((PAD, width), F32)], name="tail"
    )(rows_half, rows_other)
    tail_far = swap_fsdp(tail)
    *rest, grad_output = total(weight_own, weight_far, [((rows_each, inner), F32)] * 4, tail)
    weight_grads = rest[1:]
    (grad_inputs, grad_memory, grad_gain, grad_dense_gain, grad_bias, loss) = call(
        lambda *refs: finish_kernel(*refs, span=span, slots=slots),
        [
            ((span, width), F32),
            ((slots, 1, width), F32),
            ((1, rows_each), F32),
            ((1, rows_each), F32),
            ((heads, BUCKETS), F32),
            ((1, 128), F32),
        ],
        name="finish",
        scratch=(pltpu.VMEM((span + PAD, width), F32), pltpu.VMEM((PAD, width), F32)),
    )(rows_half, rows_other, x, memory[0], gains, grad_residual, tail_far)
    return (
        loss[0, 0],
        output[None],
        grad_inputs[None],
        jnp.swapaxes(grad_memory, 0, 1),
        grad_gain[0],
        weight_grads[0],
        weight_grads[1],
        weight_grads[2],
        grad_output,
        grad_bias,
        grad_dense_gain[0],
        grad_inner,
        grad_outer,
    )


def solution(mesh):
    return jax.shard_map(
        fast_local if fits(mesh) else general_local,
        mesh=mesh,
        in_specs=(
            P(FSDP, CONTEXT, None),
            P(FSDP, CONTEXT, None),
            P(FSDP, CONTEXT, None),
            P(FSDP, CONTEXT),
            P(FSDP, CONTEXT),
            P(FSDP, CONTEXT),
            P(ROWS),
            P(ROWS, TENSOR),
            P(ROWS, TENSOR),
            P(ROWS, TENSOR),
            P(ROWS, TENSOR),
            P(TENSOR, None),
            P(ROWS),
            P(ROWS, TENSOR),
            P(ROWS, TENSOR),
        ),
        out_specs=(
            P(),
            P(FSDP, CONTEXT, None),
            P(FSDP, CONTEXT, None),
            P(FSDP, CONTEXT, None),
            P(ROWS),
            P(ROWS, TENSOR),
            P(ROWS, TENSOR),
            P(ROWS, TENSOR),
            P(ROWS, TENSOR),
            P(TENSOR, None),
            P(ROWS),
            P(ROWS, TENSOR),
            P(ROWS, TENSOR),
        ),
        check_vma=False,
    )
```

```python
import jax
import jax.numpy as jnp
from jax import lax
from jax.experimental import pallas as pl
from jax.experimental.pallas import tpu as pltpu
from jax.sharding import PartitionSpec as P

BUCKETS = 32
FSDP = "fsdp"
CONTEXT = "context"
TENSOR = "tensor"
ROWS = (FSDP, CONTEXT)
PRODUCT_0 = "scd,df->scf"
PRODUCT_1 = "scd,di->sci"
PRODUCT_2 = "scd,scf->df"
PRODUCT_3 = "scd,sci->di"
PRODUCT_4 = "scf,df->scd"
PRODUCT_5 = "sci,di->scd"
PRODUCT_6 = "sjd,sji->di"
PRODUCT_7 = "sji,di->sjd"
PRODUCT_8 = "sqhd,skhd->sqhk"
PRODUCT_9 = "sqhk,qkb->hb"
PRODUCT_10 = "sqhk,skhd->sqhd"
PRODUCT_11 = "sqhk,sqhd->skhd"


norm_eps = 1e-06
score_floor = -1e30


def relative_bucket(distance):
    half_count = BUCKETS // 2
    exact_count = half_count // 2
    magnitude = jnp.minimum(jnp.abs(distance), 1024)
    far_bucket = jnp.full(distance.shape, exact_count, jnp.int32)
    for level_index in range(1, half_count - exact_count):
        far_bucket = far_bucket + (
            magnitude * magnitude >= exact_count * exact_count * 2**level_index
        ).astype(jnp.int32)
    bucket_ids = jnp.where(magnitude < exact_count, magnitude, far_bucket)
    return bucket_ids + (distance > 0).astype(jnp.int32) * half_count


def rms_norm(values, gain_in):
    inv_rms = lax.rsqrt(jnp.mean(values * values, axis=-1, keepdims=True) + norm_eps)
    return (values * inv_rms * gain_in, inv_rms)


def norm_back(values, inv_rms, gain_in, grad_in):
    scaled = grad_in * gain_in
    inner_mean = jnp.mean(scaled * values, axis=-1, keepdims=True)
    grad_values = inv_rms * scaled - values * inv_rms * inv_rms * inv_rms * inner_mean
    grad_gain = jnp.sum(grad_in * values * inv_rms, axis=tuple(range(values.ndim - 1)))
    return (grad_values, grad_gain)


def smooth_gate(values):
    return jax.nn.gelu(values, approximate=True)


def block_size():
    return 512


def pad_rows(values_in, block_rows, fill_value):
    blocks = -(-values_in.shape[1] // block_rows)
    missing = blocks * block_rows - values_in.shape[1]
    padding = [(0, 0)] * values_in.ndim
    padding[1] = (0, missing)
    return (jnp.pad(values_in, padding, constant_values=fill_value), blocks)


def key_places(row_ids, shard_rows, key_span):
    within = row_ids % key_span
    return (row_ids // key_span * shard_rows + within, within < shard_rows)


def scores_with_bias(
    query_blk, key_blk, query_place, query_doc, key_place, key_doc, key_token, bias_table
):
    scores = jnp.einsum(PRODUCT_8, query_blk, key_blk, preferred_element_type=jnp.float32)
    bucket = relative_bucket(key_place[None, :] - query_place[:, None])
    rel_terms = jnp.where(key_token[None, None, :], jnp.take(bias_table, bucket, axis=1), 0.0)
    scores = scores + jnp.moveaxis(rel_terms, 0, 1)[None]
    same_doc = (query_doc[:, :, None] == key_doc[:, None, :])[:, :, None, :]
    return (scores, same_doc, bucket)


def sum_grads(grad_items):
    return (
        lax.psum_scatter(grad_items[0], ROWS, scatter_dimension=0, tiled=True),
        lax.psum_scatter(grad_items[1], ROWS, scatter_dimension=0, tiled=True),
        lax.psum_scatter(grad_items[2], ROWS, scatter_dimension=0, tiled=True),
        lax.psum_scatter(grad_items[3], ROWS, scatter_dimension=0, tiled=True),
        lax.psum_scatter(grad_items[4], ROWS, scatter_dimension=0, tiled=True),
        lax.psum_scatter(grad_items[5], ROWS, scatter_dimension=0, tiled=True),
        lax.psum_scatter(grad_items[6], ROWS, scatter_dimension=0, tiled=True),
        lax.psum_scatter(grad_items[7], ROWS, scatter_dimension=0, tiled=True),
    )


def general_local(
    inputs,
    memory,
    teacher,
    segments,
    memory_owner,
    valid_mask,
    attention_gain,
    query_weight,
    key_weight,
    value_weight,
    attention_out_weight,
    position_bias,
    feedforward_gain,
    inner_weight,
    feedforward_out_weight,
):
    sequences, shard_rows, model_width = inputs.shape
    key_span = shard_rows + memory.shape[1]
    context_size = lax.axis_size(CONTEXT)
    length = shard_rows * context_size
    context_place = lax.axis_index(CONTEXT)
    local_heads = position_bias.shape[0]
    bucket_count = position_bias.shape[1]
    head_size = query_weight.shape[1] // local_heads
    local_inner = local_heads * head_size
    total_rows = sequences * length * lax.axis_size(FSDP)
    bias_table = position_bias.astype(jnp.float32)
    (
        full_query,
        full_key,
        full_value,
        full_output,
        full_inner,
        full_outer,
        full_attn_gain,
        full_dense_gain,
    ) = (
        lax.all_gather(query_weight, ROWS, axis=0, tiled=True),
        lax.all_gather(key_weight, ROWS, axis=0, tiled=True),
        lax.all_gather(value_weight, ROWS, axis=0, tiled=True),
        lax.all_gather(attention_out_weight, ROWS, axis=0, tiled=True),
        lax.all_gather(inner_weight, ROWS, axis=0, tiled=True),
        lax.all_gather(feedforward_out_weight, ROWS, axis=0, tiled=True),
        lax.all_gather(attention_gain, ROWS, axis=0, tiled=True),
        lax.all_gather(feedforward_gain, ROWS, axis=0, tiled=True),
    )
    attn_gain = full_attn_gain.astype(jnp.float32)
    dense_gain = full_dense_gain.astype(jnp.float32)
    local_docs = jnp.concatenate([segments, memory_owner], axis=1)
    key_docs = lax.all_gather(local_docs, CONTEXT, axis=1, tiled=True)
    query_docs_all = key_docs.reshape(sequences, context_size, key_span)[:, :, :shard_rows].reshape(
        sequences, length
    )
    token_count = lax.psum(jnp.sum(valid_mask.astype(jnp.float32)), ROWS)
    inputs_float = inputs.astype(jnp.float32)
    memory_float = memory.astype(jnp.float32)
    normed, input_scale = rms_norm(inputs_float, attn_gain)
    memory_normed, memory_scale = rms_norm(memory_float, attn_gain)
    normed_low = normed.astype(jnp.bfloat16)
    both_rows = jnp.concatenate([normed_low, memory_normed.astype(jnp.bfloat16)], axis=1)
    queries = jnp.dot(normed_low, full_query, preferred_element_type=jnp.float32).astype(
        jnp.bfloat16
    )
    key_local = jnp.dot(both_rows, full_key, preferred_element_type=jnp.float32).astype(
        jnp.bfloat16
    )
    value_local = jnp.dot(both_rows, full_value, preferred_element_type=jnp.float32).astype(
        jnp.bfloat16
    )
    query_heads = queries.reshape(sequences, shard_rows, local_heads, head_size)
    query_place = context_place * shard_rows + jnp.arange(shard_rows, dtype=jnp.int32)
    fold_init = (
        jnp.full((sequences, shard_rows, local_heads), score_floor, jnp.float32),
        jnp.zeros((sequences, shard_rows, local_heads), jnp.float32),
        jnp.zeros((sequences, shard_rows, local_heads, head_size), jnp.float32),
    )
    fold_state = fold_init
    key_piece = lax.all_gather(key_local, CONTEXT, axis=1, tiled=True)
    value_piece = lax.all_gather(value_local, CONTEXT, axis=1, tiled=True)
    block_rows = block_size()
    key_pad, blocks = pad_rows(key_piece, block_rows, 0)
    value_pad, blocks = pad_rows(value_piece, block_rows, 0)
    doc_pad, blocks = pad_rows(key_docs, block_rows, -1)

    def attend_advance(running, block_index):
        running_best, running_sum, summed = running
        offset = block_index * block_rows
        key_blk = lax.dynamic_slice_in_dim(key_pad, offset, block_rows, 1).reshape(
            sequences, block_rows, local_heads, head_size
        )
        value_blk = lax.dynamic_slice_in_dim(value_pad, offset, block_rows, 1).reshape(
            sequences, block_rows, local_heads, head_size
        )
        doc_blk = lax.dynamic_slice_in_dim(doc_pad, offset, block_rows, 1)
        key_place, key_token = key_places(
            offset + jnp.arange(block_rows, dtype=jnp.int32), shard_rows, key_span
        )
        scores, same_doc, bucket = scores_with_bias(
            query_heads, key_blk, query_place, segments, key_place, doc_blk, key_token, bias_table
        )
        masked = jnp.where(same_doc, scores, score_floor)
        new_best = jnp.maximum(running_best, jnp.max(masked, axis=-1))
        weights = jnp.where(same_doc, jnp.exp(scores - new_best[..., None]), 0.0)
        factor = jnp.exp(running_best - new_best)
        running_sum = running_sum * factor + jnp.sum(weights, axis=-1)
        summed = summed * factor[..., None] + jnp.einsum(
            PRODUCT_10,
            weights.astype(jnp.bfloat16),
            value_blk,
            preferred_element_type=jnp.float32,
        )
        return ((new_best, running_sum, summed), None)

    fold_state, unused = lax.scan(attend_advance, fold_state, jnp.arange(blocks, dtype=jnp.int32))
    running_best, running_sum, summed = fold_state
    attended_values = summed / running_sum[..., None]
    attended_low = attended_values.reshape(sequences, shard_rows, local_inner).astype(jnp.bfloat16)
    attention_part = jnp.einsum(
        PRODUCT_5, attended_low, full_output, preferred_element_type=jnp.float32
    )
    residual = inputs_float + lax.psum(attention_part.astype(jnp.bfloat16), TENSOR).astype(
        jnp.float32
    )
    dense_normed, dense_scale = rms_norm(residual, dense_gain)
    dense_low = dense_normed.astype(jnp.bfloat16)
    inner_pre = jnp.dot(dense_low, full_inner, preferred_element_type=jnp.float32)
    hidden_float, gate_pullback = jax.vjp(smooth_gate, inner_pre)
    hidden_low = hidden_float.astype(jnp.bfloat16)
    dense_part = jnp.einsum(
        PRODUCT_4, hidden_low, full_outer, preferred_element_type=jnp.float32
    )
    result = residual + lax.psum(dense_part.astype(jnp.bfloat16), TENSOR).astype(jnp.float32)
    target_mask = valid_mask.astype(jnp.float32)[..., None]
    misfit = result - teacher.astype(jnp.float32)
    loss_local = 0.5 * jnp.sum(target_mask * misfit * misfit)
    grad_result = total_rows / token_count * target_mask * misfit
    dense_back = grad_result.astype(jnp.bfloat16)
    grad_outer = jnp.einsum(
        PRODUCT_2, dense_back, hidden_low, preferred_element_type=jnp.float32
    )
    grad_hidden = jnp.einsum(
        PRODUCT_0, dense_back, full_outer, preferred_element_type=jnp.float32
    )
    grad_pre = gate_pullback(grad_hidden)[0].astype(jnp.bfloat16)
    grad_inner = jnp.einsum(PRODUCT_2, dense_low, grad_pre, preferred_element_type=jnp.float32)
    grad_dense_part = jnp.einsum(
        PRODUCT_4, grad_pre, full_inner, preferred_element_type=jnp.float32
    )
    grad_dense_normed = lax.psum(grad_dense_part.astype(jnp.bfloat16), TENSOR).astype(jnp.float32)
    back_residual, grad_dense_gain = norm_back(residual, dense_scale, dense_gain, grad_dense_normed)
    grad_residual = grad_result + back_residual
    attention_back = grad_residual.astype(jnp.bfloat16)
    grad_output = jnp.einsum(
        PRODUCT_3, attention_back, attended_low, preferred_element_type=jnp.float32
    )
    grad_attended = jnp.einsum(
        PRODUCT_1, attention_back, full_output, preferred_element_type=jnp.float32
    ).astype(jnp.bfloat16)
    grad_heads = grad_attended.reshape(sequences, shard_rows, local_heads, head_size)
    log_total = running_best + jnp.log(running_sum)
    delta_rows = jnp.sum(grad_heads.astype(jnp.float32) * attended_values, axis=-1)
    all_log_total, all_delta = (
        lax.all_gather(log_total, CONTEXT, axis=1, tiled=True),
        lax.all_gather(delta_rows, CONTEXT, axis=1, tiled=True),
    )
    query_init = (
        jnp.zeros((sequences, shard_rows, local_heads, head_size), jnp.float32),
        jnp.zeros((local_heads, bucket_count), jnp.float32),
    )
    fold_state = query_init
    key_piece = lax.all_gather(key_local, CONTEXT, axis=1, tiled=True)
    value_piece = lax.all_gather(value_local, CONTEXT, axis=1, tiled=True)
    query_block_rows = block_size()
    query_key_pad, blocks = pad_rows(key_piece, query_block_rows, 0)
    query_value_pad, blocks = pad_rows(value_piece, query_block_rows, 0)
    query_doc_pad, blocks = pad_rows(key_docs, query_block_rows, -1)

    def query_advance(running, block_index):
        grad_query, grad_bias = running
        offset = block_index * query_block_rows
        key_blk = lax.dynamic_slice_in_dim(query_key_pad, offset, query_block_rows, 1).reshape(
            sequences, query_block_rows, local_heads, head_size
        )
        value_blk = lax.dynamic_slice_in_dim(query_value_pad, offset, query_block_rows, 1).reshape(
            sequences, query_block_rows, local_heads, head_size
        )
        doc_blk = lax.dynamic_slice_in_dim(query_doc_pad, offset, query_block_rows, 1)
        key_place, key_token = key_places(
            offset + jnp.arange(query_block_rows, dtype=jnp.int32), shard_rows, key_span
        )
        scores, same_doc, bucket = scores_with_bias(
            query_heads, key_blk, query_place, segments, key_place, doc_blk, key_token, bias_table
        )
        probabilities = jnp.where(same_doc, jnp.exp(scores - log_total[..., None]), 0.0)
        value_dots = jnp.einsum(
            PRODUCT_8, grad_heads, value_blk, preferred_element_type=jnp.float32
        )
        grad_scores = (probabilities * (value_dots - delta_rows[..., None])).astype(jnp.bfloat16)
        grad_query = grad_query + jnp.einsum(
            PRODUCT_10, grad_scores, key_blk, preferred_element_type=jnp.float32
        )
        bucket_hits = (
            (bucket[:, :, None] == jnp.arange(bucket_count, dtype=jnp.int32)[None, None, :])
            & key_token[None, :, None]
        ).astype(jnp.bfloat16)
        grad_bias = grad_bias + jnp.einsum(
            PRODUCT_9, grad_scores, bucket_hits, preferred_element_type=jnp.float32
        )
        return ((grad_query, grad_bias), None)

    fold_state, unused = lax.scan(query_advance, fold_state, jnp.arange(blocks, dtype=jnp.int32))
    grad_query, grad_bias = fold_state
    key_heads = key_local.reshape(sequences, key_span, local_heads, head_size)
    value_heads = value_local.reshape(sequences, key_span, local_heads, head_size)
    local_place, local_token = key_places(
        context_place * key_span + jnp.arange(key_span, dtype=jnp.int32), shard_rows, key_span
    )
    key_init = (
        jnp.zeros((sequences, key_span, local_heads, head_size), jnp.float32),
        jnp.zeros((sequences, key_span, local_heads, head_size), jnp.float32),
    )
    fold_state = key_init
    query_piece = lax.all_gather(queries, CONTEXT, axis=1, tiled=True)
    grad_piece = lax.all_gather(grad_attended, CONTEXT, axis=1, tiled=True)
    key_block_rows = block_size()
    query_pad, blocks = pad_rows(query_piece, key_block_rows, 0)
    grad_pad, blocks = pad_rows(grad_piece, key_block_rows, 0)
    key_doc_pad, blocks = pad_rows(query_docs_all, key_block_rows, -1)
    total_pad, blocks = pad_rows(all_log_total, key_block_rows, 0.0)
    delta_pad, blocks = pad_rows(all_delta, key_block_rows, 0.0)

    def key_advance(running, block_index):
        grad_key, grad_value = running
        offset = block_index * key_block_rows
        query_blk = lax.dynamic_slice_in_dim(query_pad, offset, key_block_rows, 1).reshape(
            sequences, key_block_rows, local_heads, head_size
        )
        grad_blk = lax.dynamic_slice_in_dim(grad_pad, offset, key_block_rows, 1).reshape(
            sequences, key_block_rows, local_heads, head_size
        )
        doc_blk = lax.dynamic_slice_in_dim(key_doc_pad, offset, key_block_rows, 1)
        total_blk = lax.dynamic_slice_in_dim(total_pad, offset, key_block_rows, 1)
        delta_blk = lax.dynamic_slice_in_dim(delta_pad, offset, key_block_rows, 1)
        row_place = offset + jnp.arange(key_block_rows, dtype=jnp.int32)
        scores, same_doc, bucket = scores_with_bias(
            query_blk,
            key_heads,
            row_place,
            doc_blk,
            local_place,
            local_docs,
            local_token,
            bias_table,
        )
        probabilities = jnp.where(same_doc, jnp.exp(scores - total_blk[..., None]), 0.0)
        grad_value = grad_value + jnp.einsum(
            PRODUCT_11,
            probabilities.astype(jnp.bfloat16),
            grad_blk,
            preferred_element_type=jnp.float32,
        )
        value_dots = jnp.einsum(
            PRODUCT_8, grad_blk, value_heads, preferred_element_type=jnp.float32
        )
        grad_scores = (probabilities * (value_dots - delta_blk[..., None])).astype(jnp.bfloat16)
        grad_key = grad_key + jnp.einsum(
            PRODUCT_11, grad_scores, query_blk, preferred_element_type=jnp.float32
        )
        return ((grad_key, grad_value), None)

    fold_state, unused = lax.scan(key_advance, fold_state, jnp.arange(blocks, dtype=jnp.int32))
    grad_key, grad_value = fold_state
    grad_query_low = grad_query.reshape(sequences, shard_rows, local_inner).astype(jnp.bfloat16)
    grad_key_low = grad_key.reshape(sequences, key_span, local_inner).astype(jnp.bfloat16)
    grad_value_low = grad_value.reshape(sequences, key_span, local_inner).astype(jnp.bfloat16)
    grad_query_weight = jnp.einsum(
        PRODUCT_3, normed_low, grad_query_low, preferred_element_type=jnp.float32
    )
    grad_key_weight = jnp.einsum(
        PRODUCT_6, both_rows, grad_key_low, preferred_element_type=jnp.float32
    )
    grad_value_weight = jnp.einsum(
        PRODUCT_6, both_rows, grad_value_low, preferred_element_type=jnp.float32
    )
    row_part = jnp.einsum(
        PRODUCT_7, grad_key_low, full_key, preferred_element_type=jnp.float32
    ) + jnp.einsum(PRODUCT_7, grad_value_low, full_value, preferred_element_type=jnp.float32)
    token_part = row_part[:, :shard_rows] + jnp.einsum(
        PRODUCT_5, grad_query_low, full_query, preferred_element_type=jnp.float32
    )
    grad_normed, grad_memory_normed = (
        lax.psum(token_part.astype(jnp.bfloat16), TENSOR).astype(jnp.float32),
        lax.psum(row_part[:, shard_rows:].astype(jnp.bfloat16), TENSOR).astype(jnp.float32),
    )
    back_inputs, gain_tokens = norm_back(inputs_float, input_scale, attn_gain, grad_normed)
    back_memory, gain_memory = norm_back(memory_float, memory_scale, attn_gain, grad_memory_normed)
    grad_inputs = grad_residual + back_inputs
    grad_attn_gain = gain_tokens + gain_memory
    (
        shard_query,
        shard_key,
        shard_value,
        shard_output,
        shard_inner,
        shard_outer,
        shard_attn_gain,
        shard_dense_gain,
    ) = sum_grads(
        (
            grad_query_weight,
            grad_key_weight,
            grad_value_weight,
            grad_output,
            grad_inner,
            grad_outer,
            grad_attn_gain,
            grad_dense_gain,
        )
    )
    loss_sum, grad_bias_sum = lax.psum((loss_local, grad_bias), ROWS)
    return (
        loss_sum / (token_count * model_width),
        result.astype(jnp.bfloat16),
        grad_inputs,
        back_memory,
        shard_attn_gain,
        shard_query,
        shard_key,
        shard_value,
        shard_output,
        grad_bias_sum,
        shard_dense_gain,
        shard_inner,
        shard_outer,
    )


PAD = 16
BF = jnp.bfloat16
F32 = jnp.float32


def fits(mesh):
    sizes = dict(mesh.shape)
    return sizes[FSDP] == 2 and sizes[CONTEXT] == 8 and sizes[TENSOR] == 2


def swap_context(value, mask):
    return lax.ppermute(value, CONTEXT, [(i, i ^ mask) for i in range(8)])


def swap_core(pieces):
    return [swap_context(piece, 1) for piece in pieces]


def swap_fsdp(value):
    return lax.ppermute(value, FSDP, [(0, 1), (1, 0)])


def swap_tensor(value):
    return lax.ppermute(value, TENSOR, [(0, 1), (1, 0)])


def dot_nn(left, right):
    return lax.dot_general(left, right, (((1,), (0,)), ((), ())), preferred_element_type=F32)


def dot_nt(left, right):
    return lax.dot_general(left, right, (((1,), (1,)), ((), ())), preferred_element_type=F32)


def dot_tn(left, right):
    return lax.dot_general(left, right, (((0,), (0,)), ((), ())), preferred_element_type=F32)


def padded_bytes(shape, dtype):
    size = jnp.dtype(dtype).itemsize
    rows = 8 * (4 // size)
    lead = 1
    for count in shape[:-2]:
        lead *= count
    second = shape[-2] if len(shape) > 1 else 1
    return lead * -(-second // rows) * rows * -(-shape[-1] // 128) * 128 * size


def call(kernel, outs, name, ins_hbm=0, scratch=(), waits=()):
    def run(*operands):
        count = len(operands)
        specs = [pl.BlockSpec(memory_space=pltpu.VMEM)] * (count - ins_hbm)
        specs += [pl.BlockSpec(memory_space=pltpu.HBM)] * ins_hbm
        specs += [pl.BlockSpec(memory_space=pl.ANY)] * len(waits)
        held = [(item.shape, item.dtype) for item in operands[: count - ins_hbm]] + list(outs)
        held += [(item.shape, item.dtype) for item in scratch if item.memory_space == pltpu.VMEM]
        limit = 6 * 1024 * 1024 + sum(padded_bytes(shape, dtype) for shape, dtype in held)

        placed = list(operands)
        for at in range(count - ins_hbm, count):
            placed[at] = pltpu.with_memory_space_constraint(placed[at], pltpu.HBM)

        def body(*refs):
            kernel(*refs[:count], *refs[count + len(waits) :])

        return pl.pallas_call(
            body,
            out_shape=[jax.ShapeDtypeStruct(shape, dtype) for shape, dtype in outs],
            in_specs=specs,
            out_specs=[pl.BlockSpec(memory_space=pltpu.VMEM)] * len(outs),
            scratch_shapes=list(scratch),
            compiler_params=pltpu.CompilerParams(vmem_limit_bytes=limit),
            name=name,
        )(*placed, *waits)

    return run


def gate(value, *waits):
    def body(*refs):
        del refs

    return pl.pallas_call(
        body,
        out_shape=jax.ShapeDtypeStruct(value.shape, value.dtype),
        in_specs=[pl.BlockSpec(memory_space=pl.ANY)] * (1 + len(waits)),
        out_specs=pl.BlockSpec(memory_space=pl.ANY),
        input_output_aliases={0: 0},
        compiler_params=pltpu.CompilerParams(vmem_limit_bytes=1024 * 1024),
    )(value, *waits)


def diagonal(rows):
    return lax.broadcasted_iota(jnp.int32, (rows, 128), 0) == lax.broadcasted_iota(
        jnp.int32, (rows, 128), 1
    )


def row_to_column(row, rows):
    return jnp.sum(
        jnp.where(diagonal(rows), jnp.broadcast_to(row, (rows, 128)), 0.0), axis=1, keepdims=True
    )


def bucket_onehot(block_distance, span):
    lane = lax.broadcasted_iota(jnp.int32, (BUCKETS, 2 * span), 1)
    offset = jnp.where(lane < span, lane, lane - 2 * span)
    bucket = relative_bucket(block_distance * span - offset)
    return bucket == lax.broadcasted_iota(jnp.int32, (BUCKETS, 2 * span), 0)


def pack_kernel(*refs):
    sources, (own_ref, early_ref, later_ref, over_ref, block_ref) = refs[:13], refs[13:18]
    small, tail_ref, sems = refs[18:24], refs[24], refs[25]
    x, memory, segments, owner, valid, wq, wk, wv, wo, wi, wf, gain, dense_gain = sources
    span, slots = x.shape[0], memory.shape[0]
    rows_each, inner = wq.shape
    hidden = wi.shape[1]
    base = span + PAD
    half = pl.ds(pl.multiple_of(lax.axis_index(TENSOR) * inner, 128), inner)
    targets = [
        (memory, small[0]),
        (segments, small[1]),
        (owner, small[2]),
        (valid, small[3]),
        (gain, small[4]),
        (dense_gain, small[5]),
        (x.at[:, half], own_ref.at[slice(0, span), :]),
    ]
    parts = [wq, wk, wv, wo]
    parts += [w.at[:, slice(at, at + inner)] for w in (wi, wf) for at in range(0, hidden, inner)]
    starts = [base + at * rows_each for at in range(4)]
    late = base + 4 * rows_each + PAD
    starts += [late + at * rows_each for at in range(len(parts) - 4)]
    for part, start in zip(parts, starts):
        targets.append((part, own_ref.at[slice(start, start + rows_each), :]))
    copies = [
        pltpu.make_async_copy(source, target, sems.at[i])
        for i, (source, target) in enumerate(targets)
    ]
    for copy in copies:
        copy.start()
    for copy in copies[:6]:
        copy.wait()
    memory, segments, owner, valid, gain, dense_gain = small
    tail_ref[...] = jnp.zeros_like(tail_ref)
    tail_ref[0:slots, :] = memory[...].astype(F32)
    tail_ref[slots : slots + 1, 0:span] = segments[...].astype(F32)
    tail_ref[slots : slots + 1, span : span + slots] = owner[...].astype(F32)
    own_ref[span:base, :] = tail_ref[:, half].astype(BF)
    tail_ref[...] = jnp.zeros_like(tail_ref)
    tail_ref[0:1, 0:rows_each] = gain[...].astype(F32)
    tail_ref[1:2, 0:rows_each] = dense_gain[...].astype(F32)
    tail_ref[2:3, 0:1] = jnp.sum(valid[...].astype(F32), axis=1, keepdims=True)
    own_ref[late - PAD : late, :] = tail_ref[:, 0:inner].astype(BF)
    for copy in copies[6:]:
        copy.wait()
    early_ref[...] = own_ref[0:late, :]
    later_ref[...] = own_ref[late:, :]
    over_ref[...] = own_ref[base:, :]
    block_ref[...] = own_ref[0:base, :]


def split_kernel(two_ref, one_ref, first_ref, block_ref, later_ref):
    rows, first_rows = block_ref.shape[0] // 2, first_ref.shape[0] // 2
    for at, source in enumerate((two_ref, one_ref)):
        block_ref[at * rows : (at + 1) * rows, :] = source[0:rows, :]
        first_ref[at * first_rows : (at + 1) * first_rows, :] = source[rows : rows + first_rows, :]
    later_ref[...] = one_ref[rows + first_rows :, :]


def join_kernel(*refs, block_rows, first_rows):
    near, overs, blocks = refs[0:4], refs[4:6], refs[6:8]
    first_ref, block_ref, joined_ref = refs[8:]
    early_rows = block_rows + first_rows
    block_ref[...] = near[3][0:block_rows, :]
    first_ref[...] = near[3][block_rows:early_rows, :]
    at = 0
    for source, rows in [(piece, early_rows) for piece in near] + [
        (overs[0], first_rows),
        (overs[1], 2 * first_rows),
        (blocks[0], block_rows),
        (blocks[1], 2 * block_rows),
    ]:
        joined_ref[at : at + rows, :] = source[0:rows, :]
        at += rows
    rows = near[0].shape[0] - early_rows
    for source, start in ((near[0], early_rows), (near[1], early_rows), (overs[0], first_rows)):
        joined_ref[at : at + rows, :] = source[start : start + rows, :]
        at += rows


def order_kernel(*refs, rows_each):
    group = lax.axis_index(FSDP) * 8 + lax.axis_index(CONTEXT)
    target = refs[12]
    width = refs[0].shape[1]
    rows = target.shape[1] // width * rows_each
    for p in range(16):
        start = pl.ds(pl.multiple_of((group ^ p) * rows_each, 16), rows_each)
        at = (p >> 1 & 1) + 2 * (p >> 2 & 1) + 4 * (p >> 3)
        source = refs[(0, 0, 1, 2, 0, 3, 4, 5)[at] + 6 * (p & 1)]
        base = source.shape[0] - 3 * rows
        row = (base, base + rows, 0, 0, base + 2 * rows, 0, 0, 0)[at]
        for col in range(target.shape[1] // width):
            lines = slice(row + col * rows_each, row + (col + 1) * rows_each)
            target[start, col * width : (col + 1) * width] = source[lines, :]


def weights_kernel(*refs, rows_each, inner, block_rows):
    w_ref, gains_ref = refs[4:]
    group = lax.axis_index(FSDP) * 8 + lax.axis_index(CONTEXT)
    rows = 4 * rows_each + PAD
    gathered = jnp.zeros((8, gains_ref.shape[1]), F32)
    for p in range(16):
        piece = (p >> 1 & 1) + 2 * (p >> 2 & 1) + 4 * (p >> 3)
        source = refs[2 * (p & 1) + (piece == 7)]
        early = block_rows + rows
        at = piece * early + block_rows
        if piece >= 4:
            at = (4 * early, 4 * early + 2 * rows, 4 * early + rows, 0)[piece - 4]
        start = pl.multiple_of((group ^ p) * rows_each, 16)
        for which in range(4):
            w_ref[pl.ds(start, rows_each), which * inner : (which + 1) * inner] = source[
                at + which * rows_each : at + (which + 1) * rows_each, :
            ]
        lines = source[at + 4 * rows_each : at + rows, :].astype(F32)[0:8, :]
        lines = jnp.concatenate([lines, jnp.zeros_like(lines)], axis=1)
        gathered = gathered + pltpu.roll(lines, (group ^ p) * rows_each, 1)
    row_ids = lax.broadcasted_iota(jnp.int32, gathered.shape, 0)
    count = jnp.sum(gathered[2:3, :])
    gains_ref[...] = jnp.where(row_ids == 2, count, gathered)


def bias_kernel(bias_ref, toep_ref, *, span):
    for e in range(5):
        table = dot_nn(bias_ref[...], jnp.where(bucket_onehot(e - 2, span), 1.0, 0.0).astype(BF))
        for h in range(bias_ref.shape[0]):
            line = jnp.broadcast_to(table[h : h + 1, :], (span, 2 * span))
            if abs(e - 2) < 2:
                line = pltpu.roll(line, 0, 1, stride=1, stride_axis=0)
            toep_ref[h, e] = line[:, :span]


def project_kernel(*refs, span, slots, tokens, inner, first_rows):
    w_ref, gains_ref = refs[0:2]
    block_refs = refs[2:6]
    (normed_ref, kv_ref, q_ref, mask_ref, whole_ref) = refs[6:]
    block_rows = span + PAD
    early_rows = block_rows + first_rows
    side = lax.axis_index(TENSOR)
    place = lax.axis_index(CONTEXT)
    gain = gains_ref[0:1, :]
    own_docs = None
    for p in range(8):
        block = place ^ p
        piece = (p >> 1 & 1) + 2 * (p >> 2 & 1)
        for far in range(2):
            source = block_refs[2 * (p & 1) + (far and piece == 3)]
            at = piece * early_rows
            if far:
                base = 4 * early_rows + 3 * first_rows
                at = (base, base + 2 * block_rows, base + block_rows, 0)[piece]
            cols = pl.ds(pl.multiple_of((side ^ far) * inner, 128), inner)
            whole_ref[:, cols] = source[at : at + span + PAD, :].astype(F32)
        token_at = pl.multiple_of(block * span, span)
        slot_at = pl.multiple_of(tokens + block * PAD, PAD)
        values = whole_ref[0:span, :]
        scale = lax.rsqrt(jnp.mean(values * values, axis=-1, keepdims=True) + norm_eps)
        normed_ref[pl.ds(token_at, span), :] = (values * scale * gain).astype(BF)
        tail = whole_ref[span : span + PAD, :]
        docs = tail[slots : slots + 1, 0 : 2 * span]
        tail_rows = lax.broadcasted_iota(jnp.int32, tail.shape, 0)
        tail = jnp.where(tail_rows < slots, tail, 0.0)
        scale = lax.rsqrt(jnp.mean(tail * tail, axis=-1, keepdims=True) + norm_eps)
        normed_ref[pl.ds(slot_at, PAD), :] = (tail * scale * gain).astype(BF)
        if p == 0:
            own_docs = docs[:, 0:span]
        token_docs = row_to_column(docs[:, 0:span], span)
        mask_ref[pl.ds(token_at, span), :] = jnp.where(token_docs == own_docs, 0.0, score_floor)
        slot_docs = row_to_column(docs[:, span : 2 * span], PAD)
        slot_rows = lax.broadcasted_iota(jnp.int32, (PAD, 1), 0)
        slot_docs = jnp.where(slot_rows < slots, slot_docs, -1.0)
        mask_ref[pl.ds(slot_at, PAD), :] = jnp.where(slot_docs == own_docs, 0.0, score_floor)
    kv_ref[...] = dot_nn(normed_ref[...], w_ref[:, inner : 3 * inner]).astype(BF)
    own_at = pl.multiple_of(place * span, span)
    q_ref[...] = dot_nn(normed_ref[pl.ds(own_at, span), :], w_ref[:, :inner]).astype(BF)


def attend_kernel(
    w_ref,
    toep_ref,
    kv_ref,
    q_ref,
    mask_ref,
    p_ref,
    low_ref,
    wide_ref,
    part_ref,
    score_ref,
    *,
    span,
    tokens,
    inner,
):
    place = lax.axis_index(CONTEXT)
    lane = lax.broadcasted_iota(jnp.int32, (span, span), 1)
    sub = lax.broadcasted_iota(jnp.int32, (span, span), 0)
    count_blocks = tokens // span
    slot_rows_all = score_ref.shape[0] - tokens
    for t in range(inner // span):
        keys = kv_ref[:, t * span : (t + 1) * span]
        values = kv_ref[:, inner + t * span : inner + (t + 1) * span]
        pair = q_ref[:, t * span : (t + 1) * span]
        zero = jnp.zeros_like(pair)
        both = jnp.concatenate(
            [jnp.where(lane < span // 2, pair, zero), jnp.where(lane < span // 2, zero, pair)], axis=0
        )
        score_ref[...] = dot_nt(keys, both)
        best = jnp.full((1, 2 * span), score_floor, F32)
        for s in range(count_blocks):
            e = jnp.clip(s - place, -2, 2) + 2
            at = slice(s * span, (s + 1) * span)
            terms = jnp.concatenate([toep_ref[2 * t, e], toep_ref[2 * t + 1, e]], axis=1)
            mask = mask_ref[at, :]
            block = score_ref[at, :] + terms + jnp.concatenate([mask, mask], axis=1)
            score_ref[at, :] = block
            best = jnp.maximum(best, jnp.max(block, axis=0, keepdims=True))
        at = slice(tokens, tokens + slot_rows_all)
        mask = mask_ref[at, :]
        block = score_ref[at, :] + jnp.concatenate([mask, mask], axis=1)
        score_ref[at, :] = block
        best = jnp.maximum(best, jnp.max(block, axis=0, keepdims=True))
        total = jnp.zeros((1, 2 * span), F32)
        for s in range(score_ref.shape[0] // span):
            at = slice(s * span, (s + 1) * span)
            weights = jnp.exp(score_ref[at, :] - best)
            score_ref[at, :] = weights
            total = total + jnp.sum(weights, axis=0, keepdims=True)
        inverse = 1.0 / total
        for s in range(score_ref.shape[0] // span):
            at = slice(s * span, (s + 1) * span)
            p_ref[t, at, :] = (score_ref[at, :] * inverse).astype(BF)
        out = dot_tn(values, p_ref[t])
        out = jnp.where(sub < span // 2, out[:, :span], out[:, span:])
        wide_ref[t * span : (t + 1) * span, :] = out
        low_ref[:, t * span : (t + 1) * span] = jnp.transpose(out).astype(BF)
    part_ref[...] = dot_nt(low_ref[...], w_ref[:, 3 * inner :]).astype(BF)


def forward_kernel(
    x_ref,
    own_ref,
    far_ref,
    gains_ref,
    weights_ref,
    residual_ref,
    dense_ref,
    hidden_ref,
    slope_ref,
    part_ref,
):
    hidden = hidden_ref.shape[1]
    residual = x_ref[...].astype(F32) + (own_ref[...].astype(F32) + far_ref[...].astype(F32))
    residual_ref[...] = residual
    scale = lax.rsqrt(jnp.mean(residual * residual, axis=-1, keepdims=True) + norm_eps)
    dense_ref[...] = (residual * scale * gains_ref[1:2, :]).astype(BF)
    step = 256
    for at in range(0, hidden, step):
        pre = dot_nn(dense_ref[...], weights_ref[:, at : at + step])
        square = pre * pre
        root = 0.7978845608028654
        tanh = jnp.tanh(root * (pre + 0.044715 * pre * square))
        hidden_ref[:, at : at + step] = (0.5 * pre * (1.0 + tanh)).astype(BF)
        slope_ref[:, at : at + step] = 0.5 * (1.0 + tanh) + 0.5 * pre * (1.0 - tanh * tanh) * (
            root * (1.0 + 3.0 * 0.044715 * square)
        )
    part_ref[...] = dot_nt(hidden_ref[...], weights_ref[:, hidden:]).astype(BF)


def backward_kernel(
    residual_ref,
    own_ref,
    far_ref,
    teacher_ref,
    valid_ref,
    gains_ref,
    slope_ref,
    weights_ref,
    out_ref,
    grad_ref,
    part_ref,
    loss_ref,
    back_ref,
    pre_ref,
    *,
    total_rows,
):
    hidden = pre_ref.shape[1]
    result = residual_ref[...] + (own_ref[...].astype(F32) + far_ref[...].astype(F32))
    out_ref[...] = result.astype(BF)
    rows = result.shape[0]
    valid = row_to_column(valid_ref[...].astype(F32), rows)
    misfit = result - teacher_ref[...].astype(F32)
    loss = 0.5 * jnp.sum(valid * misfit * misfit)
    loss_ref[...] = jnp.full(loss_ref.shape, loss, F32)
    factor = total_rows / gains_ref[2:3, 0:1]
    grad = factor * valid * misfit
    grad_ref[...] = grad
    back_ref[...] = grad.astype(BF)
    step = 256
    for at in range(0, hidden, step):
        grad_hidden = dot_nn(back_ref[...], weights_ref[:, hidden + at : hidden + at + step])
        pre_ref[:, at : at + step] = (grad_hidden * slope_ref[:, at : at + step]).astype(BF)
    part_ref[...] = dot_nt(pre_ref[...], weights_ref[:, :hidden]).astype(BF)


def split_rows(value, target_ref, rows_each):
    place = lax.axis_index(CONTEXT)
    mine = lax.rem(place, 2)
    half = value.shape[0] // 2
    source = target_ref.at[0]
    source[...] = value
    ordered = target_ref.at[1]
    for g in range(8):
        keep = pl.multiple_of((2 * g + mine) * rows_each, 16)
        send = pl.multiple_of((2 * g + 1 - mine) * rows_each, 16)
        ordered[g * rows_each : (g + 1) * rows_each, :] = source[pl.ds(keep, rows_each), :]
        ordered[half + g * rows_each : half + (g + 1) * rows_each, :] = source[
            pl.ds(send, rows_each), :
        ]


def put_rows(product, start, keep_ref, send_refs):
    rows_each = keep_ref.shape[1]
    cols = slice(start, start + product.shape[1])
    low = product.astype(BF)
    for g in range(8):
        keep_ref[g, :, cols] = low[g * rows_each : (g + 1) * rows_each, :]
        send_ref = send_refs[g * len(send_refs) // 8]
        send_ref[g % send_ref.shape[0], :, cols] = low[(8 + g) * rows_each : (9 + g) * rows_each, :]


def dense_grad_kernel(
    left_ref,
    left_far_ref,
    right_ref,
    right_far_ref,
    next_ref,
    send_ref,
    turned_ref,
    lines_ref,
    *,
    pick,
    rows_each,
):
    mine = lax.rem(lax.axis_index(CONTEXT), 2)
    tokens = left_ref.shape[0]
    for at, source in enumerate((left_ref, left_far_ref)):
        turned = jnp.transpose(source[...].astype(F32)).astype(BF)
        turned_ref[:, at * tokens : (at + 1) * tokens] = turned
    for which in range(2):
        for g in range(4):
            row = pl.multiple_of((2 * pick(which, g) + mine) * rows_each, 16)
            start = (4 * which + g) * rows_each
            lines_ref[start : start + rows_each, :] = turned_ref[pl.ds(row, rows_each), :]
    for at in range(0, right_ref.shape[1], 512):
        cols = slice(at, at + 512)
        right = jnp.concatenate([right_ref[:, cols], right_far_ref[:, cols]], axis=0)
        product = dot_nn(lines_ref[...], right).astype(BF)
        for which, target in enumerate((next_ref, send_ref)):
            for g in range(4):
                start = (4 * which + g) * rows_each
                target[g, :, cols] = product[start : start + rows_each, :]


def attention_back_kernel(
    own_ref,
    far_ref,
    grad_ref,
    residual_ref,
    gains_ref,
    wide_ref,
    p_ref,
    kv_ref,
    q_ref,
    w_ref,
    residual_grad_ref,
    back_ref,
    dq_ref,
    dkv_ref,
    gain_ref,
    small_ref,
    ds_ref,
    diag_ref,
    *,
    inner,
    span,
    tokens,
):
    place = lax.axis_index(CONTEXT)
    incoming = own_ref[...].astype(F32) + far_ref[...].astype(F32)
    residual = residual_ref[...]
    scale = lax.rsqrt(jnp.mean(residual * residual, axis=-1, keepdims=True) + norm_eps)
    scaled = incoming * gains_ref[1:2, :]
    mean = jnp.mean(scaled * residual, axis=-1, keepdims=True)
    residual_grad = grad_ref[...] + (scale * scaled - residual * (scale * scale * scale * mean))
    residual_grad_ref[...] = residual_grad
    gain_ref[...] = jnp.broadcast_to(
        jnp.sum(incoming * residual * scale, axis=0, keepdims=True), gain_ref.shape
    )
    grads = dot_nn(residual_grad.astype(BF), w_ref[:, 3 * inner :])
    back_ref[...] = residual_grad.astype(BF)
    lane = lax.broadcasted_iota(jnp.int32, (span, span), 1)
    sub = lax.broadcasted_iota(jnp.int32, (span, span), 0)
    keys_all = p_ref.shape[1]
    blocks = tokens // span
    small_ref[...] = jnp.zeros_like(small_ref)
    tables = [bucket_onehot(d, span).astype(F32) for d in (-1, 0, 1)]
    zero = jnp.zeros((span, span), BF)
    for t in range(inner // span):
        cols = slice(t * span, (t + 1) * span)
        keys = kv_ref[:, cols]
        values = kv_ref[:, inner + t * span : inner + (t + 1) * span]
        pair = grads[:, cols].astype(BF)
        pair_back = jnp.transpose(pair.astype(F32)) * wide_ref[cols, :]
        delta = jnp.concatenate(
            [
                jnp.sum(pair_back[: span // 2], axis=0, keepdims=True),
                jnp.sum(pair_back[span // 2 :], axis=0, keepdims=True),
            ],
            axis=1,
        )
        grad_both = jnp.concatenate(
            [jnp.where(lane < span // 2, pair, zero), jnp.where(lane < span // 2, zero, pair)], axis=0
        )
        query = q_ref[:, cols]
        query_both = jnp.concatenate(
            [jnp.where(lane < span // 2, query, zero), jnp.where(lane < span // 2, zero, query)],
            axis=0,
        )
        low_sum = jnp.zeros((1, 2 * span), F32)
        high_sum = jnp.zeros((1, 2 * span), F32)
        for s in range(keys_all // span):
            at = slice(s * span, (s + 1) * span)
            dots = dot_nt(values[at, :], grad_both)
            ds = (p_ref[t, at, :].astype(F32) * (dots - delta)).astype(BF)
            ds_ref[at, :] = ds
            if s < blocks:
                line = jnp.sum(ds.astype(F32), axis=0, keepdims=True)
                low_sum = low_sum + jnp.where(s < place - 1, line, 0.0)
                high_sum = high_sum + jnp.where(s > place + 1, line, 0.0)
        dkv_ref[:, cols] = dot_nn(ds_ref[...], query_both).astype(BF)
        dkv_ref[:, inner + t * span : inner + (t + 1) * span] = dot_nn(p_ref[t], grad_both).astype(
            BF
        )
        dq = dot_tn(keys, ds_ref[...])
        dq = jnp.where(sub < span // 2, dq[:, :span], dq[:, span:])
        dq_ref[:, cols] = jnp.transpose(dq).astype(BF)
        for head in range(2):
            for which in range(3):
                s = place + which - 1
                inside = (s >= 0) & (s < blocks)
                start = pl.multiple_of(jnp.clip(s, 0, blocks - 1) * span, span)
                block = ds_ref[pl.ds(start, span), head * span : (head + 1) * span].astype(F32)
                block = jnp.where(inside, block, 0.0)
                block = jnp.concatenate([block, jnp.zeros((span, span), F32)], axis=1)
                size = span
                while size > 8:
                    size = size // 2
                    block = block[:size] + pltpu.roll(block[size:], 2 * span - size, 1)
                line = block[0:1]
                for j in range(1, 8):
                    line = line + pltpu.roll(block, 2 * span - j, 1)[j : j + 1]
                diag_ref[which, 2 * t + head : 2 * t + head + 1, :] = line
            bucket = lax.broadcasted_iota(jnp.int32, (1, 128), 1)
            part = slice(head * span, (head + 1) * span)
            low_total = jnp.sum(low_sum[:, part], axis=1, keepdims=True)
            high_total = jnp.sum(high_sum[:, part], axis=1, keepdims=True)
            small_ref[2 * t + head : 2 * t + head + 1, :] = jnp.where(
                bucket == BUCKETS // 2 - 1, low_total, 0.0
            ) + jnp.where(bucket == BUCKETS - 1, high_total, 0.0)
    heads = inner * 2 // span
    for which in range(3):
        line = lax.dot_general(
            diag_ref[which],
            tables[which],
            (((1,), (1,)), ((), ())),
            preferred_element_type=F32,
            precision=lax.Precision.HIGHEST,
        )
        small_ref[0:heads, 0:BUCKETS] += line[0:heads, :]


def rows_grad_kernel(
    dq_ref,
    dkv_ref,
    w_ref,
    normed_ref,
    gains_ref,
    dense_gain_ref,
    small_ref,
    loss_ref,
    keep_ref,
    *refs,
    inner,
    span,
    tokens,
    slots,
    heads,
):
    send_refs, (part_ref, line_ref) = refs[:-2], refs[-2:]
    place = lax.axis_index(CONTEXT)
    mine = lax.rem(place, 2)
    side = lax.axis_index(TENSOR)
    part_ref[...] = dot_nt(dkv_ref[...], w_ref[:, inner : 3 * inner])
    own_at = pl.multiple_of(place * span, span)
    part_ref[pl.ds(own_at, span), :] += dot_nt(dq_ref[...], w_ref[:, :inner])
    total = jnp.zeros((1, part_ref.shape[1]), F32)
    for s in range(part_ref.shape[0] // span):
        at = slice(s * span, (s + 1) * span)
        total = total + jnp.sum(
            part_ref[at, :] * normed_ref[at, :].astype(F32), axis=0, keepdims=True
        )
    line_ref[...] = jnp.zeros_like(line_ref)
    line_ref[slots : slots + 1, :] = total / gains_ref[0:1, :]
    line_ref[slots + 1 : slots + 2, :] = 0.5 * dense_gain_ref[0:1, :]
    for h in range(heads):
        start = pl.multiple_of(side * 128, 128)
        line_ref[slots + 2 + h : slots + 3 + h, pl.ds(start, 128)] = small_ref[h : h + 1, :]
    line_ref[slots + 2 : slots + 3, 256:384] = 0.5 * loss_ref[0:1, :]
    keep_rows = lax.broadcasted_iota(jnp.int32, line_ref.shape, 0) < slots
    for g in range(4):
        for target, block in (
            (keep_ref.at[g], 2 * g + mine),
            (send_refs[g // 2].at[g % 2], 2 * g + 1 - mine),
        ):
            token_at = pl.multiple_of(block * span, span)
            slot_at = pl.multiple_of(tokens + block * PAD, PAD)
            target[0:span, :] = part_ref[pl.ds(token_at, span), :].astype(BF)
            tail = jnp.where(keep_rows, part_ref[pl.ds(slot_at, PAD), :], line_ref[...])
            target[span : span + PAD, :] = tail.astype(BF)


def weight_grad_kernel(
    dq_ref,
    dkv_ref,
    normed_ref,
    back_ref,
    low_ref,
    keep_ref,
    *refs,
    inner,
    span,
    rows_each,
):
    send_refs, (wide_ref, line_ref) = refs[:-2], refs[-2:]
    place = lax.axis_index(CONTEXT)

    def put(product, start):
        put_rows(product, start, keep_ref, send_refs)

    split_rows(jnp.transpose(back_ref[...].astype(F32)).astype(BF), line_ref, rows_each)
    put(dot_nn(line_ref[1], low_ref[...]), 3 * inner)
    own_at = pl.multiple_of(place * span, span)
    own = normed_ref[pl.ds(own_at, span), :].astype(F32)
    split_rows(jnp.transpose(own).astype(BF), line_ref, rows_each)
    put(dot_nn(line_ref[1], dq_ref[...]), 0)
    split_rows(jnp.transpose(normed_ref[...].astype(F32)).astype(BF), wide_ref, rows_each)
    for at in range(0, 2 * inner, 256):
        put(dot_nn(wide_ref[1], dkv_ref[:, at : at + 256]), inner + at)


def halve_kernel(*refs, counts):
    targets = refs[-2:]
    mine = lax.axis_index(FSDP)
    sources, at = [], 0
    for count in counts:
        sources.append((refs[at], refs[at + 1 : at + 1 + count]))
        at += 1 + count
    for flip in range(2):

        @pl.when(mine == flip)
        def _():
            start = 0
            for keep_ref, far_refs in sources:
                width = keep_ref.shape[2]
                for g in range(8):
                    far = far_refs[g * len(far_refs) // 8][g % far_refs[0].shape[0]]
                    sums = keep_ref[g].astype(F32) + far.astype(F32)
                    targets[(g // 4) ^ flip][g % 4, :, start : start + width] = sums.astype(BF)
                start += width


def turn_kernel(keep_ref, far_ref, next_ref, send_ref, *, pick):
    for which, target in enumerate((next_ref, send_ref)):
        for g in range(max(1, keep_ref.shape[0] // 2)):
            block = pick(which, g)
            sums = keep_ref[block].astype(F32) + far_ref[block].astype(F32)
            if len(target.shape) == 2:
                target[...] = sums.astype(target.dtype)
            else:
                target[g] = sums.astype(target.dtype)


def pick_z1(which, g):
    return (g // 2) * 4 + (lax.axis_index(CONTEXT) // 2 ^ (which + 2 * (g % 2)))


def pick_half(which, g):
    return 4 * (lax.axis_index(FSDP) ^ which) + g


def pick_z2(which, g):
    return 2 * g + which


def pick_x(which, g):
    return lax.axis_index(FSDP) ^ which


def quarter_kernel(keep_ref, far_ref, next_ref, send_ref):
    place = lax.axis_index(CONTEXT) // 2
    for target, flip in ((next_ref, 0), (send_ref, 1)):
        for g in range(2):
            block = place ^ (flip + 2 * g)
            total = keep_ref[block].astype(F32) + far_ref[block].astype(F32)
            target[g] = total.astype(BF)


def eighth_kernel(keep_ref, far_ref, own_ref, send_ref):
    own_ref[...] = (keep_ref[0].astype(F32) + far_ref[0].astype(F32)).astype(own_ref.dtype)
    send_ref[...] = (keep_ref[1].astype(F32) + far_ref[1].astype(F32)).astype(BF)


def total_kernel(own_ref, far_ref, token_ref, *out_refs):
    token_ref[...] = jnp.zeros_like(token_ref)
    at = 0
    for out in out_refs:
        cols = slice(at, at + out.shape[1])
        out[...] = (own_ref[:, cols].astype(F32) + far_ref[:, cols].astype(F32)).astype(out.dtype)
        at += out.shape[1]


def columns_kernel(keep_ref, one_ref, two_ref, next_ref, send_ref):
    mine = lax.axis_index(TENSOR)
    width = next_ref.shape[2]
    for target, start in ((next_ref, mine * width), (send_ref, (1 - mine) * width)):
        cols = pl.ds(pl.multiple_of(start, 128), width)
        for half, far_ref in ((slice(0, 2), one_ref), (slice(2, 4), two_ref)):
            total = keep_ref[half, :, cols].astype(F32) + far_ref[:, :, cols].astype(F32)
            target[half] = total.astype(BF)


def tail_kernel(own_ref, far_ref, out_ref, *, span):
    mine = lax.axis_index(TENSOR)
    width = own_ref.shape[1]
    rows = slice(span, span + PAD)
    out_ref[:, pl.ds(pl.multiple_of(mine * width, 128), width)] = own_ref[rows, :].astype(F32)
    out_ref[:, pl.ds(pl.multiple_of((1 - mine) * width, 128), width)] = far_ref[rows, :].astype(F32)


def finish_kernel(
    own_ref,
    far_ref,
    x_ref,
    slots_ref,
    gains_ref,
    residual_grad_ref,
    tail_far_ref,
    inputs_ref,
    memory_ref,
    gain_ref,
    dense_gain_ref,
    bias_ref,
    loss_ref,
    full_ref,
    line_ref,
    *,
    span,
    slots,
):
    mine = lax.axis_index(TENSOR)
    group = lax.axis_index(FSDP) * 8 + lax.axis_index(CONTEXT)
    width = own_ref.shape[1]
    full_ref[:, pl.ds(pl.multiple_of(mine * width, 128), width)] = own_ref[...].astype(F32)
    full_ref[:, pl.ds(pl.multiple_of((1 - mine) * width, 128), width)] = far_ref[...].astype(F32)
    for source, target, start, extra in (
        (x_ref, inputs_ref, 0, residual_grad_ref),
        (slots_ref, memory_ref, span, None),
    ):
        values = source[...].astype(F32)
        scale = lax.rsqrt(jnp.mean(values * values, axis=-1, keepdims=True) + norm_eps)
        scaled = full_ref[start : start + values.shape[0], :] * gains_ref[0:1, :]
        mean = jnp.mean(scaled * values, axis=-1, keepdims=True)
        back = scale * scaled - values * (scale * scale * scale * mean)
        if extra is None:
            target[:, 0, :] = back
        else:
            target[...] = extra[...] + back
    line_ref[...] = full_ref[span : span + PAD, :] + tail_far_ref[...]
    lines = pltpu.roll(line_ref[...], full_ref.shape[1] - group * gain_ref.shape[1], 1)
    rows_each = gain_ref.shape[1]
    gain_ref[...] = lines[slots : slots + 1, 0:rows_each]
    dense_gain_ref[...] = lines[slots + 1 : slots + 2, 0:rows_each]
    heads = bias_ref.shape[0]
    start = pl.multiple_of(mine * 128, 128)
    bias_ref[...] = line_ref[slots + 2 : slots + 2 + heads, pl.ds(start, 128)][:, 0:BUCKETS]
    loss_ref[...] = line_ref[slots + 2 : slots + 3, 256:384] / (
        gains_ref[2:3, 0:128] * full_ref.shape[1]
    )


def fast_local(
    inputs,
    memory,
    teacher,
    segments,
    memory_owner,
    valid_mask,
    attention_gain,
    query_weight,
    key_weight,
    value_weight,
    attention_out_weight,
    position_bias,
    feedforward_gain,
    inner_weight,
    feedforward_out_weight,
):
    span, width = inputs.shape[1:]
    slots = memory.shape[1]
    rows_each, inner = query_weight.shape
    hidden = inner_weight.shape[1]
    heads = position_bias.shape[0]
    tokens = 8 * span
    keys_all = 8 * (span + PAD)
    total_rows = 2 * tokens
    x = inputs[0]
    block_rows = span + PAD
    first_rows = 4 * rows_each + PAD
    early_rows = block_rows + first_rows
    later_rows = 2 * hidden // inner * rows_each
    own, early, later, over, block = call(
        pack_kernel,
        [
            ((early_rows + later_rows, inner), BF),
            ((early_rows, inner), BF),
            ((later_rows, inner), BF),
            ((first_rows + later_rows, inner), BF),
            ((block_rows, inner), BF),
        ],
        name="pack",
        ins_hbm=13,
        scratch=(
            pltpu.VMEM((slots, width), BF),
            pltpu.VMEM((1, span), jnp.int32),
            pltpu.VMEM((1, slots), jnp.int32),
            pltpu.VMEM((1, span), jnp.int32),
            pltpu.VMEM((1, rows_each), BF),
            pltpu.VMEM((1, rows_each), BF),
            pltpu.VMEM((PAD, width), F32),
            pltpu.SemaphoreType.DMA((7 + 4 + 2 * hidden // inner,)),
        ),
    )(
        x,
        memory[0],
        segments,
        memory_owner,
        valid_mask,
        query_weight,
        key_weight,
        value_weight,
        attention_out_weight,
        inner_weight,
        feedforward_out_weight,
        attention_gain[None],
        feedforward_gain[None],
    )

    (toeplitz,) = call(
        lambda *refs: bias_kernel(*refs, span=span),
        [((heads, 5, span, span), F32)],
        name="bias",
        waits=(early,),
    )(position_bias)
    two = swap_context(early, 4)
    one = swap_context(own, 2)
    over_own = swap_fsdp(over)
    block_own = swap_tensor(block)
    first_pair, block_pair, later_one = call(
        split_kernel,
        [
            ((2 * first_rows, inner), BF),
            ((2 * block_rows, inner), BF),
            ((later_rows, inner), BF),
        ],
        name="split",
        waits=(over_own, block_own, toeplitz),
    )(two, one)
    three = swap_context(two, 2)
    over_pair = swap_fsdp(first_pair)
    block_pair = swap_tensor(block_pair)
    later_two = swap_context(gate(later, first_pair), 4)
    over_one = swap_fsdp(later_one)
    first_last, block_last, joined = call(
        lambda *refs: join_kernel(*refs, block_rows=block_rows, first_rows=first_rows),
        [
            ((first_rows, inner), BF),
            ((block_rows, inner), BF),
            ((4 * early_rows + 3 * (first_rows + block_rows + later_rows), inner), BF),
        ],
        name="join",
        waits=(later_two, over_one),
    )(own, one, two, three, over_own, over_pair, block_own, block_pair)
    over_last = swap_fsdp(first_last)
    block_last = swap_tensor(block_last)
    later_three = swap_context(later_two, 2)
    over_two = swap_fsdp(later_two)
    joined_core, over_core, block_core = swap_core([joined, over_last, block_last])
    w_all, gains = call(
        lambda *refs: weights_kernel(
            *refs, rows_each=rows_each, inner=inner, block_rows=block_rows
        ),
        [((width, 4 * inner), BF), ((8, width), F32)],
        name="weights",
    )(joined, over_last, joined_core, over_core)
    (normed, kv, queries, mask) = call(
        lambda *refs: project_kernel(
            *refs, span=span, slots=slots, tokens=tokens, inner=inner, first_rows=first_rows
        ),
        [
            ((keys_all, width), BF),
            ((keys_all, 2 * inner), BF),
            ((span, inner), BF),
            ((keys_all, span), F32),
        ],
        name="project",
        scratch=(pltpu.VMEM((span + PAD, width), F32),),
        waits=(later_three,),
    )(w_all, gains, joined, block_last, joined_core, block_core)
    (probs, low, wide, part) = call(
        lambda *refs: attend_kernel(*refs, span=span, tokens=tokens, inner=inner),
        [
            ((inner // span, keys_all, 2 * span), BF),
            ((span, inner), BF),
            ((inner, span), F32),
            ((span, width), BF),
        ],
        name="attend",
        scratch=(pltpu.VMEM((keys_all, 2 * span), F32),),
        waits=(over_two,),
    )(w_all, toeplitz, kv, queries, mask)
    far = swap_tensor(part)
    over_three = gate(swap_fsdp(later_three), far)
    later_all = [later_two, later_three, over_one, over_two]
    later_all = [gate(piece, part) for piece in later_all] + [over_three]
    (dense_weights,) = call(
        lambda *refs: order_kernel(*refs, rows_each=rows_each),
        [((width, 2 * hidden), BF)],
        name="order",
        waits=(part,),
    )(joined, *later_all, joined_core, *swap_core(later_all))
    (residual, dense_low, hidden_low, slope, dense_part) = call(
        forward_kernel,
        [
            ((span, width), F32),
            ((span, width), BF),
            ((span, hidden), BF),
            ((span, hidden), F32),
            ((span, width), BF),
        ],
        name="forward",
    )(x, part, far, gains, dense_weights)
    dense_far = swap_tensor(dense_part)
    hidden_far, dense_low_far = swap_core([hidden_low, dense_low])
    (output, grad_result, grad_part, loss_part, dense_back, grad_pre) = call(
        lambda *refs: backward_kernel(*refs, total_rows=total_rows),
        [
            ((span, width), BF),
            ((span, width), F32),
            ((span, width), BF),
            ((8, 128), F32),
            ((span, width), BF),
            ((span, hidden), BF),
        ],
        name="backward",
        waits=(hidden_far, dense_low_far),
    )(residual, dense_part, dense_far, teacher[0], valid_mask, gains, slope, dense_weights)
    grad_far = swap_tensor(grad_part)

    def halve(sources, *waits):
        columns = sum(keep.shape[2] for keep, _ in sources)
        return call(
            lambda *refs: halve_kernel(*refs, counts=[len(far) for _, far in sources]),
            [((4, rows_each, columns), BF)] * 2,
            name="halve",
            waits=waits,
        )(*[item for keep, far in sources for item in (keep, *far)])

    def quarter(keep, far_half, *waits):
        rows, columns = keep.shape[1:]
        return call(
            quarter_kernel,
            [((2, rows, columns), BF)] * 2,
            name="quarter",
            waits=waits,
        )(keep, far_half)

    def eighth(keep, far_quarter, own_type, *waits):
        rows, columns = keep.shape[1:]
        return call(
            eighth_kernel,
            [((rows, columns), own_type), ((rows, columns), BF)],
            name="eighth",
            waits=waits,
        )(keep, far_quarter)

    def total(own, far_eighth, outs, *waits):
        outs = [((8, 128), F32), *outs]
        return call(total_kernel, outs, name="total", waits=waits)(own, far_eighth)

    def turn(keep, far_blocks, pick, outs, *waits):
        return call(
            lambda *refs: turn_kernel(*refs, pick=pick), outs, name="turn", waits=waits
        )(keep, far_blocks)

    def outer_blocks(count):
        return ((count, rows_each, hidden), BF)

    def dense_grad(left, left_far, right, right_far, pick, *waits):
        return call(
            lambda *refs: dense_grad_kernel(*refs, pick=pick, rows_each=rows_each),
            [((4, rows_each, hidden), BF)] * 2,
            name="dense_grad",
            scratch=(
                pltpu.VMEM((width, 2 * span), BF),
                pltpu.VMEM((8 * rows_each, 2 * span), BF),
            ),
            waits=waits,
        )(left, left_far, right, right_far)

    dense_back_far, grad_pre_far = swap_core([dense_back, grad_pre])
    outer_next, outer_over = dense_grad(
        dense_back, dense_back_far, hidden_low, hidden_far, pick_z1
    )
    outer_far = swap_context(outer_over, 2)
    inner_next, inner_over = dense_grad(
        dense_low, dense_low_far, grad_pre, grad_pre_far, pick_half, outer_over, grad_far
    )
    inner_far = swap_fsdp(inner_over)

    (grad_residual, attention_back, dq, dkv, dense_gain_rows, small) = call(
        lambda *refs: attention_back_kernel(*refs, inner=inner, span=span, tokens=tokens),
        [
            ((span, width), F32),
            ((span, width), BF),
            ((span, inner), BF),
            ((keys_all, 2 * inner), BF),
            ((8, width), F32),
            ((8, 128), F32),
        ],
        name="attend_back",
        scratch=(
            pltpu.VMEM((keys_all, 2 * span), BF),
            pltpu.VMEM((3, 8, 2 * span), F32),
        ),
        waits=(inner_over, outer_over),
    )(grad_part, grad_far, grad_result, residual, gains, wide, probs, kv, queries, w_all)

    rows_keep, *rows_send = call(
        lambda *refs: rows_grad_kernel(
            *refs, inner=inner, span=span, tokens=tokens, slots=slots, heads=heads
        ),
        [((4, span + PAD, width), BF)] + [((2, span + PAD, width), BF)] * 2,
        name="rows_grad",
        scratch=(pltpu.VMEM((keys_all, width), F32), pltpu.VMEM((PAD, width), F32)),
    )(dq, dkv, w_all, normed, gains, dense_gain_rows, small, loss_part)
    rows_far = swap_core(rows_send)

    weight_keep, *weight_send = call(
        lambda *refs: weight_grad_kernel(*refs, inner=inner, span=span, rows_each=rows_each),
        [((8, rows_each, 4 * inner), BF)] + [((4, rows_each, 4 * inner), BF)] * 2,
        name="weight_grad",
        scratch=(
            pltpu.VMEM((2, width, keys_all), BF),
            pltpu.VMEM((2, width, span), BF),
        ),
        waits=(rows_send[0],),
    )(dq, dkv, normed, attention_back, low)
    weight_far = swap_core(weight_send)
    outer_next, outer_over = turn(
        outer_next, outer_far, pick_z2, [outer_blocks(2)] * 2, weight_send[0]
    )
    outer_far = swap_context(outer_over, 4)
    inner_next, inner_over = quarter(inner_next, inner_far, outer_over)
    inner_far = swap_context(inner_over, 2)
    weight_next, weight_over = halve([(weight_keep, weight_far)], inner_over)
    weight_far = swap_fsdp(weight_over)
    rows_next, rows_over = call(
        columns_kernel,
        [((4, span + PAD, width // 2), BF)] * 2,
        name="columns",
        waits=(weight_over,),
    )(rows_keep, *rows_far)
    rows_far = swap_tensor(rows_over)

    rows_next, rows_over = quarter(rows_next, rows_far)
    rows_far = swap_context(rows_over, 2)
    inner_own, inner_over = eighth(inner_next, inner_far, F32, rows_over)
    inner_far = swap_context(inner_over, 4)
    outer_own, outer_over = turn(
        outer_next,
        outer_far,
        pick_x,
        [((rows_each, hidden), F32), ((rows_each, hidden), BF)],
        inner_over,
    )
    outer_far = swap_fsdp(outer_over)
    weight_next, weight_over = quarter(weight_next, weight_far, outer_over)
    weight_far = swap_context(weight_over, 2)

    rows_own, rows_over = eighth(rows_next, rows_far, BF, weight_over)
    rows_far = swap_context(rows_over, 4)
    token, grad_outer = total(outer_own, outer_far, [((rows_each, hidden), F32)], rows_over)
    token, grad_inner = total(inner_own, inner_far, [((rows_each, hidden), F32)], token)
    weight_own, weight_over = eighth(weight_next, weight_far, F32, token)
    weight_far = swap_context(weight_over, 4)

    token, rows_half = total(
        rows_own, rows_far, [((span + PAD, width // 2), BF)], weight_over
    )
    rows_other = swap_tensor(rows_half)
    (tail,) = call(
        lambda *refs: tail_kernel(*refs, span=span), [((PAD, width), F32)], name="tail"
    )(rows_half, rows_other)
    tail_far = swap_fsdp(tail)
    *rest, grad_output = total(weight_own, weight_far, [((rows_each, inner), F32)] * 4, tail)
    weight_grads = rest[1:]
    (grad_inputs, grad_memory, grad_gain, grad_dense_gain, grad_bias, loss) = call(
        lambda *refs: finish_kernel(*refs, span=span, slots=slots),
        [
            ((span, width), F32),
            ((slots, 1, width), F32),
            ((1, rows_each), F32),
            ((1, rows_each), F32),
            ((heads, BUCKETS), F32),
            ((1, 128), F32),
        ],
        name="finish",
        scratch=(pltpu.VMEM((span + PAD, width), F32), pltpu.VMEM((PAD, width), F32)),
    )(rows_half, rows_other, x, memory[0], gains, grad_residual, tail_far)
    return (
        loss[0, 0],
        output[None],
        grad_inputs[None],
        jnp.swapaxes(grad_memory, 0, 1),
        grad_gain[0],
        weight_grads[0],
        weight_grads[1],
        weight_grads[2],
        grad_output,
        grad_bias,
        grad_dense_gain[0],
        grad_inner,
        grad_outer,
    )


def solution(mesh):
    return jax.shard_map(
        fast_local if fits(mesh) else general_local,
        mesh=mesh,
        in_specs=(
            P(FSDP, CONTEXT, None),
            P(FSDP, CONTEXT, None),
            P(FSDP, CONTEXT, None),
            P(FSDP, CONTEXT),
            P(FSDP, CONTEXT),
            P(FSDP, CONTEXT),
            P(ROWS),
            P(ROWS, TENSOR),
            P(ROWS, TENSOR),
            P(ROWS, TENSOR),
            P(ROWS, TENSOR),
            P(TENSOR, None),
            P(ROWS),
            P(ROWS, TENSOR),
            P(ROWS, TENSOR),
        ),
        out_specs=(
            P(),
            P(FSDP, CONTEXT, None),
            P(FSDP, CONTEXT, None),
            P(FSDP, CONTEXT, None),
            P(ROWS),
            P(ROWS, TENSOR),
            P(ROWS, TENSOR),
            P(ROWS, TENSOR),
            P(ROWS, TENSOR),
            P(TENSOR, None),
            P(ROWS),
            P(ROWS, TENSOR),
            P(ROWS, TENSOR),
        ),
        check_vma=False,
    )
```

```python
import jax
import jax.numpy as jnp
from jax import lax
from jax.experimental import pallas as pl
from jax.experimental.pallas import tpu as pltpu
from jax.sharding import PartitionSpec as P

BUCKETS = 32
FSDP = "fsdp"
CONTEXT = "context"
TENSOR = "tensor"
ROWS = (FSDP, CONTEXT)
PRODUCT_0 = "scd,df->scf"
PRODUCT_1 = "scd,di->sci"
PRODUCT_2 = "scd,scf->df"
PRODUCT_3 = "scd,sci->di"
PRODUCT_4 = "scf,df->scd"
PRODUCT_5 = "sci,di->scd"
PRODUCT_6 = "sjd,sji->di"
PRODUCT_7 = "sji,di->sjd"
PRODUCT_8 = "sqhd,skhd->sqhk"
PRODUCT_9 = "sqhk,qkb->hb"
PRODUCT_10 = "sqhk,skhd->sqhd"
PRODUCT_11 = "sqhk,sqhd->skhd"


norm_eps = 1e-06
score_floor = -1e30


def relative_bucket(distance):
    half_count = BUCKETS // 2
    exact_count = half_count // 2
    magnitude = jnp.minimum(jnp.abs(distance), 1024)
    far_bucket = jnp.full(distance.shape, exact_count, jnp.int32)
    for level_index in range(1, half_count - exact_count):
        far_bucket = far_bucket + (
            magnitude * magnitude >= exact_count * exact_count * 2**level_index
        ).astype(jnp.int32)
    bucket_ids = jnp.where(magnitude < exact_count, magnitude, far_bucket)
    return bucket_ids + (distance > 0).astype(jnp.int32) * half_count


def rms_norm(values, gain_in):
    inv_rms = lax.rsqrt(jnp.mean(values * values, axis=-1, keepdims=True) + norm_eps)
    return (values * inv_rms * gain_in, inv_rms)


def norm_back(values, inv_rms, gain_in, grad_in):
    scaled = grad_in * gain_in
    inner_mean = jnp.mean(scaled * values, axis=-1, keepdims=True)
    grad_values = inv_rms * scaled - values * inv_rms * inv_rms * inv_rms * inner_mean
    grad_gain = jnp.sum(grad_in * values * inv_rms, axis=tuple(range(values.ndim - 1)))
    return (grad_values, grad_gain)


def smooth_gate(values):
    return jax.nn.gelu(values, approximate=True)


def block_size():
    return 512


def pad_rows(values_in, block_rows, fill_value):
    blocks = -(-values_in.shape[1] // block_rows)
    missing = blocks * block_rows - values_in.shape[1]
    padding = [(0, 0)] * values_in.ndim
    padding[1] = (0, missing)
    return (jnp.pad(values_in, padding, constant_values=fill_value), blocks)


def key_places(row_ids, shard_rows, key_span):
    within = row_ids % key_span
    return (row_ids // key_span * shard_rows + within, within < shard_rows)


def scores_with_bias(
    query_blk, key_blk, query_place, query_doc, key_place, key_doc, key_token, bias_table
):
    scores = jnp.einsum(PRODUCT_8, query_blk, key_blk, preferred_element_type=jnp.float32)
    bucket = relative_bucket(key_place[None, :] - query_place[:, None])
    rel_terms = jnp.where(key_token[None, None, :], jnp.take(bias_table, bucket, axis=1), 0.0)
    scores = scores + jnp.moveaxis(rel_terms, 0, 1)[None]
    same_doc = (query_doc[:, :, None] == key_doc[:, None, :])[:, :, None, :]
    return (scores, same_doc, bucket)


def sum_grads(grad_items):
    return (
        lax.psum_scatter(grad_items[0], ROWS, scatter_dimension=0, tiled=True),
        lax.psum_scatter(grad_items[1], ROWS, scatter_dimension=0, tiled=True),
        lax.psum_scatter(grad_items[2], ROWS, scatter_dimension=0, tiled=True),
        lax.psum_scatter(grad_items[3], ROWS, scatter_dimension=0, tiled=True),
        lax.psum_scatter(grad_items[4], ROWS, scatter_dimension=0, tiled=True),
        lax.psum_scatter(grad_items[5], ROWS, scatter_dimension=0, tiled=True),
        lax.psum_scatter(grad_items[6], ROWS, scatter_dimension=0, tiled=True),
        lax.psum_scatter(grad_items[7], ROWS, scatter_dimension=0, tiled=True),
    )


def general_local(
    inputs,
    memory,
    teacher,
    segments,
    memory_owner,
    valid_mask,
    attention_gain,
    query_weight,
    key_weight,
    value_weight,
    attention_out_weight,
    position_bias,
    feedforward_gain,
    inner_weight,
    feedforward_out_weight,
):
    sequences, shard_rows, model_width = inputs.shape
    key_span = shard_rows + memory.shape[1]
    context_size = lax.axis_size(CONTEXT)
    length = shard_rows * context_size
    context_place = lax.axis_index(CONTEXT)
    local_heads = position_bias.shape[0]
    bucket_count = position_bias.shape[1]
    head_size = query_weight.shape[1] // local_heads
    local_inner = local_heads * head_size
    total_rows = sequences * length * lax.axis_size(FSDP)
    bias_table = position_bias.astype(jnp.float32)
    (
        full_query,
        full_key,
        full_value,
        full_output,
        full_inner,
        full_outer,
        full_attn_gain,
        full_dense_gain,
    ) = (
        lax.all_gather(query_weight, ROWS, axis=0, tiled=True),
        lax.all_gather(key_weight, ROWS, axis=0, tiled=True),
        lax.all_gather(value_weight, ROWS, axis=0, tiled=True),
        lax.all_gather(attention_out_weight, ROWS, axis=0, tiled=True),
        lax.all_gather(inner_weight, ROWS, axis=0, tiled=True),
        lax.all_gather(feedforward_out_weight, ROWS, axis=0, tiled=True),
        lax.all_gather(attention_gain, ROWS, axis=0, tiled=True),
        lax.all_gather(feedforward_gain, ROWS, axis=0, tiled=True),
    )
    attn_gain = full_attn_gain.astype(jnp.float32)
    dense_gain = full_dense_gain.astype(jnp.float32)
    local_docs = jnp.concatenate([segments, memory_owner], axis=1)
    key_docs = lax.all_gather(local_docs, CONTEXT, axis=1, tiled=True)
    query_docs_all = key_docs.reshape(sequences, context_size, key_span)[:, :, :shard_rows].reshape(
        sequences, length
    )
    token_count = lax.psum(jnp.sum(valid_mask.astype(jnp.float32)), ROWS)
    inputs_float = inputs.astype(jnp.float32)
    memory_float = memory.astype(jnp.float32)
    normed, input_scale = rms_norm(inputs_float, attn_gain)
    memory_normed, memory_scale = rms_norm(memory_float, attn_gain)
    normed_low = normed.astype(jnp.bfloat16)
    both_rows = jnp.concatenate([normed_low, memory_normed.astype(jnp.bfloat16)], axis=1)
    queries = jnp.dot(normed_low, full_query, preferred_element_type=jnp.float32).astype(
        jnp.bfloat16
    )
    key_local = jnp.dot(both_rows, full_key, preferred_element_type=jnp.float32).astype(
        jnp.bfloat16
    )
    value_local = jnp.dot(both_rows, full_value, preferred_element_type=jnp.float32).astype(
        jnp.bfloat16
    )
    query_heads = queries.reshape(sequences, shard_rows, local_heads, head_size)
    query_place = context_place * shard_rows + jnp.arange(shard_rows, dtype=jnp.int32)
    fold_init = (
        jnp.full((sequences, shard_rows, local_heads), score_floor, jnp.float32),
        jnp.zeros((sequences, shard_rows, local_heads), jnp.float32),
        jnp.zeros((sequences, shard_rows, local_heads, head_size), jnp.float32),
    )
    fold_state = fold_init
    key_piece = lax.all_gather(key_local, CONTEXT, axis=1, tiled=True)
    value_piece = lax.all_gather(value_local, CONTEXT, axis=1, tiled=True)
    block_rows = block_size()
    key_pad, blocks = pad_rows(key_piece, block_rows, 0)
    value_pad, blocks = pad_rows(value_piece, block_rows, 0)
    doc_pad, blocks = pad_rows(key_docs, block_rows, -1)

    def attend_advance(running, block_index):
        running_best, running_sum, summed = running
        offset = block_index * block_rows
        key_blk = lax.dynamic_slice_in_dim(key_pad, offset, block_rows, 1).reshape(
            sequences, block_rows, local_heads, head_size
        )
        value_blk = lax.dynamic_slice_in_dim(value_pad, offset, block_rows, 1).reshape(
            sequences, block_rows, local_heads, head_size
        )
        doc_blk = lax.dynamic_slice_in_dim(doc_pad, offset, block_rows, 1)
        key_place, key_token = key_places(
            offset + jnp.arange(block_rows, dtype=jnp.int32), shard_rows, key_span
        )
        scores, same_doc, bucket = scores_with_bias(
            query_heads, key_blk, query_place, segments, key_place, doc_blk, key_token, bias_table
        )
        masked = jnp.where(same_doc, scores, score_floor)
        new_best = jnp.maximum(running_best, jnp.max(masked, axis=-1))
        weights = jnp.where(same_doc, jnp.exp(scores - new_best[..., None]), 0.0)
        factor = jnp.exp(running_best - new_best)
        running_sum = running_sum * factor + jnp.sum(weights, axis=-1)
        summed = summed * factor[..., None] + jnp.einsum(
            PRODUCT_10,
            weights.astype(jnp.bfloat16),
            value_blk,
            preferred_element_type=jnp.float32,
        )
        return ((new_best, running_sum, summed), None)

    fold_state, unused = lax.scan(attend_advance, fold_state, jnp.arange(blocks, dtype=jnp.int32))
    running_best, running_sum, summed = fold_state
    attended_values = summed / running_sum[..., None]
    attended_low = attended_values.reshape(sequences, shard_rows, local_inner).astype(jnp.bfloat16)
    attention_part = jnp.einsum(
        PRODUCT_5, attended_low, full_output, preferred_element_type=jnp.float32
    )
    residual = inputs_float + lax.psum(attention_part.astype(jnp.bfloat16), TENSOR).astype(
        jnp.float32
    )
    dense_normed, dense_scale = rms_norm(residual, dense_gain)
    dense_low = dense_normed.astype(jnp.bfloat16)
    inner_pre = jnp.dot(dense_low, full_inner, preferred_element_type=jnp.float32)
    hidden_float, gate_pullback = jax.vjp(smooth_gate, inner_pre)
    hidden_low = hidden_float.astype(jnp.bfloat16)
    dense_part = jnp.einsum(
        PRODUCT_4, hidden_low, full_outer, preferred_element_type=jnp.float32
    )
    result = residual + lax.psum(dense_part.astype(jnp.bfloat16), TENSOR).astype(jnp.float32)
    target_mask = valid_mask.astype(jnp.float32)[..., None]
    misfit = result - teacher.astype(jnp.float32)
    loss_local = 0.5 * jnp.sum(target_mask * misfit * misfit)
    grad_result = total_rows / token_count * target_mask * misfit
    dense_back = grad_result.astype(jnp.bfloat16)
    grad_outer = jnp.einsum(
        PRODUCT_2, dense_back, hidden_low, preferred_element_type=jnp.float32
    )
    grad_hidden = jnp.einsum(
        PRODUCT_0, dense_back, full_outer, preferred_element_type=jnp.float32
    )
    grad_pre = gate_pullback(grad_hidden)[0].astype(jnp.bfloat16)
    grad_inner = jnp.einsum(PRODUCT_2, dense_low, grad_pre, preferred_element_type=jnp.float32)
    grad_dense_part = jnp.einsum(
        PRODUCT_4, grad_pre, full_inner, preferred_element_type=jnp.float32
    )
    grad_dense_normed = lax.psum(grad_dense_part.astype(jnp.bfloat16), TENSOR).astype(jnp.float32)
    back_residual, grad_dense_gain = norm_back(residual, dense_scale, dense_gain, grad_dense_normed)
    grad_residual = grad_result + back_residual
    attention_back = grad_residual.astype(jnp.bfloat16)
    grad_output = jnp.einsum(
        PRODUCT_3, attention_back, attended_low, preferred_element_type=jnp.float32
    )
    grad_attended = jnp.einsum(
        PRODUCT_1, attention_back, full_output, preferred_element_type=jnp.float32
    ).astype(jnp.bfloat16)
    grad_heads = grad_attended.reshape(sequences, shard_rows, local_heads, head_size)
    log_total = running_best + jnp.log(running_sum)
    delta_rows = jnp.sum(grad_heads.astype(jnp.float32) * attended_values, axis=-1)
    all_log_total, all_delta = (
        lax.all_gather(log_total, CONTEXT, axis=1, tiled=True),
        lax.all_gather(delta_rows, CONTEXT, axis=1, tiled=True),
    )
    query_init = (
        jnp.zeros((sequences, shard_rows, local_heads, head_size), jnp.float32),
        jnp.zeros((local_heads, bucket_count), jnp.float32),
    )
    fold_state = query_init
    key_piece = lax.all_gather(key_local, CONTEXT, axis=1, tiled=True)
    value_piece = lax.all_gather(value_local, CONTEXT, axis=1, tiled=True)
    query_block_rows = block_size()
    query_key_pad, blocks = pad_rows(key_piece, query_block_rows, 0)
    query_value_pad, blocks = pad_rows(value_piece, query_block_rows, 0)
    query_doc_pad, blocks = pad_rows(key_docs, query_block_rows, -1)

    def query_advance(running, block_index):
        grad_query, grad_bias = running
        offset = block_index * query_block_rows
        key_blk = lax.dynamic_slice_in_dim(query_key_pad, offset, query_block_rows, 1).reshape(
            sequences, query_block_rows, local_heads, head_size
        )
        value_blk = lax.dynamic_slice_in_dim(query_value_pad, offset, query_block_rows, 1).reshape(
            sequences, query_block_rows, local_heads, head_size
        )
        doc_blk = lax.dynamic_slice_in_dim(query_doc_pad, offset, query_block_rows, 1)
        key_place, key_token = key_places(
            offset + jnp.arange(query_block_rows, dtype=jnp.int32), shard_rows, key_span
        )
        scores, same_doc, bucket = scores_with_bias(
            query_heads, key_blk, query_place, segments, key_place, doc_blk, key_token, bias_table
        )
        probabilities = jnp.where(same_doc, jnp.exp(scores - log_total[..., None]), 0.0)
        value_dots = jnp.einsum(
            PRODUCT_8, grad_heads, value_blk, preferred_element_type=jnp.float32
        )
        grad_scores = (probabilities * (value_dots - delta_rows[..., None])).astype(jnp.bfloat16)
        grad_query = grad_query + jnp.einsum(
            PRODUCT_10, grad_scores, key_blk, preferred_element_type=jnp.float32
        )
        bucket_hits = (
            (bucket[:, :, None] == jnp.arange(bucket_count, dtype=jnp.int32)[None, None, :])
            & key_token[None, :, None]
        ).astype(jnp.bfloat16)
        grad_bias = grad_bias + jnp.einsum(
            PRODUCT_9, grad_scores, bucket_hits, preferred_element_type=jnp.float32
        )
        return ((grad_query, grad_bias), None)

    fold_state, unused = lax.scan(query_advance, fold_state, jnp.arange(blocks, dtype=jnp.int32))
    grad_query, grad_bias = fold_state
    key_heads = key_local.reshape(sequences, key_span, local_heads, head_size)
    value_heads = value_local.reshape(sequences, key_span, local_heads, head_size)
    local_place, local_token = key_places(
        context_place * key_span + jnp.arange(key_span, dtype=jnp.int32), shard_rows, key_span
    )
    key_init = (
        jnp.zeros((sequences, key_span, local_heads, head_size), jnp.float32),
        jnp.zeros((sequences, key_span, local_heads, head_size), jnp.float32),
    )
    fold_state = key_init
    query_piece = lax.all_gather(queries, CONTEXT, axis=1, tiled=True)
    grad_piece = lax.all_gather(grad_attended, CONTEXT, axis=1, tiled=True)
    key_block_rows = block_size()
    query_pad, blocks = pad_rows(query_piece, key_block_rows, 0)
    grad_pad, blocks = pad_rows(grad_piece, key_block_rows, 0)
    key_doc_pad, blocks = pad_rows(query_docs_all, key_block_rows, -1)
    total_pad, blocks = pad_rows(all_log_total, key_block_rows, 0.0)
    delta_pad, blocks = pad_rows(all_delta, key_block_rows, 0.0)

    def key_advance(running, block_index):
        grad_key, grad_value = running
        offset = block_index * key_block_rows
        query_blk = lax.dynamic_slice_in_dim(query_pad, offset, key_block_rows, 1).reshape(
            sequences, key_block_rows, local_heads, head_size
        )
        grad_blk = lax.dynamic_slice_in_dim(grad_pad, offset, key_block_rows, 1).reshape(
            sequences, key_block_rows, local_heads, head_size
        )
        doc_blk = lax.dynamic_slice_in_dim(key_doc_pad, offset, key_block_rows, 1)
        total_blk = lax.dynamic_slice_in_dim(total_pad, offset, key_block_rows, 1)
        delta_blk = lax.dynamic_slice_in_dim(delta_pad, offset, key_block_rows, 1)
        row_place = offset + jnp.arange(key_block_rows, dtype=jnp.int32)
        scores, same_doc, bucket = scores_with_bias(
            query_blk,
            key_heads,
            row_place,
            doc_blk,
            local_place,
            local_docs,
            local_token,
            bias_table,
        )
        probabilities = jnp.where(same_doc, jnp.exp(scores - total_blk[..., None]), 0.0)
        grad_value = grad_value + jnp.einsum(
            PRODUCT_11,
            probabilities.astype(jnp.bfloat16),
            grad_blk,
            preferred_element_type=jnp.float32,
        )
        value_dots = jnp.einsum(
            PRODUCT_8, grad_blk, value_heads, preferred_element_type=jnp.float32
        )
        grad_scores = (probabilities * (value_dots - delta_blk[..., None])).astype(jnp.bfloat16)
        grad_key = grad_key + jnp.einsum(
            PRODUCT_11, grad_scores, query_blk, preferred_element_type=jnp.float32
        )
        return ((grad_key, grad_value), None)

    fold_state, unused = lax.scan(key_advance, fold_state, jnp.arange(blocks, dtype=jnp.int32))
    grad_key, grad_value = fold_state
    grad_query_low = grad_query.reshape(sequences, shard_rows, local_inner).astype(jnp.bfloat16)
    grad_key_low = grad_key.reshape(sequences, key_span, local_inner).astype(jnp.bfloat16)
    grad_value_low = grad_value.reshape(sequences, key_span, local_inner).astype(jnp.bfloat16)
    grad_query_weight = jnp.einsum(
        PRODUCT_3, normed_low, grad_query_low, preferred_element_type=jnp.float32
    )
    grad_key_weight = jnp.einsum(
        PRODUCT_6, both_rows, grad_key_low, preferred_element_type=jnp.float32
    )
    grad_value_weight = jnp.einsum(
        PRODUCT_6, both_rows, grad_value_low, preferred_element_type=jnp.float32
    )
    row_part = jnp.einsum(
        PRODUCT_7, grad_key_low, full_key, preferred_element_type=jnp.float32
    ) + jnp.einsum(PRODUCT_7, grad_value_low, full_value, preferred_element_type=jnp.float32)
    token_part = row_part[:, :shard_rows] + jnp.einsum(
        PRODUCT_5, grad_query_low, full_query, preferred_element_type=jnp.float32
    )
    grad_normed, grad_memory_normed = (
        lax.psum(token_part.astype(jnp.bfloat16), TENSOR).astype(jnp.float32),
        lax.psum(row_part[:, shard_rows:].astype(jnp.bfloat16), TENSOR).astype(jnp.float32),
    )
    back_inputs, gain_tokens = norm_back(inputs_float, input_scale, attn_gain, grad_normed)
    back_memory, gain_memory = norm_back(memory_float, memory_scale, attn_gain, grad_memory_normed)
    grad_inputs = grad_residual + back_inputs
    grad_attn_gain = gain_tokens + gain_memory
    (
        shard_query,
        shard_key,
        shard_value,
        shard_output,
        shard_inner,
        shard_outer,
        shard_attn_gain,
        shard_dense_gain,
    ) = sum_grads(
        (
            grad_query_weight,
            grad_key_weight,
            grad_value_weight,
            grad_output,
            grad_inner,
            grad_outer,
            grad_attn_gain,
            grad_dense_gain,
        )
    )
    loss_sum, grad_bias_sum = lax.psum((loss_local, grad_bias), ROWS)
    return (
        loss_sum / (token_count * model_width),
        result.astype(jnp.bfloat16),
        grad_inputs,
        back_memory,
        shard_attn_gain,
        shard_query,
        shard_key,
        shard_value,
        shard_output,
        grad_bias_sum,
        shard_dense_gain,
        shard_inner,
        shard_outer,
    )


PAD = 16
BF = jnp.bfloat16
F32 = jnp.float32


def fits(mesh):
    sizes = dict(mesh.shape)
    return sizes[FSDP] == 2 and sizes[CONTEXT] == 8 and sizes[TENSOR] == 2


def swap_context(value, mask):
    return lax.ppermute(value, CONTEXT, [(i, i ^ mask) for i in range(8)])


def swap_core(pieces):
    return [swap_context(piece, 1) for piece in pieces]


def swap_fsdp(value):
    return lax.ppermute(value, FSDP, [(0, 1), (1, 0)])


def swap_tensor(value):
    return lax.ppermute(value, TENSOR, [(0, 1), (1, 0)])


def dot_nn(left, right):
    return lax.dot_general(left, right, (((1,), (0,)), ((), ())), preferred_element_type=F32)


def dot_nt(left, right):
    return lax.dot_general(left, right, (((1,), (1,)), ((), ())), preferred_element_type=F32)


def dot_tn(left, right):
    return lax.dot_general(left, right, (((0,), (0,)), ((), ())), preferred_element_type=F32)


def padded_bytes(shape, dtype):
    size = jnp.dtype(dtype).itemsize
    rows = 8 * (4 // size)
    lead = 1
    for count in shape[:-2]:
        lead *= count
    second = shape[-2] if len(shape) > 1 else 1
    return lead * -(-second // rows) * rows * -(-shape[-1] // 128) * 128 * size


def call(kernel, outs, name, ins_hbm=0, scratch=(), waits=()):
    def run(*operands):
        count = len(operands)
        specs = [pl.BlockSpec(memory_space=pltpu.VMEM)] * (count - ins_hbm)
        specs += [pl.BlockSpec(memory_space=pltpu.HBM)] * ins_hbm
        specs += [pl.BlockSpec(memory_space=pl.ANY)] * len(waits)
        held = [(item.shape, item.dtype) for item in operands[: count - ins_hbm]] + list(outs)
        held += [(item.shape, item.dtype) for item in scratch if item.memory_space == pltpu.VMEM]
        limit = 6 * 1024 * 1024 + sum(padded_bytes(shape, dtype) for shape, dtype in held)

        placed = list(operands)
        for at in range(count - ins_hbm, count):
            placed[at] = pltpu.with_memory_space_constraint(placed[at], pltpu.HBM)

        def body(*refs):
            kernel(*refs[:count], *refs[count + len(waits) :])

        return pl.pallas_call(
            body,
            out_shape=[jax.ShapeDtypeStruct(shape, dtype) for shape, dtype in outs],
            in_specs=specs,
            out_specs=[pl.BlockSpec(memory_space=pltpu.VMEM)] * len(outs),
            scratch_shapes=list(scratch),
            compiler_params=pltpu.CompilerParams(vmem_limit_bytes=limit),
            name=name,
        )(*placed, *waits)

    return run


def gate(value, *waits):
    def body(*refs):
        del refs

    return pl.pallas_call(
        body,
        out_shape=jax.ShapeDtypeStruct(value.shape, value.dtype),
        in_specs=[pl.BlockSpec(memory_space=pl.ANY)] * (1 + len(waits)),
        out_specs=pl.BlockSpec(memory_space=pl.ANY),
        input_output_aliases={0: 0},
        compiler_params=pltpu.CompilerParams(vmem_limit_bytes=1024 * 1024),
    )(value, *waits)


def diagonal(rows):
    return lax.broadcasted_iota(jnp.int32, (rows, 128), 0) == lax.broadcasted_iota(
        jnp.int32, (rows, 128), 1
    )


def row_to_column(row, rows):
    return jnp.sum(
        jnp.where(diagonal(rows), jnp.broadcast_to(row, (rows, 128)), 0.0), axis=1, keepdims=True
    )


def bucket_onehot(block_distance, span):
    lane = lax.broadcasted_iota(jnp.int32, (BUCKETS, 2 * span), 1)
    offset = jnp.where(lane < span, lane, lane - 2 * span)
    bucket = relative_bucket(block_distance * span - offset)
    return bucket == lax.broadcasted_iota(jnp.int32, (BUCKETS, 2 * span), 0)


def pack_kernel(*refs):
    sources, (own_ref, early_ref, later_ref, over_ref, block_ref) = refs[:13], refs[13:18]
    small, tail_ref, sems = refs[18:24], refs[24], refs[25]
    x, memory, segments, owner, valid, wq, wk, wv, wo, wi, wf, gain, dense_gain = sources
    span, slots = x.shape[0], memory.shape[0]
    rows_each, inner = wq.shape
    hidden = wi.shape[1]
    base = span + PAD
    half = pl.ds(pl.multiple_of(lax.axis_index(TENSOR) * inner, 128), inner)
    targets = [
        (memory, small[0]),
        (segments, small[1]),
        (owner, small[2]),
        (valid, small[3]),
        (gain, small[4]),
        (dense_gain, small[5]),
        (x.at[:, half], own_ref.at[slice(0, span), :]),
    ]
    parts = [wq, wk, wv, wo]
    parts += [w.at[:, slice(at, at + inner)] for w in (wi, wf) for at in range(0, hidden, inner)]
    starts = [base + at * rows_each for at in range(4)]
    late = base + 4 * rows_each + PAD
    starts += [late + at * rows_each for at in range(len(parts) - 4)]
    for part, start in zip(parts, starts):
        targets.append((part, own_ref.at[slice(start, start + rows_each), :]))
    copies = [
        pltpu.make_async_copy(source, target, sems.at[i])
        for i, (source, target) in enumerate(targets)
    ]
    for copy in copies:
        copy.start()
    for copy in copies[:6]:
        copy.wait()
    memory, segments, owner, valid, gain, dense_gain = small
    tail_ref[...] = jnp.zeros_like(tail_ref)
    tail_ref[0:slots, :] = memory[...].astype(F32)
    tail_ref[slots : slots + 1, 0:span] = segments[...].astype(F32)
    tail_ref[slots : slots + 1, span : span + slots] = owner[...].astype(F32)
    own_ref[span:base, :] = tail_ref[:, half].astype(BF)
    tail_ref[...] = jnp.zeros_like(tail_ref)
    tail_ref[0:1, 0:rows_each] = gain[...].astype(F32)
    tail_ref[1:2, 0:rows_each] = dense_gain[...].astype(F32)
    tail_ref[2:3, 0:1] = jnp.sum(valid[...].astype(F32), axis=1, keepdims=True)
    own_ref[late - PAD : late, :] = tail_ref[:, 0:inner].astype(BF)
    for copy in copies[6:]:
        copy.wait()
    early_ref[...] = own_ref[0:late, :]
    later_ref[...] = own_ref[late:, :]
    over_ref[...] = own_ref[base:, :]
    block_ref[...] = own_ref[0:base, :]


def split_kernel(two_ref, one_ref, first_ref, block_ref, later_ref):
    rows, first_rows = block_ref.shape[0] // 2, first_ref.shape[0] // 2
    for at, source in enumerate((two_ref, one_ref)):
        block_ref[at * rows : (at + 1) * rows, :] = source[0:rows, :]
        first_ref[at * first_rows : (at + 1) * first_rows, :] = source[rows : rows + first_rows, :]
    later_ref[...] = one_ref[rows + first_rows :, :]


def join_kernel(*refs, block_rows, first_rows):
    near, overs, blocks = refs[0:4], refs[4:6], refs[6:8]
    first_ref, block_ref, joined_ref = refs[8:]
    early_rows = block_rows + first_rows
    block_ref[...] = near[3][0:block_rows, :]
    first_ref[...] = near[3][block_rows:early_rows, :]
    at = 0
    for source, rows in [(piece, early_rows) for piece in near] + [
        (overs[0], first_rows),
        (overs[1], 2 * first_rows),
        (blocks[0], block_rows),
        (blocks[1], 2 * block_rows),
    ]:
        joined_ref[at : at + rows, :] = source[0:rows, :]
        at += rows
    rows = near[0].shape[0] - early_rows
    for source, start in ((near[0], early_rows), (near[1], early_rows), (overs[0], first_rows)):
        joined_ref[at : at + rows, :] = source[start : start + rows, :]
        at += rows


def order_kernel(*refs, rows_each):
    group = lax.axis_index(FSDP) * 8 + lax.axis_index(CONTEXT)
    target = refs[12]
    width = refs[0].shape[1]
    rows = target.shape[1] // width * rows_each
    for p in range(16):
        start = pl.ds(pl.multiple_of((group ^ p) * rows_each, 16), rows_each)
        at = (p >> 1 & 1) + 2 * (p >> 2 & 1) + 4 * (p >> 3)
        source = refs[(0, 0, 1, 2, 0, 3, 4, 5)[at] + 6 * (p & 1)]
        base = source.shape[0] - 3 * rows
        row = (base, base + rows, 0, 0, base + 2 * rows, 0, 0, 0)[at]
        for col in range(target.shape[1] // width):
            lines = slice(row + col * rows_each, row + (col + 1) * rows_each)
            target[start, col * width : (col + 1) * width] = source[lines, :]


def weights_kernel(*refs, rows_each, inner, block_rows):
    w_ref, gains_ref = refs[4:]
    group = lax.axis_index(FSDP) * 8 + lax.axis_index(CONTEXT)
    rows = 4 * rows_each + PAD
    gathered = jnp.zeros((8, gains_ref.shape[1]), F32)
    for p in range(16):
        piece = (p >> 1 & 1) + 2 * (p >> 2 & 1) + 4 * (p >> 3)
        source = refs[2 * (p & 1) + (piece == 7)]
        early = block_rows + rows
        at = piece * early + block_rows
        if piece >= 4:
            at = (4 * early, 4 * early + 2 * rows, 4 * early + rows, 0)[piece - 4]
        start = pl.multiple_of((group ^ p) * rows_each, 16)
        for which in range(4):
            w_ref[pl.ds(start, rows_each), which * inner : (which + 1) * inner] = source[
                at + which * rows_each : at + (which + 1) * rows_each, :
            ]
        lines = source[at + 4 * rows_each : at + rows, :].astype(F32)[0:8, :]
        lines = jnp.concatenate([lines, jnp.zeros_like(lines)], axis=1)
        gathered = gathered + pltpu.roll(lines, (group ^ p) * rows_each, 1)
    row_ids = lax.broadcasted_iota(jnp.int32, gathered.shape, 0)
    count = jnp.sum(gathered[2:3, :])
    gains_ref[...] = jnp.where(row_ids == 2, count, gathered)


def bias_kernel(bias_ref, toep_ref, *, span):
    for e in range(5):
        table = dot_nn(bias_ref[...], jnp.where(bucket_onehot(e - 2, span), 1.0, 0.0).astype(BF))
        for h in range(bias_ref.shape[0]):
            line = jnp.broadcast_to(table[h : h + 1, :], (span, 2 * span))
            if abs(e - 2) < 2:
                line = pltpu.roll(line, 0, 1, stride=1, stride_axis=0)
            toep_ref[h, e] = line[:, :span]


def project_kernel(*refs, span, slots, tokens, inner, first_rows):
    w_ref, gains_ref = refs[0:2]
    block_refs = refs[2:6]
    (normed_ref, kv_ref, q_ref, mask_ref, whole_ref) = refs[6:]
    block_rows = span + PAD
    early_rows = block_rows + first_rows
    side = lax.axis_index(TENSOR)
    place = lax.axis_index(CONTEXT)
    gain = gains_ref[0:1, :]
    own_docs = None
    for p in range(8):
        block = place ^ p
        piece = (p >> 1 & 1) + 2 * (p >> 2 & 1)
        for far in range(2):
            source = block_refs[2 * (p & 1) + (far and piece == 3)]
            at = piece * early_rows
            if far:
                base = 4 * early_rows + 3 * first_rows
                at = (base, base + 2 * block_rows, base + block_rows, 0)[piece]
            cols = pl.ds(pl.multiple_of((side ^ far) * inner, 128), inner)
            whole_ref[:, cols] = source[at : at + span + PAD, :].astype(F32)
        token_at = pl.multiple_of(block * span, span)
        slot_at = pl.multiple_of(tokens + block * PAD, PAD)
        values = whole_ref[0:span, :]
        scale = lax.rsqrt(jnp.mean(values * values, axis=-1, keepdims=True) + norm_eps)
        normed_ref[pl.ds(token_at, span), :] = (values * scale * gain).astype(BF)
        tail = whole_ref[span : span + PAD, :]
        docs = tail[slots : slots + 1, 0 : 2 * span]
        tail_rows = lax.broadcasted_iota(jnp.int32, tail.shape, 0)
        tail = jnp.where(tail_rows < slots, tail, 0.0)
        scale = lax.rsqrt(jnp.mean(tail * tail, axis=-1, keepdims=True) + norm_eps)
        normed_ref[pl.ds(slot_at, PAD), :] = (tail * scale * gain).astype(BF)
        if p == 0:
            own_docs = docs[:, 0:span]
        token_docs = row_to_column(docs[:, 0:span], span)
        mask_ref[pl.ds(token_at, span), :] = jnp.where(token_docs == own_docs, 0.0, score_floor)
        slot_docs = row_to_column(docs[:, span : 2 * span], PAD)
        slot_rows = lax.broadcasted_iota(jnp.int32, (PAD, 1), 0)
        slot_docs = jnp.where(slot_rows < slots, slot_docs, -1.0)
        mask_ref[pl.ds(slot_at, PAD), :] = jnp.where(slot_docs == own_docs, 0.0, score_floor)
    kv_ref[...] = dot_nn(normed_ref[...], w_ref[:, inner : 3 * inner]).astype(BF)
    own_at = pl.multiple_of(place * span, span)
    q_ref[...] = dot_nn(normed_ref[pl.ds(own_at, span), :], w_ref[:, :inner]).astype(BF)


def attend_kernel(
    w_ref,
    toep_ref,
    kv_ref,
    q_ref,
    mask_ref,
    p_ref,
    low_ref,
    wide_ref,
    part_ref,
    score_ref,
    *,
    span,
    tokens,
    inner,
):
    place = lax.axis_index(CONTEXT)
    lane = lax.broadcasted_iota(jnp.int32, (span, span), 1)
    sub = lax.broadcasted_iota(jnp.int32, (span, span), 0)
    count_blocks = tokens // span
    slot_rows_all = score_ref.shape[0] - tokens
    for t in range(inner // span):
        keys = kv_ref[:, t * span : (t + 1) * span]
        values = kv_ref[:, inner + t * span : inner + (t + 1) * span]
        pair = q_ref[:, t * span : (t + 1) * span]
        zero = jnp.zeros_like(pair)
        both = jnp.concatenate(
            [jnp.where(lane < span // 2, pair, zero), jnp.where(lane < span // 2, zero, pair)], axis=0
        )
        score_ref[...] = dot_nt(keys, both)
        best = jnp.full((1, 2 * span), score_floor, F32)
        for s in range(count_blocks):
            e = jnp.clip(s - place, -2, 2) + 2
            at = slice(s * span, (s + 1) * span)
            terms = jnp.concatenate([toep_ref[2 * t, e], toep_ref[2 * t + 1, e]], axis=1)
            mask = mask_ref[at, :]
            block = score_ref[at, :] + terms + jnp.concatenate([mask, mask], axis=1)
            score_ref[at, :] = block
            best = jnp.maximum(best, jnp.max(block, axis=0, keepdims=True))
        at = slice(tokens, tokens + slot_rows_all)
        mask = mask_ref[at, :]
        block = score_ref[at, :] + jnp.concatenate([mask, mask], axis=1)
        score_ref[at, :] = block
        best = jnp.maximum(best, jnp.max(block, axis=0, keepdims=True))
        total = jnp.zeros((1, 2 * span), F32)
        for s in range(score_ref.shape[0] // span):
            at = slice(s * span, (s + 1) * span)
            weights = jnp.exp(score_ref[at, :] - best)
            score_ref[at, :] = weights
            total = total + jnp.sum(weights, axis=0, keepdims=True)
        inverse = 1.0 / total
        for s in range(score_ref.shape[0] // span):
            at = slice(s * span, (s + 1) * span)
            p_ref[t, at, :] = (score_ref[at, :] * inverse).astype(BF)
        out = dot_tn(values, p_ref[t])
        out = jnp.where(sub < span // 2, out[:, :span], out[:, span:])
        wide_ref[t * span : (t + 1) * span, :] = out
        low_ref[:, t * span : (t + 1) * span] = jnp.transpose(out).astype(BF)
    part_ref[...] = dot_nt(low_ref[...], w_ref[:, 3 * inner :]).astype(BF)


def forward_kernel(
    x_ref,
    own_ref,
    far_ref,
    gains_ref,
    weights_ref,
    residual_ref,
    dense_ref,
    hidden_ref,
    slope_ref,
    part_ref,
):
    hidden = hidden_ref.shape[1]
    residual = x_ref[...].astype(F32) + (own_ref[...].astype(F32) + far_ref[...].astype(F32))
    residual_ref[...] = residual
    scale = lax.rsqrt(jnp.mean(residual * residual, axis=-1, keepdims=True) + norm_eps)
    dense_ref[...] = (residual * scale * gains_ref[1:2, :]).astype(BF)
    step = 256
    for at in range(0, hidden, step):
        pre = dot_nn(dense_ref[...], weights_ref[:, at : at + step])
        square = pre * pre
        root = 0.7978845608028654
        tanh = jnp.tanh(root * (pre + 0.044715 * pre * square))
        hidden_ref[:, at : at + step] = (0.5 * pre * (1.0 + tanh)).astype(BF)
        slope_ref[:, at : at + step] = 0.5 * (1.0 + tanh) + 0.5 * pre * (1.0 - tanh * tanh) * (
            root * (1.0 + 3.0 * 0.044715 * square)
        )
    part_ref[...] = dot_nt(hidden_ref[...], weights_ref[:, hidden:]).astype(BF)


def backward_kernel(
    residual_ref,
    own_ref,
    far_ref,
    teacher_ref,
    valid_ref,
    gains_ref,
    slope_ref,
    weights_ref,
    out_ref,
    grad_ref,
    part_ref,
    loss_ref,
    back_ref,
    pre_ref,
    *,
    total_rows,
):
    hidden = pre_ref.shape[1]
    result = residual_ref[...] + (own_ref[...].astype(F32) + far_ref[...].astype(F32))
    out_ref[...] = result.astype(BF)
    rows = result.shape[0]
    valid = row_to_column(valid_ref[...].astype(F32), rows)
    misfit = result - teacher_ref[...].astype(F32)
    loss = 0.5 * jnp.sum(valid * misfit * misfit)
    loss_ref[...] = jnp.full(loss_ref.shape, loss, F32)
    factor = total_rows / gains_ref[2:3, 0:1]
    grad = factor * valid * misfit
    grad_ref[...] = grad
    back_ref[...] = grad.astype(BF)
    step = 256
    for at in range(0, hidden, step):
        grad_hidden = dot_nn(back_ref[...], weights_ref[:, hidden + at : hidden + at + step])
        pre_ref[:, at : at + step] = (grad_hidden * slope_ref[:, at : at + step]).astype(BF)
    part_ref[...] = dot_nt(pre_ref[...], weights_ref[:, :hidden]).astype(BF)


def split_rows(value, target_ref, rows_each):
    place = lax.axis_index(CONTEXT)
    mine = lax.rem(place, 2)
    half = value.shape[0] // 2
    source = target_ref.at[0]
    source[...] = value
    ordered = target_ref.at[1]
    for g in range(8):
        keep = pl.multiple_of((2 * g + mine) * rows_each, 16)
        send = pl.multiple_of((2 * g + 1 - mine) * rows_each, 16)
        ordered[g * rows_each : (g + 1) * rows_each, :] = source[pl.ds(keep, rows_each), :]
        ordered[half + g * rows_each : half + (g + 1) * rows_each, :] = source[
            pl.ds(send, rows_each), :
        ]


def put_rows(product, start, keep_ref, send_refs):
    rows_each = keep_ref.shape[1]
    cols = slice(start, start + product.shape[1])
    low = product.astype(BF)
    for g in range(8):
        keep_ref[g, :, cols] = low[g * rows_each : (g + 1) * rows_each, :]
        send_ref = send_refs[g * len(send_refs) // 8]
        send_ref[g % send_ref.shape[0], :, cols] = low[(8 + g) * rows_each : (9 + g) * rows_each, :]


def dense_grad_kernel(
    left_ref,
    left_far_ref,
    right_ref,
    right_far_ref,
    next_ref,
    send_ref,
    turned_ref,
    lines_ref,
    *,
    pick,
    rows_each,
):
    mine = lax.rem(lax.axis_index(CONTEXT), 2)
    tokens = left_ref.shape[0]
    for at, source in enumerate((left_ref, left_far_ref)):
        turned = jnp.transpose(source[...].astype(F32)).astype(BF)
        turned_ref[:, at * tokens : (at + 1) * tokens] = turned
    for which in range(2):
        for g in range(4):
            row = pl.multiple_of((2 * pick(which, g) + mine) * rows_each, 16)
            start = (4 * which + g) * rows_each
            lines_ref[start : start + rows_each, :] = turned_ref[pl.ds(row, rows_each), :]
    for at in range(0, right_ref.shape[1], 512):
        cols = slice(at, at + 512)
        right = jnp.concatenate([right_ref[:, cols], right_far_ref[:, cols]], axis=0)
        product = dot_nn(lines_ref[...], right).astype(BF)
        for which, target in enumerate((next_ref, send_ref)):
            for g in range(4):
                start = (4 * which + g) * rows_each
                target[g, :, cols] = product[start : start + rows_each, :]


def attention_back_kernel(
    own_ref,
    far_ref,
    grad_ref,
    residual_ref,
    gains_ref,
    wide_ref,
    p_ref,
    kv_ref,
    q_ref,
    w_ref,
    residual_grad_ref,
    back_ref,
    dq_ref,
    dkv_ref,
    gain_ref,
    small_ref,
    ds_ref,
    diag_ref,
    *,
    inner,
    span,
    tokens,
):
    place = lax.axis_index(CONTEXT)
    incoming = own_ref[...].astype(F32) + far_ref[...].astype(F32)
    residual = residual_ref[...]
    scale = lax.rsqrt(jnp.mean(residual * residual, axis=-1, keepdims=True) + norm_eps)
    scaled = incoming * gains_ref[1:2, :]
    mean = jnp.mean(scaled * residual, axis=-1, keepdims=True)
    residual_grad = grad_ref[...] + (scale * scaled - residual * (scale * scale * scale * mean))
    residual_grad_ref[...] = residual_grad
    gain_ref[...] = jnp.broadcast_to(
        jnp.sum(incoming * residual * scale, axis=0, keepdims=True), gain_ref.shape
    )
    grads = dot_nn(residual_grad.astype(BF), w_ref[:, 3 * inner :])
    back_ref[...] = residual_grad.astype(BF)
    lane = lax.broadcasted_iota(jnp.int32, (span, span), 1)
    sub = lax.broadcasted_iota(jnp.int32, (span, span), 0)
    keys_all = p_ref.shape[1]
    blocks = tokens // span
    small_ref[...] = jnp.zeros_like(small_ref)
    tables = [bucket_onehot(d, span).astype(F32) for d in (-1, 0, 1)]
    zero = jnp.zeros((span, span), BF)
    for t in range(inner // span):
        cols = slice(t * span, (t + 1) * span)
        keys = kv_ref[:, cols]
        values = kv_ref[:, inner + t * span : inner + (t + 1) * span]
        pair = grads[:, cols].astype(BF)
        pair_back = jnp.transpose(pair.astype(F32)) * wide_ref[cols, :]
        delta = jnp.concatenate(
            [
                jnp.sum(pair_back[: span // 2], axis=0, keepdims=True),
                jnp.sum(pair_back[span // 2 :], axis=0, keepdims=True),
            ],
            axis=1,
        )
        grad_both = jnp.concatenate(
            [jnp.where(lane < span // 2, pair, zero), jnp.where(lane < span // 2, zero, pair)], axis=0
        )
        query = q_ref[:, cols]
        query_both = jnp.concatenate(
            [jnp.where(lane < span // 2, query, zero), jnp.where(lane < span // 2, zero, query)],
            axis=0,
        )
        low_sum = jnp.zeros((1, 2 * span), F32)
        high_sum = jnp.zeros((1, 2 * span), F32)
        for s in range(keys_all // span):
            at = slice(s * span, (s + 1) * span)
            dots = dot_nt(values[at, :], grad_both)
            ds = (p_ref[t, at, :].astype(F32) * (dots - delta)).astype(BF)
            ds_ref[at, :] = ds
            if s < blocks:
                line = jnp.sum(ds.astype(F32), axis=0, keepdims=True)
                low_sum = low_sum + jnp.where(s < place - 1, line, 0.0)
                high_sum = high_sum + jnp.where(s > place + 1, line, 0.0)
        dkv_ref[:, cols] = dot_nn(ds_ref[...], query_both).astype(BF)
        dkv_ref[:, inner + t * span : inner + (t + 1) * span] = dot_nn(p_ref[t], grad_both).astype(
            BF
        )
        dq = dot_tn(keys, ds_ref[...])
        dq = jnp.where(sub < span // 2, dq[:, :span], dq[:, span:])
        dq_ref[:, cols] = jnp.transpose(dq).astype(BF)
        for head in range(2):
            for which in range(3):
                s = place + which - 1
                inside = (s >= 0) & (s < blocks)
                start = pl.multiple_of(jnp.clip(s, 0, blocks - 1) * span, span)
                block = ds_ref[pl.ds(start, span), head * span : (head + 1) * span].astype(F32)
                block = jnp.where(inside, block, 0.0)
                block = jnp.concatenate([block, jnp.zeros((span, span), F32)], axis=1)
                size = span
                while size > 8:
                    size = size // 2
                    block = block[:size] + pltpu.roll(block[size:], 2 * span - size, 1)
                line = block[0:1]
                for j in range(1, 8):
                    line = line + pltpu.roll(block, 2 * span - j, 1)[j : j + 1]
                diag_ref[which, 2 * t + head : 2 * t + head + 1, :] = line
            bucket = lax.broadcasted_iota(jnp.int32, (1, 128), 1)
            part = slice(head * span, (head + 1) * span)
            low_total = jnp.sum(low_sum[:, part], axis=1, keepdims=True)
            high_total = jnp.sum(high_sum[:, part], axis=1, keepdims=True)
            small_ref[2 * t + head : 2 * t + head + 1, :] = jnp.where(
                bucket == BUCKETS // 2 - 1, low_total, 0.0
            ) + jnp.where(bucket == BUCKETS - 1, high_total, 0.0)
    heads = inner * 2 // span
    for which in range(3):
        line = lax.dot_general(
            diag_ref[which],
            tables[which],
            (((1,), (1,)), ((), ())),
            preferred_element_type=F32,
            precision=lax.Precision.HIGHEST,
        )
        small_ref[0:heads, 0:BUCKETS] += line[0:heads, :]


def rows_grad_kernel(
    dq_ref,
    dkv_ref,
    w_ref,
    normed_ref,
    gains_ref,
    dense_gain_ref,
    small_ref,
    loss_ref,
    keep_ref,
    *refs,
    inner,
    span,
    tokens,
    slots,
    heads,
):
    send_refs, (part_ref, line_ref) = refs[:-2], refs[-2:]
    place = lax.axis_index(CONTEXT)
    mine = lax.rem(place, 2)
    side = lax.axis_index(TENSOR)
    part_ref[...] = dot_nt(dkv_ref[...], w_ref[:, inner : 3 * inner])
    own_at = pl.multiple_of(place * span, span)
    part_ref[pl.ds(own_at, span), :] += dot_nt(dq_ref[...], w_ref[:, :inner])
    total = jnp.zeros((1, part_ref.shape[1]), F32)
    for s in range(part_ref.shape[0] // span):
        at = slice(s * span, (s + 1) * span)
        total = total + jnp.sum(
            part_ref[at, :] * normed_ref[at, :].astype(F32), axis=0, keepdims=True
        )
    line_ref[...] = jnp.zeros_like(line_ref)
    line_ref[slots : slots + 1, :] = total / gains_ref[0:1, :]
    line_ref[slots + 1 : slots + 2, :] = 0.5 * dense_gain_ref[0:1, :]
    for h in range(heads):
        start = pl.multiple_of(side * 128, 128)
        line_ref[slots + 2 + h : slots + 3 + h, pl.ds(start, 128)] = small_ref[h : h + 1, :]
    line_ref[slots + 2 : slots + 3, 256:384] = 0.5 * loss_ref[0:1, :]
    keep_rows = lax.broadcasted_iota(jnp.int32, line_ref.shape, 0) < slots
    for g in range(4):
        for target, block in (
            (keep_ref.at[g], 2 * g + mine),
            (send_refs[g // 2].at[g % 2], 2 * g + 1 - mine),
        ):
            token_at = pl.multiple_of(block * span, span)
            slot_at = pl.multiple_of(tokens + block * PAD, PAD)
            target[0:span, :] = part_ref[pl.ds(token_at, span), :].astype(BF)
            tail = jnp.where(keep_rows, part_ref[pl.ds(slot_at, PAD), :], line_ref[...])
            target[span : span + PAD, :] = tail.astype(BF)


def weight_grad_kernel(
    dq_ref,
    dkv_ref,
    normed_ref,
    back_ref,
    low_ref,
    keep_ref,
    *refs,
    inner,
    span,
    rows_each,
):
    send_refs, (wide_ref, line_ref) = refs[:-2], refs[-2:]
    place = lax.axis_index(CONTEXT)

    def put(product, start):
        put_rows(product, start, keep_ref, send_refs)

    split_rows(jnp.transpose(back_ref[...].astype(F32)).astype(BF), line_ref, rows_each)
    put(dot_nn(line_ref[1], low_ref[...]), 3 * inner)
    own_at = pl.multiple_of(place * span, span)
    own = normed_ref[pl.ds(own_at, span), :].astype(F32)
    split_rows(jnp.transpose(own).astype(BF), line_ref, rows_each)
    put(dot_nn(line_ref[1], dq_ref[...]), 0)
    split_rows(jnp.transpose(normed_ref[...].astype(F32)).astype(BF), wide_ref, rows_each)
    for at in range(0, 2 * inner, 256):
        put(dot_nn(wide_ref[1], dkv_ref[:, at : at + 256]), inner + at)


def halve_kernel(*refs, counts):
    targets = refs[-2:]
    mine = lax.axis_index(FSDP)
    sources, at = [], 0
    for count in counts:
        sources.append((refs[at], refs[at + 1 : at + 1 + count]))
        at += 1 + count
    for flip in range(2):

        @pl.when(mine == flip)
        def _():
            start = 0
            for keep_ref, far_refs in sources:
                width = keep_ref.shape[2]
                for g in range(8):
                    far = far_refs[g * len(far_refs) // 8][g % far_refs[0].shape[0]]
                    sums = keep_ref[g].astype(F32) + far.astype(F32)
                    targets[(g // 4) ^ flip][g % 4, :, start : start + width] = sums.astype(BF)
                start += width


def turn_kernel(keep_ref, far_ref, next_ref, send_ref, *, pick):
    for which, target in enumerate((next_ref, send_ref)):
        for g in range(max(1, keep_ref.shape[0] // 2)):
            block = pick(which, g)
            sums = keep_ref[block].astype(F32) + far_ref[block].astype(F32)
            if len(target.shape) == 2:
                target[...] = sums.astype(target.dtype)
            else:
                target[g] = sums.astype(target.dtype)


def pick_z1(which, g):
    return (g // 2) * 4 + (lax.axis_index(CONTEXT) // 2 ^ (which + 2 * (g % 2)))


def pick_half(which, g):
    return 4 * (lax.axis_index(FSDP) ^ which) + g


def pick_z2(which, g):
    return 2 * g + which


def pick_x(which, g):
    return lax.axis_index(FSDP) ^ which


def quarter_kernel(keep_ref, far_ref, next_ref, send_ref):
    place = lax.axis_index(CONTEXT) // 2
    for target, flip in ((next_ref, 0), (send_ref, 1)):
        for g in range(2):
            block = place ^ (flip + 2 * g)
            total = keep_ref[block].astype(F32) + far_ref[block].astype(F32)
            target[g] = total.astype(BF)


def eighth_kernel(keep_ref, far_ref, own_ref, send_ref):
    own_ref[...] = (keep_ref[0].astype(F32) + far_ref[0].astype(F32)).astype(own_ref.dtype)
    send_ref[...] = (keep_ref[1].astype(F32) + far_ref[1].astype(F32)).astype(BF)


def total_kernel(own_ref, far_ref, token_ref, *out_refs):
    token_ref[...] = jnp.zeros_like(token_ref)
    at = 0
    for out in out_refs:
        cols = slice(at, at + out.shape[1])
        out[...] = (own_ref[:, cols].astype(F32) + far_ref[:, cols].astype(F32)).astype(out.dtype)
        at += out.shape[1]


def columns_kernel(keep_ref, one_ref, two_ref, next_ref, send_ref):
    mine = lax.axis_index(TENSOR)
    width = next_ref.shape[2]
    for target, start in ((next_ref, mine * width), (send_ref, (1 - mine) * width)):
        cols = pl.ds(pl.multiple_of(start, 128), width)
        for half, far_ref in ((slice(0, 2), one_ref), (slice(2, 4), two_ref)):
            total = keep_ref[half, :, cols].astype(F32) + far_ref[:, :, cols].astype(F32)
            target[half] = total.astype(BF)


def tail_kernel(own_ref, far_ref, out_ref, *, span):
    mine = lax.axis_index(TENSOR)
    width = own_ref.shape[1]
    rows = slice(span, span + PAD)
    out_ref[:, pl.ds(pl.multiple_of(mine * width, 128), width)] = own_ref[rows, :].astype(F32)
    out_ref[:, pl.ds(pl.multiple_of((1 - mine) * width, 128), width)] = far_ref[rows, :].astype(F32)


def finish_kernel(
    own_ref,
    far_ref,
    x_ref,
    slots_ref,
    gains_ref,
    residual_grad_ref,
    tail_far_ref,
    inputs_ref,
    memory_ref,
    gain_ref,
    dense_gain_ref,
    bias_ref,
    loss_ref,
    full_ref,
    line_ref,
    *,
    span,
    slots,
):
    mine = lax.axis_index(TENSOR)
    group = lax.axis_index(FSDP) * 8 + lax.axis_index(CONTEXT)
    width = own_ref.shape[1]
    full_ref[:, pl.ds(pl.multiple_of(mine * width, 128), width)] = own_ref[...].astype(F32)
    full_ref[:, pl.ds(pl.multiple_of((1 - mine) * width, 128), width)] = far_ref[...].astype(F32)
    for source, target, start, extra in (
        (x_ref, inputs_ref, 0, residual_grad_ref),
        (slots_ref, memory_ref, span, None),
    ):
        values = source[...].astype(F32)
        scale = lax.rsqrt(jnp.mean(values * values, axis=-1, keepdims=True) + norm_eps)
        scaled = full_ref[start : start + values.shape[0], :] * gains_ref[0:1, :]
        mean = jnp.mean(scaled * values, axis=-1, keepdims=True)
        back = scale * scaled - values * (scale * scale * scale * mean)
        if extra is None:
            target[:, 0, :] = back
        else:
            target[...] = extra[...] + back
    line_ref[...] = full_ref[span : span + PAD, :] + tail_far_ref[...]
    lines = pltpu.roll(line_ref[...], full_ref.shape[1] - group * gain_ref.shape[1], 1)
    rows_each = gain_ref.shape[1]
    gain_ref[...] = lines[slots : slots + 1, 0:rows_each]
    dense_gain_ref[...] = lines[slots + 1 : slots + 2, 0:rows_each]
    heads = bias_ref.shape[0]
    start = pl.multiple_of(mine * 128, 128)
    bias_ref[...] = line_ref[slots + 2 : slots + 2 + heads, pl.ds(start, 128)][:, 0:BUCKETS]
    loss_ref[...] = line_ref[slots + 2 : slots + 3, 256:384] / (
        gains_ref[2:3, 0:128] * full_ref.shape[1]
    )


def fast_local(
    inputs,
    memory,
    teacher,
    segments,
    memory_owner,
    valid_mask,
    attention_gain,
    query_weight,
    key_weight,
    value_weight,
    attention_out_weight,
    position_bias,
    feedforward_gain,
    inner_weight,
    feedforward_out_weight,
):
    span, width = inputs.shape[1:]
    slots = memory.shape[1]
    rows_each, inner = query_weight.shape
    hidden = inner_weight.shape[1]
    heads = position_bias.shape[0]
    tokens = 8 * span
    keys_all = 8 * (span + PAD)
    total_rows = 2 * tokens
    x = inputs[0]
    block_rows = span + PAD
    first_rows = 4 * rows_each + PAD
    early_rows = block_rows + first_rows
    later_rows = 2 * hidden // inner * rows_each
    own, early, later, over, block = call(
        pack_kernel,
        [
            ((early_rows + later_rows, inner), BF),
            ((early_rows, inner), BF),
            ((later_rows, inner), BF),
            ((first_rows + later_rows, inner), BF),
            ((block_rows, inner), BF),
        ],
        name="pack",
        ins_hbm=13,
        scratch=(
            pltpu.VMEM((slots, width), BF),
            pltpu.VMEM((1, span), jnp.int32),
            pltpu.VMEM((1, slots), jnp.int32),
            pltpu.VMEM((1, span), jnp.int32),
            pltpu.VMEM((1, rows_each), BF),
            pltpu.VMEM((1, rows_each), BF),
            pltpu.VMEM((PAD, width), F32),
            pltpu.SemaphoreType.DMA((7 + 4 + 2 * hidden // inner,)),
        ),
    )(
        x,
        memory[0],
        segments,
        memory_owner,
        valid_mask,
        query_weight,
        key_weight,
        value_weight,
        attention_out_weight,
        inner_weight,
        feedforward_out_weight,
        attention_gain[None],
        feedforward_gain[None],
    )

    (toeplitz,) = call(
        lambda *refs: bias_kernel(*refs, span=span),
        [((heads, 5, span, span), F32)],
        name="bias",
        waits=(early,),
    )(position_bias)
    two = swap_context(early, 4)
    one = swap_context(own, 2)
    over_own = swap_fsdp(over)
    block_own = swap_tensor(block)
    first_pair, block_pair, later_one = call(
        split_kernel,
        [
            ((2 * first_rows, inner), BF),
            ((2 * block_rows, inner), BF),
            ((later_rows, inner), BF),
        ],
        name="split",
        waits=(over_own, block_own, toeplitz),
    )(two, one)
    three = swap_context(two, 2)
    over_pair = swap_fsdp(first_pair)
    block_pair = swap_tensor(block_pair)
    later_two = swap_context(gate(later, first_pair), 4)
    over_one = swap_fsdp(later_one)
    first_last, block_last, joined = call(
        lambda *refs: join_kernel(*refs, block_rows=block_rows, first_rows=first_rows),
        [
            ((first_rows, inner), BF),
            ((block_rows, inner), BF),
            ((4 * early_rows + 3 * (first_rows + block_rows + later_rows), inner), BF),
        ],
        name="join",
        waits=(later_two, over_one),
    )(own, one, two, three, over_own, over_pair, block_own, block_pair)
    over_last = swap_fsdp(first_last)
    block_last = swap_tensor(block_last)
    later_three = swap_context(later_two, 2)
    over_two = swap_fsdp(later_two)
    joined_core, over_core, block_core = swap_core([joined, over_last, block_last])
    w_all, gains = call(
        lambda *refs: weights_kernel(
            *refs, rows_each=rows_each, inner=inner, block_rows=block_rows
        ),
        [((width, 4 * inner), BF), ((8, width), F32)],
        name="weights",
    )(joined, over_last, joined_core, over_core)
    (normed, kv, queries, mask) = call(
        lambda *refs: project_kernel(
            *refs, span=span, slots=slots, tokens=tokens, inner=inner, first_rows=first_rows
        ),
        [
            ((keys_all, width), BF),
            ((keys_all, 2 * inner), BF),
            ((span, inner), BF),
            ((keys_all, span), F32),
        ],
        name="project",
        scratch=(pltpu.VMEM((span + PAD, width), F32),),
        waits=(later_three,),
    )(w_all, gains, joined, block_last, joined_core, block_core)
    (probs, low, wide, part) = call(
        lambda *refs: attend_kernel(*refs, span=span, tokens=tokens, inner=inner),
        [
            ((inner // span, keys_all, 2 * span), BF),
            ((span, inner), BF),
            ((inner, span), F32),
            ((span, width), BF),
        ],
        name="attend",
        scratch=(pltpu.VMEM((keys_all, 2 * span), F32),),
        waits=(over_two,),
    )(w_all, toeplitz, kv, queries, mask)
    far = swap_tensor(part)
    over_three = gate(swap_fsdp(later_three), far)
    later_all = [later_two, later_three, over_one, over_two]
    later_all = [gate(piece, part) for piece in later_all] + [over_three]
    (dense_weights,) = call(
        lambda *refs: order_kernel(*refs, rows_each=rows_each),
        [((width, 2 * hidden), BF)],
        name="order",
        waits=(part,),
    )(joined, *later_all, joined_core, *swap_core(later_all))
    (residual, dense_low, hidden_low, slope, dense_part) = call(
        forward_kernel,
        [
            ((span, width), F32),
            ((span, width), BF),
            ((span, hidden), BF),
            ((span, hidden), F32),
            ((span, width), BF),
        ],
        name="forward",
    )(x, part, far, gains, dense_weights)
    dense_far = swap_tensor(dense_part)
    hidden_far, dense_low_far = swap_core([hidden_low, dense_low])
    (output, grad_result, grad_part, loss_part, dense_back, grad_pre) = call(
        lambda *refs: backward_kernel(*refs, total_rows=total_rows),
        [
            ((span, width), BF),
            ((span, width), F32),
            ((span, width), BF),
            ((8, 128), F32),
            ((span, width), BF),
            ((span, hidden), BF),
        ],
        name="backward",
        waits=(hidden_far, dense_low_far),
    )(residual, dense_part, dense_far, teacher[0], valid_mask, gains, slope, dense_weights)
    grad_far = swap_tensor(grad_part)

    def halve(sources, *waits):
        columns = sum(keep.shape[2] for keep, _ in sources)
        return call(
            lambda *refs: halve_kernel(*refs, counts=[len(far) for _, far in sources]),
            [((4, rows_each, columns), BF)] * 2,
            name="halve",
            waits=waits,
        )(*[item for keep, far in sources for item in (keep, *far)])

    def quarter(keep, far_half, *waits):
        rows, columns = keep.shape[1:]
        return call(
            quarter_kernel,
            [((2, rows, columns), BF)] * 2,
            name="quarter",
            waits=waits,
        )(keep, far_half)

    def eighth(keep, far_quarter, own_type, *waits):
        rows, columns = keep.shape[1:]
        return call(
            eighth_kernel,
            [((rows, columns), own_type), ((rows, columns), BF)],
            name="eighth",
            waits=waits,
        )(keep, far_quarter)

    def total(own, far_eighth, outs, *waits):
        outs = [((8, 128), F32), *outs]
        return call(total_kernel, outs, name="total", waits=waits)(own, far_eighth)

    def turn(keep, far_blocks, pick, outs, *waits):
        return call(
            lambda *refs: turn_kernel(*refs, pick=pick), outs, name="turn", waits=waits
        )(keep, far_blocks)

    def outer_blocks(count):
        return ((count, rows_each, hidden), BF)

    def dense_grad(left, left_far, right, right_far, pick, *waits):
        return call(
            lambda *refs: dense_grad_kernel(*refs, pick=pick, rows_each=rows_each),
            [((4, rows_each, hidden), BF)] * 2,
            name="dense_grad",
            scratch=(
                pltpu.VMEM((width, 2 * span), BF),
                pltpu.VMEM((8 * rows_each, 2 * span), BF),
            ),
            waits=waits,
        )(left, left_far, right, right_far)

    dense_back_far, grad_pre_far = swap_core([dense_back, grad_pre])
    outer_next, outer_over = dense_grad(
        dense_back, dense_back_far, hidden_low, hidden_far, pick_z1
    )
    outer_far = swap_context(outer_over, 2)
    inner_next, inner_over = dense_grad(
        dense_low, dense_low_far, grad_pre, grad_pre_far, pick_half, outer_over
    )
    inner_far = swap_fsdp(inner_over)

    (grad_residual, attention_back, dq, dkv, dense_gain_rows, small) = call(
        lambda *refs: attention_back_kernel(*refs, inner=inner, span=span, tokens=tokens),
        [
            ((span, width), F32),
            ((span, width), BF),
            ((span, inner), BF),
            ((keys_all, 2 * inner), BF),
            ((8, width), F32),
            ((8, 128), F32),
        ],
        name="attend_back",
        scratch=(
            pltpu.VMEM((keys_all, 2 * span), BF),
            pltpu.VMEM((3, 8, 2 * span), F32),
        ),
        waits=(inner_over, outer_over),
    )(grad_part, grad_far, grad_result, residual, gains, wide, probs, kv, queries, w_all)

    rows_keep, *rows_send = call(
        lambda *refs: rows_grad_kernel(
            *refs, inner=inner, span=span, tokens=tokens, slots=slots, heads=heads
        ),
        [((4, span + PAD, width), BF)] + [((2, span + PAD, width), BF)] * 2,
        name="rows_grad",
        scratch=(pltpu.VMEM((keys_all, width), F32), pltpu.VMEM((PAD, width), F32)),
    )(dq, dkv, w_all, normed, gains, dense_gain_rows, small, loss_part)
    rows_far = swap_core(rows_send)

    weight_keep, *weight_send = call(
        lambda *refs: weight_grad_kernel(*refs, inner=inner, span=span, rows_each=rows_each),
        [((8, rows_each, 4 * inner), BF)] + [((4, rows_each, 4 * inner), BF)] * 2,
        name="weight_grad",
        scratch=(
            pltpu.VMEM((2, width, keys_all), BF),
            pltpu.VMEM((2, width, span), BF),
        ),
        waits=(rows_send[0],),
    )(dq, dkv, normed, attention_back, low)
    weight_far = swap_core(weight_send)
    outer_next, outer_over = turn(
        outer_next, outer_far, pick_z2, [outer_blocks(2)] * 2, weight_send[0]
    )
    outer_far = swap_context(outer_over, 4)
    inner_next, inner_over = quarter(inner_next, inner_far, outer_over)
    inner_far = swap_context(inner_over, 2)
    weight_next, weight_over = halve([(weight_keep, weight_far)], inner_over)
    weight_far = swap_fsdp(weight_over)
    rows_next, rows_over = call(
        columns_kernel,
        [((4, span + PAD, width // 2), BF)] * 2,
        name="columns",
        waits=(weight_over,),
    )(rows_keep, *rows_far)
    rows_far = swap_tensor(rows_over)

    rows_next, rows_over = quarter(rows_next, rows_far)
    rows_far = swap_context(rows_over, 2)
    inner_own, inner_over = eighth(inner_next, inner_far, F32, rows_over)
    inner_far = swap_context(inner_over, 4)
    outer_own, outer_over = turn(
        outer_next,
        outer_far,
        pick_x,
        [((rows_each, hidden), F32), ((rows_each, hidden), BF)],
        inner_over,
    )
    outer_far = swap_fsdp(outer_over)
    weight_next, weight_over = quarter(weight_next, weight_far, outer_over)
    weight_far = swap_context(weight_over, 2)

    rows_own, rows_over = eighth(rows_next, rows_far, BF, weight_over)
    rows_far = swap_context(rows_over, 4)
    token, grad_outer = total(outer_own, outer_far, [((rows_each, hidden), F32)], rows_over)
    token, grad_inner = total(inner_own, inner_far, [((rows_each, hidden), F32)], token)
    weight_own, weight_over = eighth(weight_next, weight_far, F32, token)
    weight_far = swap_context(weight_over, 4)

    token, rows_half = total(
        rows_own, rows_far, [((span + PAD, width // 2), BF)], weight_over
    )
    rows_other = swap_tensor(rows_half)
    (tail,) = call(
        lambda *refs: tail_kernel(*refs, span=span), [((PAD, width), F32)], name="tail"
    )(rows_half, rows_other)
    tail_far = swap_fsdp(tail)
    *rest, grad_output = total(weight_own, weight_far, [((rows_each, inner), F32)] * 4, tail)
    weight_grads = rest[1:]
    (grad_inputs, grad_memory, grad_gain, grad_dense_gain, grad_bias, loss) = call(
        lambda *refs: finish_kernel(*refs, span=span, slots=slots),
        [
            ((span, width), F32),
            ((slots, 1, width), F32),
            ((1, rows_each), F32),
            ((1, rows_each), F32),
            ((heads, BUCKETS), F32),
            ((1, 128), F32),
        ],
        name="finish",
        scratch=(pltpu.VMEM((span + PAD, width), F32), pltpu.VMEM((PAD, width), F32)),
    )(rows_half, rows_other, x, memory[0], gains, grad_residual, tail_far)
    return (
        loss[0, 0],
        output[None],
        grad_inputs[None],
        jnp.swapaxes(grad_memory, 0, 1),
        grad_gain[0],
        weight_grads[0],
        weight_grads[1],
        weight_grads[2],
        grad_output,
        grad_bias,
        grad_dense_gain[0],
        grad_inner,
        grad_outer,
    )


def solution(mesh):
    return jax.shard_map(
        fast_local if fits(mesh) else general_local,
        mesh=mesh,
        in_specs=(
            P(FSDP, CONTEXT, None),
            P(FSDP, CONTEXT, None),
            P(FSDP, CONTEXT, None),
            P(FSDP, CONTEXT),
            P(FSDP, CONTEXT),
            P(FSDP, CONTEXT),
            P(ROWS),
            P(ROWS, TENSOR),
            P(ROWS, TENSOR),
            P(ROWS, TENSOR),
            P(ROWS, TENSOR),
            P(TENSOR, None),
            P(ROWS),
            P(ROWS, TENSOR),
            P(ROWS, TENSOR),
        ),
        out_specs=(
            P(),
            P(FSDP, CONTEXT, None),
            P(FSDP, CONTEXT, None),
            P(FSDP, CONTEXT, None),
            P(ROWS),
            P(ROWS, TENSOR),
            P(ROWS, TENSOR),
            P(ROWS, TENSOR),
            P(ROWS, TENSOR),
            P(TENSOR, None),
            P(ROWS),
            P(ROWS, TENSOR),
            P(ROWS, TENSOR),
        ),
        check_vma=False,
    )
```

```python
import jax
import jax.numpy as jnp
from jax import lax
from jax.experimental import pallas as pl
from jax.experimental.pallas import tpu as pltpu
from jax.sharding import PartitionSpec as P

BUCKETS = 32
FSDP = "fsdp"
CONTEXT = "context"
TENSOR = "tensor"
ROWS = (FSDP, CONTEXT)
PRODUCT_0 = "scd,df->scf"
PRODUCT_1 = "scd,di->sci"
PRODUCT_2 = "scd,scf->df"
PRODUCT_3 = "scd,sci->di"
PRODUCT_4 = "scf,df->scd"
PRODUCT_5 = "sci,di->scd"
PRODUCT_6 = "sjd,sji->di"
PRODUCT_7 = "sji,di->sjd"
PRODUCT_8 = "sqhd,skhd->sqhk"
PRODUCT_9 = "sqhk,qkb->hb"
PRODUCT_10 = "sqhk,skhd->sqhd"
PRODUCT_11 = "sqhk,sqhd->skhd"


norm_eps = 1e-06
score_floor = -1e30


def relative_bucket(distance):
    half_count = BUCKETS // 2
    exact_count = half_count // 2
    magnitude = jnp.minimum(jnp.abs(distance), 1024)
    far_bucket = jnp.full(distance.shape, exact_count, jnp.int32)
    for level_index in range(1, half_count - exact_count):
        far_bucket = far_bucket + (
            magnitude * magnitude >= exact_count * exact_count * 2**level_index
        ).astype(jnp.int32)
    bucket_ids = jnp.where(magnitude < exact_count, magnitude, far_bucket)
    return bucket_ids + (distance > 0).astype(jnp.int32) * half_count


def rms_norm(values, gain_in):
    inv_rms = lax.rsqrt(jnp.mean(values * values, axis=-1, keepdims=True) + norm_eps)
    return (values * inv_rms * gain_in, inv_rms)


def norm_back(values, inv_rms, gain_in, grad_in):
    scaled = grad_in * gain_in
    inner_mean = jnp.mean(scaled * values, axis=-1, keepdims=True)
    grad_values = inv_rms * scaled - values * inv_rms * inv_rms * inv_rms * inner_mean
    grad_gain = jnp.sum(grad_in * values * inv_rms, axis=tuple(range(values.ndim - 1)))
    return (grad_values, grad_gain)


def smooth_gate(values):
    return jax.nn.gelu(values, approximate=True)


def block_size():
    return 512


def pad_rows(values_in, block_rows, fill_value):
    blocks = -(-values_in.shape[1] // block_rows)
    missing = blocks * block_rows - values_in.shape[1]
    padding = [(0, 0)] * values_in.ndim
    padding[1] = (0, missing)
    return (jnp.pad(values_in, padding, constant_values=fill_value), blocks)


def key_places(row_ids, shard_rows, key_span):
    within = row_ids % key_span
    return (row_ids // key_span * shard_rows + within, within < shard_rows)


def scores_with_bias(
    query_blk, key_blk, query_place, query_doc, key_place, key_doc, key_token, bias_table
):
    scores = jnp.einsum(PRODUCT_8, query_blk, key_blk, preferred_element_type=jnp.float32)
    bucket = relative_bucket(key_place[None, :] - query_place[:, None])
    rel_terms = jnp.where(key_token[None, None, :], jnp.take(bias_table, bucket, axis=1), 0.0)
    scores = scores + jnp.moveaxis(rel_terms, 0, 1)[None]
    same_doc = (query_doc[:, :, None] == key_doc[:, None, :])[:, :, None, :]
    return (scores, same_doc, bucket)


def sum_grads(grad_items):
    return (
        lax.psum_scatter(grad_items[0], ROWS, scatter_dimension=0, tiled=True),
        lax.psum_scatter(grad_items[1], ROWS, scatter_dimension=0, tiled=True),
        lax.psum_scatter(grad_items[2], ROWS, scatter_dimension=0, tiled=True),
        lax.psum_scatter(grad_items[3], ROWS, scatter_dimension=0, tiled=True),
        lax.psum_scatter(grad_items[4], ROWS, scatter_dimension=0, tiled=True),
        lax.psum_scatter(grad_items[5], ROWS, scatter_dimension=0, tiled=True),
        lax.psum_scatter(grad_items[6], ROWS, scatter_dimension=0, tiled=True),
        lax.psum_scatter(grad_items[7], ROWS, scatter_dimension=0, tiled=True),
    )


def general_local(
    inputs,
    memory,
    teacher,
    segments,
    memory_owner,
    valid_mask,
    attention_gain,
    query_weight,
    key_weight,
    value_weight,
    attention_out_weight,
    position_bias,
    feedforward_gain,
    inner_weight,
    feedforward_out_weight,
):
    sequences, shard_rows, model_width = inputs.shape
    key_span = shard_rows + memory.shape[1]
    context_size = lax.axis_size(CONTEXT)
    length = shard_rows * context_size
    context_place = lax.axis_index(CONTEXT)
    local_heads = position_bias.shape[0]
    bucket_count = position_bias.shape[1]
    head_size = query_weight.shape[1] // local_heads
    local_inner = local_heads * head_size
    total_rows = sequences * length * lax.axis_size(FSDP)
    bias_table = position_bias.astype(jnp.float32)
    (
        full_query,
        full_key,
        full_value,
        full_output,
        full_inner,
        full_outer,
        full_attn_gain,
        full_dense_gain,
    ) = (
        lax.all_gather(query_weight, ROWS, axis=0, tiled=True),
        lax.all_gather(key_weight, ROWS, axis=0, tiled=True),
        lax.all_gather(value_weight, ROWS, axis=0, tiled=True),
        lax.all_gather(attention_out_weight, ROWS, axis=0, tiled=True),
        lax.all_gather(inner_weight, ROWS, axis=0, tiled=True),
        lax.all_gather(feedforward_out_weight, ROWS, axis=0, tiled=True),
        lax.all_gather(attention_gain, ROWS, axis=0, tiled=True),
        lax.all_gather(feedforward_gain, ROWS, axis=0, tiled=True),
    )
    attn_gain = full_attn_gain.astype(jnp.float32)
    dense_gain = full_dense_gain.astype(jnp.float32)
    local_docs = jnp.concatenate([segments, memory_owner], axis=1)
    key_docs = lax.all_gather(local_docs, CONTEXT, axis=1, tiled=True)
    query_docs_all = key_docs.reshape(sequences, context_size, key_span)[:, :, :shard_rows].reshape(
        sequences, length
    )
    token_count = lax.psum(jnp.sum(valid_mask.astype(jnp.float32)), ROWS)
    inputs_float = inputs.astype(jnp.float32)
    memory_float = memory.astype(jnp.float32)
    normed, input_scale = rms_norm(inputs_float, attn_gain)
    memory_normed, memory_scale = rms_norm(memory_float, attn_gain)
    normed_low = normed.astype(jnp.bfloat16)
    both_rows = jnp.concatenate([normed_low, memory_normed.astype(jnp.bfloat16)], axis=1)
    queries = jnp.dot(normed_low, full_query, preferred_element_type=jnp.float32).astype(
        jnp.bfloat16
    )
    key_local = jnp.dot(both_rows, full_key, preferred_element_type=jnp.float32).astype(
        jnp.bfloat16
    )
    value_local = jnp.dot(both_rows, full_value, preferred_element_type=jnp.float32).astype(
        jnp.bfloat16
    )
    query_heads = queries.reshape(sequences, shard_rows, local_heads, head_size)
    query_place = context_place * shard_rows + jnp.arange(shard_rows, dtype=jnp.int32)
    fold_init = (
        jnp.full((sequences, shard_rows, local_heads), score_floor, jnp.float32),
        jnp.zeros((sequences, shard_rows, local_heads), jnp.float32),
        jnp.zeros((sequences, shard_rows, local_heads, head_size), jnp.float32),
    )
    fold_state = fold_init
    key_piece = lax.all_gather(key_local, CONTEXT, axis=1, tiled=True)
    value_piece = lax.all_gather(value_local, CONTEXT, axis=1, tiled=True)
    block_rows = block_size()
    key_pad, blocks = pad_rows(key_piece, block_rows, 0)
    value_pad, blocks = pad_rows(value_piece, block_rows, 0)
    doc_pad, blocks = pad_rows(key_docs, block_rows, -1)

    def attend_advance(running, block_index):
        running_best, running_sum, summed = running
        offset = block_index * block_rows
        key_blk = lax.dynamic_slice_in_dim(key_pad, offset, block_rows, 1).reshape(
            sequences, block_rows, local_heads, head_size
        )
        value_blk = lax.dynamic_slice_in_dim(value_pad, offset, block_rows, 1).reshape(
            sequences, block_rows, local_heads, head_size
        )
        doc_blk = lax.dynamic_slice_in_dim(doc_pad, offset, block_rows, 1)
        key_place, key_token = key_places(
            offset + jnp.arange(block_rows, dtype=jnp.int32), shard_rows, key_span
        )
        scores, same_doc, bucket = scores_with_bias(
            query_heads, key_blk, query_place, segments, key_place, doc_blk, key_token, bias_table
        )
        masked = jnp.where(same_doc, scores, score_floor)
        new_best = jnp.maximum(running_best, jnp.max(masked, axis=-1))
        weights = jnp.where(same_doc, jnp.exp(scores - new_best[..., None]), 0.0)
        factor = jnp.exp(running_best - new_best)
        running_sum = running_sum * factor + jnp.sum(weights, axis=-1)
        summed = summed * factor[..., None] + jnp.einsum(
            PRODUCT_10,
            weights.astype(jnp.bfloat16),
            value_blk,
            preferred_element_type=jnp.float32,
        )
        return ((new_best, running_sum, summed), None)

    fold_state, unused = lax.scan(attend_advance, fold_state, jnp.arange(blocks, dtype=jnp.int32))
    running_best, running_sum, summed = fold_state
    attended_values = summed / running_sum[..., None]
    attended_low = attended_values.reshape(sequences, shard_rows, local_inner).astype(jnp.bfloat16)
    attention_part = jnp.einsum(
        PRODUCT_5, attended_low, full_output, preferred_element_type=jnp.float32
    )
    residual = inputs_float + lax.psum(attention_part.astype(jnp.bfloat16), TENSOR).astype(
        jnp.float32
    )
    dense_normed, dense_scale = rms_norm(residual, dense_gain)
    dense_low = dense_normed.astype(jnp.bfloat16)
    inner_pre = jnp.dot(dense_low, full_inner, preferred_element_type=jnp.float32)
    hidden_float, gate_pullback = jax.vjp(smooth_gate, inner_pre)
    hidden_low = hidden_float.astype(jnp.bfloat16)
    dense_part = jnp.einsum(
        PRODUCT_4, hidden_low, full_outer, preferred_element_type=jnp.float32
    )
    result = residual + lax.psum(dense_part.astype(jnp.bfloat16), TENSOR).astype(jnp.float32)
    target_mask = valid_mask.astype(jnp.float32)[..., None]
    misfit = result - teacher.astype(jnp.float32)
    loss_local = 0.5 * jnp.sum(target_mask * misfit * misfit)
    grad_result = total_rows / token_count * target_mask * misfit
    dense_back = grad_result.astype(jnp.bfloat16)
    grad_outer = jnp.einsum(
        PRODUCT_2, dense_back, hidden_low, preferred_element_type=jnp.float32
    )
    grad_hidden = jnp.einsum(
        PRODUCT_0, dense_back, full_outer, preferred_element_type=jnp.float32
    )
    grad_pre = gate_pullback(grad_hidden)[0].astype(jnp.bfloat16)
    grad_inner = jnp.einsum(PRODUCT_2, dense_low, grad_pre, preferred_element_type=jnp.float32)
    grad_dense_part = jnp.einsum(
        PRODUCT_4, grad_pre, full_inner, preferred_element_type=jnp.float32
    )
    grad_dense_normed = lax.psum(grad_dense_part.astype(jnp.bfloat16), TENSOR).astype(jnp.float32)
    back_residual, grad_dense_gain = norm_back(residual, dense_scale, dense_gain, grad_dense_normed)
    grad_residual = grad_result + back_residual
    attention_back = grad_residual.astype(jnp.bfloat16)
    grad_output = jnp.einsum(
        PRODUCT_3, attention_back, attended_low, preferred_element_type=jnp.float32
    )
    grad_attended = jnp.einsum(
        PRODUCT_1, attention_back, full_output, preferred_element_type=jnp.float32
    ).astype(jnp.bfloat16)
    grad_heads = grad_attended.reshape(sequences, shard_rows, local_heads, head_size)
    log_total = running_best + jnp.log(running_sum)
    delta_rows = jnp.sum(grad_heads.astype(jnp.float32) * attended_values, axis=-1)
    all_log_total, all_delta = (
        lax.all_gather(log_total, CONTEXT, axis=1, tiled=True),
        lax.all_gather(delta_rows, CONTEXT, axis=1, tiled=True),
    )
    query_init = (
        jnp.zeros((sequences, shard_rows, local_heads, head_size), jnp.float32),
        jnp.zeros((local_heads, bucket_count), jnp.float32),
    )
    fold_state = query_init
    key_piece = lax.all_gather(key_local, CONTEXT, axis=1, tiled=True)
    value_piece = lax.all_gather(value_local, CONTEXT, axis=1, tiled=True)
    query_block_rows = block_size()
    query_key_pad, blocks = pad_rows(key_piece, query_block_rows, 0)
    query_value_pad, blocks = pad_rows(value_piece, query_block_rows, 0)
    query_doc_pad, blocks = pad_rows(key_docs, query_block_rows, -1)

    def query_advance(running, block_index):
        grad_query, grad_bias = running
        offset = block_index * query_block_rows
        key_blk = lax.dynamic_slice_in_dim(query_key_pad, offset, query_block_rows, 1).reshape(
            sequences, query_block_rows, local_heads, head_size
        )
        value_blk = lax.dynamic_slice_in_dim(query_value_pad, offset, query_block_rows, 1).reshape(
            sequences, query_block_rows, local_heads, head_size
        )
        doc_blk = lax.dynamic_slice_in_dim(query_doc_pad, offset, query_block_rows, 1)
        key_place, key_token = key_places(
            offset + jnp.arange(query_block_rows, dtype=jnp.int32), shard_rows, key_span
        )
        scores, same_doc, bucket = scores_with_bias(
            query_heads, key_blk, query_place, segments, key_place, doc_blk, key_token, bias_table
        )
        probabilities = jnp.where(same_doc, jnp.exp(scores - log_total[..., None]), 0.0)
        value_dots = jnp.einsum(
            PRODUCT_8, grad_heads, value_blk, preferred_element_type=jnp.float32
        )
        grad_scores = (probabilities * (value_dots - delta_rows[..., None])).astype(jnp.bfloat16)
        grad_query = grad_query + jnp.einsum(
            PRODUCT_10, grad_scores, key_blk, preferred_element_type=jnp.float32
        )
        bucket_hits = (
            (bucket[:, :, None] == jnp.arange(bucket_count, dtype=jnp.int32)[None, None, :])
            & key_token[None, :, None]
        ).astype(jnp.bfloat16)
        grad_bias = grad_bias + jnp.einsum(
            PRODUCT_9, grad_scores, bucket_hits, preferred_element_type=jnp.float32
        )
        return ((grad_query, grad_bias), None)

    fold_state, unused = lax.scan(query_advance, fold_state, jnp.arange(blocks, dtype=jnp.int32))
    grad_query, grad_bias = fold_state
    key_heads = key_local.reshape(sequences, key_span, local_heads, head_size)
    value_heads = value_local.reshape(sequences, key_span, local_heads, head_size)
    local_place, local_token = key_places(
        context_place * key_span + jnp.arange(key_span, dtype=jnp.int32), shard_rows, key_span
    )
    key_init = (
        jnp.zeros((sequences, key_span, local_heads, head_size), jnp.float32),
        jnp.zeros((sequences, key_span, local_heads, head_size), jnp.float32),
    )
    fold_state = key_init
    query_piece = lax.all_gather(queries, CONTEXT, axis=1, tiled=True)
    grad_piece = lax.all_gather(grad_attended, CONTEXT, axis=1, tiled=True)
    key_block_rows = block_size()
    query_pad, blocks = pad_rows(query_piece, key_block_rows, 0)
    grad_pad, blocks = pad_rows(grad_piece, key_block_rows, 0)
    key_doc_pad, blocks = pad_rows(query_docs_all, key_block_rows, -1)
    total_pad, blocks = pad_rows(all_log_total, key_block_rows, 0.0)
    delta_pad, blocks = pad_rows(all_delta, key_block_rows, 0.0)

    def key_advance(running, block_index):
        grad_key, grad_value = running
        offset = block_index * key_block_rows
        query_blk = lax.dynamic_slice_in_dim(query_pad, offset, key_block_rows, 1).reshape(
            sequences, key_block_rows, local_heads, head_size
        )
        grad_blk = lax.dynamic_slice_in_dim(grad_pad, offset, key_block_rows, 1).reshape(
            sequences, key_block_rows, local_heads, head_size
        )
        doc_blk = lax.dynamic_slice_in_dim(key_doc_pad, offset, key_block_rows, 1)
        total_blk = lax.dynamic_slice_in_dim(total_pad, offset, key_block_rows, 1)
        delta_blk = lax.dynamic_slice_in_dim(delta_pad, offset, key_block_rows, 1)
        row_place = offset + jnp.arange(key_block_rows, dtype=jnp.int32)
        scores, same_doc, bucket = scores_with_bias(
            query_blk,
            key_heads,
            row_place,
            doc_blk,
            local_place,
            local_docs,
            local_token,
            bias_table,
        )
        probabilities = jnp.where(same_doc, jnp.exp(scores - total_blk[..., None]), 0.0)
        grad_value = grad_value + jnp.einsum(
            PRODUCT_11,
            probabilities.astype(jnp.bfloat16),
            grad_blk,
            preferred_element_type=jnp.float32,
        )
        value_dots = jnp.einsum(
            PRODUCT_8, grad_blk, value_heads, preferred_element_type=jnp.float32
        )
        grad_scores = (probabilities * (value_dots - delta_blk[..., None])).astype(jnp.bfloat16)
        grad_key = grad_key + jnp.einsum(
            PRODUCT_11, grad_scores, query_blk, preferred_element_type=jnp.float32
        )
        return ((grad_key, grad_value), None)

    fold_state, unused = lax.scan(key_advance, fold_state, jnp.arange(blocks, dtype=jnp.int32))
    grad_key, grad_value = fold_state
    grad_query_low = grad_query.reshape(sequences, shard_rows, local_inner).astype(jnp.bfloat16)
    grad_key_low = grad_key.reshape(sequences, key_span, local_inner).astype(jnp.bfloat16)
    grad_value_low = grad_value.reshape(sequences, key_span, local_inner).astype(jnp.bfloat16)
    grad_query_weight = jnp.einsum(
        PRODUCT_3, normed_low, grad_query_low, preferred_element_type=jnp.float32
    )
    grad_key_weight = jnp.einsum(
        PRODUCT_6, both_rows, grad_key_low, preferred_element_type=jnp.float32
    )
    grad_value_weight = jnp.einsum(
        PRODUCT_6, both_rows, grad_value_low, preferred_element_type=jnp.float32
    )
    row_part = jnp.einsum(
        PRODUCT_7, grad_key_low, full_key, preferred_element_type=jnp.float32
    ) + jnp.einsum(PRODUCT_7, grad_value_low, full_value, preferred_element_type=jnp.float32)
    token_part = row_part[:, :shard_rows] + jnp.einsum(
        PRODUCT_5, grad_query_low, full_query, preferred_element_type=jnp.float32
    )
    grad_normed, grad_memory_normed = (
        lax.psum(token_part.astype(jnp.bfloat16), TENSOR).astype(jnp.float32),
        lax.psum(row_part[:, shard_rows:].astype(jnp.bfloat16), TENSOR).astype(jnp.float32),
    )
    back_inputs, gain_tokens = norm_back(inputs_float, input_scale, attn_gain, grad_normed)
    back_memory, gain_memory = norm_back(memory_float, memory_scale, attn_gain, grad_memory_normed)
    grad_inputs = grad_residual + back_inputs
    grad_attn_gain = gain_tokens + gain_memory
    (
        shard_query,
        shard_key,
        shard_value,
        shard_output,
        shard_inner,
        shard_outer,
        shard_attn_gain,
        shard_dense_gain,
    ) = sum_grads(
        (
            grad_query_weight,
            grad_key_weight,
            grad_value_weight,
            grad_output,
            grad_inner,
            grad_outer,
            grad_attn_gain,
            grad_dense_gain,
        )
    )
    loss_sum, grad_bias_sum = lax.psum((loss_local, grad_bias), ROWS)
    return (
        loss_sum / (token_count * model_width),
        result.astype(jnp.bfloat16),
        grad_inputs,
        back_memory,
        shard_attn_gain,
        shard_query,
        shard_key,
        shard_value,
        shard_output,
        grad_bias_sum,
        shard_dense_gain,
        shard_inner,
        shard_outer,
    )


PAD = 16
BF = jnp.bfloat16
F32 = jnp.float32


def fits(mesh):
    sizes = dict(mesh.shape)
    return sizes[FSDP] == 2 and sizes[CONTEXT] == 8 and sizes[TENSOR] == 2


def swap_context(value, mask):
    return lax.ppermute(value, CONTEXT, [(i, i ^ mask) for i in range(8)])


def swap_core(pieces):
    return [swap_context(piece, 1) for piece in pieces]


def swap_fsdp(value):
    return lax.ppermute(value, FSDP, [(0, 1), (1, 0)])


def swap_tensor(value):
    return lax.ppermute(value, TENSOR, [(0, 1), (1, 0)])


def dot_nn(left, right):
    return lax.dot_general(left, right, (((1,), (0,)), ((), ())), preferred_element_type=F32)


def dot_nt(left, right):
    return lax.dot_general(left, right, (((1,), (1,)), ((), ())), preferred_element_type=F32)


def dot_tn(left, right):
    return lax.dot_general(left, right, (((0,), (0,)), ((), ())), preferred_element_type=F32)


def padded_bytes(shape, dtype):
    size = jnp.dtype(dtype).itemsize
    rows = 8 * (4 // size)
    lead = 1
    for count in shape[:-2]:
        lead *= count
    second = shape[-2] if len(shape) > 1 else 1
    return lead * -(-second // rows) * rows * -(-shape[-1] // 128) * 128 * size


def call(kernel, outs, name, ins_hbm=0, scratch=(), waits=()):
    def run(*operands):
        count = len(operands)
        specs = [pl.BlockSpec(memory_space=pltpu.VMEM)] * (count - ins_hbm)
        specs += [pl.BlockSpec(memory_space=pltpu.HBM)] * ins_hbm
        specs += [pl.BlockSpec(memory_space=pl.ANY)] * len(waits)
        held = [(item.shape, item.dtype) for item in operands[: count - ins_hbm]] + list(outs)
        held += [(item.shape, item.dtype) for item in scratch if item.memory_space == pltpu.VMEM]
        limit = 6 * 1024 * 1024 + sum(padded_bytes(shape, dtype) for shape, dtype in held)

        placed = list(operands)
        for at in range(count - ins_hbm, count):
            placed[at] = pltpu.with_memory_space_constraint(placed[at], pltpu.HBM)

        def body(*refs):
            kernel(*refs[:count], *refs[count + len(waits) :])

        return pl.pallas_call(
            body,
            out_shape=[jax.ShapeDtypeStruct(shape, dtype) for shape, dtype in outs],
            in_specs=specs,
            out_specs=[pl.BlockSpec(memory_space=pltpu.VMEM)] * len(outs),
            scratch_shapes=list(scratch),
            compiler_params=pltpu.CompilerParams(vmem_limit_bytes=limit),
            name=name,
        )(*placed, *waits)

    return run


def gate(value, *waits):
    def body(*refs):
        del refs

    return pl.pallas_call(
        body,
        out_shape=jax.ShapeDtypeStruct(value.shape, value.dtype),
        in_specs=[pl.BlockSpec(memory_space=pl.ANY)] * (1 + len(waits)),
        out_specs=pl.BlockSpec(memory_space=pl.ANY),
        input_output_aliases={0: 0},
        compiler_params=pltpu.CompilerParams(vmem_limit_bytes=1024 * 1024),
    )(value, *waits)


def diagonal(rows):
    return lax.broadcasted_iota(jnp.int32, (rows, 128), 0) == lax.broadcasted_iota(
        jnp.int32, (rows, 128), 1
    )


def row_to_column(row, rows):
    return jnp.sum(
        jnp.where(diagonal(rows), jnp.broadcast_to(row, (rows, 128)), 0.0), axis=1, keepdims=True
    )


def bucket_onehot(block_distance, span):
    lane = lax.broadcasted_iota(jnp.int32, (BUCKETS, 2 * span), 1)
    offset = jnp.where(lane < span, lane, lane - 2 * span)
    bucket = relative_bucket(block_distance * span - offset)
    return bucket == lax.broadcasted_iota(jnp.int32, (BUCKETS, 2 * span), 0)


def pack_kernel(*refs):
    sources, (own_ref, early_ref, later_ref, over_ref, block_ref) = refs[:13], refs[13:18]
    small, tail_ref, sems = refs[18:24], refs[24], refs[25]
    x, memory, segments, owner, valid, wq, wk, wv, wo, wi, wf, gain, dense_gain = sources
    span, slots = x.shape[0], memory.shape[0]
    rows_each, inner = wq.shape
    hidden = wi.shape[1]
    base = span + PAD
    half = pl.ds(pl.multiple_of(lax.axis_index(TENSOR) * inner, 128), inner)
    targets = [
        (memory, small[0]),
        (segments, small[1]),
        (owner, small[2]),
        (valid, small[3]),
        (gain, small[4]),
        (dense_gain, small[5]),
        (x.at[:, half], own_ref.at[slice(0, span), :]),
    ]
    parts = [wq, wk, wv, wo]
    parts += [w.at[:, slice(at, at + inner)] for w in (wi, wf) for at in range(0, hidden, inner)]
    starts = [base + at * rows_each for at in range(4)]
    late = base + 4 * rows_each + PAD
    starts += [late + at * rows_each for at in range(len(parts) - 4)]
    for part, start in zip(parts, starts):
        targets.append((part, own_ref.at[slice(start, start + rows_each), :]))
    copies = [
        pltpu.make_async_copy(source, target, sems.at[i])
        for i, (source, target) in enumerate(targets)
    ]
    for copy in copies:
        copy.start()
    for copy in copies[:6]:
        copy.wait()
    memory, segments, owner, valid, gain, dense_gain = small
    tail_ref[...] = jnp.zeros_like(tail_ref)
    tail_ref[0:slots, :] = memory[...].astype(F32)
    tail_ref[slots : slots + 1, 0:span] = segments[...].astype(F32)
    tail_ref[slots : slots + 1, span : span + slots] = owner[...].astype(F32)
    own_ref[span:base, :] = tail_ref[:, half].astype(BF)
    tail_ref[...] = jnp.zeros_like(tail_ref)
    tail_ref[0:1, 0:rows_each] = gain[...].astype(F32)
    tail_ref[1:2, 0:rows_each] = dense_gain[...].astype(F32)
    tail_ref[2:3, 0:1] = jnp.sum(valid[...].astype(F32), axis=1, keepdims=True)
    own_ref[late - PAD : late, :] = tail_ref[:, 0:inner].astype(BF)
    for copy in copies[6:]:
        copy.wait()
    early_ref[...] = own_ref[0:late, :]
    later_ref[...] = own_ref[late:, :]
    over_ref[...] = own_ref[base:, :]
    block_ref[...] = own_ref[0:base, :]


def split_kernel(two_ref, one_ref, first_ref, block_ref, later_ref):
    rows, first_rows = block_ref.shape[0] // 2, first_ref.shape[0] // 2
    for at, source in enumerate((two_ref, one_ref)):
        block_ref[at * rows : (at + 1) * rows, :] = source[0:rows, :]
        first_ref[at * first_rows : (at + 1) * first_rows, :] = source[rows : rows + first_rows, :]
    later_ref[...] = one_ref[rows + first_rows :, :]


def join_kernel(*refs, block_rows, first_rows):
    near, overs, blocks = refs[0:4], refs[4:6], refs[6:8]
    first_ref, block_ref, joined_ref = refs[8:]
    early_rows = block_rows + first_rows
    block_ref[...] = near[3][0:block_rows, :]
    first_ref[...] = near[3][block_rows:early_rows, :]
    at = 0
    for source, rows in [(piece, early_rows) for piece in near] + [
        (overs[0], first_rows),
        (overs[1], 2 * first_rows),
        (blocks[0], block_rows),
        (blocks[1], 2 * block_rows),
    ]:
        joined_ref[at : at + rows, :] = source[0:rows, :]
        at += rows
    rows = near[0].shape[0] - early_rows
    for source, start in ((near[0], early_rows), (near[1], early_rows), (overs[0], first_rows)):
        joined_ref[at : at + rows, :] = source[start : start + rows, :]
        at += rows


def order_kernel(*refs, rows_each):
    group = lax.axis_index(FSDP) * 8 + lax.axis_index(CONTEXT)
    target = refs[12]
    width = refs[0].shape[1]
    rows = target.shape[1] // width * rows_each
    for p in range(16):
        start = pl.ds(pl.multiple_of((group ^ p) * rows_each, 16), rows_each)
        at = (p >> 1 & 1) + 2 * (p >> 2 & 1) + 4 * (p >> 3)
        source = refs[(0, 0, 1, 2, 0, 3, 4, 5)[at] + 6 * (p & 1)]
        base = source.shape[0] - 3 * rows
        row = (base, base + rows, 0, 0, base + 2 * rows, 0, 0, 0)[at]
        for col in range(target.shape[1] // width):
            lines = slice(row + col * rows_each, row + (col + 1) * rows_each)
            target[start, col * width : (col + 1) * width] = source[lines, :]


def weights_kernel(*refs, rows_each, inner, block_rows):
    w_ref, gains_ref = refs[4:]
    group = lax.axis_index(FSDP) * 8 + lax.axis_index(CONTEXT)
    rows = 4 * rows_each + PAD
    gathered = jnp.zeros((8, gains_ref.shape[1]), F32)
    for p in range(16):
        piece = (p >> 1 & 1) + 2 * (p >> 2 & 1) + 4 * (p >> 3)
        source = refs[2 * (p & 1) + (piece == 7)]
        early = block_rows + rows
        at = piece * early + block_rows
        if piece >= 4:
            at = (4 * early, 4 * early + 2 * rows, 4 * early + rows, 0)[piece - 4]
        start = pl.multiple_of((group ^ p) * rows_each, 16)
        for which in range(4):
            w_ref[pl.ds(start, rows_each), which * inner : (which + 1) * inner] = source[
                at + which * rows_each : at + (which + 1) * rows_each, :
            ]
        lines = source[at + 4 * rows_each : at + rows, :].astype(F32)[0:8, :]
        lines = jnp.concatenate([lines, jnp.zeros_like(lines)], axis=1)
        gathered = gathered + pltpu.roll(lines, (group ^ p) * rows_each, 1)
    row_ids = lax.broadcasted_iota(jnp.int32, gathered.shape, 0)
    count = jnp.sum(gathered[2:3, :])
    gains_ref[...] = jnp.where(row_ids == 2, count, gathered)


def bias_kernel(bias_ref, toep_ref, *, span):
    for e in range(5):
        table = dot_nn(bias_ref[...], jnp.where(bucket_onehot(e - 2, span), 1.0, 0.0).astype(BF))
        for h in range(bias_ref.shape[0]):
            line = jnp.broadcast_to(table[h : h + 1, :], (span, 2 * span))
            if abs(e - 2) < 2:
                line = pltpu.roll(line, 0, 1, stride=1, stride_axis=0)
            toep_ref[h, e] = line[:, :span]


def project_kernel(*refs, span, slots, tokens, inner, first_rows):
    w_ref, gains_ref = refs[0:2]
    block_refs = refs[2:6]
    (normed_ref, kv_ref, q_ref, mask_ref, whole_ref) = refs[6:]
    block_rows = span + PAD
    early_rows = block_rows + first_rows
    side = lax.axis_index(TENSOR)
    place = lax.axis_index(CONTEXT)
    gain = gains_ref[0:1, :]
    own_docs = None
    for p in range(8):
        block = place ^ p
        piece = (p >> 1 & 1) + 2 * (p >> 2 & 1)
        for far in range(2):
            source = block_refs[2 * (p & 1) + (far and piece == 3)]
            at = piece * early_rows
            if far:
                base = 4 * early_rows + 3 * first_rows
                at = (base, base + 2 * block_rows, base + block_rows, 0)[piece]
            cols = pl.ds(pl.multiple_of((side ^ far) * inner, 128), inner)
            whole_ref[:, cols] = source[at : at + span + PAD, :].astype(F32)
        token_at = pl.multiple_of(block * span, span)
        slot_at = pl.multiple_of(tokens + block * PAD, PAD)
        values = whole_ref[0:span, :]
        scale = lax.rsqrt(jnp.mean(values * values, axis=-1, keepdims=True) + norm_eps)
        normed_ref[pl.ds(token_at, span), :] = (values * scale * gain).astype(BF)
        tail = whole_ref[span : span + PAD, :]
        docs = tail[slots : slots + 1, 0 : 2 * span]
        tail_rows = lax.broadcasted_iota(jnp.int32, tail.shape, 0)
        tail = jnp.where(tail_rows < slots, tail, 0.0)
        scale = lax.rsqrt(jnp.mean(tail * tail, axis=-1, keepdims=True) + norm_eps)
        normed_ref[pl.ds(slot_at, PAD), :] = (tail * scale * gain).astype(BF)
        if p == 0:
            own_docs = docs[:, 0:span]
        token_docs = row_to_column(docs[:, 0:span], span)
        mask_ref[pl.ds(token_at, span), :] = jnp.where(token_docs == own_docs, 0.0, score_floor)
        slot_docs = row_to_column(docs[:, span : 2 * span], PAD)
        slot_rows = lax.broadcasted_iota(jnp.int32, (PAD, 1), 0)
        slot_docs = jnp.where(slot_rows < slots, slot_docs, -1.0)
        mask_ref[pl.ds(slot_at, PAD), :] = jnp.where(slot_docs == own_docs, 0.0, score_floor)
    kv_ref[...] = dot_nn(normed_ref[...], w_ref[:, inner : 3 * inner]).astype(BF)
    own_at = pl.multiple_of(place * span, span)
    q_ref[...] = dot_nn(normed_ref[pl.ds(own_at, span), :], w_ref[:, :inner]).astype(BF)


def attend_kernel(
    w_ref,
    toep_ref,
    kv_ref,
    q_ref,
    mask_ref,
    p_ref,
    low_ref,
    wide_ref,
    part_ref,
    score_ref,
    *,
    span,
    tokens,
    inner,
):
    place = lax.axis_index(CONTEXT)
    lane = lax.broadcasted_iota(jnp.int32, (span, span), 1)
    sub = lax.broadcasted_iota(jnp.int32, (span, span), 0)
    count_blocks = tokens // span
    slot_rows_all = score_ref.shape[0] - tokens
    for t in range(inner // span):
        keys = kv_ref[:, t * span : (t + 1) * span]
        values = kv_ref[:, inner + t * span : inner + (t + 1) * span]
        pair = q_ref[:, t * span : (t + 1) * span]
        zero = jnp.zeros_like(pair)
        both = jnp.concatenate(
            [jnp.where(lane < span // 2, pair, zero), jnp.where(lane < span // 2, zero, pair)], axis=0
        )
        score_ref[...] = dot_nt(keys, both)
        best = jnp.full((1, 2 * span), score_floor, F32)
        for s in range(count_blocks):
            e = jnp.clip(s - place, -2, 2) + 2
            at = slice(s * span, (s + 1) * span)
            terms = jnp.concatenate([toep_ref[2 * t, e], toep_ref[2 * t + 1, e]], axis=1)
            mask = mask_ref[at, :]
            block = score_ref[at, :] + terms + jnp.concatenate([mask, mask], axis=1)
            score_ref[at, :] = block
            best = jnp.maximum(best, jnp.max(block, axis=0, keepdims=True))
        at = slice(tokens, tokens + slot_rows_all)
        mask = mask_ref[at, :]
        block = score_ref[at, :] + jnp.concatenate([mask, mask], axis=1)
        score_ref[at, :] = block
        best = jnp.maximum(best, jnp.max(block, axis=0, keepdims=True))
        total = jnp.zeros((1, 2 * span), F32)
        for s in range(score_ref.shape[0] // span):
            at = slice(s * span, (s + 1) * span)
            weights = jnp.exp(score_ref[at, :] - best)
            score_ref[at, :] = weights
            total = total + jnp.sum(weights, axis=0, keepdims=True)
        inverse = 1.0 / total
        for s in range(score_ref.shape[0] // span):
            at = slice(s * span, (s + 1) * span)
            p_ref[t, at, :] = (score_ref[at, :] * inverse).astype(BF)
        out = dot_tn(values, p_ref[t])
        out = jnp.where(sub < span // 2, out[:, :span], out[:, span:])
        wide_ref[t * span : (t + 1) * span, :] = out
        low_ref[:, t * span : (t + 1) * span] = jnp.transpose(out).astype(BF)
    part_ref[...] = dot_nt(low_ref[...], w_ref[:, 3 * inner :]).astype(BF)


def forward_kernel(
    x_ref,
    own_ref,
    far_ref,
    gains_ref,
    weights_ref,
    residual_ref,
    dense_ref,
    hidden_ref,
    slope_ref,
    part_ref,
):
    hidden = hidden_ref.shape[1]
    residual = x_ref[...].astype(F32) + (own_ref[...].astype(F32) + far_ref[...].astype(F32))
    residual_ref[...] = residual
    scale = lax.rsqrt(jnp.mean(residual * residual, axis=-1, keepdims=True) + norm_eps)
    dense_ref[...] = (residual * scale * gains_ref[1:2, :]).astype(BF)
    step = 256
    for at in range(0, hidden, step):
        pre = dot_nn(dense_ref[...], weights_ref[:, at : at + step])
        square = pre * pre
        root = 0.7978845608028654
        tanh = jnp.tanh(root * (pre + 0.044715 * pre * square))
        hidden_ref[:, at : at + step] = (0.5 * pre * (1.0 + tanh)).astype(BF)
        slope_ref[:, at : at + step] = 0.5 * (1.0 + tanh) + 0.5 * pre * (1.0 - tanh * tanh) * (
            root * (1.0 + 3.0 * 0.044715 * square)
        )
    part_ref[...] = dot_nt(hidden_ref[...], weights_ref[:, hidden:]).astype(BF)


def backward_kernel(
    residual_ref,
    own_ref,
    far_ref,
    teacher_ref,
    valid_ref,
    gains_ref,
    slope_ref,
    weights_ref,
    out_ref,
    grad_ref,
    part_ref,
    loss_ref,
    back_ref,
    pre_ref,
    *,
    total_rows,
):
    hidden = pre_ref.shape[1]
    result = residual_ref[...] + (own_ref[...].astype(F32) + far_ref[...].astype(F32))
    out_ref[...] = result.astype(BF)
    rows = result.shape[0]
    valid = row_to_column(valid_ref[...].astype(F32), rows)
    misfit = result - teacher_ref[...].astype(F32)
    loss = 0.5 * jnp.sum(valid * misfit * misfit)
    loss_ref[...] = jnp.full(loss_ref.shape, loss, F32)
    factor = total_rows / gains_ref[2:3, 0:1]
    grad = factor * valid * misfit
    grad_ref[...] = grad
    back_ref[...] = grad.astype(BF)
    step = 256
    for at in range(0, hidden, step):
        grad_hidden = dot_nn(back_ref[...], weights_ref[:, hidden + at : hidden + at + step])
        pre_ref[:, at : at + step] = (grad_hidden * slope_ref[:, at : at + step]).astype(BF)
    part_ref[...] = dot_nt(pre_ref[...], weights_ref[:, :hidden]).astype(BF)


def split_rows(value, target_ref, rows_each):
    place = lax.axis_index(CONTEXT)
    mine = lax.rem(place, 2)
    half = value.shape[0] // 2
    source = target_ref.at[0]
    source[...] = value
    ordered = target_ref.at[1]
    for g in range(8):
        keep = pl.multiple_of((2 * g + mine) * rows_each, 16)
        send = pl.multiple_of((2 * g + 1 - mine) * rows_each, 16)
        ordered[g * rows_each : (g + 1) * rows_each, :] = source[pl.ds(keep, rows_each), :]
        ordered[half + g * rows_each : half + (g + 1) * rows_each, :] = source[
            pl.ds(send, rows_each), :
        ]


def put_rows(product, start, keep_ref, send_refs):
    rows_each = keep_ref.shape[1]
    cols = slice(start, start + product.shape[1])
    low = product.astype(BF)
    for g in range(8):
        keep_ref[g, :, cols] = low[g * rows_each : (g + 1) * rows_each, :]
        send_ref = send_refs[g * len(send_refs) // 8]
        send_ref[g % send_ref.shape[0], :, cols] = low[(8 + g) * rows_each : (9 + g) * rows_each, :]


def dense_grad_kernel(
    left_ref,
    left_far_ref,
    right_ref,
    right_far_ref,
    next_ref,
    send_ref,
    turned_ref,
    lines_ref,
    *,
    pick,
    rows_each,
):
    mine = lax.rem(lax.axis_index(CONTEXT), 2)
    tokens = left_ref.shape[0]
    for at, source in enumerate((left_ref, left_far_ref)):
        turned = jnp.transpose(source[...].astype(F32)).astype(BF)
        turned_ref[:, at * tokens : (at + 1) * tokens] = turned
    for which in range(2):
        for g in range(4):
            row = pl.multiple_of((2 * pick(which, g) + mine) * rows_each, 16)
            start = (4 * which + g) * rows_each
            lines_ref[start : start + rows_each, :] = turned_ref[pl.ds(row, rows_each), :]
    for at in range(0, right_ref.shape[1], 512):
        cols = slice(at, at + 512)
        right = jnp.concatenate([right_ref[:, cols], right_far_ref[:, cols]], axis=0)
        product = dot_nn(lines_ref[...], right).astype(BF)
        for which, target in enumerate((next_ref, send_ref)):
            for g in range(4):
                start = (4 * which + g) * rows_each
                target[g, :, cols] = product[start : start + rows_each, :]


def attention_back_kernel(
    own_ref,
    far_ref,
    grad_ref,
    residual_ref,
    gains_ref,
    wide_ref,
    p_ref,
    kv_ref,
    q_ref,
    w_ref,
    residual_grad_ref,
    back_ref,
    dq_ref,
    dkv_ref,
    gain_ref,
    small_ref,
    ds_ref,
    diag_ref,
    *,
    inner,
    span,
    tokens,
):
    place = lax.axis_index(CONTEXT)
    incoming = own_ref[...].astype(F32) + far_ref[...].astype(F32)
    residual = residual_ref[...]
    scale = lax.rsqrt(jnp.mean(residual * residual, axis=-1, keepdims=True) + norm_eps)
    scaled = incoming * gains_ref[1:2, :]
    mean = jnp.mean(scaled * residual, axis=-1, keepdims=True)
    residual_grad = grad_ref[...] + (scale * scaled - residual * (scale * scale * scale * mean))
    residual_grad_ref[...] = residual_grad
    gain_ref[...] = jnp.broadcast_to(
        jnp.sum(incoming * residual * scale, axis=0, keepdims=True), gain_ref.shape
    )
    grads = dot_nn(residual_grad.astype(BF), w_ref[:, 3 * inner :])
    back_ref[...] = residual_grad.astype(BF)
    lane = lax.broadcasted_iota(jnp.int32, (span, span), 1)
    sub = lax.broadcasted_iota(jnp.int32, (span, span), 0)
    keys_all = p_ref.shape[1]
    blocks = tokens // span
    small_ref[...] = jnp.zeros_like(small_ref)
    tables = [bucket_onehot(d, span).astype(F32) for d in (-1, 0, 1)]
    zero = jnp.zeros((span, span), BF)
    for t in range(inner // span):
        cols = slice(t * span, (t + 1) * span)
        keys = kv_ref[:, cols]
        values = kv_ref[:, inner + t * span : inner + (t + 1) * span]
        pair = grads[:, cols].astype(BF)
        pair_back = jnp.transpose(pair.astype(F32)) * wide_ref[cols, :]
        delta = jnp.concatenate(
            [
                jnp.sum(pair_back[: span // 2], axis=0, keepdims=True),
                jnp.sum(pair_back[span // 2 :], axis=0, keepdims=True),
            ],
            axis=1,
        )
        grad_both = jnp.concatenate(
            [jnp.where(lane < span // 2, pair, zero), jnp.where(lane < span // 2, zero, pair)], axis=0
        )
        query = q_ref[:, cols]
        query_both = jnp.concatenate(
            [jnp.where(lane < span // 2, query, zero), jnp.where(lane < span // 2, zero, query)],
            axis=0,
        )
        low_sum = jnp.zeros((1, 2 * span), F32)
        high_sum = jnp.zeros((1, 2 * span), F32)
        for s in range(keys_all // span):
            at = slice(s * span, (s + 1) * span)
            dots = dot_nt(values[at, :], grad_both)
            ds = (p_ref[t, at, :].astype(F32) * (dots - delta)).astype(BF)
            ds_ref[at, :] = ds
            if s < blocks:
                line = jnp.sum(ds.astype(F32), axis=0, keepdims=True)
                low_sum = low_sum + jnp.where(s < place - 1, line, 0.0)
                high_sum = high_sum + jnp.where(s > place + 1, line, 0.0)
        dkv_ref[:, cols] = dot_nn(ds_ref[...], query_both).astype(BF)
        dkv_ref[:, inner + t * span : inner + (t + 1) * span] = dot_nn(p_ref[t], grad_both).astype(
            BF
        )
        dq = dot_tn(keys, ds_ref[...])
        dq = jnp.where(sub < span // 2, dq[:, :span], dq[:, span:])
        dq_ref[:, cols] = jnp.transpose(dq).astype(BF)
        for head in range(2):
            for which in range(3):
                s = place + which - 1
                inside = (s >= 0) & (s < blocks)
                start = pl.multiple_of(jnp.clip(s, 0, blocks - 1) * span, span)
                block = ds_ref[pl.ds(start, span), head * span : (head + 1) * span].astype(F32)
                block = jnp.where(inside, block, 0.0)
                block = jnp.concatenate([block, jnp.zeros((span, span), F32)], axis=1)
                size = span
                while size > 8:
                    size = size // 2
                    block = block[:size] + pltpu.roll(block[size:], 2 * span - size, 1)
                line = block[0:1]
                for j in range(1, 8):
                    line = line + pltpu.roll(block, 2 * span - j, 1)[j : j + 1]
                diag_ref[which, 2 * t + head : 2 * t + head + 1, :] = line
            bucket = lax.broadcasted_iota(jnp.int32, (1, 128), 1)
            part = slice(head * span, (head + 1) * span)
            low_total = jnp.sum(low_sum[:, part], axis=1, keepdims=True)
            high_total = jnp.sum(high_sum[:, part], axis=1, keepdims=True)
            small_ref[2 * t + head : 2 * t + head + 1, :] = jnp.where(
                bucket == BUCKETS // 2 - 1, low_total, 0.0
            ) + jnp.where(bucket == BUCKETS - 1, high_total, 0.0)
    heads = inner * 2 // span
    for which in range(3):
        line = lax.dot_general(
            diag_ref[which],
            tables[which],
            (((1,), (1,)), ((), ())),
            preferred_element_type=F32,
            precision=lax.Precision.HIGHEST,
        )
        small_ref[0:heads, 0:BUCKETS] += line[0:heads, :]


def rows_grad_kernel(
    dq_ref,
    dkv_ref,
    w_ref,
    normed_ref,
    gains_ref,
    dense_gain_ref,
    small_ref,
    loss_ref,
    keep_ref,
    *refs,
    inner,
    span,
    tokens,
    slots,
    heads,
):
    send_refs, (part_ref, line_ref) = refs[:-2], refs[-2:]
    place = lax.axis_index(CONTEXT)
    mine = lax.rem(place, 2)
    side = lax.axis_index(TENSOR)
    part_ref[...] = dot_nt(dkv_ref[...], w_ref[:, inner : 3 * inner])
    own_at = pl.multiple_of(place * span, span)
    part_ref[pl.ds(own_at, span), :] += dot_nt(dq_ref[...], w_ref[:, :inner])
    total = jnp.zeros((1, part_ref.shape[1]), F32)
    for s in range(part_ref.shape[0] // span):
        at = slice(s * span, (s + 1) * span)
        total = total + jnp.sum(
            part_ref[at, :] * normed_ref[at, :].astype(F32), axis=0, keepdims=True
        )
    line_ref[...] = jnp.zeros_like(line_ref)
    line_ref[slots : slots + 1, :] = total / gains_ref[0:1, :]
    line_ref[slots + 1 : slots + 2, :] = 0.5 * dense_gain_ref[0:1, :]
    for h in range(heads):
        start = pl.multiple_of(side * 128, 128)
        line_ref[slots + 2 + h : slots + 3 + h, pl.ds(start, 128)] = small_ref[h : h + 1, :]
    line_ref[slots + 2 : slots + 3, 256:384] = 0.5 * loss_ref[0:1, :]
    keep_rows = lax.broadcasted_iota(jnp.int32, line_ref.shape, 0) < slots
    for g in range(4):
        for target, block in (
            (keep_ref.at[g], 2 * g + mine),
            (send_refs[g // 2].at[g % 2], 2 * g + 1 - mine),
        ):
            token_at = pl.multiple_of(block * span, span)
            slot_at = pl.multiple_of(tokens + block * PAD, PAD)
            target[0:span, :] = part_ref[pl.ds(token_at, span), :].astype(BF)
            tail = jnp.where(keep_rows, part_ref[pl.ds(slot_at, PAD), :], line_ref[...])
            target[span : span + PAD, :] = tail.astype(BF)


def weight_grad_kernel(
    dq_ref,
    dkv_ref,
    normed_ref,
    back_ref,
    low_ref,
    keep_ref,
    *refs,
    inner,
    span,
    rows_each,
):
    send_refs, (wide_ref, line_ref) = refs[:-2], refs[-2:]
    place = lax.axis_index(CONTEXT)

    def put(product, start):
        put_rows(product, start, keep_ref, send_refs)

    split_rows(jnp.transpose(back_ref[...].astype(F32)).astype(BF), line_ref, rows_each)
    put(dot_nn(line_ref[1], low_ref[...]), 3 * inner)
    own_at = pl.multiple_of(place * span, span)
    own = normed_ref[pl.ds(own_at, span), :].astype(F32)
    split_rows(jnp.transpose(own).astype(BF), line_ref, rows_each)
    put(dot_nn(line_ref[1], dq_ref[...]), 0)
    split_rows(jnp.transpose(normed_ref[...].astype(F32)).astype(BF), wide_ref, rows_each)
    for at in range(0, 2 * inner, 256):
        put(dot_nn(wide_ref[1], dkv_ref[:, at : at + 256]), inner + at)


def halve_kernel(*refs, counts):
    targets = refs[-2:]
    mine = lax.axis_index(FSDP)
    sources, at = [], 0
    for count in counts:
        sources.append((refs[at], refs[at + 1 : at + 1 + count]))
        at += 1 + count
    for flip in range(2):

        @pl.when(mine == flip)
        def _():
            start = 0
            for keep_ref, far_refs in sources:
                width = keep_ref.shape[2]
                for g in range(8):
                    far = far_refs[g * len(far_refs) // 8][g % far_refs[0].shape[0]]
                    sums = keep_ref[g].astype(F32) + far.astype(F32)
                    targets[(g // 4) ^ flip][g % 4, :, start : start + width] = sums.astype(BF)
                start += width


def turn_kernel(keep_ref, far_ref, next_ref, send_ref, *, pick):
    for which, target in enumerate((next_ref, send_ref)):
        for g in range(max(1, keep_ref.shape[0] // 2)):
            block = pick(which, g)
            sums = keep_ref[block].astype(F32) + far_ref[block].astype(F32)
            if len(target.shape) == 2:
                target[...] = sums.astype(target.dtype)
            else:
                target[g] = sums.astype(target.dtype)


def pick_z1(which, g):
    return (g // 2) * 4 + (lax.axis_index(CONTEXT) // 2 ^ (which + 2 * (g % 2)))


def pick_half(which, g):
    return 4 * (lax.axis_index(FSDP) ^ which) + g


def pick_z2(which, g):
    return 2 * g + which


def pick_x(which, g):
    return lax.axis_index(FSDP) ^ which


def quarter_kernel(keep_ref, far_ref, next_ref, send_ref):
    place = lax.axis_index(CONTEXT) // 2
    for target, flip in ((next_ref, 0), (send_ref, 1)):
        for g in range(2):
            block = place ^ (flip + 2 * g)
            total = keep_ref[block].astype(F32) + far_ref[block].astype(F32)
            target[g] = total.astype(BF)


def eighth_kernel(keep_ref, far_ref, own_ref, send_ref):
    own_ref[...] = (keep_ref[0].astype(F32) + far_ref[0].astype(F32)).astype(own_ref.dtype)
    send_ref[...] = (keep_ref[1].astype(F32) + far_ref[1].astype(F32)).astype(BF)


def total_kernel(own_ref, far_ref, token_ref, *out_refs):
    token_ref[...] = jnp.zeros_like(token_ref)
    at = 0
    for out in out_refs:
        cols = slice(at, at + out.shape[1])
        out[...] = (own_ref[:, cols].astype(F32) + far_ref[:, cols].astype(F32)).astype(out.dtype)
        at += out.shape[1]


def columns_kernel(keep_ref, one_ref, two_ref, next_ref, send_ref):
    mine = lax.axis_index(TENSOR)
    width = next_ref.shape[2]
    for target, start in ((next_ref, mine * width), (send_ref, (1 - mine) * width)):
        cols = pl.ds(pl.multiple_of(start, 128), width)
        for half, far_ref in ((slice(0, 2), one_ref), (slice(2, 4), two_ref)):
            total = keep_ref[half, :, cols].astype(F32) + far_ref[:, :, cols].astype(F32)
            target[half] = total.astype(BF)


def tail_kernel(own_ref, far_ref, out_ref, *, span):
    mine = lax.axis_index(TENSOR)
    width = own_ref.shape[1]
    rows = slice(span, span + PAD)
    out_ref[:, pl.ds(pl.multiple_of(mine * width, 128), width)] = own_ref[rows, :].astype(F32)
    out_ref[:, pl.ds(pl.multiple_of((1 - mine) * width, 128), width)] = far_ref[rows, :].astype(F32)


def finish_kernel(
    own_ref,
    far_ref,
    x_ref,
    slots_ref,
    gains_ref,
    residual_grad_ref,
    tail_far_ref,
    inputs_ref,
    memory_ref,
    gain_ref,
    dense_gain_ref,
    bias_ref,
    loss_ref,
    full_ref,
    line_ref,
    *,
    span,
    slots,
):
    mine = lax.axis_index(TENSOR)
    group = lax.axis_index(FSDP) * 8 + lax.axis_index(CONTEXT)
    width = own_ref.shape[1]
    full_ref[:, pl.ds(pl.multiple_of(mine * width, 128), width)] = own_ref[...].astype(F32)
    full_ref[:, pl.ds(pl.multiple_of((1 - mine) * width, 128), width)] = far_ref[...].astype(F32)
    for source, target, start, extra in (
        (x_ref, inputs_ref, 0, residual_grad_ref),
        (slots_ref, memory_ref, span, None),
    ):
        values = source[...].astype(F32)
        scale = lax.rsqrt(jnp.mean(values * values, axis=-1, keepdims=True) + norm_eps)
        scaled = full_ref[start : start + values.shape[0], :] * gains_ref[0:1, :]
        mean = jnp.mean(scaled * values, axis=-1, keepdims=True)
        back = scale * scaled - values * (scale * scale * scale * mean)
        if extra is None:
            target[:, 0, :] = back
        else:
            target[...] = extra[...] + back
    line_ref[...] = full_ref[span : span + PAD, :] + tail_far_ref[...]
    lines = pltpu.roll(line_ref[...], full_ref.shape[1] - group * gain_ref.shape[1], 1)
    rows_each = gain_ref.shape[1]
    gain_ref[...] = lines[slots : slots + 1, 0:rows_each]
    dense_gain_ref[...] = lines[slots + 1 : slots + 2, 0:rows_each]
    heads = bias_ref.shape[0]
    start = pl.multiple_of(mine * 128, 128)
    bias_ref[...] = line_ref[slots + 2 : slots + 2 + heads, pl.ds(start, 128)][:, 0:BUCKETS]
    loss_ref[...] = line_ref[slots + 2 : slots + 3, 256:384] / (
        gains_ref[2:3, 0:128] * full_ref.shape[1]
    )


def fast_local(
    inputs,
    memory,
    teacher,
    segments,
    memory_owner,
    valid_mask,
    attention_gain,
    query_weight,
    key_weight,
    value_weight,
    attention_out_weight,
    position_bias,
    feedforward_gain,
    inner_weight,
    feedforward_out_weight,
):
    span, width = inputs.shape[1:]
    slots = memory.shape[1]
    rows_each, inner = query_weight.shape
    hidden = inner_weight.shape[1]
    heads = position_bias.shape[0]
    tokens = 8 * span
    keys_all = 8 * (span + PAD)
    total_rows = 2 * tokens
    x = inputs[0]
    block_rows = span + PAD
    first_rows = 4 * rows_each + PAD
    early_rows = block_rows + first_rows
    later_rows = 2 * hidden // inner * rows_each
    own, early, later, over, block = call(
        pack_kernel,
        [
            ((early_rows + later_rows, inner), BF),
            ((early_rows, inner), BF),
            ((later_rows, inner), BF),
            ((first_rows + later_rows, inner), BF),
            ((block_rows, inner), BF),
        ],
        name="pack",
        ins_hbm=13,
        scratch=(
            pltpu.VMEM((slots, width), BF),
            pltpu.VMEM((1, span), jnp.int32),
            pltpu.VMEM((1, slots), jnp.int32),
            pltpu.VMEM((1, span), jnp.int32),
            pltpu.VMEM((1, rows_each), BF),
            pltpu.VMEM((1, rows_each), BF),
            pltpu.VMEM((PAD, width), F32),
            pltpu.SemaphoreType.DMA((7 + 4 + 2 * hidden // inner,)),
        ),
    )(
        x,
        memory[0],
        segments,
        memory_owner,
        valid_mask,
        query_weight,
        key_weight,
        value_weight,
        attention_out_weight,
        inner_weight,
        feedforward_out_weight,
        attention_gain[None],
        feedforward_gain[None],
    )

    (toeplitz,) = call(
        lambda *refs: bias_kernel(*refs, span=span),
        [((heads, 5, span, span), F32)],
        name="bias",
        waits=(early,),
    )(position_bias)
    two = swap_context(early, 4)
    one = swap_context(own, 2)
    over_own = swap_fsdp(over)
    block_own = swap_tensor(block)
    first_pair, block_pair, later_one = call(
        split_kernel,
        [
            ((2 * first_rows, inner), BF),
            ((2 * block_rows, inner), BF),
            ((later_rows, inner), BF),
        ],
        name="split",
        waits=(over_own, block_own, toeplitz),
    )(two, one)
    three = swap_context(two, 2)
    over_pair = swap_fsdp(first_pair)
    block_pair = swap_tensor(block_pair)
    later_two = swap_context(gate(later, first_pair), 4)
    over_one = swap_fsdp(later_one)
    first_last, block_last, joined = call(
        lambda *refs: join_kernel(*refs, block_rows=block_rows, first_rows=first_rows),
        [
            ((first_rows, inner), BF),
            ((block_rows, inner), BF),
            ((4 * early_rows + 3 * (first_rows + block_rows + later_rows), inner), BF),
        ],
        name="join",
        waits=(later_two, over_one),
    )(own, one, two, three, over_own, over_pair, block_own, block_pair)
    over_last = swap_fsdp(first_last)
    block_last = swap_tensor(block_last)
    later_three = swap_context(later_two, 2)
    over_two = swap_fsdp(later_two)
    joined_core, over_core, block_core = swap_core([joined, over_last, block_last])
    w_all, gains = call(
        lambda *refs: weights_kernel(
            *refs, rows_each=rows_each, inner=inner, block_rows=block_rows
        ),
        [((width, 4 * inner), BF), ((8, width), F32)],
        name="weights",
    )(joined, over_last, joined_core, over_core)
    (normed, kv, queries, mask) = call(
        lambda *refs: project_kernel(
            *refs, span=span, slots=slots, tokens=tokens, inner=inner, first_rows=first_rows
        ),
        [
            ((keys_all, width), BF),
            ((keys_all, 2 * inner), BF),
            ((span, inner), BF),
            ((keys_all, span), F32),
        ],
        name="project",
        scratch=(pltpu.VMEM((span + PAD, width), F32),),
        waits=(later_three,),
    )(w_all, gains, joined, block_last, joined_core, block_core)
    (probs, low, wide, part) = call(
        lambda *refs: attend_kernel(*refs, span=span, tokens=tokens, inner=inner),
        [
            ((inner // span, keys_all, 2 * span), BF),
            ((span, inner), BF),
            ((inner, span), F32),
            ((span, width), BF),
        ],
        name="attend",
        scratch=(pltpu.VMEM((keys_all, 2 * span), F32),),
        waits=(over_two,),
    )(w_all, toeplitz, kv, queries, mask)
    far = swap_tensor(part)
    over_three = gate(swap_fsdp(later_three), far)
    later_all = [later_two, later_three, over_one, over_two]
    later_all = [gate(piece, part) for piece in later_all] + [over_three]
    (dense_weights,) = call(
        lambda *refs: order_kernel(*refs, rows_each=rows_each),
        [((width, 2 * hidden), BF)],
        name="order",
        waits=(part,),
    )(joined, *later_all, joined_core, *swap_core(later_all))
    (residual, dense_low, hidden_low, slope, dense_part) = call(
        forward_kernel,
        [
            ((span, width), F32),
            ((span, width), BF),
            ((span, hidden), BF),
            ((span, hidden), F32),
            ((span, width), BF),
        ],
        name="forward",
    )(x, part, far, gains, dense_weights)
    dense_far = swap_tensor(dense_part)
    hidden_far, dense_low_far = swap_core([hidden_low, dense_low])
    (output, grad_result, grad_part, loss_part, dense_back, grad_pre) = call(
        lambda *refs: backward_kernel(*refs, total_rows=total_rows),
        [
            ((span, width), BF),
            ((span, width), F32),
            ((span, width), BF),
            ((8, 128), F32),
            ((span, width), BF),
            ((span, hidden), BF),
        ],
        name="backward",
        waits=(hidden_far, dense_low_far),
    )(residual, dense_part, dense_far, teacher[0], valid_mask, gains, slope, dense_weights)
    grad_far = swap_tensor(grad_part)

    def halve(sources, *waits):
        columns = sum(keep.shape[2] for keep, _ in sources)
        return call(
            lambda *refs: halve_kernel(*refs, counts=[len(far) for _, far in sources]),
            [((4, rows_each, columns), BF)] * 2,
            name="halve",
            waits=waits,
        )(*[item for keep, far in sources for item in (keep, *far)])

    def quarter(keep, far_half, *waits):
        rows, columns = keep.shape[1:]
        return call(
            quarter_kernel,
            [((2, rows, columns), BF)] * 2,
            name="quarter",
            waits=waits,
        )(keep, far_half)

    def eighth(keep, far_quarter, own_type, *waits):
        rows, columns = keep.shape[1:]
        return call(
            eighth_kernel,
            [((rows, columns), own_type), ((rows, columns), BF)],
            name="eighth",
            waits=waits,
        )(keep, far_quarter)

    def total(own, far_eighth, outs, *waits):
        outs = [((8, 128), F32), *outs]
        return call(total_kernel, outs, name="total", waits=waits)(own, far_eighth)

    def turn(keep, far_blocks, pick, outs, *waits):
        return call(
            lambda *refs: turn_kernel(*refs, pick=pick), outs, name="turn", waits=waits
        )(keep, far_blocks)

    def outer_blocks(count):
        return ((count, rows_each, hidden), BF)

    def dense_grad(left, left_far, right, right_far, pick, *waits):
        return call(
            lambda *refs: dense_grad_kernel(*refs, pick=pick, rows_each=rows_each),
            [((4, rows_each, hidden), BF)] * 2,
            name="dense_grad",
            scratch=(
                pltpu.VMEM((width, 2 * span), BF),
                pltpu.VMEM((8 * rows_each, 2 * span), BF),
            ),
            waits=waits,
        )(left, left_far, right, right_far)

    dense_back_far, grad_pre_far = swap_core([dense_back, grad_pre])
    outer_next, outer_over = dense_grad(
        dense_back, dense_back_far, hidden_low, hidden_far, pick_z1
    )
    outer_far = swap_context(outer_over, 2)
    inner_next, inner_over = dense_grad(
        dense_low, dense_low_far, grad_pre, grad_pre_far, pick_half, outer_over
    )
    inner_far = swap_fsdp(inner_over)

    (grad_residual, attention_back, dq, dkv, dense_gain_rows, small) = call(
        lambda *refs: attention_back_kernel(*refs, inner=inner, span=span, tokens=tokens),
        [
            ((span, width), F32),
            ((span, width), BF),
            ((span, inner), BF),
            ((keys_all, 2 * inner), BF),
            ((8, width), F32),
            ((8, 128), F32),
        ],
        name="attend_back",
        scratch=(
            pltpu.VMEM((keys_all, 2 * span), BF),
            pltpu.VMEM((3, 8, 2 * span), F32),
        ),
        waits=(inner_over, outer_over),
    )(grad_part, grad_far, grad_result, residual, gains, wide, probs, kv, queries, w_all)

    rows_keep, *rows_send = call(
        lambda *refs: rows_grad_kernel(
            *refs, inner=inner, span=span, tokens=tokens, slots=slots, heads=heads
        ),
        [((4, span + PAD, width), BF)] + [((2, span + PAD, width), BF)] * 2,
        name="rows_grad",
        scratch=(pltpu.VMEM((keys_all, width), F32), pltpu.VMEM((PAD, width), F32)),
    )(dq, dkv, w_all, normed, gains, dense_gain_rows, small, loss_part)
    rows_far = swap_core(rows_send)

    weight_keep, *weight_send = call(
        lambda *refs: weight_grad_kernel(*refs, inner=inner, span=span, rows_each=rows_each),
        [((8, rows_each, 4 * inner), BF)] + [((4, rows_each, 4 * inner), BF)] * 2,
        name="weight_grad",
        scratch=(
            pltpu.VMEM((2, width, keys_all), BF),
            pltpu.VMEM((2, width, span), BF),
        ),
        waits=(rows_send[0],),
    )(dq, dkv, normed, attention_back, low)
    weight_far = swap_core(weight_send)
    outer_next, outer_over = turn(
        outer_next, outer_far, pick_z2, [outer_blocks(2)] * 2, weight_send[0]
    )
    outer_far = swap_context(outer_over, 4)
    inner_next, inner_over = quarter(inner_next, inner_far, outer_over)
    inner_far = swap_context(inner_over, 2)
    weight_next, weight_over = halve([(weight_keep, weight_far)], inner_over)
    weight_far = swap_fsdp(weight_over)
    rows_next, rows_over = call(
        columns_kernel,
        [((4, span + PAD, width // 2), BF)] * 2,
        name="columns",
        waits=(weight_over,),
    )(rows_keep, *rows_far)
    rows_far = swap_tensor(rows_over)

    rows_next, rows_over = quarter(rows_next, rows_far)
    rows_far = swap_context(rows_over, 2)
    inner_own, inner_over = eighth(inner_next, inner_far, F32, rows_over)
    inner_far = swap_context(inner_over, 4)
    outer_own, outer_over = turn(
        outer_next,
        outer_far,
        pick_x,
        [((rows_each, hidden), F32), ((rows_each, hidden), BF)],
        inner_over,
    )
    outer_far = swap_fsdp(outer_over)
    weight_next, weight_over = quarter(weight_next, weight_far, outer_over)
    weight_far = swap_context(weight_over, 2)

    rows_own, rows_over = eighth(rows_next, rows_far, BF, weight_over)
    rows_far = swap_context(rows_over, 4)
    token, grad_outer = total(outer_own, outer_far, [((rows_each, hidden), F32)], rows_over)
    token, grad_inner = total(inner_own, inner_far, [((rows_each, hidden), F32)], token)
    token, rows_half = total(rows_own, rows_far, [((span + PAD, width // 2), BF)], token)
    weight_own, weight_over = eighth(weight_next, weight_far, F32, token)
    weight_far = swap_context(weight_over, 4)
    rows_other = swap_tensor(rows_half)
    (tail,) = call(
        lambda *refs: tail_kernel(*refs, span=span), [((PAD, width), F32)], name="tail"
    )(rows_half, rows_other)
    tail_far = swap_fsdp(tail)
    *rest, grad_output = total(weight_own, weight_far, [((rows_each, inner), F32)] * 4, tail)
    weight_grads = rest[1:]
    (grad_inputs, grad_memory, grad_gain, grad_dense_gain, grad_bias, loss) = call(
        lambda *refs: finish_kernel(*refs, span=span, slots=slots),
        [
            ((span, width), F32),
            ((slots, 1, width), F32),
            ((1, rows_each), F32),
            ((1, rows_each), F32),
            ((heads, BUCKETS), F32),
            ((1, 128), F32),
        ],
        name="finish",
        scratch=(pltpu.VMEM((span + PAD, width), F32), pltpu.VMEM((PAD, width), F32)),
    )(rows_half, rows_other, x, memory[0], gains, grad_residual, tail_far)
    return (
        loss[0, 0],
        output[None],
        grad_inputs[None],
        jnp.swapaxes(grad_memory, 0, 1),
        grad_gain[0],
        weight_grads[0],
        weight_grads[1],
        weight_grads[2],
        grad_output,
        grad_bias,
        grad_dense_gain[0],
        grad_inner,
        grad_outer,
    )


def solution(mesh):
    return jax.shard_map(
        fast_local if fits(mesh) else general_local,
        mesh=mesh,
        in_specs=(
            P(FSDP, CONTEXT, None),
            P(FSDP, CONTEXT, None),
            P(FSDP, CONTEXT, None),
            P(FSDP, CONTEXT),
            P(FSDP, CONTEXT),
            P(FSDP, CONTEXT),
            P(ROWS),
            P(ROWS, TENSOR),
            P(ROWS, TENSOR),
            P(ROWS, TENSOR),
            P(ROWS, TENSOR),
            P(TENSOR, None),
            P(ROWS),
            P(ROWS, TENSOR),
            P(ROWS, TENSOR),
        ),
        out_specs=(
            P(),
            P(FSDP, CONTEXT, None),
            P(FSDP, CONTEXT, None),
            P(FSDP, CONTEXT, None),
            P(ROWS),
            P(ROWS, TENSOR),
            P(ROWS, TENSOR),
            P(ROWS, TENSOR),
            P(ROWS, TENSOR),
            P(TENSOR, None),
            P(ROWS),
            P(ROWS, TENSOR),
            P(ROWS, TENSOR),
        ),
        check_vma=False,
    )
```
